32 devices in a mesh: dp: 16 (over z, y, x), tensor: 2 (over core).
Axes of the slice: x: 2, y: 2, z: 4, core: 2. Of those that a mesh axis runs over, the one named last changes fastest.
Arguments:
- incoming_embeddings: bfloat16 [16, 1024, 1024], P('dp', 'tensor'), may hold values from -6 to 6
- text_boundary_indicators: int32 [16, 1024], P('dp', 'tensor'), may hold values from 0 to 1, as said below
- upstream_sensitivity: bfloat16 [16, 1024, 1024], P('dp', 'tensor'), may hold values from -6 to 6
- primary_standardize_scaling: bfloat16 [1024], P(('dp', 'tensor')), may hold values from 0.5 to 1.5
- primary_standardize_offset: bfloat16 [1024], P(('dp', 'tensor')), may hold values from -1 to 1
- secondary_standardize_scaling: bfloat16 [1024], P(('dp', 'tensor')), may hold values from 0.5 to 1.5
- secondary_standardize_offset: bfloat16 [1024], P(('dp', 'tensor')), may hold values from -1 to 1
- feature_fading_logarithms: bfloat16 [1024], P(('dp', 'tensor')), may hold values from -8.6 to -3.2
- present_symbol_reward: bfloat16 [1024], P(('dp', 'tensor')), may hold values from -1 to 1
- timemix_lookup_blend: bfloat16 [1024], P(('dp', 'tensor')), may hold values from 0 to 1
- timemix_payload_blend: bfloat16 [1024], P(('dp', 'tensor')), may hold values from 0 to 1
- timemix_gate_blend: bfloat16 [1024], P(('dp', 'tensor')), may hold values from 0 to 1
- timemix_lookup_proj: bfloat16 [1024, 1024], P(('dp', 'tensor')), may hold values from -0.1875 to 0.1875
- timemix_payload_proj: bfloat16 [1024, 1024], P(('dp', 'tensor')), may hold values from -0.1875 to 0.1875
- timemix_gate_proj: bfloat16 [1024, 1024], P(('dp', 'tensor')), may hold values from -0.1875 to 0.1875
- timemix_emit_proj: bfloat16 [1024, 1024], P(('dp', 'tensor')), may hold values from -1.5 to 1.5
- feedmix_lookup_blend: bfloat16 [1024], P(('dp', 'tensor')), may hold values from 0 to 1
- feedmix_gate_blend: bfloat16 [1024], P(('dp', 'tensor')), may hold values from 0 to 1
- feedmix_gate_proj: bfloat16 [1024, 1024], P(('dp', 'tensor')), may hold values from -0.1875 to 0.1875
- feedmix_lookup_proj: bfloat16 [1024, 4096], P('dp', 'tensor'), may hold values from -0.1875 to 0.1875
- feedmix_payload_proj: bfloat16 [4096, 1024], P('tensor', 'dp'), may hold values from -0.09375 to 0.09375
Outputs:
- layer_out: bfloat16 [16, 1024, 1024], P('dp', 'tensor')
- grad_tokens: float32 [16, 1024, 1024], P('dp', 'tensor')
- grad_ln1_gain: float32 [1024], P(('dp', 'tensor'))
- grad_ln1_bias: float32 [1024], P(('dp', 'tensor'))
- grad_ln2_gain: float32 [1024], P(('dp', 'tensor'))
- grad_ln2_bias: float32 [1024], P(('dp', 'tensor'))
- grad_time_decay: float32 [1024], P(('dp', 'tensor'))
- grad_time_bonus: float32 [1024], P(('dp', 'tensor'))
- grad_att_mix_k: float32 [1024], P(('dp', 'tensor'))
- grad_att_mix_v: float32 [1024], P(('dp', 'tensor'))
- grad_att_mix_r: float32 [1024], P(('dp', 'tensor'))
- grad_att_key: float32 [1024, 1024], P(('dp', 'tensor'))
- grad_att_value: float32 [1024, 1024], P(('dp', 'tensor'))
- grad_att_recept: float32 [1024, 1024], P(('dp', 'tensor'))
- grad_att_out: float32 [1024, 1024], P(('dp', 'tensor'))
- grad_ffn_mix_k: float32 [1024], P(('dp', 'tensor'))
- grad_ffn_mix_r: float32 [1024], P(('dp', 'tensor'))
- grad_ffn_recept: float32 [1024, 1024], P(('dp', 'tensor'))
- grad_ffn_key: float32 [1024, 4096], P('dp', 'tensor')
- grad_ffn_value: float32 [4096, 1024], P('tensor', 'dp')
The draws below stay inside these ranges and needn't reach their ends.
Inputs may be any that keep to these rules, and one draw needn't show every extreme that they name: `text_boundary_indicators`: position 0 of every row is a document start, and each row has at most 3 further starts.
All inputs are finite; a program needn't handle non-finite values.
Results may differ from the reference program's by a relative error of at most 0.02.
Values may be sent and summed in bfloat16 or wider, within the bound.
A program may use at most 192 MiB of HBM per device.

```python
import math
import jax
import jax.numpy as jnp
from jax import lax

EMBED_SIZE = 1024
FF = 4096
SEQ = 1024
ROWS = 16


def draw_text_boundary_indicators(key, part):
    starts = jax.random.randint(key, (ROWS, 3), 1, SEQ)
    places = jnp.arange(SEQ, dtype=jnp.int32)
    marked = jnp.any(places[None, :, None] == starts[:, None, :], axis=-1) | (places[None, :] == 0)
    return marked.astype(jnp.int32)


def draw_feature_fading_logarithms(key, part):
    pick_key, slow_key, fast_key = jax.random.split(key, 3)
    share = 0.5
    slow_log = jax.random.uniform(slow_key, (EMBED_SIZE,), jnp.float32, math.log(0.0002), math.log(0.0015))
    fast_log = jax.random.uniform(fast_key, (EMBED_SIZE,), jnp.float32, math.log(0.02), math.log(0.04))
    return jnp.where(jax.random.uniform(pick_key, (EMBED_SIZE,), jnp.float32) < share, slow_log, fast_log).astype(jnp.bfloat16)


def block_levels(own_key, extent, cuts, low, high):
    gain, own = 1.0, jax.random.fold_in(own_key, 6)
    for axis_at, parts in cuts:
        draws = jnp.exp(jax.random.uniform(jax.random.fold_in(own, axis_at), (parts,), jnp.float32, low / len(cuts), high / len(cuts)))
        gain = gain * jnp.repeat(draws, extent[axis_at] // parts).reshape([-1 if axis == axis_at else 1 for axis in range(len(extent))])
    return gain


def bell_draw(own_key, shape, scale, limit, cuts=(), kind=jnp.bfloat16):
    entries = jax.random.normal(own_key, shape, jnp.float32) * scale
    if len(cuts) > 0:
        entries = block_levels(own_key, shape, cuts, -0.22, 0.18) * entries
    return jnp.clip(entries, min=-limit, max=limit).astype(kind)


def setup_inputs(seed: int = 0) -> dict:
    splits = jax.random.split(jax.random.key(seed), 22)
    incoming_embeddings = bell_draw(splits[0], (ROWS, SEQ, EMBED_SIZE), 1.0, 6.0, ((0, 16), (1, 2)))
    text_boundary_indicators = draw_text_boundary_indicators(jax.random.fold_in(splits[21], 71), 0)
    upstream_sensitivity = bell_draw(splits[2], (ROWS, SEQ, EMBED_SIZE), 1.0, 6.0, ((0, 16), (1, 2)))
    primary_standardize_scaling = jnp.clip(1.0 + 0.1 * jax.random.normal(splits[3], (EMBED_SIZE,), jnp.float32), 0.5, 1.5).astype(jnp.bfloat16)
    primary_standardize_offset = bell_draw(splits[4], (EMBED_SIZE,), 0.2, 1.0, ((0, 32),))
    secondary_standardize_scaling = jnp.clip(1.0 + 0.1 * jax.random.normal(splits[5], (EMBED_SIZE,), jnp.float32), 0.5, 1.5).astype(jnp.bfloat16)
    secondary_standardize_offset = bell_draw(splits[6], (EMBED_SIZE,), 0.2, 1.0, ((0, 32),))
    feature_fading_logarithms = draw_feature_fading_logarithms(jax.random.fold_in(splits[21], 71), 0)
    present_symbol_reward = jnp.clip(jax.random.uniform(splits[8], (EMBED_SIZE,), jnp.float32, -1.0, 1.0) * block_levels(splits[8], (EMBED_SIZE,), ((0, 32),), -0.4, 0.0), -1.0, 1.0).astype(jnp.bfloat16)
    timemix_lookup_blend = jnp.clip(1.0 * jax.random.uniform(splits[9], (EMBED_SIZE,), jnp.float32) ** block_levels(splits[9], (EMBED_SIZE,), ((0, 32),), -0.2, 0.2), 0.0, 1.0).astype(jnp.bfloat16)
    timemix_payload_blend = jnp.clip(1.0 * jax.random.uniform(splits[10], (EMBED_SIZE,), jnp.float32) ** block_levels(splits[10], (EMBED_SIZE,), ((0, 32),), -0.2, 0.2), 0.0, 1.0).astype(jnp.bfloat16)
    timemix_gate_blend = jnp.clip(1.0 * jax.random.uniform(splits[11], (EMBED_SIZE,), jnp.float32) ** block_levels(splits[11], (EMBED_SIZE,), ((0, 32),), -0.2, 0.2), 0.0, 1.0).astype(jnp.bfloat16)
    timemix_lookup_proj = bell_draw(splits[12], (EMBED_SIZE, EMBED_SIZE), EMBED_SIZE ** -0.5, 0.1875, ((0, 32),))
    timemix_payload_proj = bell_draw(splits[13], (EMBED_SIZE, EMBED_SIZE), EMBED_SIZE ** -0.5, 0.1875, ((0, 32),))
    timemix_gate_proj = bell_draw(splits[14], (EMBED_SIZE, EMBED_SIZE), EMBED_SIZE ** -0.5, 0.1875, ((0, 32),))
    timemix_emit_proj = bell_draw(splits[15], (EMBED_SIZE, EMBED_SIZE), (EMBED_SIZE // 64) ** -0.5, 1.5, ((0, 32),))
    feedmix_lookup_blend = jnp.clip(1.0 * jax.random.uniform(splits[16], (EMBED_SIZE,), jnp.float32) ** block_levels(splits[16], (EMBED_SIZE,), ((0, 32),), -0.2, 0.2), 0.0, 1.0).astype(jnp.bfloat16)
    feedmix_gate_blend = jnp.clip(1.0 * jax.random.uniform(splits[17], (EMBED_SIZE,), jnp.float32) ** block_levels(splits[17], (EMBED_SIZE,), ((0, 32),), -0.2, 0.2), 0.0, 1.0).astype(jnp.bfloat16)
    feedmix_gate_proj = bell_draw(splits[18], (EMBED_SIZE, EMBED_SIZE), EMBED_SIZE ** -0.5, 0.1875, ((0, 32),))
    feedmix_lookup_proj = bell_draw(splits[19], (EMBED_SIZE, FF), EMBED_SIZE ** -0.5, 0.1875, ((0, 16), (1, 2)))
    feedmix_payload_proj = bell_draw(splits[20], (FF, EMBED_SIZE), FF ** -0.5, 0.09375, ((0, 2), (1, 16)))
    return dict(incoming_embeddings=incoming_embeddings, text_boundary_indicators=text_boundary_indicators, upstream_sensitivity=upstream_sensitivity, primary_standardize_scaling=primary_standardize_scaling, primary_standardize_offset=primary_standardize_offset, secondary_standardize_scaling=secondary_standardize_scaling, secondary_standardize_offset=secondary_standardize_offset, feature_fading_logarithms=feature_fading_logarithms, present_symbol_reward=present_symbol_reward, timemix_lookup_blend=timemix_lookup_blend, timemix_payload_blend=timemix_payload_blend, timemix_gate_blend=timemix_gate_blend, timemix_lookup_proj=timemix_lookup_proj, timemix_payload_proj=timemix_payload_proj, timemix_gate_proj=timemix_gate_proj, timemix_emit_proj=timemix_emit_proj, feedmix_lookup_blend=feedmix_lookup_blend, feedmix_gate_blend=feedmix_gate_blend, feedmix_gate_proj=feedmix_gate_proj, feedmix_lookup_proj=feedmix_lookup_proj, feedmix_payload_proj=feedmix_payload_proj)


@jax.custom_vjp
def low(v):
    return lax.optimization_barrier(v.astype(jnp.bfloat16)).astype(jnp.float32)

@jax.custom_vjp
def low_back(v):
    return v

def low_keep(v):
    return (low(v), None)

def low_pass(kept, grad):
    return (grad,)

def back_keep(v):
    return (v, None)

def back_low(kept, grad):
    return (low(grad),)
low.defvjp(low_keep, low_pass)
low_back.defvjp(back_keep, back_low)

def layer_norm(values, scale_vec, shift_vec):
    center = values - lax.optimization_barrier(jnp.mean(values, axis=-1, keepdims=True))
    spread = lax.optimization_barrier(jnp.mean(center * center, axis=-1, keepdims=True))
    return center * lax.rsqrt(spread + 1e-05) * scale_vec + shift_vec

def shift_prev(values, persist_indicator):
    earlier = jnp.concatenate([jnp.zeros_like(values[:, :1]), values[:, :-1]], axis=1)
    return earlier * persist_indicator[:, :, None]

def project(values, matrix):
    return jnp.einsum('rtd,de->rte', values, matrix, precision=lax.Precision.HIGHEST)

def blended_scan_state(lookup_wide, payload_wide, persist_indicator, fading_power, reward_coords):
    fade_rate = jnp.exp(-jnp.exp(fading_power))

    def advance(state_pair, scanned):
        accrued_dividend_sum, accrued_divisor_sum = state_pair
        lookup_per_moment, payload_per_moment, keep_t = scanned
        accrued_dividend_sum = accrued_dividend_sum * keep_t[:, None]
        accrued_divisor_sum = accrued_divisor_sum * keep_t[:, None]
        reward_multiplier = jnp.exp(reward_coords + lookup_per_moment)
        concluding_answer = (accrued_dividend_sum + reward_multiplier * payload_per_moment) / (accrued_divisor_sum + reward_multiplier)
        key_term = jnp.exp(lookup_per_moment)
        return ((fade_rate * accrued_dividend_sum + key_term * payload_per_moment, fade_rate * accrued_divisor_sum + key_term), concluding_answer)
    initial = jnp.zeros(lookup_wide[:, 0].shape, jnp.float32)
    scanned = (jnp.swapaxes(lookup_wide, 0, 1), jnp.swapaxes(payload_wide, 0, 1), jnp.swapaxes(persist_indicator, 0, 1))
    unused_item, results = lax.scan(jax.checkpoint(advance), (initial, initial), scanned)
    return jnp.swapaxes(results, 0, 1)

def block_forward(inputs, persist_indicator, block_coefficients):
    initial_scaling_coords, initial_offset_coords, later_scaling_coords, later_offset_coords, fading_power, reward_coords, lookup_blend_initial, payload_blend_initial, gate_blend_initial, lookup_coefficients_initial, payload_coefficients_initial, gate_coefficients_initial, emit_coefficients_initial, lookup_blend_later, gate_blend_later, gate_coefficients_later, lookup_coefficients_later, payload_coefficients_later = block_coefficients
    normed_one = layer_norm(inputs, initial_scaling_coords, initial_offset_coords)
    prev_one = shift_prev(normed_one, persist_indicator)
    in_key = low(prev_one + (normed_one - prev_one) * lookup_blend_initial)
    in_value = low(prev_one + (normed_one - prev_one) * payload_blend_initial)
    in_recept = low(prev_one + (normed_one - prev_one) * gate_blend_initial)
    initial_lookup_lines = low_back(project(in_key, lookup_coefficients_initial))
    initial_payload_lines = low_back(project(in_value, payload_coefficients_initial))
    recept_one = low_back(project(in_recept, gate_coefficients_initial))
    blended_mean_state = blended_scan_state(initial_lookup_lines, initial_payload_lines, persist_indicator, fading_power, reward_coords)
    mixed_att = low(jax.nn.sigmoid(recept_one) * blended_mean_state)
    resid_one = inputs + low_back(project(mixed_att, emit_coefficients_initial))
    normed_two = layer_norm(resid_one, later_scaling_coords, later_offset_coords)
    prev_two = shift_prev(normed_two, persist_indicator)
    in_key_two = low(prev_two + (normed_two - prev_two) * lookup_blend_later)
    in_recept_two = low(prev_two + (normed_two - prev_two) * gate_blend_later)
    hidden_pre = low_back(project(in_key_two, lookup_coefficients_later))
    hidden = low(jnp.square(jax.nn.relu(hidden_pre)))
    value_two = low_back(project(hidden, payload_coefficients_later))
    recept_two = low_back(project(in_recept_two, gate_coefficients_later))
    return resid_one + jax.nn.sigmoid(recept_two) * value_two

def reference(incoming_embeddings, text_boundary_indicators, upstream_sensitivity, primary_standardize_scaling, primary_standardize_offset, secondary_standardize_scaling, secondary_standardize_offset, feature_fading_logarithms, present_symbol_reward, timemix_lookup_blend, timemix_payload_blend, timemix_gate_blend, timemix_lookup_proj, timemix_payload_proj, timemix_gate_proj, timemix_emit_proj, feedmix_lookup_blend, feedmix_gate_blend, feedmix_gate_proj, feedmix_lookup_proj, feedmix_payload_proj):
    block_coefficients = tuple((lookup_cell_record.astype(jnp.float32) for lookup_cell_record in (primary_standardize_scaling, primary_standardize_offset, secondary_standardize_scaling, secondary_standardize_offset, feature_fading_logarithms, present_symbol_reward, timemix_lookup_blend, timemix_payload_blend, timemix_gate_blend, timemix_lookup_proj, timemix_payload_proj, timemix_gate_proj, timemix_emit_proj, feedmix_lookup_blend, feedmix_gate_blend, feedmix_gate_proj, feedmix_lookup_proj, feedmix_payload_proj)))
    persist_indicator = (1 - text_boundary_indicators).astype(jnp.float32)
    group_rows = math.gcd(ROWS, 4)
    group_count = ROWS // group_rows

    def regroup(values):
        return values.reshape((group_count, group_rows) + values.shape[1:])

    def visit_group(totals, scanned):
        inputs, keep_group, cot_group = scanned
        concluding_answer, reverse_pass_rule = jax.vjp(lambda first, second: block_forward(first, keep_group, second), inputs, block_coefficients)
        grad_in, grad_params = reverse_pass_rule(cot_group)
        totals = jax.tree.map(jnp.add, totals, grad_params)
        return (totals, (concluding_answer.astype(jnp.bfloat16), grad_in))
    zero_grads = jax.tree.map(jnp.zeros_like, block_coefficients)
    totals, (outputs, grad_inputs) = lax.scan(visit_group, zero_grads, (regroup(incoming_embeddings.astype(jnp.float32)), regroup(persist_indicator), regroup(upstream_sensitivity.astype(jnp.float32))))
    return (outputs.reshape(ROWS, SEQ, EMBED_SIZE), grad_inputs.reshape(ROWS, SEQ, EMBED_SIZE), totals[0], totals[1], totals[2], totals[3], totals[4], totals[5], totals[6], totals[7], totals[8], totals[9], totals[10], totals[11], totals[12], totals[13], totals[14], totals[15], totals[16], totals[17])
```

```python
import functools

import jax
import jax.numpy as jnp
from jax import lax
from jax.experimental import pallas as pl
from jax.experimental.pallas import tpu as pltpu
from jax.sharding import PartitionSpec as P

F32, BF16 = jnp.float32, jnp.bfloat16
MESH_ID = pl.DeviceIdType.MESH
MIB = 1 << 20
PIECES = 13


def place():
    i, c = lax.axis_index("dp"), lax.axis_index("tensor")
    return i // 4, i % 4, c


def neighbours(z, yx):
    x = yx + 1 - 2 * (yx % 2)
    y = (yx + 2) % 4
    d = (x + 2) % 4
    zs = (z + 1 - 2 * (z % 2), (z + 2) % 4, 3 - z)
    return x, y, d, zs


def enter(z, yx, c):
    x, y, d, zs = neighbours(z, yx)
    barrier = pltpu.get_barrier_semaphore()
    targets = [(z * 4 + yx, 1 - c), (z * 4 + x, c), (z * 4 + y, c)]
    targets += [(peer * 4 + yx, c) for peer in zs]
    for target in targets:
        pl.semaphore_signal(barrier, inc=1, device_id=target, device_id_type=MESH_ID)
    pl.semaphore_wait(barrier, len(targets))


def remote(src, dst, send, recv, target):
    return pltpu.make_async_remote_copy(
        src_ref=src, dst_ref=dst, send_sem=send, recv_sem=recv,
        device_id=target, device_id_type=MESH_ID,
    )


class Gather:
    def __init__(self, view, sends, recvs, first=0):
        self.view, self.sends, self.recvs, self.first = view, sends, recvs, first
        self.z, self.yx, self.c = place()
        self.x, self.y, self.d, self.zs = neighbours(self.z, self.yx)

    def to(self, z, yx):
        return (z * 4 + yx, self.c)

    def copy(self, p, k, ref, target):
        return remote(ref, ref, self.sends.at[p, k], self.recvs.at[p, k], target)

    def along(self, p):
        own = self.view(p).at[self.z, self.yx]
        return [self.copy(p, k, own, self.to(peer, self.yx)) for k, peer in enumerate(self.zs)]

    def plane(self, p):
        own = self.view(p).at[:, self.yx]
        return [self.copy(p, 3, own, self.to(self.z, self.x)), self.copy(p, 4, own, self.to(self.z, self.y))]

    def onward(self, p):
        return [
            self.copy(p, 5, self.view(p).at[0:2, self.x], self.to(self.z, self.y)),
            self.copy(p, 6, self.view(p).at[2:4, self.y], self.to(self.z, self.x)),
        ]

    def start(self, copies):
        for copy in copies:
            copy.start()

    def arrive(self, copies):
        for copy in copies:
            copy.wait_recv()

    def step(self, p):
        self.arrive(self.along(p))
        self.start(self.plane(p))

    def forward(self, p):
        self.arrive(self.plane(p))
        self.start(self.onward(p))

    def finish(self, p):
        for copy in self.along(p) + self.plane(p) + self.onward(p):
            copy.wait_send()


def gather_kernel(own4, other4, rest, vec, g, gv, local_sem, ex_send, ex_recv, sends, recvs, vsends, vrecvs):
    z, yx, c = place()
    enter(z, yx, c)
    half = own4.shape[1]
    mine = pl.ds(pl.multiple_of(c * half, half), half)
    partner = (z * 4 + yx, 1 - c)
    swaps = [
        remote(other4, g.at[0:4, z, yx, mine], ex_send.at[0], ex_recv.at[0], partner),
        remote(vec, gv.at[z, yx, c], ex_send.at[1], ex_recv.at[1], partner),
    ]
    locals_ = [
        pltpu.make_async_copy(own4, g.at[0:4, z, yx, mine], local_sem.at[0]),
        pltpu.make_async_copy(rest, g.at[4:PIECES, z, yx], local_sem.at[1]),
        pltpu.make_async_copy(vec, gv.at[z, yx, c], local_sem.at[2]),
    ]
    for copy in swaps + locals_:
        copy.start()
    for copy in swaps + locals_:
        copy.wait()
    weights = Gather(lambda p: g.at[p], sends, recvs)
    vectors = Gather(lambda p: gv, vsends, vrecvs)
    vectors.start(vectors.along(0))

    def launch(p, carry):
        weights.start(weights.along(p))
        return carry

    lax.fori_loop(0, PIECES, launch, 0)
    vectors.step(0)

    def turn(p, carry):
        weights.step(p)

        @pl.when(p > 0)
        def _():
            weights.forward(p - 1)

        return carry

    weights.step(0)
    vectors.forward(0)
    lax.fori_loop(1, PIECES, turn, 0)
    weights.forward(PIECES - 1)

    def close(p, carry):
        weights.arrive(weights.onward(p))
        weights.finish(p)
        return carry

    lax.fori_loop(0, PIECES, close, 0)
    vectors.arrive(vectors.onward(0))
    vectors.finish(0)


def gather_weights(own4, other4, rest, vec):
    any_ = pl.BlockSpec(memory_space=pl.ANY)
    return pl.pallas_call(
        gather_kernel,
        out_shape=(
            jax.ShapeDtypeStruct((PIECES, 4, 4) + rest.shape[1:], BF16),
            jax.ShapeDtypeStruct((4, 4, 2) + vec.shape, BF16),
        ),
        in_specs=[any_] * 4,
        out_specs=(any_, any_),
        scratch_shapes=[
            pltpu.SemaphoreType.DMA((3,)),
            pltpu.SemaphoreType.DMA((2,)),
            pltpu.SemaphoreType.DMA((2,)),
            pltpu.SemaphoreType.DMA((PIECES, 7)),
            pltpu.SemaphoreType.DMA((PIECES, 7)),
            pltpu.SemaphoreType.DMA((1, 7)),
            pltpu.SemaphoreType.DMA((1, 7)),
        ],
        compiler_params=pltpu.CompilerParams(collective_id=0, has_side_effects=True),
        name="gather_weights",
    )(own4, other4, rest, vec)


class Reduce:
    def __init__(self, part, ring1, ring2, line, out, sends, recvs):
        self.part, self.ring1, self.ring2, self.line, self.out = part, ring1, ring2, line, out
        self.sends, self.recvs = sends, recvs
        self.z, self.yx, self.c = place()
        self.x, self.y, self.d, self.zs = neighbours(self.z, self.yx)

    def copy(self, p, k, src, dst, z, yx):
        return remote(src, dst, self.sends.at[p, k], self.recvs.at[p, k], (z * 4 + yx, self.c))

    def diagonal(self, p):
        part, z = self.part.at[p], self.z
        return [
            self.copy(p, 0, part.at[0:2, self.d], self.ring1.at[p, 0], z, self.x),
            self.copy(p, 1, part.at[2:4, self.d], self.ring1.at[p, 1], z, self.y),
        ]

    def side(self, p):
        part, z = self.part.at[p], self.z
        return [
            self.copy(p, 2, part.at[:, self.x], self.ring2.at[p, 0], z, self.x),
            self.copy(p, 3, part.at[:, self.y], self.ring2.at[p, 1], z, self.y),
        ]

    def down(self, p):
        part = self.part.at[p]
        return [
            self.copy(p, 4 + k, part.at[peer, self.yx], self.line.at[p, k], peer, self.yx)
            for k, peer in enumerate(self.zs)
        ]

    def start(self, copies):
        for copy in copies:
            copy.start()

    def arrive(self, copies):
        for copy in copies:
            copy.wait_recv()

    def add(self, p, a, yx, pieces):
        total = self.part[p, a, yx].astype(F32)
        for piece in pieces:
            total = total + piece.astype(F32)
        return total

    def stage1(self, p):
        self.start(self.diagonal(p))

    def stage2(self, p):
        self.arrive(self.diagonal(p))
        for a in range(2):
            self.part[p, a, self.y] = self.add(p, a, self.y, [self.ring1[p, 0, a]]).astype(BF16)
            self.part[p, a + 2, self.x] = self.add(p, a + 2, self.x, [self.ring1[p, 1, a]]).astype(BF16)
        self.start(self.side(p))

    def stage3(self, p):
        self.arrive(self.side(p))
        for a in range(4):
            self.part[p, a, self.yx] = self.add(
                p, a, self.yx, [self.ring2[p, 0, a], self.ring2[p, 1, a]]
            ).astype(BF16)
        self.start(self.down(p))

    def stage4(self, p):
        self.arrive(self.down(p))
        self.out[p] = self.add(p, self.z, self.yx, [self.line[p, k] for k in range(3)])

    def finish(self, p):
        for copy in self.diagonal(p) + self.side(p) + self.down(p):
            copy.wait_send()


def reduce_kernel(
    partial, vec, out, recv4, vout, part, ring1, ring2, line, vbuf, local_sem, sends, recvs, vsends, vrecvs, ex_send, ex_recv
):
    z, yx, c = place()
    x, y, d, zs = neighbours(z, yx)
    enter(z, yx, c)
    sums = Reduce(part, ring1, ring2, line, out, sends, recvs)

    def local(p):
        return pltpu.make_async_copy(partial.at[p], part.at[p], local_sem.at[p])

    def vec_copy(k, target):
        return remote(vout, vbuf.at[k], vsends.at[k], vrecvs.at[k], target)

    vcopies = [
        [vec_copy(0, (z * 4 + yx, 1 - c))],
        [vec_copy(1, (z * 4 + x, c))],
        [vec_copy(2, (z * 4 + y, c))],
        [vec_copy(3 + k, (peer * 4 + yx, c)) for k, peer in enumerate(zs)],
    ]

    vout[...] = vec[...]

    def fetch(p, carry):
        local(p).start()
        return carry

    lax.fori_loop(0, PIECES, fetch, 0)
    for copy in vcopies[0]:
        copy.start()

    def turn(p, carry):
        @pl.when(p < PIECES)
        def _():
            local(p).wait()
            sums.stage1(p)

        @pl.when((p >= 1) & (p < PIECES + 1))
        def _():
            sums.stage2(p - 1)

        @pl.when((p >= 2) & (p < PIECES + 2))
        def _():
            sums.stage3(p - 2)

        @pl.when(p >= 3)
        def _():
            sums.stage4(p - 3)

        return carry

    lax.fori_loop(0, 4, turn, 0)
    at = 4
    for k, copies in enumerate(vcopies):
        for copy in copies:
            copy.wait()
        vout[...] = functools.reduce(
            lambda a, b: a + b, [vbuf[j] for j in ([k] if k < 3 else [3, 4, 5])], vout[...]
        )
        if k + 1 < len(vcopies):
            for copy in vcopies[k + 1]:
                copy.start()
        upto = at + 3 if k + 1 < len(vcopies) else PIECES + 3
        lax.fori_loop(at, upto, turn, 0)
        at = upto
    half = recv4.shape[1]
    others = pl.ds(pl.multiple_of((1 - c) * half, half), half)
    swap = remote(out.at[0:4, others], recv4, ex_send, ex_recv, (z * 4 + yx, 1 - c))
    swap.start()

    def close(p, carry):
        sums.finish(p)
        return carry

    lax.fori_loop(0, PIECES, close, 0)
    swap.wait()


def reduce_weights(partial, vec):
    rows, width = partial.shape[3:]
    any_ = pl.BlockSpec(memory_space=pl.ANY)
    vmem = pl.BlockSpec(memory_space=pltpu.VMEM)
    return pl.pallas_call(
        reduce_kernel,
        out_shape=(
            jax.ShapeDtypeStruct((PIECES, rows, width), F32),
            jax.ShapeDtypeStruct((4, rows // 2, width), F32),
            jax.ShapeDtypeStruct(vec.shape, F32),
        ),
        in_specs=[any_, vmem],
        out_specs=(vmem, vmem, vmem),
        scratch_shapes=[
            pltpu.VMEM((PIECES, 4, 4, rows, width), BF16),
            pltpu.VMEM((PIECES, 2, 2, rows, width), BF16),
            pltpu.VMEM((PIECES, 2, 4, rows, width), BF16),
            pltpu.VMEM((PIECES, 3, rows, width), BF16),
            pltpu.VMEM((6,) + vec.shape, F32),
            pltpu.SemaphoreType.DMA((PIECES,)),
            pltpu.SemaphoreType.DMA((PIECES, 7)),
            pltpu.SemaphoreType.DMA((PIECES, 7)),
            pltpu.SemaphoreType.DMA((6,)),
            pltpu.SemaphoreType.DMA((6,)),
            pltpu.SemaphoreType.DMA,
            pltpu.SemaphoreType.DMA,
        ],
        compiler_params=pltpu.CompilerParams(
            collective_id=1, has_side_effects=True, vmem_limit_bytes=48 * MIB
        ),
        name="reduce_weights",
    )(partial, vec)


def spread(column):
    return jnp.broadcast_to(column[:, None], (column.shape[0], 128)).astype(F32)


def resets(keep):
    length = keep.shape[0]
    place_in = jnp.arange(length) % 8

    def masks(step, inside):
        one = step
        two = one * inside(one, 1)
        four = two * inside(two, 2)
        return one, two, four

    def down(v, n):
        return jnp.concatenate([jnp.zeros_like(v[:n]), v[:-n]])

    def up(v, n):
        return jnp.concatenate([v[n:], jnp.zeros_like(v[:n])])

    f1, f2, f4 = masks(keep, down)
    after = up(keep, 1)
    b1, b2, b4 = masks(after, up)
    grouped = keep.reshape(-1, 8)
    fp = jnp.cumprod(grouped, axis=1).reshape(-1)
    bp = jnp.cumprod(after.reshape(-1, 8)[:, ::-1], axis=1)[:, ::-1].reshape(-1)
    forward = [
        keep,
        jnp.where(place_in >= 1, f1, 0.0),
        jnp.where(place_in >= 2, f2, 0.0),
        jnp.where(place_in >= 4, f4, 0.0),
        fp,
    ]
    backward = [
        after,
        jnp.where(place_in <= 6, b1, 0.0),
        jnp.where(place_in <= 5, b2, 0.0),
        jnp.where(place_in <= 3, b4, 0.0),
        bp,
    ]
    return jnp.stack([spread(m) for m in forward]), jnp.stack([spread(m) for m in backward])


def decay_rows(fading, reward):
    rate = jnp.exp(fading)
    d = jnp.exp(-rate)
    steps = jnp.arange(8, dtype=F32)[:, None]
    rising = jnp.exp(-(steps + 1.0) * rate)
    falling = jnp.exp(-(8.0 - steps) * rate)
    zero = jnp.zeros_like(d)
    head = jnp.stack([d, jnp.exp(-2.0 * rate), jnp.exp(-4.0 * rate), jnp.exp(reward), rate * d, zero, zero, zero])
    return jnp.concatenate([head, rising, falling])


def lanes(j):
    return slice(j * 128, (j + 1) * 128)


def bottom(v):
    return jnp.broadcast_to(v[7:8], v.shape)


def top(v):
    return jnp.broadcast_to(v[0:1], v.shape)


def wkv_forward(k_ref, v_ref, r_ref, masks_ref, rows_ref, mixed_ref, sn_ref, sd_ref):
    length, width = k_ref.shape
    tiles = width // 128
    first = lax.broadcasted_iota(jnp.int32, (8, 128), 0) == 0
    zero = jnp.zeros((8, 128), F32)

    def pair(g, carry):
        carry = list(carry)
        base = pl.multiple_of(g * 16, 16)
        for j in range(tiles):
            d1, d2, d4, eu = (rows_ref[n : n + 1, lanes(j)] for n in range(4))
            dp = rows_ref[8:16, lanes(j)]
            made = []
            for h in range(2):
                at = pl.ds(base + 8 * h, 8)
                keep, m1, m2, m4, mp = (masks_ref[n, at, :] for n in range(5))
                ek = jnp.exp(k_ref[at, lanes(j)])
                v = v_ref[at, lanes(j)]
                num, den = ek * v, ek
                x, b = num, eu * ek
                for n, coef in ((1, m1 * d1), (2, m2 * d2), (4, m4 * d4)):
                    num = num + coef * pltpu.roll(num, n, 0)
                    den = den + coef * pltpu.roll(den, n, 0)
                coef = mp * dp
                cn, cd = carry[2 * j], carry[2 * j + 1]
                num = num + coef * cn
                den = den + coef * cd
                sn = keep * jnp.where(first, cn, pltpu.roll(num, 1, 0))
                sd = keep * jnp.where(first, cd, pltpu.roll(den, 1, 0))
                carry[2 * j], carry[2 * j + 1] = bottom(num), bottom(den)
                sn_ref[at, lanes(j)] = sn
                sd_ref[at, lanes(j)] = sd
                weighted = (sn + eu * x) / (sd + b)
                made.append(jax.nn.sigmoid(r_ref[at, lanes(j)]) * weighted)
            mixed_ref[pl.ds(base, 16), lanes(j)] = jnp.concatenate(made, axis=0).astype(BF16)
        return tuple(carry)

    lax.fori_loop(0, length // 16, pair, (zero,) * (2 * tiles))


def wkv_backward(
    g_ref, k_ref, v_ref, r_ref, sn_ref, sd_ref, masks_ref, rows_ref, gk_ref, gv_ref, gr_ref, sums_ref
):
    length, width = k_ref.shape
    tiles = width // 128
    last = lax.broadcasted_iota(jnp.int32, (8, 128), 0) == 7
    zero = jnp.zeros((8, 128), F32)
    pairs = length // 16

    def pair(step, carry):
        carry = list(carry)
        base = pl.multiple_of((pairs - 1 - step) * 16, 16)
        for j in range(tiles):
            d1, d2, d4, eu = (rows_ref[n : n + 1, lanes(j)] for n in range(4))
            dp = rows_ref[16:24, lanes(j)]
            made = [None, None]
            for h in (1, 0):
                at = pl.ds(base + 8 * h, 8)
                after, m1, m2, m4, mp = (masks_ref[n, at, :] for n in range(5))
                ek = jnp.exp(k_ref[at, lanes(j)])
                v = v_ref[at, lanes(j)]
                sn, sd = sn_ref[at, lanes(j)], sd_ref[at, lanes(j)]
                s = jax.nn.sigmoid(r_ref[at, lanes(j)])
                b = eu * ek
                inverse = 1.0 / (sd + b)
                weighted = (sn + b * v) * inverse
                g = g_ref[at, lanes(j)]
                gs = g * s
                p = gs * inverse
                q = -p * weighted
                gr = gs * weighted * (1.0 - s)
                hp, hq = p, q
                for n, coef in ((1, m1 * d1), (2, m2 * d2), (4, m4 * d4)):
                    hp = hp + coef * pltpu.roll(hp, 8 - n, 0)
                    hq = hq + coef * pltpu.roll(hq, 8 - n, 0)
                coef = mp * dp
                cp, cq = carry[4 * j], carry[4 * j + 1]
                hp = hp + coef * cp
                hq = hq + coef * cq
                ap = after * jnp.where(last, cp, pltpu.roll(hp, 7, 0))
                aq = after * jnp.where(last, cq, pltpu.roll(hq, 7, 0))
                carry[4 * j], carry[4 * j + 1] = top(hp), top(hq)
                bonus = b * (v * p + q)
                gv = ek * ap + b * p
                gk = ek * (v * ap + aq) + bonus
                carry[4 * j + 2] = carry[4 * j + 2] + bonus
                carry[4 * j + 3] = carry[4 * j + 3] + (ap * sn + aq * sd)
                made[h] = (gk, gv, gr)
            both = pl.ds(base, 16)
            for n, ref in enumerate((gk_ref, gv_ref, gr_ref)):
                ref[both, lanes(j)] = jnp.concatenate([made[0][n], made[1][n]], axis=0).astype(BF16)
        return tuple(carry)

    carry = lax.fori_loop(0, pairs, pair, (zero,) * (4 * tiles))
    for j in range(tiles):
        rate_d = rows_ref[4:5, lanes(j)]
        sums_ref[0:1, lanes(j)] = jnp.sum(carry[4 * j + 2], axis=0, keepdims=True)
        sums_ref[1:2, lanes(j)] = -rate_d * jnp.sum(carry[4 * j + 3], axis=0, keepdims=True)


def shifted(value, axis, steps):
    count = lax.axis_size(axis)
    first, last = (max(0, -steps), min(count, count - steps))
    return lax.ppermute(value, axis, [(source, source + steps) for source in range(first, last)])


def carried_in(array, axis, join, neutral):
    place = lax.axis_index(axis)
    gathered = jax.tree.map(
        lambda a, kind: lax.all_gather(a.astype(kind), axis),
        array,
        (jnp.bfloat16, jnp.bfloat16, jnp.bfloat16),
    )
    state = jax.tree.map(lambda a, e: jnp.zeros_like(a) + jnp.asarray(e, a.dtype), array, neutral)

    def one(turn, state):
        return join(
            state,
            jax.tree.map(
                lambda a, own: lax.dynamic_index_in_dim(a, turn, 0, False).astype(own.dtype),
                gathered,
                array,
            ),
        )

    return lax.fori_loop(0, place, one, state)


def entering(array, axis, combine, identity):
    count, place = (lax.axis_size(axis), lax.axis_index(axis))
    everything = jax.tree.map(
        lambda part, kind: lax.all_gather(part.astype(kind), axis),
        array,
        jax.tree.map(lambda a: jnp.bfloat16 if a.dtype == jnp.float32 else a.dtype, array),
    )
    start = jax.tree.map(
        lambda part, zero: jnp.broadcast_to(jnp.asarray(zero, part.dtype), part.shape),
        array,
        identity,
    )

    def turn(k, before):
        at = count - 1 - k
        reached = at > place
        new = combine(
            before, jax.tree.map(lambda part, own: part[at].astype(own.dtype), everything, array)
        )
        return jax.tree.map(lambda a, b: jnp.where(reached, a, b), new, before)

    return lax.fori_loop(0, count, turn, start)


def wide_layer_norm(values, scale_vec, shift_vec):
    center = values - jnp.mean(values, axis=-1, keepdims=True)
    inverse = lax.rsqrt(jnp.mean(center * center, axis=-1, keepdims=True) + 1e-05)
    normed = center * inverse
    return (normed * scale_vec + shift_vec, normed, inverse)


def wide_norm_back(upstream, normed, inverse, scale_vec):
    scaled = upstream * scale_vec
    inner = (
        scaled
        - jnp.mean(scaled, axis=-1, keepdims=True)
        - normed * jnp.mean(scaled * normed, axis=-1, keepdims=True)
    )
    return (
        inverse * inner,
        jnp.sum(upstream * normed, axis=(0, 1)),
        jnp.sum(upstream, axis=(0, 1)),
    )


def shift_prev(values, persist_indicator):
    arrived = shifted(values[:, -1:, :], "tensor", 1)
    return jnp.concatenate([arrived, values[:, :-1]], axis=1) * persist_indicator[:, :, None]


def shift_back(upstream, persist_indicator):
    masked = upstream * persist_indicator[:, :, None]
    arrived = shifted(masked[:, :1, :], "tensor", -1)
    return jnp.concatenate([masked[:, 1:], arrived], axis=1)


def project(values, matrix):
    return jnp.einsum("rtd,de->rte", values, matrix, preferred_element_type=jnp.float32)


def project_back(upstream, matrix):
    return jnp.einsum("rte,de->rtd", upstream, matrix, preferred_element_type=jnp.float32)


def outer_sum(values, upstream):
    return jnp.einsum("rtd,rte->de", values, upstream, preferred_element_type=jnp.float32)


def mix_back(upstreams, shares, differ, persist_indicator):
    toward = jnp.zeros_like(differ)
    behind = jnp.zeros_like(differ)
    share_grads = []
    for upstream, share in zip(upstreams, shares):
        toward = toward + upstream * share
        behind = behind + upstream * (1.0 - share)
        share_grads.append(jnp.sum(upstream * differ, axis=(0, 1)))
    return (toward + shift_back(behind, persist_indicator), share_grads)


def chain_combine(earlier, later):
    return (
        earlier[0] * later[0],
        later[0] * earlier[1] + later[1],
        later[0] * earlier[2] + later[2],
    )


def scan_fragments(
    lookup_wide, payload_wide, fading_power, reward_coords, text_boundary_indicators
):
    decay_rate = jnp.exp(fading_power)
    row_count, span_len, width_len = lookup_wide.shape
    block_len = min(32, span_len)
    block_count = span_len // block_len
    places = jnp.arange(block_len, dtype=jnp.float32)
    rising = jnp.exp(places[:, None] * decay_rate)
    falling = jnp.exp(-(places[:, None] - 1.0) * decay_rate)
    trailing = jnp.exp(-(block_len - 1.0 - places)[:, None] * decay_rate)
    leading = jnp.exp(-places[:, None] * decay_rate)
    settle = jnp.exp(-block_len * decay_rate)
    before = places[:, None] > places[None, :]

    def split_blocks(values):
        return jnp.swapaxes(
            values.reshape((row_count, block_count, block_len) + values.shape[2:]), 0, 1
        )

    def advance(state_pair, scanned):
        accrued_dividend_sum, accrued_divisor_sum = state_pair
        lookup_narrow, payload_narrow, reset_b = scanned
        tree_levels = jnp.cumsum(reset_b, axis=1)
        linked = ((tree_levels[:, :, None] == tree_levels[:, None, :]) & before).astype(jnp.float32)
        key_term = jnp.exp(lookup_narrow)
        keyed_value = key_term * payload_narrow
        inside_numerator = falling * jnp.einsum(
            "rti,rid->rtd", linked, rising * keyed_value, precision=lax.Precision.HIGHEST
        )
        interior_divisor_sum = falling * jnp.einsum(
            "rti,rid->rtd", linked, rising * key_term, precision=lax.Precision.HIGHEST
        )
        leftover_multiplier = (tree_levels == 0).astype(jnp.float32)[:, :, None] * leading
        reward_multiplier = jnp.exp(reward_coords + lookup_narrow)
        above_total = (
            inside_numerator
            + reward_multiplier * payload_narrow
            + leftover_multiplier * accrued_dividend_sum[:, None, :]
        )
        below_total = (
            interior_divisor_sum
            + reward_multiplier
            + leftover_multiplier * accrued_divisor_sum[:, None, :]
        )
        ending = (tree_levels == tree_levels[:, -1:]).astype(jnp.float32)[:, :, None] * trailing
        intact = (tree_levels[:, -1] == 0).astype(jnp.float32)[:, None] * settle
        new_num = intact * accrued_dividend_sum + jnp.sum(ending * keyed_value, axis=1)
        new_den = intact * accrued_divisor_sum + jnp.sum(ending * key_term, axis=1)
        return ((new_num, new_den), (above_total, below_total))

    initial = jnp.zeros((row_count, width_len), jnp.float32)
    (total_num, total_den), (uppers, lowers) = lax.scan(
        advance,
        (initial, initial),
        (
            split_blocks(lookup_wide),
            split_blocks(payload_wide),
            split_blocks(text_boundary_indicators),
        ),
    )

    def join_blocks(values):
        return jnp.swapaxes(values, 0, 1).reshape(row_count, span_len, width_len)

    tree_levels = jnp.cumsum(text_boundary_indicators, axis=1)
    reaching = (tree_levels == 0).astype(jnp.float32)[:, :, None] * jnp.exp(
        -jnp.arange(span_len, dtype=jnp.float32)[:, None] * decay_rate
    )
    passing = (tree_levels[:, -1] == 0).astype(jnp.float32)[:, None] * jnp.exp(
        -span_len * decay_rate
    )
    return (join_blocks(uppers), join_blocks(lowers), reaching, total_num, total_den, passing)


def recurrence_finish(pieces_list, incoming_num, incoming_den):
    above_total = pieces_list[0] + pieces_list[2] * incoming_num[:, None, :]
    below_total = pieces_list[1] + pieces_list[2] * incoming_den[:, None, :]
    return (above_total / below_total, below_total)


def ffn_apply(inputs, key_weight, value_weight):
    hidden_pre = project(inputs, key_weight)
    hidden = jnp.square(jax.nn.relu(hidden_pre)).astype(jnp.bfloat16)
    return (hidden_pre, hidden, project(hidden, value_weight))


def ffn_grads(inputs, hidden_pre, hidden, upstream, key_weight, value_weight):
    g_hidden = jnp.einsum("rtd,fd->rtf", upstream, value_weight, preferred_element_type=jnp.float32)
    grad_value = jnp.einsum("rtf,rtd->fd", hidden, upstream, preferred_element_type=jnp.float32)
    g_pre = (2.0 * jax.nn.relu(hidden_pre) * g_hidden).astype(jnp.bfloat16)
    grad_key = jnp.einsum("rtd,rtf->df", inputs, g_pre, preferred_element_type=jnp.float32)
    g_inputs = jnp.einsum("rtf,df->rtd", g_pre, key_weight, preferred_element_type=jnp.float32)
    return (g_inputs, grad_key, grad_value)


def wide_shards(
    incoming_embeddings,
    text_boundary_indicators,
    upstream_sensitivity,
    primary_standardize_scaling,
    primary_standardize_offset,
    secondary_standardize_scaling,
    secondary_standardize_offset,
    feature_fading_logarithms,
    present_symbol_reward,
    timemix_lookup_blend,
    timemix_payload_blend,
    timemix_gate_blend,
    timemix_lookup_proj,
    timemix_payload_proj,
    timemix_gate_proj,
    timemix_emit_proj,
    feedmix_lookup_blend,
    feedmix_gate_blend,
    feedmix_gate_proj,
    feedmix_lookup_proj,
    feedmix_payload_proj,
):
    gathered_portions = (
        lax.all_gather(primary_standardize_scaling, ("dp", "tensor"), axis=0, tiled=True),
        lax.all_gather(primary_standardize_offset, ("dp", "tensor"), axis=0, tiled=True),
        lax.all_gather(secondary_standardize_scaling, ("dp", "tensor"), axis=0, tiled=True),
        lax.all_gather(secondary_standardize_offset, ("dp", "tensor"), axis=0, tiled=True),
        lax.all_gather(feature_fading_logarithms, ("dp", "tensor"), axis=0, tiled=True),
        lax.all_gather(present_symbol_reward, ("dp", "tensor"), axis=0, tiled=True),
        lax.all_gather(timemix_lookup_blend, ("dp", "tensor"), axis=0, tiled=True),
        lax.all_gather(timemix_payload_blend, ("dp", "tensor"), axis=0, tiled=True),
        lax.all_gather(timemix_gate_blend, ("dp", "tensor"), axis=0, tiled=True),
        lax.all_gather(timemix_lookup_proj, ("dp", "tensor"), axis=0, tiled=True),
        lax.all_gather(timemix_payload_proj, ("dp", "tensor"), axis=0, tiled=True),
        lax.all_gather(timemix_gate_proj, ("dp", "tensor"), axis=0, tiled=True),
        lax.all_gather(timemix_emit_proj, ("dp", "tensor"), axis=0, tiled=True),
        lax.all_gather(feedmix_lookup_blend, ("dp", "tensor"), axis=0, tiled=True),
        lax.all_gather(feedmix_gate_blend, ("dp", "tensor"), axis=0, tiled=True),
        lax.all_gather(feedmix_gate_proj, ("dp", "tensor"), axis=0, tiled=True),
    )
    initial_scaling_coords = gathered_portions[0].astype(jnp.float32)
    initial_offset_coords = gathered_portions[1].astype(jnp.float32)
    later_scaling_coords = gathered_portions[2].astype(jnp.float32)
    later_offset_coords = gathered_portions[3].astype(jnp.float32)
    fading_power = gathered_portions[4].astype(jnp.float32)
    reward_coords = gathered_portions[5].astype(jnp.float32)
    share_k1 = gathered_portions[6].astype(jnp.float32)
    share_v1 = gathered_portions[7].astype(jnp.float32)
    share_r1 = gathered_portions[8].astype(jnp.float32)
    lookup_coefficients_initial = gathered_portions[9]
    payload_coefficients_initial = gathered_portions[10]
    gate_coefficients_initial = gathered_portions[11]
    emit_coefficients_initial = gathered_portions[12]
    share_k2 = gathered_portions[13].astype(jnp.float32)
    share_r2 = gathered_portions[14].astype(jnp.float32)
    gate_coefficients_later = gathered_portions[15]
    lookup_coefficients_later, payload_coefficients_later = (
        lax.all_gather(feedmix_lookup_proj, "dp", axis=0, tiled=True),
        lax.all_gather(feedmix_payload_proj, "dp", axis=1, tiled=True),
    )
    persist_indicator = (1 - text_boundary_indicators).astype(jnp.float32)
    inputs = incoming_embeddings.astype(jnp.float32)
    normed_one, unit_one, inverse_one = wide_layer_norm(
        inputs, initial_scaling_coords, initial_offset_coords
    )
    prev_one = shift_prev(normed_one, persist_indicator)
    differ_one = normed_one - prev_one
    in_key = (prev_one + differ_one * share_k1).astype(jnp.bfloat16)
    in_value = (prev_one + differ_one * share_v1).astype(jnp.bfloat16)
    in_recept = (prev_one + differ_one * share_r1).astype(jnp.bfloat16)
    initial_lookup_lines = project(in_key, lookup_coefficients_initial)
    initial_payload_lines = project(in_value, payload_coefficients_initial)
    recept_one = project(in_recept, gate_coefficients_initial)
    pieces_list = scan_fragments(
        initial_lookup_lines,
        initial_payload_lines,
        fading_power,
        reward_coords,
        text_boundary_indicators,
    )
    passing = pieces_list[5]
    identity = (jnp.ones_like(passing), jnp.zeros_like(passing), jnp.zeros_like(passing))
    unused_item, incoming_num, incoming_den = carried_in(
        (passing, pieces_list[3], pieces_list[4]), "tensor", chain_combine, identity
    )
    blended_mean_state, below_total = recurrence_finish(pieces_list, incoming_num, incoming_den)
    sig_one = jax.nn.sigmoid(recept_one)
    mixed_att = (sig_one * blended_mean_state).astype(jnp.bfloat16)
    resid_one = inputs + project(mixed_att, emit_coefficients_initial)
    normed_two, unit_two, inverse_two = wide_layer_norm(
        resid_one, later_scaling_coords, later_offset_coords
    )
    prev_two = shift_prev(normed_two, persist_indicator)
    differ_two = normed_two - prev_two
    in_key_two = (prev_two + differ_two * share_k2).astype(jnp.bfloat16)
    in_recept_two = (prev_two + differ_two * share_r2).astype(jnp.bfloat16)
    recept_two = project(in_recept_two, gate_coefficients_later)
    sig_two = jax.nn.sigmoid(recept_two)
    row_inputs = lax.all_gather(in_key_two, "tensor", axis=1, tiled=True)
    hidden_pre, hidden, partial_value = ffn_apply(
        row_inputs, lookup_coefficients_later, payload_coefficients_later
    )
    value_two = lax.psum_scatter(
        partial_value.astype(jnp.bfloat16), "tensor", scatter_dimension=1, tiled=True
    ).astype(jnp.float32)
    layer_out = (resid_one + sig_two * value_two).astype(jnp.bfloat16)
    upstream = upstream_sensitivity.astype(jnp.float32)
    g_value_two = (upstream * sig_two).astype(jnp.bfloat16)
    g_recept_two = (upstream * value_two * sig_two * (1.0 - sig_two)).astype(jnp.bfloat16)
    grad_recept_two = outer_sum(in_recept_two, g_recept_two)
    g_mix_r2 = project_back(g_recept_two, gate_coefficients_later)
    row_grads = lax.all_gather(g_value_two, "tensor", axis=1, tiled=True)
    partial_grad, grad_key_two, grad_value_two = ffn_grads(
        row_inputs,
        hidden_pre,
        hidden,
        row_grads,
        lookup_coefficients_later,
        payload_coefficients_later,
    )
    g_mix_k2 = lax.psum_scatter(
        partial_grad.astype(jnp.bfloat16), "tensor", scatter_dimension=1, tiled=True
    ).astype(jnp.float32)
    sum_key_two, sum_value_two = (
        lax.psum_scatter(
            grad_key_two.astype(jnp.bfloat16), "dp", scatter_dimension=0, tiled=True
        ).astype(jnp.float32),
        lax.psum_scatter(
            grad_value_two.astype(jnp.bfloat16), "dp", scatter_dimension=1, tiled=True
        ).astype(jnp.float32),
    )
    g_normed_two, shares_two = mix_back(
        (g_mix_k2, g_mix_r2), (share_k2, share_r2), differ_two, persist_indicator
    )
    g_resid_part, grad_gain_two, grad_bias_two = wide_norm_back(
        g_normed_two, unit_two, inverse_two, later_scaling_coords
    )
    g_resid = upstream + g_resid_part
    g_branch = g_resid.astype(jnp.bfloat16)
    grad_out_one = outer_sum(mixed_att, g_branch)
    g_mixed = project_back(g_branch, emit_coefficients_initial)
    g_weighted = g_mixed * sig_one
    g_recept_one = (g_mixed * blended_mean_state * sig_one * (1.0 - sig_one)).astype(jnp.bfloat16)
    reaching = pieces_list[2]
    g_in_num = jnp.sum(g_weighted * reaching / below_total, axis=1)
    g_in_den = -jnp.sum(g_weighted * reaching * blended_mean_state / below_total, axis=1)
    unused_item, back_num, back_den = entering(
        (passing, g_in_num, g_in_den), "tensor", chain_combine, identity
    )
    g_passing = back_num * incoming_num + back_den * incoming_den

    def device_fragment(lookup_wide, payload_wide, fading_coords, reward_power):
        shard_pieces = scan_fragments(
            lookup_wide, payload_wide, fading_coords, reward_power, text_boundary_indicators
        )
        local_out, unused_item = recurrence_finish(shard_pieces, incoming_num, incoming_den)
        return (local_out, shard_pieces[3], shard_pieces[4], shard_pieces[5])

    unused_item, reverse_pass_rule = jax.vjp(
        device_fragment, initial_lookup_lines, initial_payload_lines, fading_power, reward_coords
    )
    derivative_lookup_wide, derivative_payload_wide, fading_derivative, reward_derivative = (
        reverse_pass_rule((g_weighted, back_num, back_den, g_passing))
    )
    g_key_one = derivative_lookup_wide.astype(jnp.bfloat16)
    g_value_one = derivative_payload_wide.astype(jnp.bfloat16)
    grad_key_one = outer_sum(in_key, g_key_one)
    grad_value_one = outer_sum(in_value, g_value_one)
    grad_recept_one = outer_sum(in_recept, g_recept_one)
    g_mix_k1 = project_back(g_key_one, lookup_coefficients_initial)
    g_mix_v1 = project_back(g_value_one, payload_coefficients_initial)
    g_mix_r1 = project_back(g_recept_one, gate_coefficients_initial)
    g_normed_one, shares_one = mix_back(
        (g_mix_k1, g_mix_v1, g_mix_r1),
        (share_k1, share_v1, share_r1),
        differ_one,
        persist_indicator,
    )
    g_input_part, grad_gain_one, grad_bias_one = wide_norm_back(
        g_normed_one, unit_one, inverse_one, initial_scaling_coords
    )
    grad_tokens = g_resid + g_input_part
    summed = (
        lax.psum_scatter(grad_gain_one, ("dp", "tensor"), scatter_dimension=0, tiled=True),
        lax.psum_scatter(grad_bias_one, ("dp", "tensor"), scatter_dimension=0, tiled=True),
        lax.psum_scatter(grad_gain_two, ("dp", "tensor"), scatter_dimension=0, tiled=True),
        lax.psum_scatter(grad_bias_two, ("dp", "tensor"), scatter_dimension=0, tiled=True),
        lax.psum_scatter(fading_derivative, ("dp", "tensor"), scatter_dimension=0, tiled=True),
        lax.psum_scatter(reward_derivative, ("dp", "tensor"), scatter_dimension=0, tiled=True),
        lax.psum_scatter(shares_one[0], ("dp", "tensor"), scatter_dimension=0, tiled=True),
        lax.psum_scatter(shares_one[1], ("dp", "tensor"), scatter_dimension=0, tiled=True),
        lax.psum_scatter(shares_one[2], ("dp", "tensor"), scatter_dimension=0, tiled=True),
        lax.psum_scatter(grad_key_one, ("dp", "tensor"), scatter_dimension=0, tiled=True),
        lax.psum_scatter(grad_value_one, ("dp", "tensor"), scatter_dimension=0, tiled=True),
        lax.psum_scatter(grad_recept_one, ("dp", "tensor"), scatter_dimension=0, tiled=True),
        lax.psum_scatter(grad_out_one, ("dp", "tensor"), scatter_dimension=0, tiled=True),
        lax.psum_scatter(shares_two[0], ("dp", "tensor"), scatter_dimension=0, tiled=True),
        lax.psum_scatter(shares_two[1], ("dp", "tensor"), scatter_dimension=0, tiled=True),
        lax.psum_scatter(grad_recept_two, ("dp", "tensor"), scatter_dimension=0, tiled=True),
    )
    return (
        layer_out,
        grad_tokens,
        summed[0],
        summed[1],
        summed[2],
        summed[3],
        summed[4],
        summed[5],
        summed[6],
        summed[7],
        summed[8],
        summed[9],
        summed[10],
        summed[11],
        summed[12],
        summed[13],
        summed[14],
        summed[15],
        sum_key_two,
        sum_value_two,
    )


def local_call(body, outs, name, *args):
    vmem = pl.BlockSpec(memory_space=pltpu.VMEM)
    return pl.pallas_call(
        body,
        out_shape=outs,
        in_specs=[vmem] * len(args),
        out_specs=tuple([vmem] * len(outs)),
        compiler_params=pltpu.CompilerParams(vmem_limit_bytes=48 * MIB),
        name=name,
    )(*args)


def split_columns(w, parts):
    rows, width = w.shape
    return w.reshape(rows, parts, 2, width // (2 * parts)).transpose(2, 0, 1, 3).reshape(2, rows, width // 2)


def join_columns(own, other, c, parts):
    rows, half = own.shape[-2:]
    a = jnp.where(c == 0, own, other).reshape(own.shape[:-1] + (parts, half // parts))
    b = jnp.where(c == 0, other, own).reshape(own.shape[:-1] + (parts, half // parts))
    return jnp.stack([a, b], axis=-2).reshape(own.shape[:-1] + (2 * half,))


def pair_row(a, axis):
    return lax.all_gather(a, "tensor", axis=axis, tiled=True)


def pair_sum(a):
    return lax.psum(a.astype(BF16), "tensor").astype(F32)


def dot(a, b, dims, out=F32):
    return lax.dot_general(a, b, (dims, ((), ())), preferred_element_type=out)


NN, NT, TN = ((1,), (0,)), ((1,), (1,)), ((0,), (0,))


def layer_norm(values, gain, bias):
    center = values - jnp.mean(values, axis=-1, keepdims=True)
    inverse = lax.rsqrt(jnp.mean(center * center, axis=-1, keepdims=True) + 1e-05)
    normed = center * inverse
    return normed * gain + bias, normed, inverse


def norm_back(g, normed, inverse, gain):
    q = g * gain
    return inverse * (
        q - jnp.mean(q, axis=-1, keepdims=True) - normed * jnp.mean(q * normed, axis=-1, keepdims=True)
    )


def shift_down(v, keep):
    return jnp.concatenate([jnp.zeros_like(v[:1]), v[:-1]]) * keep[:, None]


def shift_up(v, keep):
    v = v * keep[:, None]
    return jnp.concatenate([v[1:], jnp.zeros_like(v[:1])])


VECTORS = 11


def shards(
    tokens, starts, upstream, gain1, bias1, gain2, bias2, fading, reward,
    mk1, mv1, mr1, wk, wv, wr, wo, mk2, mr2, wg, fk, fv,
):
    c = lax.axis_index("tensor")
    i = lax.axis_index("dp")
    count = lax.axis_size("dp")
    own_rows, width = wk.shape
    half = width // 2
    hidden = fk.shape[1]
    block = width // (2 * count)

    by_core = jnp.stack([split_columns(wk, count), split_columns(wv, count), split_columns(wr, count), split_columns(wg, 1)])
    own4 = lax.dynamic_index_in_dim(by_core, c, 1, False)
    other4 = lax.dynamic_index_in_dim(by_core, 1 - c, 1, False)
    emit = wo.reshape(own_rows, 2, half).transpose(1, 0, 2).reshape(1, 2 * own_rows, half)
    key4 = fk.reshape(2 * own_rows, 4, hidden // 4).transpose(1, 0, 2)
    value4 = fv.reshape(4, hidden // 4, 2 * own_rows).transpose(0, 2, 1)
    rest = jnp.concatenate([emit, key4, value4])
    vectors = jnp.stack([gain1, bias1, gain2, bias2, fading, reward, mk1, mv1, mr1, mk2, mr2])
    vectors = jnp.pad(vectors, ((0, 16 - VECTORS), (0, 0)))
    slot = (2 * i + c) % (128 // own_rows)
    lane = jnp.arange(128) // own_rows
    vec = jnp.where(lane[None, :] == slot, jnp.tile(vectors, (1, 128 // own_rows)), 0).astype(BF16)

    g, gv = gather_weights(own4, other4, rest, vec)

    full = gv.reshape(count * 2 * own_rows // 128, 128 // own_rows, 16, 128).astype(F32).sum(1)
    full = full.transpose(1, 0, 2).reshape(16, width)
    gain1, bias1, gain2, bias2, fading, reward, mk1, mv1, mr1, mk2, mr2 = (full[n] for n in range(VECTORS))
    g = g.reshape((PIECES, count, 2 * own_rows, half))
    wk, wv, wr, wg = (g[n].reshape(width, half) for n in range(4))
    wo = g[4].reshape(count, 2, own_rows, half).transpose(0, 2, 1, 3).reshape(half, width)
    fk = jnp.concatenate([g[5 + n].reshape(width, hidden // 4) for n in range(4)], axis=1)
    fv = jnp.concatenate([g[9 + n].reshape(width, hidden // 4) for n in range(4)], axis=1)

    def own_channels(v):
        return lax.dynamic_index_in_dim(split_columns(v[None], count)[:, 0], c, 0, False)

    keep = pair_row((1 - starts[0]).astype(F32), 0)
    x = pair_row(tokens[0], 0).astype(F32)
    up_half = lax.dynamic_slice_in_dim(pair_row(upstream[0], 0), c * half, half, 1).astype(F32)
    n1, u1, i1 = layer_norm(x, gain1, bias1)
    p1 = shift_down(n1, keep)
    d1 = n1 - p1
    in_k, in_v, in_r = ((p1 + d1 * m).astype(BF16) for m in (mk1, mv1, mr1))
    k, v, r = dot(in_k, wk, NN), dot(in_v, wv, NN), dot(in_r, wr, NN)
    fmask, bmask = resets(keep)
    rows = decay_rows(own_channels(fading), own_channels(reward))
    shape = jax.ShapeDtypeStruct(k.shape, F32)
    low = jax.ShapeDtypeStruct(k.shape, BF16)
    mixed, sn, sd = local_call(wkv_forward, (low, shape, shape), "wkv_forward", k, v, r, fmask, rows)
    resid = x + pair_sum(dot(mixed, wo, NN))
    n2, u2, i2 = layer_norm(resid, gain2, bias2)
    p2 = shift_down(n2, keep)
    d2 = n2 - p2
    in_k2, in_r2 = ((p2 + d2 * m).astype(BF16) for m in (mk2, mr2))
    s2 = jax.nn.sigmoid(dot(in_r2, wg, NN))
    pre = jax.nn.relu(dot(in_k2, fk, NN))
    act = (pre * pre).astype(BF16)
    value = lax.psum_scatter(dot(act, fv, NT).astype(BF16), "tensor", scatter_dimension=1, tiled=True).astype(F32)
    resid_half = lax.dynamic_slice_in_dim(resid, c * half, half, 1)
    out_half = (resid_half + s2 * value).astype(BF16)
    layer_out = lax.all_to_all(out_half, "tensor", 0, 1, tiled=True)
    g_value = (up_half * s2).astype(BF16)
    g_recept2 = (up_half * value * s2 * (1.0 - s2)).astype(BF16)
    g_value = pair_row(g_value, 1)
    grad_fv = dot(g_value, act, TN)
    g_pre = (2.0 * pre * dot(g_value, fv, NN)).astype(BF16)
    grad_fk = dot(in_k2, g_pre, TN)
    grad_wg = dot(in_r2, g_recept2, TN)
    gk2 = dot(g_pre, fk, NT)
    gr2 = dot(g_recept2, wg, NT)
    grad_mk2, grad_mr2 = jnp.sum(gk2 * d2, 0), jnp.sum(gr2 * d2, 0)
    gn2 = gk2 * mk2 + gr2 * mr2 + shift_up(gk2 * (1 - mk2) + gr2 * (1 - mr2), keep)
    grad_gain2, grad_bias2 = jnp.sum(gn2 * u2, 0), jnp.sum(gn2, 0)
    upstream_row = pair_row(upstream[0], 0).astype(F32)
    g_resid = upstream_row + norm_back(pair_sum(gn2), u2, i2, gain2)
    g_branch = g_resid.astype(BF16)
    grad_wo = dot(mixed, g_branch, TN)
    g_mixed = dot(g_branch, wo, NT)
    gk1, gv1, gr1, wsums = local_call(
        wkv_backward, (low, low, low, jax.ShapeDtypeStruct((8, half), F32)), "wkv_backward",
        g_mixed, k, v, r, sn, sd, bmask, rows,
    )
    grad_wk, grad_wv, grad_wr = dot(in_k, gk1, TN), dot(in_v, gv1, TN), dot(in_r, gr1, TN)
    toward, behind, grad_mix = 0.0, 0.0, []
    for grad, w, m in ((gk1, wk, mk1), (gv1, wv, mv1), (gr1, wr, mr1)):
        back = dot(grad, w, NT)
        toward = toward + back * m
        behind = behind + back * (1 - m)
        grad_mix.append(jnp.sum(back * d1, 0))
    gn1 = toward + shift_up(behind, keep)
    grad_gain1, grad_bias1 = jnp.sum(gn1 * u1, 0), jnp.sum(gn1, 0)
    gn1 = lax.psum_scatter(gn1.astype(BF16), "tensor", scatter_dimension=0, tiled=True).astype(F32)
    span = tokens.shape[1]

    def mine(v):
        return lax.dynamic_slice_in_dim(v, c * span, span, 0)

    grad_tokens = mine(g_resid) + norm_back(gn1, mine(u1), mine(i1), gain1)

    blocks = (4, 4) if count == 16 else (count,)

    def pieces(m):
        return m.reshape((1,) + blocks + (2 * own_rows, half))

    grad_wo = grad_wo.reshape(count, own_rows, 2, half).transpose(0, 2, 1, 3)
    grad_fk, grad_fv = (
        m.reshape(width, 4, hidden // 4).transpose(1, 0, 2).reshape((4,) + blocks + (2 * own_rows, half))
        for m in (grad_fk, grad_fv)
    )
    partial = jnp.concatenate(
        [pieces(grad_wk), pieces(grad_wv), pieces(grad_wr), pieces(grad_wg), pieces(grad_wo), grad_fk, grad_fv]
    ).astype(BF16)

    def all_channels(v):
        z = jnp.zeros_like(v)
        return join_columns(jnp.where(c == 0, v, z)[None], jnp.where(c == 1, v, z)[None], 0, count)[0]

    vsums = jnp.stack([
        grad_gain1, grad_bias1, grad_gain2, grad_bias2, all_channels(wsums[1]), all_channels(wsums[0]),
        *grad_mix, grad_mk2, grad_mr2,
    ])
    vsums = jnp.pad(vsums, ((0, 16 - VECTORS), (0, 0)))
    total, recv4, vtotal = reduce_weights(partial, vsums)
    vtotal = lax.dynamic_slice_in_dim(vtotal, (2 * i + c) * own_rows, own_rows, 1)
    own = lax.dynamic_slice_in_dim(total[:4], c * own_rows, own_rows, 1)
    out_k, out_v, out_r = (join_columns(own[n], recv4[n], c, count) for n in range(3))
    out_g = join_columns(own[3], recv4[3], c, 1)
    out_o = total[4].reshape(2, own_rows, half).transpose(1, 0, 2).reshape(own_rows, width)
    out_fk = total[5:9].transpose(1, 0, 2).reshape(2 * own_rows, hidden)
    out_fv = total[9:13].transpose(0, 2, 1).reshape(hidden, 2 * own_rows)
    return (
        layer_out[None], grad_tokens[None], *(vtotal[n] for n in range(9)),
        out_k, out_v, out_r, out_o, vtotal[9], vtotal[10], out_g, out_fk, out_fv,
    )


def solution(mesh):
    row, vector, matrix = P("dp", "tensor", None), P(("dp", "tensor")), P(("dp", "tensor"), None)
    key, value = P("dp", "tensor"), P("tensor", "dp")
    in_specs = (row, P("dp", "tensor"), row) + (vector,) * 9 + (matrix,) * 4 + (vector,) * 2 + (matrix, key, value)
    out_specs = (row, row) + (vector,) * 9 + (matrix,) * 4 + (vector,) * 2 + (matrix, key, value)
    body = shards if (mesh.shape["dp"], mesh.shape["tensor"]) == (16, 2) else wide_shards
    return jax.shard_map(body, mesh=mesh, in_specs=in_specs, out_specs=out_specs, check_vma=False)
```

```python
import functools

import jax
import jax.numpy as jnp
from jax import lax
from jax.experimental import pallas as pl
from jax.experimental.pallas import tpu as pltpu
from jax.sharding import PartitionSpec as P

F32, BF16 = jnp.float32, jnp.bfloat16
MESH_ID = pl.DeviceIdType.MESH
MIB = 1 << 20
PIECES = 13


def place():
    i, c = lax.axis_index("dp"), lax.axis_index("tensor")
    return i // 4, i % 4, c


def neighbours(z, yx):
    x = yx + 1 - 2 * (yx % 2)
    y = (yx + 2) % 4
    d = (x + 2) % 4
    zs = (z + 1 - 2 * (z % 2), (z + 2) % 4, 3 - z)
    return x, y, d, zs


def enter(z, yx, c):
    x, y, d, zs = neighbours(z, yx)
    barrier = pltpu.get_barrier_semaphore()
    targets = [(z * 4 + yx, 1 - c), (z * 4 + x, c), (z * 4 + y, c)]
    targets += [(peer * 4 + yx, c) for peer in zs]
    for target in targets:
        pl.semaphore_signal(barrier, inc=1, device_id=target, device_id_type=MESH_ID)
    pl.semaphore_wait(barrier, len(targets))


def remote(src, dst, send, recv, target):
    return pltpu.make_async_remote_copy(
        src_ref=src, dst_ref=dst, send_sem=send, recv_sem=recv,
        device_id=target, device_id_type=MESH_ID,
    )


class Gather:
    def __init__(self, view, sends, recvs, first=0):
        self.view, self.sends, self.recvs, self.first = view, sends, recvs, first
        self.z, self.yx, self.c = place()
        self.x, self.y, self.d, self.zs = neighbours(self.z, self.yx)

    def to(self, z, yx):
        return (z * 4 + yx, self.c)

    def copy(self, p, k, ref, target):
        return remote(ref, ref, self.sends.at[p, k], self.recvs.at[p, k], target)

    def along(self, p):
        own = self.view(p).at[self.z, self.yx]
        return [self.copy(p, k, own, self.to(peer, self.yx)) for k, peer in enumerate(self.zs)]

    def plane(self, p):
        own = self.view(p).at[:, self.yx]
        return [self.copy(p, 3, own, self.to(self.z, self.x)), self.copy(p, 4, own, self.to(self.z, self.y))]

    def onward(self, p):
        return [
            self.copy(p, 5, self.view(p).at[0:2, self.x], self.to(self.z, self.y)),
            self.copy(p, 6, self.view(p).at[2:4, self.y], self.to(self.z, self.x)),
        ]

    def start(self, copies):
        for copy in copies:
            copy.start()

    def arrive(self, copies):
        for copy in copies:
            copy.wait_recv()

    def step(self, p):
        self.arrive(self.along(p))
        self.start(self.plane(p))

    def forward(self, p):
        self.arrive(self.plane(p))
        self.start(self.onward(p))

    def finish(self, p):
        for copy in self.along(p) + self.plane(p) + self.onward(p):
            copy.wait_send()


class Reduce:
    def __init__(self, part, ring1, ring2, line, out, sends, recvs):
        self.part, self.ring1, self.ring2, self.line, self.out = part, ring1, ring2, line, out
        self.sends, self.recvs = sends, recvs
        self.z, self.yx, self.c = place()
        self.x, self.y, self.d, self.zs = neighbours(self.z, self.yx)

    def copy(self, p, k, src, dst, z, yx):
        return remote(src, dst, self.sends.at[p, k], self.recvs.at[p, k], (z * 4 + yx, self.c))

    def diagonal(self, p):
        part, z = self.part.at[p], self.z
        return [
            self.copy(p, 0, part.at[0:2, self.d], self.ring1.at[p, 0], z, self.x),
            self.copy(p, 1, part.at[2:4, self.d], self.ring1.at[p, 1], z, self.y),
        ]

    def side(self, p):
        part, z = self.part.at[p], self.z
        return [
            self.copy(p, 2, part.at[:, self.x], self.ring2.at[p, 0], z, self.x),
            self.copy(p, 3, part.at[:, self.y], self.ring2.at[p, 1], z, self.y),
        ]

    def down(self, p):
        part = self.part.at[p]
        return [
            self.copy(p, 4 + k, part.at[peer, self.yx], self.line.at[p, k], peer, self.yx)
            for k, peer in enumerate(self.zs)
        ]

    def start(self, copies):
        for copy in copies:
            copy.start()

    def arrive(self, copies):
        for copy in copies:
            copy.wait_recv()

    def add(self, p, a, yx, pieces):
        total = self.part[p, a, yx].astype(F32)
        for piece in pieces:
            total = total + piece.astype(F32)
        return total

    def stage1(self, p):
        self.start(self.diagonal(p))

    def stage2(self, p):
        self.arrive(self.diagonal(p))
        for a in range(2):
            self.part[p, a, self.y] = self.add(p, a, self.y, [self.ring1[p, 0, a]]).astype(BF16)
            self.part[p, a + 2, self.x] = self.add(p, a + 2, self.x, [self.ring1[p, 1, a]]).astype(BF16)
        self.start(self.side(p))

    def stage3(self, p):
        self.arrive(self.side(p))
        for a in range(4):
            self.part[p, a, self.yx] = self.add(
                p, a, self.yx, [self.ring2[p, 0, a], self.ring2[p, 1, a]]
            ).astype(BF16)
        self.start(self.down(p))

    def stage4(self, p):
        self.arrive(self.down(p))
        self.out[p] = self.add(p, self.z, self.yx, [self.line[p, k] for k in range(3)])

    def finish(self, p):
        for copy in self.diagonal(p) + self.side(p) + self.down(p):
            copy.wait_send()


def reduce_kernel(
    partial, vec, out, recv4, vout, part, ring1, ring2, line, vbuf, local_sem, sends, recvs, vsends, vrecvs, ex_send, ex_recv
):
    z, yx, c = place()
    x, y, d, zs = neighbours(z, yx)
    enter(z, yx, c)
    sums = Reduce(part, ring1, ring2, line, out, sends, recvs)

    def local(p):
        return pltpu.make_async_copy(partial.at[p], part.at[p], local_sem.at[p])

    def vec_copy(k, target):
        return remote(vout, vbuf.at[k], vsends.at[k], vrecvs.at[k], target)

    vcopies = [
        [vec_copy(0, (z * 4 + yx, 1 - c))],
        [vec_copy(1, (z * 4 + x, c))],
        [vec_copy(2, (z * 4 + y, c))],
        [vec_copy(3 + k, (peer * 4 + yx, c)) for k, peer in enumerate(zs)],
    ]

    vout[...] = vec[...]

    def fetch(p, carry):
        local(p).start()
        return carry

    lax.fori_loop(0, PIECES, fetch, 0)
    for copy in vcopies[0]:
        copy.start()

    def turn(p, carry):
        @pl.when(p < PIECES)
        def _():
            local(p).wait()
            sums.stage1(p)

        @pl.when((p >= 1) & (p < PIECES + 1))
        def _():
            sums.stage2(p - 1)

        @pl.when((p >= 2) & (p < PIECES + 2))
        def _():
            sums.stage3(p - 2)

        @pl.when(p >= 3)
        def _():
            sums.stage4(p - 3)

        return carry

    lax.fori_loop(0, 4, turn, 0)
    at = 4
    for k, copies in enumerate(vcopies):
        for copy in copies:
            copy.wait()
        vout[...] = functools.reduce(
            lambda a, b: a + b, [vbuf[j] for j in ([k] if k < 3 else [3, 4, 5])], vout[...]
        )
        if k + 1 < len(vcopies):
            for copy in vcopies[k + 1]:
                copy.start()
        upto = at + 3 if k + 1 < len(vcopies) else PIECES + 3
        lax.fori_loop(at, upto, turn, 0)
        at = upto
    half = recv4.shape[1]
    others = pl.ds(pl.multiple_of((1 - c) * half, half), half)
    swap = remote(out.at[0:4, others], recv4, ex_send, ex_recv, (z * 4 + yx, 1 - c))
    swap.start()

    def close(p, carry):
        sums.finish(p)
        return carry

    lax.fori_loop(0, PIECES, close, 0)
    swap.wait()


def reduce_weights(partial, vec):
    rows, width = partial.shape[3:]
    any_ = pl.BlockSpec(memory_space=pl.ANY)
    vmem = pl.BlockSpec(memory_space=pltpu.VMEM)
    return pl.pallas_call(
        reduce_kernel,
        out_shape=(
            jax.ShapeDtypeStruct((PIECES, rows, width), F32),
            jax.ShapeDtypeStruct((4, rows // 2, width), F32),
            jax.ShapeDtypeStruct(vec.shape, F32),
        ),
        in_specs=[any_, vmem],
        out_specs=(vmem, vmem, vmem),
        scratch_shapes=[
            pltpu.VMEM((PIECES, 4, 4, rows, width), BF16),
            pltpu.VMEM((PIECES, 2, 2, rows, width), BF16),
            pltpu.VMEM((PIECES, 2, 4, rows, width), BF16),
            pltpu.VMEM((PIECES, 3, rows, width), BF16),
            pltpu.VMEM((6,) + vec.shape, F32),
            pltpu.SemaphoreType.DMA((PIECES,)),
            pltpu.SemaphoreType.DMA((PIECES, 7)),
            pltpu.SemaphoreType.DMA((PIECES, 7)),
            pltpu.SemaphoreType.DMA((6,)),
            pltpu.SemaphoreType.DMA((6,)),
            pltpu.SemaphoreType.DMA,
            pltpu.SemaphoreType.DMA,
        ],
        compiler_params=pltpu.CompilerParams(
            collective_id=1, has_side_effects=True, vmem_limit_bytes=48 * MIB
        ),
        name="reduce_weights",
    )(partial, vec)


def lanes(j):
    return slice(j * 128, (j + 1) * 128)


def bottom(v):
    return jnp.broadcast_to(v[7:8], v.shape)


def top(v):
    return jnp.broadcast_to(v[0:1], v.shape)


def masks_down(keep, place_in):
    m1 = jnp.where(place_in >= 1, keep, 0.0)
    m2 = m1 * pltpu.roll(m1, 1, 0)
    m4 = m2 * pltpu.roll(m2, 2, 0)
    for n in (1, 2, 4):
        keep = keep * jnp.where(place_in >= n, pltpu.roll(keep, n, 0), 1.0)
    return m1, m2, m4, keep


def masks_up(after, place_in):
    m1 = jnp.where(place_in <= 6, after, 0.0)
    m2 = m1 * pltpu.roll(m1, 7, 0)
    m4 = m2 * pltpu.roll(m2, 6, 0)
    for n in (1, 2, 4):
        after = after * jnp.where(place_in <= 7 - n, pltpu.roll(after, 8 - n, 0), 1.0)
    return m1, m2, m4, after


def wkv_forward(k_ref, v_ref, r_ref, keep_ref, rows_ref, mixed_ref, sn_ref, sd_ref):
    length, width = k_ref.shape
    tiles = width // 128
    place_in = lax.broadcasted_iota(jnp.int32, (8, 128), 0)
    first = place_in == 0
    zero = jnp.zeros((8, 128), F32)

    def pair(g, carry):
        carry = list(carry)
        base = pl.multiple_of(g * 16, 16)
        keeps = [keep_ref[pl.ds(base + 8 * h, 8), :] for h in range(2)]
        masks = [masks_down(keep, place_in) for keep in keeps]
        for j in range(tiles):
            d1, d2, d4, eu = (rows_ref[n : n + 1, lanes(j)] for n in range(4))
            dp = rows_ref[8:16, lanes(j)]
            made = []
            for h in range(2):
                at = pl.ds(base + 8 * h, 8)
                keep, (m1, m2, m4, mp) = keeps[h], masks[h]
                ek = jnp.exp(k_ref[at, lanes(j)])
                v = v_ref[at, lanes(j)]
                num, den = ek * v, ek
                x, b = num, eu * ek
                for n, coef in ((1, m1 * d1), (2, m2 * d2), (4, m4 * d4)):
                    num = num + coef * pltpu.roll(num, n, 0)
                    den = den + coef * pltpu.roll(den, n, 0)
                coef = mp * dp
                cn, cd = carry[2 * j], carry[2 * j + 1]
                num = num + coef * cn
                den = den + coef * cd
                sn = keep * jnp.where(first, cn, pltpu.roll(num, 1, 0))
                sd = keep * jnp.where(first, cd, pltpu.roll(den, 1, 0))
                carry[2 * j], carry[2 * j + 1] = bottom(num), bottom(den)
                sn_ref[at, lanes(j)] = sn
                sd_ref[at, lanes(j)] = sd
                weighted = (sn + eu * x) / (sd + b)
                made.append(jax.nn.sigmoid(r_ref[at, lanes(j)]) * weighted)
            mixed_ref[pl.ds(base, 16), lanes(j)] = jnp.concatenate(made, axis=0).astype(BF16)
        return tuple(carry)

    lax.fori_loop(0, length // 16, pair, (zero,) * (2 * tiles))


def wkv_backward(
    g_ref, k_ref, v_ref, r_ref, sn_ref, sd_ref, keep_ref, rows_ref, gk_ref, gv_ref, gr_ref, sums_ref
):
    length, width = k_ref.shape
    tiles = width // 128
    place_in = lax.broadcasted_iota(jnp.int32, (8, 128), 0)
    last = place_in == 7
    zero = jnp.zeros((8, 128), F32)
    pairs = length // 16

    def pair(step, carry):
        carry = list(carry)
        base = pl.multiple_of((pairs - 1 - step) * 16, 16)
        low, high = (keep_ref[pl.ds(base + 8 * h, 8), :] for h in range(2))
        afters = [
            jnp.where(last, top(high), pltpu.roll(low, 7, 0)),
            jnp.where(last, carry[4 * tiles], pltpu.roll(high, 7, 0)),
        ]
        masks = [masks_up(after, place_in) for after in afters]
        carry[4 * tiles] = top(low)
        for j in range(tiles):
            d1, d2, d4, eu = (rows_ref[n : n + 1, lanes(j)] for n in range(4))
            dp = rows_ref[16:24, lanes(j)]
            made = [None, None]
            for h in (1, 0):
                at = pl.ds(base + 8 * h, 8)
                after, (m1, m2, m4, mp) = afters[h], masks[h]
                ek = jnp.exp(k_ref[at, lanes(j)])
                v = v_ref[at, lanes(j)]
                sn, sd = sn_ref[at, lanes(j)], sd_ref[at, lanes(j)]
                s = jax.nn.sigmoid(r_ref[at, lanes(j)])
                b = eu * ek
                inverse = 1.0 / (sd + b)
                weighted = (sn + b * v) * inverse
                g = g_ref[at, lanes(j)]
                gs = g * s
                p = gs * inverse
                q = -p * weighted
                gr = gs * weighted * (1.0 - s)
                hp, hq = p, q
                for n, coef in ((1, m1 * d1), (2, m2 * d2), (4, m4 * d4)):
                    hp = hp + coef * pltpu.roll(hp, 8 - n, 0)
                    hq = hq + coef * pltpu.roll(hq, 8 - n, 0)
                coef = mp * dp
                cp, cq = carry[4 * j], carry[4 * j + 1]
                hp = hp + coef * cp
                hq = hq + coef * cq
                ap = after * jnp.where(last, cp, pltpu.roll(hp, 7, 0))
                aq = after * jnp.where(last, cq, pltpu.roll(hq, 7, 0))
                carry[4 * j], carry[4 * j + 1] = top(hp), top(hq)
                bonus = b * (v * p + q)
                gv = ek * ap + b * p
                gk = ek * (v * ap + aq) + bonus
                carry[4 * j + 2] = carry[4 * j + 2] + bonus
                carry[4 * j + 3] = carry[4 * j + 3] + (ap * sn + aq * sd)
                made[h] = (gk, gv, gr)
            both = pl.ds(base, 16)
            for n, ref in enumerate((gk_ref, gv_ref, gr_ref)):
                ref[both, lanes(j)] = jnp.concatenate([made[0][n], made[1][n]], axis=0).astype(BF16)
        return tuple(carry)

    carry = lax.fori_loop(0, pairs, pair, (zero,) * (4 * tiles + 1))
    for j in range(tiles):
        rate_d = rows_ref[4:5, lanes(j)]
        sums_ref[0:1, lanes(j)] = jnp.sum(carry[4 * j + 2], axis=0, keepdims=True)
        sums_ref[1:2, lanes(j)] = -rate_d * jnp.sum(carry[4 * j + 3], axis=0, keepdims=True)


NN, NT, TN = ((1,), (0,)), ((1,), (1,)), ((0,), (0,))
KEY, VALUE, GATE, EMIT, GATE2, FFN = 0, 1, 2, 3, 4, 5
VECTORS = 11
GAIN1, BIAS1, GAIN2, BIAS2, FADE, REWARD, MK1, MV1, MR1, MK2, MR2, OWN_FADE, OWN_REWARD = range(13)


def dot(a, b, dims):
    return lax.dot_general(a, b, (dims, ((), ())), preferred_element_type=F32)


def strip(i, size):
    return pl.ds(pl.multiple_of(i * size, size), size)


def over_rows(length, size, body):
    def step(i, carry):
        body(strip(i, size))
        return carry

    lax.fori_loop(0, length // size, step, 0)


def matrix(ref):
    return ref[...].reshape(16 * ref.shape[2], ref.shape[3])


def emit_half(ref, h):
    rows = ref.shape[2] // 2
    return ref[:, :, h * rows : (h + 1) * rows, :].reshape(16 * rows, ref.shape[3])


def wide(column, width):
    return jnp.concatenate([column] * (width // 128), axis=1)


def norm(x):
    center = x - jnp.mean(x, axis=-1, keepdims=True)
    inverse = lax.rsqrt(jnp.mean(center * center, axis=-1, keepdims=True) + 1e-05)
    return center * inverse, inverse


def norm_and_mix(length, width, load, gain, bias, keep_ref, mixes, outs):
    first = lax.broadcasted_iota(jnp.int32, (16, width), 0) == 0

    def step(i, before):
        at = strip(i, 16)
        unit, _ = norm(load(at))
        normed = unit * gain + bias
        prev = jnp.where(first, before, pltpu.roll(normed, 1, 0)) * wide(keep_ref[at, :], width)
        differ = normed - prev
        for share, out in zip(mixes, outs):
            out[at, :] = (prev + differ * share).astype(BF16)
        return normed[15:16]

    lax.fori_loop(0, length // 16, step, jnp.zeros((1, width), F32))


def forward_kernel(
    own4, other4, rest, vec, x_own, up_own, keep_own,
    g, out, x_out, up_out, ins_out, kvr_out, sn_out, sd_out, mixed_out, resid_out, ins2_out, pre_out, act_out,
    gv_out, gr_out, vec_out, rows_out, keep_out,
    gv, w, x, up, ins, kvr, sn, sd, mixed, sum_own, sum_other, resid, ins2, pre, act, v_send, v_other, gval, grec, low_half,
    local_sem, ex_send, ex_recv, sends, recvs, vsends, vrecvs, stage_sem, out_sem, sum_send, sum_recv, val_send, val_recv,
):
    z, yx, c = place()
    length, width = x.shape
    half = width // 2
    span = length // 2
    partner = (z * 4 + yx, 1 - c)
    enter(z, yx, c)

    block = own4.shape[1]
    mine = strip(c, block)
    rows_mine = strip(c, span)
    swaps = [
        (vec, gv.at[z, yx, c]),
        (other4.at[0:3], g.at[0:3, z, yx, mine]),
        (other4.at[3], g.at[GATE2, z, yx, mine]),
        (x_own, x.at[rows_mine]),
        (keep_own, keep_out.at[rows_mine]),
        (up_own, up.at[rows_mine]),
    ]
    swaps = [remote(a, b, ex_send.at[n], ex_recv.at[n], partner) for n, (a, b) in enumerate(swaps)]
    keeps = [
        (vec, gv.at[z, yx, c]),
        (own4.at[0:3], g.at[0:3, z, yx, mine]),
        (own4.at[3], g.at[GATE2, z, yx, mine]),
        (x_own, x.at[rows_mine]),
        (keep_own, keep_out.at[rows_mine]),
        (up_own, up.at[rows_mine]),
        (rest.at[0], g.at[EMIT, z, yx]),
        (rest.at[1:9], g.at[FFN : FFN + 8, z, yx]),
    ]
    keeps = [pltpu.make_async_copy(a, b, local_sem.at[n]) for n, (a, b) in enumerate(keeps)]
    for copy in swaps + keeps:
        copy.start()
    weights = Gather(lambda p: g.at[p], sends, recvs)
    vectors = Gather(lambda p: gv, vsends, vrecvs)

    outs = []

    def put(src, dst):
        copy = pltpu.make_async_copy(src, dst, out_sem.at[len(outs)])
        copy.start()
        outs.append(copy)
        return copy

    def stage(p):
        return pltpu.make_async_copy(g.at[p], w.at[p % 3], stage_sem.at[p])

    def turn(n):
        if n < PIECES:
            weights.step(n)
            if n + 2 < PIECES:
                weights.start(weights.along(n + 2))
        if 1 <= n <= PIECES:
            weights.forward(n - 1)
        if n >= 2:
            weights.arrive(weights.onward(n - 2))
            stage(n - 2).start()

    def staged(p):
        stage(p).wait()
        return w.at[p % 3]

    for n in (0, 1, 2):
        swaps[n].wait()
        keeps[n].wait()
    vectors.start(vectors.along(0))
    weights.start(weights.along(0))
    for copy in keeps[6:]:
        copy.wait()
    weights.start(weights.along(1))
    vectors.step(0)
    turn(0)
    vectors.forward(0)
    for n in (3, 4, 5):
        swaps[n].wait()
        keeps[n].wait()
    x_copy, up_copy = put(x, x_out), put(up, up_out)
    turn(1)
    vectors.arrive(vectors.onward(0))

    for t in range(width // 128):
        parts = [gv[(2 * t + k) // 4, (2 * t + k) % 4, core].astype(F32) for k in range(2) for core in range(2)]
        vec_out[:, lanes(t)] = functools.reduce(lambda a, b: a + b, parts)
    ramp = lax.broadcasted_iota(jnp.int32, (8, 128), 0).astype(F32)
    for t in range(half // 128):
        own = functools.reduce(lambda a, b: a + b, [gv[t, k, c].astype(F32) for k in range(4)])
        rate = jnp.exp(own[OWN_FADE : OWN_FADE + 1])
        head = [
            jnp.exp(-rate), jnp.exp(-2.0 * rate), jnp.exp(-4.0 * rate), jnp.exp(own[OWN_REWARD : OWN_REWARD + 1]),
            rate * jnp.exp(-rate),
        ]
        for n, row in enumerate(head):
            rows_out[n : n + 1, lanes(t)] = row
        rows_out[8:16, lanes(t)] = jnp.exp(-(ramp + 1.0) * rate)
        rows_out[16:24, lanes(t)] = jnp.exp(-(8.0 - ramp) * rate)

    def row(n):
        return vec_out[n : n + 1, :]

    norm_and_mix(
        length, width, lambda at: x[at, :].astype(F32), row(GAIN1), row(BIAS1), keep_out,
        [row(MK1), row(MV1), row(MR1)], [ins.at[n] for n in range(3)],
    )
    put(ins, ins_out)
    kvr_copies = []
    for n in range(3):
        turn(n + 2)
        weight = staged(n)

        def project(at):
            kvr[n, at, :] = dot(ins[n, at, :], matrix(weight), NN)

        over_rows(length, 256, project)
        kvr_copies.append(put(kvr.at[n], kvr_out.at[n]))
    wkv_forward(kvr.at[0], kvr.at[1], kvr.at[2], keep_out, rows_out, mixed, sn, sd)
    put(mixed, mixed_out)
    put(sn, sn_out)
    put(sd, sd_out)
    turn(5)
    weight = staged(EMIT)
    quarters = length // 4
    sums = []
    for n in range(4):
        at = pl.ds(n * quarters, quarters)
        for h in range(2):
            sum_own[at, h * half : (h + 1) * half] = dot(mixed[at, :], emit_half(weight, h), NN).astype(BF16)
        sums.append(remote(sum_own.at[at], sum_other.at[at], sum_send.at[n], sum_recv.at[n], partner))
        sums[-1].start()
    turn(6)
    for copy in sums:
        copy.wait()

    def add_up(at):
        total = x[at, :].astype(F32) + (sum_own[at, :].astype(F32) + sum_other[at, :].astype(F32))
        resid[0, at, :] = total[:, :half]
        resid[1, at, :] = total[:, half:]
        return total

    norm_and_mix(
        length, width, add_up, row(GAIN2), row(BIAS2), keep_out, [row(MK2), row(MR2)], [ins2.at[n] for n in range(2)]
    )
    put(resid, resid_out)
    put(ins2, ins2_out)
    for copy in kvr_copies:
        copy.wait()
    weight = staged(GATE2)

    def gate(at):
        kvr[2, at, :] = jax.nn.sigmoid(dot(ins2[1, at, :], matrix(weight), NN))

    over_rows(length, 256, gate)
    pre_copies = []
    for j in range(4):
        turn(FFN + 2 * j + 2)
        weight = staged(FFN + 2 * j)
        if j >= 2:
            pre_copies[j - 2].wait()

        def expand(at):
            positive = jnp.maximum(dot(ins2[0, at, :], matrix(weight), NN), 0.0)
            pre[j % 2, at, :] = positive.astype(BF16)
            act[j, at, :] = (positive * positive).astype(BF16)

        over_rows(length, 256, expand)
        pre_copies.append(put(pre.at[j % 2], pre_out.at[j]))
        put(act.at[j], act_out.at[j])
        turn(FFN + 2 * j + 3)
        weight = staged(FFN + 2 * j + 1)

        def contract(at):
            for h in range(2):
                part = dot(act[j, at, :], weight[2 * h : 2 * h + 2].reshape(half, -1), NT)
                kvr[h, at, :] = part if j == 0 else kvr[h, at, :] + part

        over_rows(length, 256, contract)

    vals = []
    for n in range(4):
        at = pl.ds(n * quarters, quarters)
        v_send[at, :] = kvr[1 - c, at, :].astype(BF16)
        vals.append(remote(v_send.at[at], v_other.at[at], val_send.at[n], val_recv.at[n], partner))
        vals[-1].start()
    columns = strip(c, half)
    backs = []
    for n in range(4):
        vals[n].wait()

        def finish(i, carry):
            at = strip(n * (quarters // 16) + i, 16)
            value = kvr[c, at, :] + v_other[at, :].astype(F32)
            s = kvr[2, at, :]
            low_half[at, :] = (resid[c, at, :] + s * value).astype(BF16)
            upstream = up[at, columns].astype(F32)
            gval[c, at, :] = (upstream * s).astype(BF16)
            grec[at, :] = (upstream * value * s * (1.0 - s)).astype(BF16)
            return carry

        lax.fori_loop(0, quarters // 16, finish, 0)
        at = pl.ds(n * quarters, quarters)
        backs.append(remote(gval.at[c, at], gval.at[c, at], val_send.at[4 + n], val_recv.at[4 + n], partner))
        backs[-1].start()
    give = remote(low_half.at[strip(1 - c, span)], out.at[:, columns], val_send.at[8], val_recv.at[8], partner)
    give.start()
    put(low_half.at[rows_mine], out.at[:, columns])
    put(grec, gr_out)
    for copy in backs:
        copy.wait()
    put(gval, gv_out)
    give.wait()

    def close(p, carry):
        weights.finish(p)
        return carry

    lax.fori_loop(0, PIECES, close, 0)
    vectors.finish(0)
    waited = kvr_copies + pre_copies[:2]
    for copy in outs:
        if not any(copy is other for other in waited):
            copy.wait()


def forward_call(own4, other4, rest, vec, x_own, up_own, keep_own):
    span, width = x_own.shape
    length, half = 2 * span, width // 2
    block = rest.shape[1:]
    any_, vmem = pl.BlockSpec(memory_space=pl.ANY), pl.BlockSpec(memory_space=pltpu.VMEM)
    full, col = (length, width), (length, half)

    def shape(dims, kind):
        return jax.ShapeDtypeStruct(dims, kind)

    outs = (
        (shape((PIECES, 4, 4) + block, BF16), any_),
        (shape((span, width), BF16), any_),
        (shape(full, BF16), any_),
        (shape(full, BF16), any_),
        (shape((3,) + full, BF16), any_),
        (shape((3,) + col, F32), any_),
        (shape(col, F32), any_),
        (shape(col, F32), any_),
        (shape(col, BF16), any_),
        (shape((2,) + col, F32), any_),
        (shape((2,) + full, BF16), any_),
        (shape((4,) + col, BF16), any_),
        (shape((4,) + col, BF16), any_),
        (shape((2,) + col, BF16), any_),
        (shape(col, BF16), any_),
        (shape((16, width), F32), vmem),
        (shape((24, half), F32), vmem),
        (shape((length, 128), F32), vmem),
    )
    dma = pltpu.SemaphoreType.DMA
    return pl.pallas_call(
        forward_kernel,
        out_shape=tuple(o[0] for o in outs),
        in_specs=[any_] * 7,
        out_specs=tuple(o[1] for o in outs),
        scratch_shapes=[
            pltpu.VMEM((4, 4, 2) + vec.shape, BF16),
            pltpu.VMEM((3, 4, 4) + block, BF16),
            pltpu.VMEM(full, BF16),
            pltpu.VMEM(full, BF16),
            pltpu.VMEM((3,) + full, BF16),
            pltpu.VMEM((3,) + col, F32),
            pltpu.VMEM(col, F32),
            pltpu.VMEM(col, F32),
            pltpu.VMEM(col, BF16),
            pltpu.VMEM(full, BF16),
            pltpu.VMEM(full, BF16),
            pltpu.VMEM((2,) + col, F32),
            pltpu.VMEM((2,) + full, BF16),
            pltpu.VMEM((2,) + col, BF16),
            pltpu.VMEM((4,) + col, BF16),
            pltpu.VMEM(col, BF16),
            pltpu.VMEM(col, BF16),
            pltpu.VMEM((2,) + col, BF16),
            pltpu.VMEM(col, BF16),
            pltpu.VMEM(col, BF16),
            dma((8,)), dma((6,)), dma((6,)),
            dma((PIECES, 7)), dma((PIECES, 7)), dma((1, 7)), dma((1, 7)),
            dma((PIECES,)), dma((24,)), dma((4,)), dma((4,)), dma((9,)), dma((9,)),
        ],
        compiler_params=pltpu.CompilerParams(
            collective_id=0, has_side_effects=True, vmem_limit_bytes=60 * MIB
        ),
        name="forward",
    )(own4, other4, rest, vec, x_own, up_own, keep_own)


def shifted(value, axis, steps):
    count = lax.axis_size(axis)
    first, last = (max(0, -steps), min(count, count - steps))
    return lax.ppermute(value, axis, [(source, source + steps) for source in range(first, last)])


def carried_in(array, axis, join, neutral):
    place = lax.axis_index(axis)
    gathered = jax.tree.map(
        lambda a, kind: lax.all_gather(a.astype(kind), axis),
        array,
        (jnp.bfloat16, jnp.bfloat16, jnp.bfloat16),
    )
    state = jax.tree.map(lambda a, e: jnp.zeros_like(a) + jnp.asarray(e, a.dtype), array, neutral)

    def one(turn, state):
        return join(
            state,
            jax.tree.map(
                lambda a, own: lax.dynamic_index_in_dim(a, turn, 0, False).astype(own.dtype),
                gathered,
                array,
            ),
        )

    return lax.fori_loop(0, place, one, state)


def entering(array, axis, combine, identity):
    count, place = (lax.axis_size(axis), lax.axis_index(axis))
    everything = jax.tree.map(
        lambda part, kind: lax.all_gather(part.astype(kind), axis),
        array,
        jax.tree.map(lambda a: jnp.bfloat16 if a.dtype == jnp.float32 else a.dtype, array),
    )
    start = jax.tree.map(
        lambda part, zero: jnp.broadcast_to(jnp.asarray(zero, part.dtype), part.shape),
        array,
        identity,
    )

    def turn(k, before):
        at = count - 1 - k
        reached = at > place
        new = combine(
            before, jax.tree.map(lambda part, own: part[at].astype(own.dtype), everything, array)
        )
        return jax.tree.map(lambda a, b: jnp.where(reached, a, b), new, before)

    return lax.fori_loop(0, count, turn, start)


def wide_layer_norm(values, scale_vec, shift_vec):
    center = values - jnp.mean(values, axis=-1, keepdims=True)
    inverse = lax.rsqrt(jnp.mean(center * center, axis=-1, keepdims=True) + 1e-05)
    normed = center * inverse
    return (normed * scale_vec + shift_vec, normed, inverse)


def wide_norm_back(upstream, normed, inverse, scale_vec):
    scaled = upstream * scale_vec
    inner = (
        scaled
        - jnp.mean(scaled, axis=-1, keepdims=True)
        - normed * jnp.mean(scaled * normed, axis=-1, keepdims=True)
    )
    return (
        inverse * inner,
        jnp.sum(upstream * normed, axis=(0, 1)),
        jnp.sum(upstream, axis=(0, 1)),
    )


def shift_prev(values, persist_indicator):
    arrived = shifted(values[:, -1:, :], "tensor", 1)
    return jnp.concatenate([arrived, values[:, :-1]], axis=1) * persist_indicator[:, :, None]


def shift_back(upstream, persist_indicator):
    masked = upstream * persist_indicator[:, :, None]
    arrived = shifted(masked[:, :1, :], "tensor", -1)
    return jnp.concatenate([masked[:, 1:], arrived], axis=1)


def project(values, matrix):
    return jnp.einsum("rtd,de->rte", values, matrix, preferred_element_type=jnp.float32)


def project_back(upstream, matrix):
    return jnp.einsum("rte,de->rtd", upstream, matrix, preferred_element_type=jnp.float32)


def outer_sum(values, upstream):
    return jnp.einsum("rtd,rte->de", values, upstream, preferred_element_type=jnp.float32)


def mix_back(upstreams, shares, differ, persist_indicator):
    toward = jnp.zeros_like(differ)
    behind = jnp.zeros_like(differ)
    share_grads = []
    for upstream, share in zip(upstreams, shares):
        toward = toward + upstream * share
        behind = behind + upstream * (1.0 - share)
        share_grads.append(jnp.sum(upstream * differ, axis=(0, 1)))
    return (toward + shift_back(behind, persist_indicator), share_grads)


def chain_combine(earlier, later):
    return (
        earlier[0] * later[0],
        later[0] * earlier[1] + later[1],
        later[0] * earlier[2] + later[2],
    )


def scan_fragments(
    lookup_wide, payload_wide, fading_power, reward_coords, text_boundary_indicators
):
    decay_rate = jnp.exp(fading_power)
    row_count, span_len, width_len = lookup_wide.shape
    block_len = min(32, span_len)
    block_count = span_len // block_len
    places = jnp.arange(block_len, dtype=jnp.float32)
    rising = jnp.exp(places[:, None] * decay_rate)
    falling = jnp.exp(-(places[:, None] - 1.0) * decay_rate)
    trailing = jnp.exp(-(block_len - 1.0 - places)[:, None] * decay_rate)
    leading = jnp.exp(-places[:, None] * decay_rate)
    settle = jnp.exp(-block_len * decay_rate)
    before = places[:, None] > places[None, :]

    def split_blocks(values):
        return jnp.swapaxes(
            values.reshape((row_count, block_count, block_len) + values.shape[2:]), 0, 1
        )

    def advance(state_pair, scanned):
        accrued_dividend_sum, accrued_divisor_sum = state_pair
        lookup_narrow, payload_narrow, reset_b = scanned
        tree_levels = jnp.cumsum(reset_b, axis=1)
        linked = ((tree_levels[:, :, None] == tree_levels[:, None, :]) & before).astype(jnp.float32)
        key_term = jnp.exp(lookup_narrow)
        keyed_value = key_term * payload_narrow
        inside_numerator = falling * jnp.einsum(
            "rti,rid->rtd", linked, rising * keyed_value, precision=lax.Precision.HIGHEST
        )
        interior_divisor_sum = falling * jnp.einsum(
            "rti,rid->rtd", linked, rising * key_term, precision=lax.Precision.HIGHEST
        )
        leftover_multiplier = (tree_levels == 0).astype(jnp.float32)[:, :, None] * leading
        reward_multiplier = jnp.exp(reward_coords + lookup_narrow)
        above_total = (
            inside_numerator
            + reward_multiplier * payload_narrow
            + leftover_multiplier * accrued_dividend_sum[:, None, :]
        )
        below_total = (
            interior_divisor_sum
            + reward_multiplier
            + leftover_multiplier * accrued_divisor_sum[:, None, :]
        )
        ending = (tree_levels == tree_levels[:, -1:]).astype(jnp.float32)[:, :, None] * trailing
        intact = (tree_levels[:, -1] == 0).astype(jnp.float32)[:, None] * settle
        new_num = intact * accrued_dividend_sum + jnp.sum(ending * keyed_value, axis=1)
        new_den = intact * accrued_divisor_sum + jnp.sum(ending * key_term, axis=1)
        return ((new_num, new_den), (above_total, below_total))

    initial = jnp.zeros((row_count, width_len), jnp.float32)
    (total_num, total_den), (uppers, lowers) = lax.scan(
        advance,
        (initial, initial),
        (
            split_blocks(lookup_wide),
            split_blocks(payload_wide),
            split_blocks(text_boundary_indicators),
        ),
    )

    def join_blocks(values):
        return jnp.swapaxes(values, 0, 1).reshape(row_count, span_len, width_len)

    tree_levels = jnp.cumsum(text_boundary_indicators, axis=1)
    reaching = (tree_levels == 0).astype(jnp.float32)[:, :, None] * jnp.exp(
        -jnp.arange(span_len, dtype=jnp.float32)[:, None] * decay_rate
    )
    passing = (tree_levels[:, -1] == 0).astype(jnp.float32)[:, None] * jnp.exp(
        -span_len * decay_rate
    )
    return (join_blocks(uppers), join_blocks(lowers), reaching, total_num, total_den, passing)


def recurrence_finish(pieces_list, incoming_num, incoming_den):
    above_total = pieces_list[0] + pieces_list[2] * incoming_num[:, None, :]
    below_total = pieces_list[1] + pieces_list[2] * incoming_den[:, None, :]
    return (above_total / below_total, below_total)


def ffn_apply(inputs, key_weight, value_weight):
    hidden_pre = project(inputs, key_weight)
    hidden = jnp.square(jax.nn.relu(hidden_pre)).astype(jnp.bfloat16)
    return (hidden_pre, hidden, project(hidden, value_weight))


def ffn_grads(inputs, hidden_pre, hidden, upstream, key_weight, value_weight):
    g_hidden = jnp.einsum("rtd,fd->rtf", upstream, value_weight, preferred_element_type=jnp.float32)
    grad_value = jnp.einsum("rtf,rtd->fd", hidden, upstream, preferred_element_type=jnp.float32)
    g_pre = (2.0 * jax.nn.relu(hidden_pre) * g_hidden).astype(jnp.bfloat16)
    grad_key = jnp.einsum("rtd,rtf->df", inputs, g_pre, preferred_element_type=jnp.float32)
    g_inputs = jnp.einsum("rtf,df->rtd", g_pre, key_weight, preferred_element_type=jnp.float32)
    return (g_inputs, grad_key, grad_value)


def wide_shards(
    incoming_embeddings,
    text_boundary_indicators,
    upstream_sensitivity,
    primary_standardize_scaling,
    primary_standardize_offset,
    secondary_standardize_scaling,
    secondary_standardize_offset,
    feature_fading_logarithms,
    present_symbol_reward,
    timemix_lookup_blend,
    timemix_payload_blend,
    timemix_gate_blend,
    timemix_lookup_proj,
    timemix_payload_proj,
    timemix_gate_proj,
    timemix_emit_proj,
    feedmix_lookup_blend,
    feedmix_gate_blend,
    feedmix_gate_proj,
    feedmix_lookup_proj,
    feedmix_payload_proj,
):
    gathered_portions = (
        lax.all_gather(primary_standardize_scaling, ("dp", "tensor"), axis=0, tiled=True),
        lax.all_gather(primary_standardize_offset, ("dp", "tensor"), axis=0, tiled=True),
        lax.all_gather(secondary_standardize_scaling, ("dp", "tensor"), axis=0, tiled=True),
        lax.all_gather(secondary_standardize_offset, ("dp", "tensor"), axis=0, tiled=True),
        lax.all_gather(feature_fading_logarithms, ("dp", "tensor"), axis=0, tiled=True),
        lax.all_gather(present_symbol_reward, ("dp", "tensor"), axis=0, tiled=True),
        lax.all_gather(timemix_lookup_blend, ("dp", "tensor"), axis=0, tiled=True),
        lax.all_gather(timemix_payload_blend, ("dp", "tensor"), axis=0, tiled=True),
        lax.all_gather(timemix_gate_blend, ("dp", "tensor"), axis=0, tiled=True),
        lax.all_gather(timemix_lookup_proj, ("dp", "tensor"), axis=0, tiled=True),
        lax.all_gather(timemix_payload_proj, ("dp", "tensor"), axis=0, tiled=True),
        lax.all_gather(timemix_gate_proj, ("dp", "tensor"), axis=0, tiled=True),
        lax.all_gather(timemix_emit_proj, ("dp", "tensor"), axis=0, tiled=True),
        lax.all_gather(feedmix_lookup_blend, ("dp", "tensor"), axis=0, tiled=True),
        lax.all_gather(feedmix_gate_blend, ("dp", "tensor"), axis=0, tiled=True),
        lax.all_gather(feedmix_gate_proj, ("dp", "tensor"), axis=0, tiled=True),
    )
    initial_scaling_coords = gathered_portions[0].astype(jnp.float32)
    initial_offset_coords = gathered_portions[1].astype(jnp.float32)
    later_scaling_coords = gathered_portions[2].astype(jnp.float32)
    later_offset_coords = gathered_portions[3].astype(jnp.float32)
    fading_power = gathered_portions[4].astype(jnp.float32)
    reward_coords = gathered_portions[5].astype(jnp.float32)
    share_k1 = gathered_portions[6].astype(jnp.float32)
    share_v1 = gathered_portions[7].astype(jnp.float32)
    share_r1 = gathered_portions[8].astype(jnp.float32)
    lookup_coefficients_initial = gathered_portions[9]
    payload_coefficients_initial = gathered_portions[10]
    gate_coefficients_initial = gathered_portions[11]
    emit_coefficients_initial = gathered_portions[12]
    share_k2 = gathered_portions[13].astype(jnp.float32)
    share_r2 = gathered_portions[14].astype(jnp.float32)
    gate_coefficients_later = gathered_portions[15]
    lookup_coefficients_later, payload_coefficients_later = (
        lax.all_gather(feedmix_lookup_proj, "dp", axis=0, tiled=True),
        lax.all_gather(feedmix_payload_proj, "dp", axis=1, tiled=True),
    )
    persist_indicator = (1 - text_boundary_indicators).astype(jnp.float32)
    inputs = incoming_embeddings.astype(jnp.float32)
    normed_one, unit_one, inverse_one = wide_layer_norm(
        inputs, initial_scaling_coords, initial_offset_coords
    )
    prev_one = shift_prev(normed_one, persist_indicator)
    differ_one = normed_one - prev_one
    in_key = (prev_one + differ_one * share_k1).astype(jnp.bfloat16)
    in_value = (prev_one + differ_one * share_v1).astype(jnp.bfloat16)
    in_recept = (prev_one + differ_one * share_r1).astype(jnp.bfloat16)
    initial_lookup_lines = project(in_key, lookup_coefficients_initial)
    initial_payload_lines = project(in_value, payload_coefficients_initial)
    recept_one = project(in_recept, gate_coefficients_initial)
    pieces_list = scan_fragments(
        initial_lookup_lines,
        initial_payload_lines,
        fading_power,
        reward_coords,
        text_boundary_indicators,
    )
    passing = pieces_list[5]
    identity = (jnp.ones_like(passing), jnp.zeros_like(passing), jnp.zeros_like(passing))
    unused_item, incoming_num, incoming_den = carried_in(
        (passing, pieces_list[3], pieces_list[4]), "tensor", chain_combine, identity
    )
    blended_mean_state, below_total = recurrence_finish(pieces_list, incoming_num, incoming_den)
    sig_one = jax.nn.sigmoid(recept_one)
    mixed_att = (sig_one * blended_mean_state).astype(jnp.bfloat16)
    resid_one = inputs + project(mixed_att, emit_coefficients_initial)
    normed_two, unit_two, inverse_two = wide_layer_norm(
        resid_one, later_scaling_coords, later_offset_coords
    )
    prev_two = shift_prev(normed_two, persist_indicator)
    differ_two = normed_two - prev_two
    in_key_two = (prev_two + differ_two * share_k2).astype(jnp.bfloat16)
    in_recept_two = (prev_two + differ_two * share_r2).astype(jnp.bfloat16)
    recept_two = project(in_recept_two, gate_coefficients_later)
    sig_two = jax.nn.sigmoid(recept_two)
    row_inputs = lax.all_gather(in_key_two, "tensor", axis=1, tiled=True)
    hidden_pre, hidden, partial_value = ffn_apply(
        row_inputs, lookup_coefficients_later, payload_coefficients_later
    )
    value_two = lax.psum_scatter(
        partial_value.astype(jnp.bfloat16), "tensor", scatter_dimension=1, tiled=True
    ).astype(jnp.float32)
    layer_out = (resid_one + sig_two * value_two).astype(jnp.bfloat16)
    upstream = upstream_sensitivity.astype(jnp.float32)
    g_value_two = (upstream * sig_two).astype(jnp.bfloat16)
    g_recept_two = (upstream * value_two * sig_two * (1.0 - sig_two)).astype(jnp.bfloat16)
    grad_recept_two = outer_sum(in_recept_two, g_recept_two)
    g_mix_r2 = project_back(g_recept_two, gate_coefficients_later)
    row_grads = lax.all_gather(g_value_two, "tensor", axis=1, tiled=True)
    partial_grad, grad_key_two, grad_value_two = ffn_grads(
        row_inputs,
        hidden_pre,
        hidden,
        row_grads,
        lookup_coefficients_later,
        payload_coefficients_later,
    )
    g_mix_k2 = lax.psum_scatter(
        partial_grad.astype(jnp.bfloat16), "tensor", scatter_dimension=1, tiled=True
    ).astype(jnp.float32)
    sum_key_two, sum_value_two = (
        lax.psum_scatter(
            grad_key_two.astype(jnp.bfloat16), "dp", scatter_dimension=0, tiled=True
        ).astype(jnp.float32),
        lax.psum_scatter(
            grad_value_two.astype(jnp.bfloat16), "dp", scatter_dimension=1, tiled=True
        ).astype(jnp.float32),
    )
    g_normed_two, shares_two = mix_back(
        (g_mix_k2, g_mix_r2), (share_k2, share_r2), differ_two, persist_indicator
    )
    g_resid_part, grad_gain_two, grad_bias_two = wide_norm_back(
        g_normed_two, unit_two, inverse_two, later_scaling_coords
    )
    g_resid = upstream + g_resid_part
    g_branch = g_resid.astype(jnp.bfloat16)
    grad_out_one = outer_sum(mixed_att, g_branch)
    g_mixed = project_back(g_branch, emit_coefficients_initial)
    g_weighted = g_mixed * sig_one
    g_recept_one = (g_mixed * blended_mean_state * sig_one * (1.0 - sig_one)).astype(jnp.bfloat16)
    reaching = pieces_list[2]
    g_in_num = jnp.sum(g_weighted * reaching / below_total, axis=1)
    g_in_den = -jnp.sum(g_weighted * reaching * blended_mean_state / below_total, axis=1)
    unused_item, back_num, back_den = entering(
        (passing, g_in_num, g_in_den), "tensor", chain_combine, identity
    )
    g_passing = back_num * incoming_num + back_den * incoming_den

    def device_fragment(lookup_wide, payload_wide, fading_coords, reward_power):
        shard_pieces = scan_fragments(
            lookup_wide, payload_wide, fading_coords, reward_power, text_boundary_indicators
        )
        local_out, unused_item = recurrence_finish(shard_pieces, incoming_num, incoming_den)
        return (local_out, shard_pieces[3], shard_pieces[4], shard_pieces[5])

    unused_item, reverse_pass_rule = jax.vjp(
        device_fragment, initial_lookup_lines, initial_payload_lines, fading_power, reward_coords
    )
    derivative_lookup_wide, derivative_payload_wide, fading_derivative, reward_derivative = (
        reverse_pass_rule((g_weighted, back_num, back_den, g_passing))
    )
    g_key_one = derivative_lookup_wide.astype(jnp.bfloat16)
    g_value_one = derivative_payload_wide.astype(jnp.bfloat16)
    grad_key_one = outer_sum(in_key, g_key_one)
    grad_value_one = outer_sum(in_value, g_value_one)
    grad_recept_one = outer_sum(in_recept, g_recept_one)
    g_mix_k1 = project_back(g_key_one, lookup_coefficients_initial)
    g_mix_v1 = project_back(g_value_one, payload_coefficients_initial)
    g_mix_r1 = project_back(g_recept_one, gate_coefficients_initial)
    g_normed_one, shares_one = mix_back(
        (g_mix_k1, g_mix_v1, g_mix_r1),
        (share_k1, share_v1, share_r1),
        differ_one,
        persist_indicator,
    )
    g_input_part, grad_gain_one, grad_bias_one = wide_norm_back(
        g_normed_one, unit_one, inverse_one, initial_scaling_coords
    )
    grad_tokens = g_resid + g_input_part
    summed = (
        lax.psum_scatter(grad_gain_one, ("dp", "tensor"), scatter_dimension=0, tiled=True),
        lax.psum_scatter(grad_bias_one, ("dp", "tensor"), scatter_dimension=0, tiled=True),
        lax.psum_scatter(grad_gain_two, ("dp", "tensor"), scatter_dimension=0, tiled=True),
        lax.psum_scatter(grad_bias_two, ("dp", "tensor"), scatter_dimension=0, tiled=True),
        lax.psum_scatter(fading_derivative, ("dp", "tensor"), scatter_dimension=0, tiled=True),
        lax.psum_scatter(reward_derivative, ("dp", "tensor"), scatter_dimension=0, tiled=True),
        lax.psum_scatter(shares_one[0], ("dp", "tensor"), scatter_dimension=0, tiled=True),
        lax.psum_scatter(shares_one[1], ("dp", "tensor"), scatter_dimension=0, tiled=True),
        lax.psum_scatter(shares_one[2], ("dp", "tensor"), scatter_dimension=0, tiled=True),
        lax.psum_scatter(grad_key_one, ("dp", "tensor"), scatter_dimension=0, tiled=True),
        lax.psum_scatter(grad_value_one, ("dp", "tensor"), scatter_dimension=0, tiled=True),
        lax.psum_scatter(grad_recept_one, ("dp", "tensor"), scatter_dimension=0, tiled=True),
        lax.psum_scatter(grad_out_one, ("dp", "tensor"), scatter_dimension=0, tiled=True),
        lax.psum_scatter(shares_two[0], ("dp", "tensor"), scatter_dimension=0, tiled=True),
        lax.psum_scatter(shares_two[1], ("dp", "tensor"), scatter_dimension=0, tiled=True),
        lax.psum_scatter(grad_recept_two, ("dp", "tensor"), scatter_dimension=0, tiled=True),
    )
    return (
        layer_out,
        grad_tokens,
        summed[0],
        summed[1],
        summed[2],
        summed[3],
        summed[4],
        summed[5],
        summed[6],
        summed[7],
        summed[8],
        summed[9],
        summed[10],
        summed[11],
        summed[12],
        summed[13],
        summed[14],
        summed[15],
        sum_key_two,
        sum_value_two,
    )


def local_call(body, outs, name, *args):
    vmem = pl.BlockSpec(memory_space=pltpu.VMEM)
    return pl.pallas_call(
        body,
        out_shape=outs,
        in_specs=[vmem] * len(args),
        out_specs=tuple([vmem] * len(outs)),
        compiler_params=pltpu.CompilerParams(vmem_limit_bytes=48 * MIB),
        name=name,
    )(*args)


def split_columns(w, parts):
    rows, width = w.shape
    return w.reshape(rows, parts, 2, width // (2 * parts)).transpose(2, 0, 1, 3).reshape(2, rows, width // 2)


def join_columns(own, other, c, parts):
    rows, half = own.shape[-2:]
    a = jnp.where(c == 0, own, other).reshape(own.shape[:-1] + (parts, half // parts))
    b = jnp.where(c == 0, other, own).reshape(own.shape[:-1] + (parts, half // parts))
    return jnp.stack([a, b], axis=-2).reshape(own.shape[:-1] + (2 * half,))


def pair_sum(a):
    return lax.psum(a.astype(BF16), "tensor").astype(F32)


def layer_norm(values, gain, bias):
    normed, inverse = norm(values)
    return normed * gain + bias, normed, inverse


def norm_back(g, normed, inverse, gain):
    q = g * gain
    return inverse * (
        q - jnp.mean(q, axis=-1, keepdims=True) - normed * jnp.mean(q * normed, axis=-1, keepdims=True)
    )


def shift_down(v, keep):
    return jnp.concatenate([jnp.zeros_like(v[:1]), v[:-1]]) * keep[:, None]


def shift_up(v, keep):
    v = v * keep[:, None]
    return jnp.concatenate([v[1:], jnp.zeros_like(v[:1])])


def pack(tokens, starts, upstream, gain1, bias1, gain2, bias2, fading, reward, mk1, mv1, mr1, wk, wv, wr, wo, mk2, mr2, wg, fk, fv):
    i, c, count = lax.axis_index("dp"), lax.axis_index("tensor"), lax.axis_size("dp")
    own_rows, width = wk.shape
    half, hidden = width // 2, fk.shape[1]
    by_core = jnp.stack([split_columns(wk, count), split_columns(wv, count), split_columns(wr, count), split_columns(wg, 1)])
    own4 = lax.dynamic_index_in_dim(by_core, c, 1, False)
    other4 = lax.dynamic_index_in_dim(by_core, 1 - c, 1, False)
    emit = wo.reshape(own_rows, 2, half).transpose(1, 0, 2).reshape(1, 2 * own_rows, half)
    key4 = fk.reshape(2 * own_rows, 4, hidden // 4).transpose(1, 0, 2)
    value4 = fv.reshape(4, hidden // 4, 2 * own_rows).transpose(0, 2, 1)
    ffn = jnp.stack([key4, value4], axis=1).reshape(8, 2 * own_rows, hidden // 4)
    rest = jnp.concatenate([emit, ffn])
    slots = 128 // own_rows
    everywhere = jnp.stack([gain1, bias1, gain2, bias2, fading, reward, mk1, mv1, mr1, mk2, mr2])
    own = jnp.stack([fading, reward, jnp.zeros_like(fading), jnp.zeros_like(fading), jnp.zeros_like(fading)])
    lane = jnp.arange(128)[None, :] // own_rows
    vec = jnp.concatenate([
        jnp.where(lane == (2 * i + c) % slots, jnp.tile(everywhere, (1, slots)), 0),
        jnp.where(lane == i % slots, jnp.tile(own, (1, slots)), 0),
    ]).astype(BF16)
    keep = jnp.broadcast_to((1 - starts[0]).astype(F32)[:, None], (starts.shape[1], 128))
    return own4, other4, rest, vec, tokens[0], upstream[0], keep


def shards(*args):
    tokens = args[0]
    c = lax.axis_index("tensor")
    i = lax.axis_index("dp")
    count = lax.axis_size("dp")
    own_rows, width = args[12].shape
    hidden = args[19].shape[1]
    half = width // 2
    (
        g, layer_out, x, up, ins, kvr, sn, sd, mixed, resid, ins2, pre, act, g_value, g_recept2, vec, rows, keep,
    ) = forward_call(*pack(*args))

    gain1, bias1, gain2, bias2, fading, reward, mk1, mv1, mr1, mk2, mr2 = (vec[n] for n in range(VECTORS))
    keep_rows, keep = keep, keep[:, 0]
    g = g.reshape((PIECES, width, half))
    wk, wv, wr, wg = g[KEY], g[VALUE], g[GATE], g[GATE2]
    wo = g[EMIT].reshape(count, 2, own_rows, half).transpose(0, 2, 1, 3).reshape(half, width)
    fk = jnp.concatenate([g[FFN + 2 * n] for n in range(4)], axis=1)
    fv = jnp.concatenate([g[FFN + 1 + 2 * n] for n in range(4)], axis=1)
    x, up = x.astype(F32), up.astype(F32)
    n1, u1, i1 = layer_norm(x, gain1, bias1)
    d1 = n1 - shift_down(n1, keep)
    in_k, in_v, in_r = (ins[n] for n in range(3))
    k, v, r = (kvr[n] for n in range(3))
    resid = jnp.concatenate([resid[0], resid[1]], axis=1)
    n2, u2, i2 = layer_norm(resid, gain2, bias2)
    d2 = n2 - shift_down(n2, keep)
    in_k2, in_r2 = ins2[0], ins2[1]
    pre = jnp.concatenate([pre[n] for n in range(4)], axis=1).astype(F32)
    act = jnp.concatenate([act[n] for n in range(4)], axis=1)
    g_value = jnp.concatenate([g_value[0], g_value[1]], axis=1)
    low = jax.ShapeDtypeStruct(k.shape, BF16)
    grad_fv = dot(g_value, act, TN)
    g_pre = (2.0 * pre * dot(g_value, fv, NN)).astype(BF16)
    grad_fk = dot(in_k2, g_pre, TN)
    grad_wg = dot(in_r2, g_recept2, TN)
    gk2 = dot(g_pre, fk, NT)
    gr2 = dot(g_recept2, wg, NT)
    grad_mk2, grad_mr2 = jnp.sum(gk2 * d2, 0), jnp.sum(gr2 * d2, 0)
    gn2 = gk2 * mk2 + gr2 * mr2 + shift_up(gk2 * (1 - mk2) + gr2 * (1 - mr2), keep)
    grad_gain2, grad_bias2 = jnp.sum(gn2 * u2, 0), jnp.sum(gn2, 0)
    g_resid = up + norm_back(pair_sum(gn2), u2, i2, gain2)
    g_branch = g_resid.astype(BF16)
    grad_wo = dot(mixed, g_branch, TN)
    g_mixed = dot(g_branch, wo, NT)
    gk1, gv1, gr1, wsums = local_call(
        wkv_backward, (low, low, low, jax.ShapeDtypeStruct((8, half), F32)), "wkv_backward",
        g_mixed, k, v, r, sn, sd, keep_rows, rows,
    )
    grad_wk, grad_wv, grad_wr = dot(in_k, gk1, TN), dot(in_v, gv1, TN), dot(in_r, gr1, TN)
    toward, behind, grad_mix = 0.0, 0.0, []
    for grad, w, m in ((gk1, wk, mk1), (gv1, wv, mv1), (gr1, wr, mr1)):
        back = dot(grad, w, NT)
        toward = toward + back * m
        behind = behind + back * (1 - m)
        grad_mix.append(jnp.sum(back * d1, 0))
    gn1 = toward + shift_up(behind, keep)
    grad_gain1, grad_bias1 = jnp.sum(gn1 * u1, 0), jnp.sum(gn1, 0)
    gn1 = lax.psum_scatter(gn1.astype(BF16), "tensor", scatter_dimension=0, tiled=True).astype(F32)
    span = tokens.shape[1]

    def mine(v):
        return lax.dynamic_slice_in_dim(v, c * span, span, 0)

    grad_tokens = mine(g_resid) + norm_back(gn1, mine(u1), mine(i1), gain1)

    def pieces(m):
        return m.reshape(1, 4, 4, 2 * own_rows, half)

    grad_wo = grad_wo.reshape(count, own_rows, 2, half).transpose(0, 2, 1, 3)
    grad_fk, grad_fv = (
        m.reshape(width, 4, hidden // 4).transpose(1, 0, 2).reshape((4, 4, 4) + (2 * own_rows, half))
        for m in (grad_fk, grad_fv)
    )
    partial = jnp.concatenate(
        [pieces(grad_wk), pieces(grad_wv), pieces(grad_wr), pieces(grad_wg), pieces(grad_wo), grad_fk, grad_fv]
    ).astype(BF16)

    def all_channels(v):
        z = jnp.zeros_like(v)
        return jnp.where(c == 0, jnp.concatenate([v, z]), jnp.concatenate([z, v]))

    vsums = jnp.stack([
        grad_gain1, grad_bias1, grad_gain2, grad_bias2, all_channels(wsums[1]), all_channels(wsums[0]),
        *grad_mix, grad_mk2, grad_mr2,
    ])
    vsums = jnp.pad(vsums, ((0, 16 - VECTORS), (0, 0)))
    total, recv4, vtotal = reduce_weights(partial, vsums)
    own_scan = lax.dynamic_slice_in_dim(vtotal, c * half + i * own_rows, own_rows, 1)
    vtotal = lax.dynamic_slice_in_dim(vtotal, (2 * i + c) * own_rows, own_rows, 1)
    own = lax.dynamic_slice_in_dim(total[:4], c * own_rows, own_rows, 1)
    out_k, out_v, out_r = (join_columns(own[n], recv4[n], c, count) for n in range(3))
    out_g = join_columns(own[3], recv4[3], c, 1)
    out_o = total[4].reshape(2, own_rows, half).transpose(1, 0, 2).reshape(own_rows, width)
    out_fk = total[5:9].transpose(1, 0, 2).reshape(2 * own_rows, hidden)
    out_fv = total[9:13].transpose(0, 2, 1).reshape(hidden, 2 * own_rows)
    return (
        layer_out[None], grad_tokens[None], *(vtotal[n] for n in range(4)), own_scan[4], own_scan[5],
        *(vtotal[n] for n in range(6, 9)), out_k, out_v, out_r, out_o, vtotal[9], vtotal[10], out_g, out_fk, out_fv,
    )


def solution(mesh):
    row, vector, matrix_ = P("dp", "tensor", None), P(("dp", "tensor")), P(("dp", "tensor"), None)
    key, value = P("dp", "tensor"), P("tensor", "dp")
    in_specs = (row, P("dp", "tensor"), row) + (vector,) * 9 + (matrix_,) * 4 + (vector,) * 2 + (matrix_, key, value)
    out_specs = (row, row) + (vector,) * 9 + (matrix_,) * 4 + (vector,) * 2 + (matrix_, key, value)
    body = shards if (mesh.shape["dp"], mesh.shape["tensor"]) == (16, 2) else wide_shards
    return jax.shard_map(body, mesh=mesh, in_specs=in_specs, out_specs=out_specs, check_vma=False)
```

```python
import functools

import jax
import jax.numpy as jnp
from jax import lax
from jax.experimental import pallas as pl
from jax.experimental.pallas import tpu as pltpu
from jax.sharding import PartitionSpec as P

F32, BF16 = jnp.float32, jnp.bfloat16
MESH_ID = pl.DeviceIdType.MESH
MIB = 1 << 20
PARTS = 10
PIECES = 13


def place():
    i, c = lax.axis_index("dp"), lax.axis_index("tensor")
    return i // 4, i % 4, c


def neighbours(z, yx):
    x = yx + 1 - 2 * (yx % 2)
    y = (yx + 2) % 4
    d = (x + 2) % 4
    zs = (z + 1 - 2 * (z % 2), (z + 2) % 4, 3 - z)
    return x, y, d, zs


def enter(z, yx, c):
    x, y, d, zs = neighbours(z, yx)
    barrier = pltpu.get_barrier_semaphore()
    targets = [(z * 4 + yx, 1 - c), (z * 4 + x, c), (z * 4 + y, c)]
    targets += [(peer * 4 + yx, c) for peer in zs]
    for target in targets:
        pl.semaphore_signal(barrier, inc=1, device_id=target, device_id_type=MESH_ID)
    pl.semaphore_wait(barrier, len(targets))


def remote(src, dst, send, recv, target):
    return pltpu.make_async_remote_copy(
        src_ref=src, dst_ref=dst, send_sem=send, recv_sem=recv,
        device_id=target, device_id_type=MESH_ID,
    )


class Gather:
    def __init__(self, view, sends, recvs, first=0):
        self.view, self.sends, self.recvs, self.first = view, sends, recvs, first
        self.z, self.yx, self.c = place()
        self.x, self.y, self.d, self.zs = neighbours(self.z, self.yx)

    def to(self, z, yx):
        return (z * 4 + yx, self.c)

    def copy(self, p, k, ref, target):
        return remote(ref, ref, self.sends.at[p, k], self.recvs.at[p, k], target)

    def along(self, p):
        own = self.view(p).at[self.z, self.yx]
        return [self.copy(p, k, own, self.to(peer, self.yx)) for k, peer in enumerate(self.zs)]

    def plane(self, p):
        own = self.view(p).at[:, self.yx]
        return [self.copy(p, 3, own, self.to(self.z, self.x)), self.copy(p, 4, own, self.to(self.z, self.y))]

    def onward(self, p):
        return [
            self.copy(p, 5, self.view(p).at[0:2, self.x], self.to(self.z, self.y)),
            self.copy(p, 6, self.view(p).at[2:4, self.y], self.to(self.z, self.x)),
        ]

    def start(self, copies):
        for copy in copies:
            copy.start()

    def arrive(self, copies):
        for copy in copies:
            copy.wait_recv()

    def step(self, p):
        self.arrive(self.along(p))
        self.start(self.plane(p))

    def forward(self, p):
        self.arrive(self.plane(p))
        self.start(self.onward(p))

    def finish(self, p):
        for copy in self.along(p) + self.plane(p) + self.onward(p):
            copy.wait_send()


class Reduce:
    def __init__(self, part, ring1, ring2, line, out, sends, recvs):
        self.all_parts, self.ring1, self.ring2, self.line, self.out = part, ring1, ring2, line, out
        self.sends, self.recvs = sends, recvs
        self.z, self.yx, self.c = place()
        self.x, self.y, self.d, self.zs = neighbours(self.z, self.yx)

    def copy(self, p, k, src, dst, z, yx):
        return remote(src, dst, self.sends.at[p, k], self.recvs.at[p, k], (z * 4 + yx, self.c))

    def part(self, p):
        return self.all_parts.at[p % PARTS]

    def diagonal(self, p):
        part, z = self.part(p), self.z
        return [
            self.copy(p, 0, part.at[0:2, self.d], self.ring1.at[p, 0], z, self.x),
            self.copy(p, 1, part.at[2:4, self.d], self.ring1.at[p, 1], z, self.y),
        ]

    def side(self, p):
        part, z = self.part(p), self.z
        return [
            self.copy(p, 2, part.at[:, self.x], self.ring2.at[p, 0], z, self.x),
            self.copy(p, 3, part.at[:, self.y], self.ring2.at[p, 1], z, self.y),
        ]

    def down(self, p):
        part = self.part(p)
        return [
            self.copy(p, 4 + k, part.at[peer, self.yx], self.line.at[p, k], peer, self.yx)
            for k, peer in enumerate(self.zs)
        ]

    def start(self, copies):
        for copy in copies:
            copy.start()

    def arrive(self, copies):
        for copy in copies:
            copy.wait_recv()

    def add(self, p, a, yx, pieces):
        total = self.part(p)[a, yx].astype(F32)
        for piece in pieces:
            total = total + piece.astype(F32)
        return total

    def stage1(self, p):
        self.start(self.diagonal(p))

    def stage2(self, p):
        self.arrive(self.diagonal(p))
        for a in range(2):
            self.part(p)[a, self.y] = self.add(p, a, self.y, [self.ring1[p, 0, a]]).astype(BF16)
            self.part(p)[a + 2, self.x] = self.add(p, a + 2, self.x, [self.ring1[p, 1, a]]).astype(BF16)
        self.start(self.side(p))

    def stage3(self, p):
        self.arrive(self.side(p))
        for a in range(4):
            self.part(p)[a, self.yx] = self.add(
                p, a, self.yx, [self.ring2[p, 0, a], self.ring2[p, 1, a]]
            ).astype(BF16)
        self.start(self.down(p))

    def stage4(self, p):
        self.arrive(self.down(p))
        self.out[p] = self.add(p, self.z, self.yx, [self.line[p, k] for k in range(3)])

    def finish(self, p):
        for copy in self.diagonal(p) + self.side(p) + self.down(p):
            copy.wait_send()


def lanes(j):
    return slice(j * 128, (j + 1) * 128)


def bottom(v):
    return jnp.broadcast_to(v[7:8], v.shape)


def top(v):
    return jnp.broadcast_to(v[0:1], v.shape)


def masks_down(keep, place_in):
    m1 = jnp.where(place_in >= 1, keep, 0.0)
    m2 = m1 * pltpu.roll(m1, 1, 0)
    m4 = m2 * pltpu.roll(m2, 2, 0)
    for n in (1, 2, 4):
        keep = keep * jnp.where(place_in >= n, pltpu.roll(keep, n, 0), 1.0)
    return m1, m2, m4, keep


def masks_up(after, place_in):
    m1 = jnp.where(place_in <= 6, after, 0.0)
    m2 = m1 * pltpu.roll(m1, 7, 0)
    m4 = m2 * pltpu.roll(m2, 6, 0)
    for n in (1, 2, 4):
        after = after * jnp.where(place_in <= 7 - n, pltpu.roll(after, 8 - n, 0), 1.0)
    return m1, m2, m4, after


def wkv_forward(k_ref, v_ref, r_ref, keep_ref, rows_ref, mixed_ref, sn_ref, sd_ref):
    length, width = k_ref.shape
    tiles = width // 128
    place_in = lax.broadcasted_iota(jnp.int32, (8, 128), 0)
    first = place_in == 0
    zero = jnp.zeros((8, 128), F32)

    def pair(g, carry):
        carry = list(carry)
        base = pl.multiple_of(g * 16, 16)
        keeps = [keep_ref[pl.ds(base + 8 * h, 8), :] for h in range(2)]
        masks = [masks_down(keep, place_in) for keep in keeps]
        for j in range(tiles):
            d1, d2, d4, eu = (rows_ref[n : n + 1, lanes(j)] for n in range(4))
            dp = rows_ref[8:16, lanes(j)]
            made = []
            for h in range(2):
                at = pl.ds(base + 8 * h, 8)
                keep, (m1, m2, m4, mp) = keeps[h], masks[h]
                ek = jnp.exp(k_ref[at, lanes(j)])
                v = v_ref[at, lanes(j)]
                num, den = ek * v, ek
                x, b = num, eu * ek
                for n, coef in ((1, m1 * d1), (2, m2 * d2), (4, m4 * d4)):
                    num = num + coef * pltpu.roll(num, n, 0)
                    den = den + coef * pltpu.roll(den, n, 0)
                coef = mp * dp
                cn, cd = carry[2 * j], carry[2 * j + 1]
                num = num + coef * cn
                den = den + coef * cd
                sn = keep * jnp.where(first, cn, pltpu.roll(num, 1, 0))
                sd = keep * jnp.where(first, cd, pltpu.roll(den, 1, 0))
                carry[2 * j], carry[2 * j + 1] = bottom(num), bottom(den)
                sn_ref[at, lanes(j)] = sn
                sd_ref[at, lanes(j)] = sd
                weighted = (sn + eu * x) / (sd + b)
                made.append(jax.nn.sigmoid(r_ref[at, lanes(j)]) * weighted)
            mixed_ref[pl.ds(base, 16), lanes(j)] = jnp.concatenate(made, axis=0).astype(BF16)
        return tuple(carry)

    lax.fori_loop(0, length // 16, pair, (zero,) * (2 * tiles))


def wkv_backward(
    g_ref, k_ref, v_ref, r_ref, sn_ref, sd_ref, keep_ref, rows_ref, gk_ref, gv_ref, gr_ref, begin, end, carry
):
    length, width = k_ref.shape
    tiles = width // 128
    place_in = lax.broadcasted_iota(jnp.int32, (8, 128), 0)
    last = place_in == 7
    zero = jnp.zeros((8, 128), F32)
    pairs = length // 16

    def pair(step, carry):
        carry = list(carry)
        base = pl.multiple_of((pairs - 1 - step) * 16, 16)
        low, high = (keep_ref[pl.ds(base + 8 * h, 8), :] for h in range(2))
        afters = [
            jnp.where(last, top(high), pltpu.roll(low, 7, 0)),
            jnp.where(last, carry[4 * tiles], pltpu.roll(high, 7, 0)),
        ]
        masks = [masks_up(after, place_in) for after in afters]
        carry[4 * tiles] = top(low)
        for j in range(tiles):
            d1, d2, d4, eu = (rows_ref[n : n + 1, lanes(j)] for n in range(4))
            dp = rows_ref[16:24, lanes(j)]
            made = [None, None]
            for h in (1, 0):
                at = pl.ds(base + 8 * h, 8)
                after, (m1, m2, m4, mp) = afters[h], masks[h]
                ek = jnp.exp(k_ref[at, lanes(j)])
                v = v_ref[at, lanes(j)]
                sn, sd = sn_ref[at, lanes(j)], sd_ref[at, lanes(j)]
                s = jax.nn.sigmoid(r_ref[at, lanes(j)])
                b = eu * ek
                inverse = 1.0 / (sd + b)
                weighted = (sn + b * v) * inverse
                g = g_ref[at, lanes(j)]
                gs = g * s
                p = gs * inverse
                q = -p * weighted
                gr = gs * weighted * (1.0 - s)
                hp, hq = p, q
                for n, coef in ((1, m1 * d1), (2, m2 * d2), (4, m4 * d4)):
                    hp = hp + coef * pltpu.roll(hp, 8 - n, 0)
                    hq = hq + coef * pltpu.roll(hq, 8 - n, 0)
                coef = mp * dp
                cp, cq = carry[4 * j], carry[4 * j + 1]
                hp = hp + coef * cp
                hq = hq + coef * cq
                ap = after * jnp.where(last, cp, pltpu.roll(hp, 7, 0))
                aq = after * jnp.where(last, cq, pltpu.roll(hq, 7, 0))
                carry[4 * j], carry[4 * j + 1] = top(hp), top(hq)
                bonus = b * (v * p + q)
                gv = ek * ap + b * p
                gk = ek * (v * ap + aq) + bonus
                carry[4 * j + 2] = carry[4 * j + 2] + bonus
                carry[4 * j + 3] = carry[4 * j + 3] + (ap * sn + aq * sd)
                made[h] = (gk, gv, gr)
            both = pl.ds(base, 16)
            for n, ref in enumerate((gk_ref, gv_ref, gr_ref)):
                ref[both, lanes(j)] = jnp.concatenate([made[0][n], made[1][n]], axis=0).astype(BF16)
        return tuple(carry)

    return lax.fori_loop(begin, end, pair, (zero,) * (4 * tiles + 1) if carry is None else carry)


def wkv_sums(carry, rows_ref, decay_ref, bonus_ref):
    for j in range(decay_ref.shape[1] // 128):
        bonus_ref[0:1, lanes(j)] = jnp.sum(carry[4 * j + 2], axis=0, keepdims=True)
        decay_ref[0:1, lanes(j)] = -rows_ref[4:5, lanes(j)] * jnp.sum(carry[4 * j + 3], axis=0, keepdims=True)


NN, NT, TN = ((1,), (0,)), ((1,), (1,)), ((0,), (0,))
KEY, VALUE, GATE, EMIT, GATE2, FFN = 0, 1, 2, 3, 4, 5
VECTORS = 11
GAIN1, BIAS1, GAIN2, BIAS2, FADE, REWARD, MK1, MV1, MR1, MK2, MR2, OWN_FADE, OWN_REWARD = range(13)


def dot(a, b, dims):
    return lax.dot_general(a, b, (dims, ((), ())), preferred_element_type=F32)


def strip(i, size):
    return pl.ds(pl.multiple_of(i * size, size), size)


def over_rows(length, size, body):
    def step(i, carry):
        body(strip(i, size))
        return carry

    lax.fori_loop(0, length // size, step, 0)


def matrix(ref):
    return ref[...].reshape(16 * ref.shape[2], ref.shape[3])


def emit_half(ref, h):
    rows = ref.shape[2] // 2
    return ref[:, :, h * rows : (h + 1) * rows, :].reshape(16 * rows, ref.shape[3])


def wide(column, width):
    return jnp.concatenate([column] * (width // 128), axis=1)


def norm(x):
    center = x - jnp.mean(x, axis=-1, keepdims=True)
    inverse = lax.rsqrt(jnp.mean(center * center, axis=-1, keepdims=True) + 1e-05)
    return center * inverse, inverse


def norm_and_mix(length, width, load, gain, bias, keep_ref, mixes, outs):
    first = lax.broadcasted_iota(jnp.int32, (16, width), 0) == 0

    def step(i, before):
        at = strip(i, 16)
        unit, _ = norm(load(at))
        normed = unit * gain + bias
        prev = jnp.where(first, before, pltpu.roll(normed, 1, 0)) * wide(keep_ref[at, :], width)
        differ = normed - prev
        for share, out in zip(mixes, outs):
            out[at, :] = (prev + differ * share).astype(BF16)
        return normed[15:16]

    lax.fori_loop(0, length // 16, step, jnp.zeros((1, width), F32))


def forward_kernel(
    own4, other4, rest, vec, x_own, up_own, keep_own,
    g, out, x_out, up_out, ins_out, kvr_out, sn_out, sd_out, mixed_out, resid_out, ins2_out, pre_out, act_out,
    gv_out, gr_out, vec_out, rows_out, keep_out,
    gv, w, x, up, ins, kvr, sn, sd, mixed, sum_own, sum_other, resid, ins2, pre, act, v_send, v_other, gval, grec, low_half,
    local_sem, ex_send, ex_recv, sends, recvs, vsends, vrecvs, stage_sem, out_sem, sum_send, sum_recv, val_send, val_recv,
):
    z, yx, c = place()
    length, width = x.shape
    half = width // 2
    span = length // 2
    partner = (z * 4 + yx, 1 - c)
    enter(z, yx, c)

    block = own4.shape[1]
    mine = strip(c, block)
    rows_mine = strip(c, span)
    swaps = [
        (vec, gv.at[z, yx, c]),
        (other4.at[0:3], g.at[0:3, z, yx, mine]),
        (other4.at[3], g.at[GATE2, z, yx, mine]),
        (x_own, x.at[rows_mine]),
        (keep_own, keep_out.at[rows_mine]),
        (up_own, up.at[rows_mine]),
    ]
    swaps = [remote(a, b, ex_send.at[n], ex_recv.at[n], partner) for n, (a, b) in enumerate(swaps)]
    keeps = [
        (vec, gv.at[z, yx, c]),
        (own4.at[0:3], g.at[0:3, z, yx, mine]),
        (own4.at[3], g.at[GATE2, z, yx, mine]),
        (x_own, x.at[rows_mine]),
        (keep_own, keep_out.at[rows_mine]),
        (up_own, up.at[rows_mine]),
        (rest.at[0], g.at[EMIT, z, yx]),
        (rest.at[1:9], g.at[FFN : FFN + 8, z, yx]),
    ]
    keeps = [pltpu.make_async_copy(a, b, local_sem.at[n]) for n, (a, b) in enumerate(keeps)]
    for copy in swaps + keeps:
        copy.start()
    weights = Gather(lambda p: g.at[p], sends, recvs)
    vectors = Gather(lambda p: gv, vsends, vrecvs)

    outs = []

    def put(src, dst):
        copy = pltpu.make_async_copy(src, dst, out_sem.at[len(outs)])
        copy.start()
        outs.append(copy)
        return copy

    def stage(p):
        return pltpu.make_async_copy(g.at[p], w.at[p % 3], stage_sem.at[p])

    def turn(n):
        if n < PIECES:
            weights.step(n)
            if n + 2 < PIECES:
                weights.start(weights.along(n + 2))
        if 1 <= n <= PIECES:
            weights.forward(n - 1)
        if n >= 2:
            weights.arrive(weights.onward(n - 2))
            stage(n - 2).start()

    def staged(p):
        stage(p).wait()
        return w.at[p % 3]

    for n in (0, 1, 2):
        swaps[n].wait()
        keeps[n].wait()
    vectors.start(vectors.along(0))
    weights.start(weights.along(0))
    for copy in keeps[6:]:
        copy.wait()
    weights.start(weights.along(1))
    vectors.step(0)
    turn(0)
    vectors.forward(0)
    for n in (3, 4, 5):
        swaps[n].wait()
        keeps[n].wait()
    x_copy, up_copy = put(x, x_out), put(up, up_out)
    turn(1)
    vectors.arrive(vectors.onward(0))

    for t in range(width // 128):
        parts = [gv[(2 * t + k) // 4, (2 * t + k) % 4, core].astype(F32) for k in range(2) for core in range(2)]
        vec_out[:, lanes(t)] = functools.reduce(lambda a, b: a + b, parts)
    ramp = lax.broadcasted_iota(jnp.int32, (8, 128), 0).astype(F32)
    for t in range(half // 128):
        own = functools.reduce(lambda a, b: a + b, [gv[t, k, c].astype(F32) for k in range(4)])
        rate = jnp.exp(own[OWN_FADE : OWN_FADE + 1])
        head = [
            jnp.exp(-rate), jnp.exp(-2.0 * rate), jnp.exp(-4.0 * rate), jnp.exp(own[OWN_REWARD : OWN_REWARD + 1]),
            rate * jnp.exp(-rate),
        ]
        for n, row in enumerate(head):
            rows_out[n : n + 1, lanes(t)] = row
        rows_out[8:16, lanes(t)] = jnp.exp(-(ramp + 1.0) * rate)
        rows_out[16:24, lanes(t)] = jnp.exp(-(8.0 - ramp) * rate)

    def row(n):
        return vec_out[n : n + 1, :]

    norm_and_mix(
        length, width, lambda at: x[at, :].astype(F32), row(GAIN1), row(BIAS1), keep_out,
        [row(MK1), row(MV1), row(MR1)], [ins.at[n] for n in range(3)],
    )
    put(ins, ins_out)
    kvr_copies = []
    for n in range(3):
        turn(n + 2)
        weight = staged(n)

        def project(at):
            kvr[n, at, :] = dot(ins[n, at, :], matrix(weight), NN)

        over_rows(length, 256, project)
        kvr_copies.append(put(kvr.at[n], kvr_out.at[n]))
    wkv_forward(kvr.at[0], kvr.at[1], kvr.at[2], keep_out, rows_out, mixed, sn, sd)
    put(mixed, mixed_out)
    put(sn, sn_out)
    put(sd, sd_out)
    turn(5)
    weight = staged(EMIT)
    quarters = length // 4
    sums = []
    for n in range(4):
        at = pl.ds(n * quarters, quarters)
        for h in range(2):
            sum_own[at, h * half : (h + 1) * half] = dot(mixed[at, :], emit_half(weight, h), NN).astype(BF16)
        sums.append(remote(sum_own.at[at], sum_other.at[at], sum_send.at[n], sum_recv.at[n], partner))
        sums[-1].start()
    turn(6)
    for copy in sums:
        copy.wait()

    def add_up(at):
        total = x[at, :].astype(F32) + (sum_own[at, :].astype(F32) + sum_other[at, :].astype(F32))
        resid[0, at, :] = total[:, :half]
        resid[1, at, :] = total[:, half:]
        return total

    norm_and_mix(
        length, width, add_up, row(GAIN2), row(BIAS2), keep_out, [row(MK2), row(MR2)], [ins2.at[n] for n in range(2)]
    )
    put(resid, resid_out)
    put(ins2, ins2_out)
    for copy in kvr_copies:
        copy.wait()
    weight = staged(GATE2)

    def gate(at):
        kvr[2, at, :] = jax.nn.sigmoid(dot(ins2[1, at, :], matrix(weight), NN))

    over_rows(length, 256, gate)
    pre_copies = []
    for j in range(4):
        turn(FFN + 2 * j + 2)
        weight = staged(FFN + 2 * j)
        if j >= 2:
            pre_copies[j - 2].wait()

        def expand(at):
            positive = jnp.maximum(dot(ins2[0, at, :], matrix(weight), NN), 0.0)
            pre[j % 2, at, :] = positive.astype(BF16)
            act[j, at, :] = (positive * positive).astype(BF16)

        over_rows(length, 256, expand)
        pre_copies.append(put(pre.at[j % 2], pre_out.at[j]))
        put(act.at[j], act_out.at[j])
        turn(FFN + 2 * j + 3)
        weight = staged(FFN + 2 * j + 1)

        def contract(at):
            for h in range(2):
                part = dot(act[j, at, :], weight[2 * h : 2 * h + 2].reshape(half, -1), NT)
                kvr[h, at, :] = part if j == 0 else kvr[h, at, :] + part

        over_rows(length, 256, contract)

    vals = []
    for n in range(4):
        at = pl.ds(n * quarters, quarters)
        v_send[at, :] = kvr[1 - c, at, :].astype(BF16)
        vals.append(remote(v_send.at[at], v_other.at[at], val_send.at[n], val_recv.at[n], partner))
        vals[-1].start()
    columns = strip(c, half)
    backs = []
    for n in range(4):
        vals[n].wait()

        def finish(i, carry):
            at = strip(n * (quarters // 16) + i, 16)
            value = kvr[c, at, :] + v_other[at, :].astype(F32)
            s = kvr[2, at, :]
            low_half[at, :] = (resid[c, at, :] + s * value).astype(BF16)
            upstream = up[at, columns].astype(F32)
            gval[c, at, :] = (upstream * s).astype(BF16)
            grec[at, :] = (upstream * value * s * (1.0 - s)).astype(BF16)
            return carry

        lax.fori_loop(0, quarters // 16, finish, 0)
        at = pl.ds(n * quarters, quarters)
        backs.append(remote(gval.at[c, at], gval.at[c, at], val_send.at[4 + n], val_recv.at[4 + n], partner))
        backs[-1].start()
    give = remote(low_half.at[strip(1 - c, span)], out.at[:, columns], val_send.at[8], val_recv.at[8], partner)
    give.start()
    put(low_half.at[rows_mine], out.at[:, columns])
    put(grec, gr_out)
    for copy in backs:
        copy.wait()
    put(gval, gv_out)
    give.wait()

    def close(p, carry):
        weights.finish(p)
        return carry

    lax.fori_loop(0, PIECES, close, 0)
    vectors.finish(0)
    waited = kvr_copies + pre_copies[:2]
    for copy in outs:
        if not any(copy is other for other in waited):
            copy.wait()


def forward_call(own4, other4, rest, vec, x_own, up_own, keep_own):
    span, width = x_own.shape
    length, half = 2 * span, width // 2
    block = rest.shape[1:]
    any_, vmem = pl.BlockSpec(memory_space=pl.ANY), pl.BlockSpec(memory_space=pltpu.VMEM)
    full, col = (length, width), (length, half)

    def shape(dims, kind):
        return jax.ShapeDtypeStruct(dims, kind)

    outs = (
        (shape((PIECES, 4, 4) + block, BF16), any_),
        (shape((span, width), BF16), any_),
        (shape(full, BF16), any_),
        (shape(full, BF16), any_),
        (shape((3,) + full, BF16), any_),
        (shape((3,) + col, F32), any_),
        (shape(col, F32), any_),
        (shape(col, F32), any_),
        (shape(col, BF16), any_),
        (shape((2,) + col, F32), any_),
        (shape((2,) + full, BF16), any_),
        (shape((4,) + col, BF16), any_),
        (shape((4,) + col, BF16), any_),
        (shape((2,) + col, BF16), any_),
        (shape(col, BF16), any_),
        (shape((16, width), F32), vmem),
        (shape((24, half), F32), vmem),
        (shape((length, 128), F32), vmem),
    )
    dma = pltpu.SemaphoreType.DMA
    return pl.pallas_call(
        forward_kernel,
        out_shape=tuple(o[0] for o in outs),
        in_specs=[any_] * 7,
        out_specs=tuple(o[1] for o in outs),
        scratch_shapes=[
            pltpu.VMEM((4, 4, 2) + vec.shape, BF16),
            pltpu.VMEM((3, 4, 4) + block, BF16),
            pltpu.VMEM(full, BF16),
            pltpu.VMEM(full, BF16),
            pltpu.VMEM((3,) + full, BF16),
            pltpu.VMEM((3,) + col, F32),
            pltpu.VMEM(col, F32),
            pltpu.VMEM(col, F32),
            pltpu.VMEM(col, BF16),
            pltpu.VMEM(full, BF16),
            pltpu.VMEM(full, BF16),
            pltpu.VMEM((2,) + col, F32),
            pltpu.VMEM((2,) + full, BF16),
            pltpu.VMEM((2,) + col, BF16),
            pltpu.VMEM((4,) + col, BF16),
            pltpu.VMEM(col, BF16),
            pltpu.VMEM(col, BF16),
            pltpu.VMEM((2,) + col, BF16),
            pltpu.VMEM(col, BF16),
            pltpu.VMEM(col, BF16),
            dma((8,)), dma((6,)), dma((6,)),
            dma((PIECES, 7)), dma((PIECES, 7)), dma((1, 7)), dma((1, 7)),
            dma((PIECES,)), dma((24,)), dma((4,)), dma((4,)), dma((9,)), dma((9,)),
        ],
        compiler_params=pltpu.CompilerParams(
            collective_id=0, has_side_effects=True, vmem_limit_bytes=60 * MIB
        ),
        name="forward",
    )(own4, other4, rest, vec, x_own, up_own, keep_own)


R_VALUE, R_KEY, R_GATE2, R_EMIT, R_TIME = 0, 4, 8, 9, 10
WEIGHT_ORDER = [FFN + 1, FFN, FFN + 3, FFN + 2, FFN + 5, FFN + 4, FFN + 7, FFN + 6, GATE2, EMIT, KEY, VALUE, GATE]
S_GAIN1, S_BIAS1, S_GAIN2, S_BIAS2, S_DECAY, S_BONUS, S_MK1, S_MV1, S_MR1, S_MK2, S_MR2 = range(11)
SLOTS = 12


def whole(ref, at):
    return jnp.concatenate([ref[0, at, :], ref[1, at, :]], axis=1)


def halves(ref, at, value):
    half = value.shape[1] // 2
    ref[0, at, :] = value[:, :half].astype(ref.dtype)
    ref[1, at, :] = value[:, half:].astype(ref.dtype)


def fold(value):
    return value[:8] + value[8:16]


def back_through_norm(g, unit, inverse, gain):
    q = g * gain
    return inverse * (
        q - jnp.mean(q, axis=-1, keepdims=True) - unit * jnp.mean(q * unit, axis=-1, keepdims=True)
    )


def lifted(now, following, last):
    return jnp.where(last, following[0:1], pltpu.roll(now, now.shape[0] - 1, 0))


def backward_kernel(
    plan,
    g, x_in, up_in, ins_in, kvr_in, sn_in, sd_in, mixed_in, resid_in, ins2_in, pre_in, act_in, gv_in, gr_in,
    vec, rows, keep,
    out, recv4, vout, gtok,
    part, ring1, ring2, line, vbuf, b, w, f, resid, sum_other, n1_other, acc,
    load_sem, w_sem, sends, recvs, vsends, vrecvs, ex_send, ex_recv, sum_send, sum_recv,
):
    z, yx, c = place()
    nx, ny, nd, zs = neighbours(z, yx)
    length, half = b.shape[1:]
    width = 2 * half
    span = length // 2
    quarter = length // 4
    partner = (z * 4 + yx, 1 - c)
    loads = {}

    def load(name, src, dst):
        copy = pltpu.make_async_copy(src, dst, load_sem.at[len(loads)])
        copy.start()
        loads[name] = copy

    def loaded(*names):
        for name in names:
            loads[name].wait()

    def pair(n):
        return b.at[n : n + 2]

    def load_pair(name, src, n):
        for h in range(2):
            load((name, h), src.at[:, h * half : (h + 1) * half], b.at[n + h])

    def loaded_pair(name):
        loaded((name, 0), (name, 1))

    def weight_copy(n):
        return pltpu.make_async_copy(g.at[WEIGHT_ORDER[n]], w.at[n % 3], w_sem.at[n])

    def weight(n):
        weight_copy(n).wait()
        return w.at[n % 3]

    GVAL, ACT, PRE, IN_K2, IN_R2, GREC, GPRE = 0, 2, 4, 6, 8, 10, 11
    load("gv0", gv_in.at[0], b.at[GVAL])
    load("gv1", gv_in.at[1], b.at[GVAL + 1])
    for j in range(2):
        load(("act", j), act_in.at[j], b.at[ACT + j])
    load_pair("in_k2", ins2_in.at[0], IN_K2)
    for j in range(2):
        load(("pre", j), pre_in.at[j], b.at[PRE + j])
    for n in range(3):
        weight_copy(n).start()
    load_pair("in_r2", ins2_in.at[1], IN_R2)
    load("gr", gr_in, b.at[GREC])
    load("resid", resid_in, resid)
    enter(z, yx, c)

    sums = Reduce(part, ring1, ring2, line, out, sends, recvs)
    stages = (None, sums.stage1, sums.stage2, sums.stage3, sums.stage4)
    calls = iter(plan)

    def pump():
        for stage, p in next(calls):
            stages[stage](p)

    def gradient(p, lhs, rhs):
        for a in range(4):
            block = lhs[a // 2, :, (a % 2) * (half // 2) : (a % 2 + 1) * (half // 2)]
            part[p % PARTS, a] = dot(block, rhs[...], TN).astype(BF16).reshape(part.shape[2:])

    def thirds(ref, h):
        return ref[2 * h : 2 * h + 2].reshape(half, half)

    loaded("gv0", "gv1")
    for j in range(4):
        loaded(("act", j))
        gradient(R_VALUE + j, pair(GVAL), b.at[ACT + j % 2])
        if j < 2:
            load(("act", j + 2), act_in.at[j + 2], b.at[ACT + j])
        pump()
    loaded_pair("in_k2")
    for j in range(4):
        loaded(("pre", j))
        value_w = weight(2 * j)

        def through(at):
            g_hidden = sum(dot(b[GVAL + h, at, :], thirds(value_w, h), NN) for h in range(2))
            b[GPRE, at, :] = (2.0 * b[PRE + j % 2, at, :].astype(F32) * g_hidden).astype(BF16)

        over_rows(length, 256, through)
        if j < 2:
            load(("pre", j + 2), pre_in.at[j + 2], b.at[PRE + j])
        weight_copy(2 * j + 3).start()
        gradient(R_KEY + j, pair(IN_K2), b.at[GPRE])
        pump()
        key_w = weight(2 * j + 1)

        def collect(at):
            for h in range(2):
                piece = dot(b[GPRE, at, :], thirds(key_w, h), NT)
                f[h, at, :] = piece if j == 0 else f[h, at, :] + piece

        over_rows(length, 256, collect)
        weight_copy(2 * j + 4).start()
    loaded_pair("in_r2")
    loaded("gr")
    gradient(R_GATE2, pair(IN_R2), b.at[GREC])
    pump()
    gate_w = weight(8)

    def gate_back(at):
        for h in range(2):
            f[2 + h, at, :] = dot(b[GREC, at, :], thirds(gate_w, h), NT)

    over_rows(length, 256, gate_back)
    weight_copy(11).start()
    loaded("resid")

    SUM_OWN, UP, BRANCH, MIXED, G3, X, IN_K, IN_V, IN_R, SEND = 0, 2, 4, 6, 7, 4, 10, 0, 2, 6
    load_pair("up", up_in, UP)
    load("mixed", mixed_in, b.at[MIXED])
    acc[...] = jnp.zeros_like(acc)
    last = lax.broadcasted_iota(jnp.int32, (16, width), 0) == 15

    def row(n):
        return vec[n : n + 1, :]

    def kept(at, n):
        return wide(keep[at, :], width) if n is None else wide(keep[n, :], width)

    gain2, bias2, mk2, mr2 = (GAIN2, BIAS2, MK2, MR2)
    sum_copies = []
    for q in range(4):

        def tile(i, carry):
            base = q * quarter + i * 16
            at = pl.ds(pl.multiple_of(base, 16), 16)
            after = pl.ds(pl.multiple_of(jnp.minimum(base + 16, length - 8), 8), 8)
            inside = jnp.where(base + 16 < length, 1.0, 0.0)
            keep_at, keep_after = wide(keep[at, :], width), wide(keep[after, :], width) * inside
            unit, _ = norm(whole(resid, at))
            normed = unit * row(gain2) + row(bias2)
            total = jnp.zeros_like(unit)
            for n, share in enumerate((mk2, mr2)):
                back = whole(f.at[2 * n : 2 * n + 2], at)
                ahead = lifted(back * keep_at, whole(f.at[2 * n : 2 * n + 2], after) * keep_after, last)
                total = total + ahead + (back - ahead) * row(share)
                acc[S_MK2 + n] = acc[S_MK2 + n] + fold(normed * (back - ahead))
            acc[S_GAIN2] = acc[S_GAIN2] + fold(total * unit)
            acc[S_BIAS2] = acc[S_BIAS2] + fold(total)
            halves(b.at[SUM_OWN : SUM_OWN + 2], at, total)
            return carry

        lax.fori_loop(0, quarter // 16, tile, 0)
        at = pl.ds(q * quarter, quarter)
        sum_copies.append(
            remote(b.at[SUM_OWN : SUM_OWN + 2, at], sum_other.at[:, at], sum_send.at[q], sum_recv.at[q], partner)
        )
        sum_copies[-1].start()
        pump()
    for n in range(3):
        load(("kvr", n), kvr_in.at[n], f.at[n])
    load("sn", sn_in, f.at[3])
    load("sd", sd_in, f.at[4])
    load_pair("in_k", ins_in.at[0], IN_K)

    loaded_pair("up")
    for q in range(4):
        sum_copies[q].wait_recv()

        def tile(i, carry):
            at = pl.ds(pl.multiple_of(q * quarter + i * 16, 16), 16)
            unit, inverse = norm(whole(resid, at))
            total = whole(b.at[SUM_OWN : SUM_OWN + 2], at).astype(F32) + whole(sum_other, at).astype(F32)
            back = whole(pair(UP), at).astype(F32) + back_through_norm(total, unit, inverse, row(gain2))
            halves(pair(BRANCH), at, back)

            @pl.when(c == q // 2)
            def _():
                gtok[pl.ds(pl.multiple_of((q % 2) * quarter + i * 16, 16), 16), :] = back

            return carry

        lax.fori_loop(0, quarter // 16, tile, 0)
        pump()
    for copy in sum_copies:
        copy.wait_send()
    load_pair("in_v", ins_in.at[1], IN_V)
    load_pair("in_r", ins_in.at[2], IN_R)

    loaded("mixed")
    for h in range(2):
        for a in range(2):
            block = dot(b[MIXED, :, a * (half // 2) : (a + 1) * (half // 2)], b[BRANCH + h], TN).astype(BF16)
            rows_h = part.shape[3] // 2
            part[R_EMIT, 2 * a : 2 * a + 2, :, h * rows_h : (h + 1) * rows_h, :] = block.reshape(2, 4, rows_h, half)
    pump()
    emit_w = weight(9)

    def emit_back(at):
        resid[0, at, :] = sum(dot(b[BRANCH + h, at, :], emit_half(emit_w, h), NT) for h in range(2))

    over_rows(length, 256, emit_back)
    weight_copy(12).start()
    load_pair("x", x_in, X)

    loaded(("kvr", 0), ("kvr", 1), ("kvr", 2), "sn", "sd")
    carry = None
    for q in range(4):
        carry = wkv_backward(
            resid.at[0], f.at[0], f.at[1], f.at[2], f.at[3], f.at[4], keep, rows, b.at[G3], b.at[G3 + 1], b.at[G3 + 2],
            q * (length // 64), (q + 1) * (length // 64), carry,
        )
        pump()
    vout[...] = jnp.zeros_like(vout)
    columns = strip(c, half)
    wkv_sums(carry, rows, acc.at[S_DECAY, :, 0:half], acc.at[S_BONUS, :, 0:half])
    vout[S_DECAY : S_DECAY + 1, columns] = acc[S_DECAY, 0:1, 0:half]
    vout[S_BONUS : S_BONUS + 1, columns] = acc[S_BONUS, 0:1, 0:half]

    for n, (name, slot) in enumerate((("in_k", IN_K), ("in_v", IN_V), ("in_r", IN_R))):
        loaded_pair(name)
        sums.finish(R_TIME + n - PARTS)
        gradient(R_TIME + n, pair(slot), b.at[G3 + n])
        pump()
    loaded_pair("x")
    time_w = [weight(10 + n) for n in range(3)]
    for n in range(3):
        for h in range(2):
            f[n, pl.ds(h * span + quarter, 8), :] = jnp.zeros((8, half), F32)
    n1_copies = []
    for q in (3, 2, 1, 0):
        for n in range(3):
            for h in range(2):
                if q < 3:
                    f[n, pl.ds(h * span + quarter, 8), :] = f[n, pl.ds(h * span, 8), :]
                f[n, pl.ds(h * span, quarter), :] = dot(
                    b[G3 + n, pl.ds(q * quarter, quarter), :], thirds(time_w[n], h), NT
                )

        def tile(i, carry):
            base = q * quarter + i * 16
            at = pl.ds(pl.multiple_of(base, 16), 16)
            after = pl.ds(pl.multiple_of(jnp.minimum(base + 16, length - 8), 8), 8)
            keep_at, keep_after = wide(keep[at, :], width), wide(keep[after, :], width)

            def take(n, start, size):
                return jnp.concatenate(
                    [f[n, pl.ds(pl.multiple_of(h * span + start, 8), size), :] for h in range(2)], axis=1
                )

            unit, _ = norm(whole(pair(X), at).astype(F32))
            normed = unit * row(GAIN1) + row(BIAS1)
            total = jnp.zeros_like(unit)
            for n, share in enumerate((MK1, MV1, MR1)):
                back = take(n, i * 16, 16)
                ahead = lifted(back * keep_at, take(n, i * 16 + 16, 8) * keep_after, last)
                total = total + ahead + (back - ahead) * row(share)
                acc[S_MK1 + n] = acc[S_MK1 + n] + fold(normed * (back - ahead))
            acc[S_GAIN1] = acc[S_GAIN1] + fold(total * unit)
            acc[S_BIAS1] = acc[S_BIAS1] + fold(total)
            rows_q = [pl.ds(pl.multiple_of(h * span + (q % 2) * quarter + i * 16, 16), 16) for h in range(2)]

            @pl.when(c == q // 2)
            def _():
                for h in range(2):
                    f[3, rows_q[h], :] = total[:, h * half : (h + 1) * half]

            @pl.when(c != q // 2)
            def _():
                for h in range(2):
                    b[SEND, rows_q[h], :] = total[:, h * half : (h + 1) * half].astype(BF16)

            return carry

        lax.fori_loop(0, quarter // 16, tile, 0)
        pump()
    swap_n1 = remote(b.at[SEND], n1_other, sum_send.at[4], sum_recv.at[4], partner)
    swap_n1.start()

    for n in (S_GAIN1, S_BIAS1, S_GAIN2, S_BIAS2, S_MK1, S_MV1, S_MR1, S_MK2, S_MR2):
        vout[n : n + 1, :] = jnp.sum(acc[n], axis=0, keepdims=True)

    def vec_copy(k, target):
        return remote(vout, vbuf.at[k], vsends.at[k], vrecvs.at[k], target)

    vec_stages = [
        [vec_copy(0, partner)],
        [vec_copy(1, (z * 4 + nx, c))],
        [vec_copy(2, (z * 4 + ny, c))],
        [vec_copy(3 + k, (peer * 4 + yx, c)) for k, peer in enumerate(zs)],
    ]

    def vec_start(k):
        for copy in vec_stages[k]:
            copy.start()

    def vec_add(k):
        for copy in vec_stages[k]:
            copy.wait()
        for j in [k] if k < 3 else [3, 4, 5]:
            vout[...] = vout[...] + vbuf[j]

    vec_start(0)
    pump()
    swap_n1.wait()

    def tokens(i, carry):
        at = strip(i, 16)
        spans = [pl.ds(pl.multiple_of(h * span + i * 16, 16), 16) for h in range(2)]
        unit, inverse = norm(whole(pair(X), pl.ds(pl.multiple_of(c * span + i * 16, 16), 16)).astype(F32))
        total = jnp.concatenate([f[3, s, :] + n1_other[s, :].astype(F32) for s in spans], axis=1)
        gtok[at, :] = gtok[at, :] + back_through_norm(total, unit, inverse, row(GAIN1))
        return carry

    lax.fori_loop(0, span // 16, tokens, 0)
    vec_add(0)
    vec_start(1)
    pump()
    vec_add(1)
    vec_start(2)
    pump()
    vec_add(2)
    vec_start(3)
    pump()
    vec_add(3)
    for actions in calls:
        for stage, p in actions:
            stages[stage](p)
    rows4 = recv4.shape[1]
    others = strip(1 - c, rows4)
    swaps = [
        remote(out.at[R_TIME : R_TIME + 3, others], recv4.at[0:3], ex_send.at[0], ex_recv.at[0], partner),
        remote(out.at[R_GATE2, others], recv4.at[3], ex_send.at[1], ex_recv.at[1], partner),
    ]
    for copy in swaps:
        copy.start()
    for p in range(PIECES - PARTS, PIECES):
        sums.finish(p)
    for copy in swaps:
        copy.wait()


def make_plan():
    plan = [
        [(1, 0)], [(1, 1)], [(1, 2)], [(1, 3), (2, 0)],
        [(1, 4)], [(1, 5), (2, 1)], [(1, 6)], [(1, 7), (2, 2)],
        [(1, 8)],
        [(2, 3)], [(3, 0)], [(2, 4)], [(3, 1)],
        [(2, 5)], [(3, 2)], [(4, 0)], [(2, 6), (3, 3)],
        [(1, 9), (4, 1)],
        [(2, 7), (3, 4)], [(4, 2)], [(2, 8), (3, 5)], [(4, 3)],
        [(1, 10), (2, 9), (4, 4)], [(1, 11), (3, 6)], [(1, 12), (3, 7)],
        [(2, 10)], [(3, 8)], [(2, 11)], [(3, 9), (4, 5)],
        [(2, 12), (4, 6)], [(3, 10)], [(3, 11)], [(3, 12)],
        [(4, p) for p in range(7, 13)],
    ]
    return plan


def backward_call(g, x, up, ins, kvr, sn, sd, mixed, resid, ins2, pre, act, g_value, g_recept, vec, rows, keep):
    block = g.shape[3:]
    length, half = sn.shape
    any_, vmem = pl.BlockSpec(memory_space=pl.ANY), pl.BlockSpec(memory_space=pltpu.VMEM)
    dma = pltpu.SemaphoreType.DMA

    def shape(*dims):
        return jax.ShapeDtypeStruct(dims, F32)

    return pl.pallas_call(
        functools.partial(backward_kernel, make_plan()),
        out_shape=(
            shape(PIECES, *block), shape(4, block[0] // 2, block[1]), shape(16, 2 * half), shape(length // 2, 2 * half),
        ),
        in_specs=[any_] * 14 + [vmem] * 3,
        out_specs=(vmem,) * 4,
        scratch_shapes=[
            pltpu.VMEM((PARTS, 4, 4) + block, BF16),
            pltpu.VMEM((PIECES, 2, 2) + block, BF16),
            pltpu.VMEM((PIECES, 2, 4) + block, BF16),
            pltpu.VMEM((PIECES, 3) + block, BF16),
            pltpu.VMEM((6, 16, 2 * half), F32),
            pltpu.VMEM((SLOTS, length, half), BF16),
            pltpu.VMEM((3, 4, 4) + block, BF16),
            pltpu.VMEM((5, length, half), F32),
            pltpu.VMEM((2, length, half), F32),
            pltpu.VMEM((2, length, half), BF16),
            pltpu.VMEM((length, half), BF16),
            pltpu.VMEM((11, 8, 2 * half), F32),
            dma((40,)), dma((PIECES,)), dma((PIECES, 7)), dma((PIECES, 7)), dma((6,)), dma((6,)), dma((2,)), dma((2,)),
            dma((5,)), dma((5,)),
        ],
        compiler_params=pltpu.CompilerParams(collective_id=1, has_side_effects=True, vmem_limit_bytes=63 * MIB),
        name="backward",
    )(g, x, up, ins, kvr, sn, sd, mixed, resid, ins2, pre, act, g_value, g_recept, vec, rows, keep)


def shifted(value, axis, steps):
    count = lax.axis_size(axis)
    first, last = (max(0, -steps), min(count, count - steps))
    return lax.ppermute(value, axis, [(source, source + steps) for source in range(first, last)])


def carried_in(array, axis, join, neutral):
    place = lax.axis_index(axis)
    gathered = jax.tree.map(
        lambda a, kind: lax.all_gather(a.astype(kind), axis),
        array,
        (jnp.bfloat16, jnp.bfloat16, jnp.bfloat16),
    )
    state = jax.tree.map(lambda a, e: jnp.zeros_like(a) + jnp.asarray(e, a.dtype), array, neutral)

    def one(turn, state):
        return join(
            state,
            jax.tree.map(
                lambda a, own: lax.dynamic_index_in_dim(a, turn, 0, False).astype(own.dtype),
                gathered,
                array,
            ),
        )

    return lax.fori_loop(0, place, one, state)


def entering(array, axis, combine, identity):
    count, place = (lax.axis_size(axis), lax.axis_index(axis))
    everything = jax.tree.map(
        lambda part, kind: lax.all_gather(part.astype(kind), axis),
        array,
        jax.tree.map(lambda a: jnp.bfloat16 if a.dtype == jnp.float32 else a.dtype, array),
    )
    start = jax.tree.map(
        lambda part, zero: jnp.broadcast_to(jnp.asarray(zero, part.dtype), part.shape),
        array,
        identity,
    )

    def turn(k, before):
        at = count - 1 - k
        reached = at > place
        new = combine(
            before, jax.tree.map(lambda part, own: part[at].astype(own.dtype), everything, array)
        )
        return jax.tree.map(lambda a, b: jnp.where(reached, a, b), new, before)

    return lax.fori_loop(0, count, turn, start)


def wide_layer_norm(values, scale_vec, shift_vec):
    center = values - jnp.mean(values, axis=-1, keepdims=True)
    inverse = lax.rsqrt(jnp.mean(center * center, axis=-1, keepdims=True) + 1e-05)
    normed = center * inverse
    return (normed * scale_vec + shift_vec, normed, inverse)


def wide_norm_back(upstream, normed, inverse, scale_vec):
    scaled = upstream * scale_vec
    inner = (
        scaled
        - jnp.mean(scaled, axis=-1, keepdims=True)
        - normed * jnp.mean(scaled * normed, axis=-1, keepdims=True)
    )
    return (
        inverse * inner,
        jnp.sum(upstream * normed, axis=(0, 1)),
        jnp.sum(upstream, axis=(0, 1)),
    )


def shift_prev(values, persist_indicator):
    arrived = shifted(values[:, -1:, :], "tensor", 1)
    return jnp.concatenate([arrived, values[:, :-1]], axis=1) * persist_indicator[:, :, None]


def shift_back(upstream, persist_indicator):
    masked = upstream * persist_indicator[:, :, None]
    arrived = shifted(masked[:, :1, :], "tensor", -1)
    return jnp.concatenate([masked[:, 1:], arrived], axis=1)


def project(values, matrix):
    return jnp.einsum("rtd,de->rte", values, matrix, preferred_element_type=jnp.float32)


def project_back(upstream, matrix):
    return jnp.einsum("rte,de->rtd", upstream, matrix, preferred_element_type=jnp.float32)


def outer_sum(values, upstream):
    return jnp.einsum("rtd,rte->de", values, upstream, preferred_element_type=jnp.float32)


def mix_back(upstreams, shares, differ, persist_indicator):
    toward = jnp.zeros_like(differ)
    behind = jnp.zeros_like(differ)
    share_grads = []
    for upstream, share in zip(upstreams, shares):
        toward = toward + upstream * share
        behind = behind + upstream * (1.0 - share)
        share_grads.append(jnp.sum(upstream * differ, axis=(0, 1)))
    return (toward + shift_back(behind, persist_indicator), share_grads)


def chain_combine(earlier, later):
    return (
        earlier[0] * later[0],
        later[0] * earlier[1] + later[1],
        later[0] * earlier[2] + later[2],
    )


def scan_fragments(
    lookup_wide, payload_wide, fading_power, reward_coords, text_boundary_indicators
):
    decay_rate = jnp.exp(fading_power)
    row_count, span_len, width_len = lookup_wide.shape
    block_len = min(32, span_len)
    block_count = span_len // block_len
    places = jnp.arange(block_len, dtype=jnp.float32)
    rising = jnp.exp(places[:, None] * decay_rate)
    falling = jnp.exp(-(places[:, None] - 1.0) * decay_rate)
    trailing = jnp.exp(-(block_len - 1.0 - places)[:, None] * decay_rate)
    leading = jnp.exp(-places[:, None] * decay_rate)
    settle = jnp.exp(-block_len * decay_rate)
    before = places[:, None] > places[None, :]

    def split_blocks(values):
        return jnp.swapaxes(
            values.reshape((row_count, block_count, block_len) + values.shape[2:]), 0, 1
        )

    def advance(state_pair, scanned):
        accrued_dividend_sum, accrued_divisor_sum = state_pair
        lookup_narrow, payload_narrow, reset_b = scanned
        tree_levels = jnp.cumsum(reset_b, axis=1)
        linked = ((tree_levels[:, :, None] == tree_levels[:, None, :]) & before).astype(jnp.float32)
        key_term = jnp.exp(lookup_narrow)
        keyed_value = key_term * payload_narrow
        inside_numerator = falling * jnp.einsum(
            "rti,rid->rtd", linked, rising * keyed_value, precision=lax.Precision.HIGHEST
        )
        interior_divisor_sum = falling * jnp.einsum(
            "rti,rid->rtd", linked, rising * key_term, precision=lax.Precision.HIGHEST
        )
        leftover_multiplier = (tree_levels == 0).astype(jnp.float32)[:, :, None] * leading
        reward_multiplier = jnp.exp(reward_coords + lookup_narrow)
        above_total = (
            inside_numerator
            + reward_multiplier * payload_narrow
            + leftover_multiplier * accrued_dividend_sum[:, None, :]
        )
        below_total = (
            interior_divisor_sum
            + reward_multiplier
            + leftover_multiplier * accrued_divisor_sum[:, None, :]
        )
        ending = (tree_levels == tree_levels[:, -1:]).astype(jnp.float32)[:, :, None] * trailing
        intact = (tree_levels[:, -1] == 0).astype(jnp.float32)[:, None] * settle
        new_num = intact * accrued_dividend_sum + jnp.sum(ending * keyed_value, axis=1)
        new_den = intact * accrued_divisor_sum + jnp.sum(ending * key_term, axis=1)
        return ((new_num, new_den), (above_total, below_total))

    initial = jnp.zeros((row_count, width_len), jnp.float32)
    (total_num, total_den), (uppers, lowers) = lax.scan(
        advance,
        (initial, initial),
        (
            split_blocks(lookup_wide),
            split_blocks(payload_wide),
            split_blocks(text_boundary_indicators),
        ),
    )

    def join_blocks(values):
        return jnp.swapaxes(values, 0, 1).reshape(row_count, span_len, width_len)

    tree_levels = jnp.cumsum(text_boundary_indicators, axis=1)
    reaching = (tree_levels == 0).astype(jnp.float32)[:, :, None] * jnp.exp(
        -jnp.arange(span_len, dtype=jnp.float32)[:, None] * decay_rate
    )
    passing = (tree_levels[:, -1] == 0).astype(jnp.float32)[:, None] * jnp.exp(
        -span_len * decay_rate
    )
    return (join_blocks(uppers), join_blocks(lowers), reaching, total_num, total_den, passing)


def recurrence_finish(pieces_list, incoming_num, incoming_den):
    above_total = pieces_list[0] + pieces_list[2] * incoming_num[:, None, :]
    below_total = pieces_list[1] + pieces_list[2] * incoming_den[:, None, :]
    return (above_total / below_total, below_total)


def ffn_apply(inputs, key_weight, value_weight):
    hidden_pre = project(inputs, key_weight)
    hidden = jnp.square(jax.nn.relu(hidden_pre)).astype(jnp.bfloat16)
    return (hidden_pre, hidden, project(hidden, value_weight))


def ffn_grads(inputs, hidden_pre, hidden, upstream, key_weight, value_weight):
    g_hidden = jnp.einsum("rtd,fd->rtf", upstream, value_weight, preferred_element_type=jnp.float32)
    grad_value = jnp.einsum("rtf,rtd->fd", hidden, upstream, preferred_element_type=jnp.float32)
    g_pre = (2.0 * jax.nn.relu(hidden_pre) * g_hidden).astype(jnp.bfloat16)
    grad_key = jnp.einsum("rtd,rtf->df", inputs, g_pre, preferred_element_type=jnp.float32)
    g_inputs = jnp.einsum("rtf,df->rtd", g_pre, key_weight, preferred_element_type=jnp.float32)
    return (g_inputs, grad_key, grad_value)


def wide_shards(
    incoming_embeddings,
    text_boundary_indicators,
    upstream_sensitivity,
    primary_standardize_scaling,
    primary_standardize_offset,
    secondary_standardize_scaling,
    secondary_standardize_offset,
    feature_fading_logarithms,
    present_symbol_reward,
    timemix_lookup_blend,
    timemix_payload_blend,
    timemix_gate_blend,
    timemix_lookup_proj,
    timemix_payload_proj,
    timemix_gate_proj,
    timemix_emit_proj,
    feedmix_lookup_blend,
    feedmix_gate_blend,
    feedmix_gate_proj,
    feedmix_lookup_proj,
    feedmix_payload_proj,
):
    gathered_portions = (
        lax.all_gather(primary_standardize_scaling, ("dp", "tensor"), axis=0, tiled=True),
        lax.all_gather(primary_standardize_offset, ("dp", "tensor"), axis=0, tiled=True),
        lax.all_gather(secondary_standardize_scaling, ("dp", "tensor"), axis=0, tiled=True),
        lax.all_gather(secondary_standardize_offset, ("dp", "tensor"), axis=0, tiled=True),
        lax.all_gather(feature_fading_logarithms, ("dp", "tensor"), axis=0, tiled=True),
        lax.all_gather(present_symbol_reward, ("dp", "tensor"), axis=0, tiled=True),
        lax.all_gather(timemix_lookup_blend, ("dp", "tensor"), axis=0, tiled=True),
        lax.all_gather(timemix_payload_blend, ("dp", "tensor"), axis=0, tiled=True),
        lax.all_gather(timemix_gate_blend, ("dp", "tensor"), axis=0, tiled=True),
        lax.all_gather(timemix_lookup_proj, ("dp", "tensor"), axis=0, tiled=True),
        lax.all_gather(timemix_payload_proj, ("dp", "tensor"), axis=0, tiled=True),
        lax.all_gather(timemix_gate_proj, ("dp", "tensor"), axis=0, tiled=True),
        lax.all_gather(timemix_emit_proj, ("dp", "tensor"), axis=0, tiled=True),
        lax.all_gather(feedmix_lookup_blend, ("dp", "tensor"), axis=0, tiled=True),
        lax.all_gather(feedmix_gate_blend, ("dp", "tensor"), axis=0, tiled=True),
        lax.all_gather(feedmix_gate_proj, ("dp", "tensor"), axis=0, tiled=True),
    )
    initial_scaling_coords = gathered_portions[0].astype(jnp.float32)
    initial_offset_coords = gathered_portions[1].astype(jnp.float32)
    later_scaling_coords = gathered_portions[2].astype(jnp.float32)
    later_offset_coords = gathered_portions[3].astype(jnp.float32)
    fading_power = gathered_portions[4].astype(jnp.float32)
    reward_coords = gathered_portions[5].astype(jnp.float32)
    share_k1 = gathered_portions[6].astype(jnp.float32)
    share_v1 = gathered_portions[7].astype(jnp.float32)
    share_r1 = gathered_portions[8].astype(jnp.float32)
    lookup_coefficients_initial = gathered_portions[9]
    payload_coefficients_initial = gathered_portions[10]
    gate_coefficients_initial = gathered_portions[11]
    emit_coefficients_initial = gathered_portions[12]
    share_k2 = gathered_portions[13].astype(jnp.float32)
    share_r2 = gathered_portions[14].astype(jnp.float32)
    gate_coefficients_later = gathered_portions[15]
    lookup_coefficients_later, payload_coefficients_later = (
        lax.all_gather(feedmix_lookup_proj, "dp", axis=0, tiled=True),
        lax.all_gather(feedmix_payload_proj, "dp", axis=1, tiled=True),
    )
    persist_indicator = (1 - text_boundary_indicators).astype(jnp.float32)
    inputs = incoming_embeddings.astype(jnp.float32)
    normed_one, unit_one, inverse_one = wide_layer_norm(
        inputs, initial_scaling_coords, initial_offset_coords
    )
    prev_one = shift_prev(normed_one, persist_indicator)
    differ_one = normed_one - prev_one
    in_key = (prev_one + differ_one * share_k1).astype(jnp.bfloat16)
    in_value = (prev_one + differ_one * share_v1).astype(jnp.bfloat16)
    in_recept = (prev_one + differ_one * share_r1).astype(jnp.bfloat16)
    initial_lookup_lines = project(in_key, lookup_coefficients_initial)
    initial_payload_lines = project(in_value, payload_coefficients_initial)
    recept_one = project(in_recept, gate_coefficients_initial)
    pieces_list = scan_fragments(
        initial_lookup_lines,
        initial_payload_lines,
        fading_power,
        reward_coords,
        text_boundary_indicators,
    )
    passing = pieces_list[5]
    identity = (jnp.ones_like(passing), jnp.zeros_like(passing), jnp.zeros_like(passing))
    unused_item, incoming_num, incoming_den = carried_in(
        (passing, pieces_list[3], pieces_list[4]), "tensor", chain_combine, identity
    )
    blended_mean_state, below_total = recurrence_finish(pieces_list, incoming_num, incoming_den)
    sig_one = jax.nn.sigmoid(recept_one)
    mixed_att = (sig_one * blended_mean_state).astype(jnp.bfloat16)
    resid_one = inputs + project(mixed_att, emit_coefficients_initial)
    normed_two, unit_two, inverse_two = wide_layer_norm(
        resid_one, later_scaling_coords, later_offset_coords
    )
    prev_two = shift_prev(normed_two, persist_indicator)
    differ_two = normed_two - prev_two
    in_key_two = (prev_two + differ_two * share_k2).astype(jnp.bfloat16)
    in_recept_two = (prev_two + differ_two * share_r2).astype(jnp.bfloat16)
    recept_two = project(in_recept_two, gate_coefficients_later)
    sig_two = jax.nn.sigmoid(recept_two)
    row_inputs = lax.all_gather(in_key_two, "tensor", axis=1, tiled=True)
    hidden_pre, hidden, partial_value = ffn_apply(
        row_inputs, lookup_coefficients_later, payload_coefficients_later
    )
    value_two = lax.psum_scatter(
        partial_value.astype(jnp.bfloat16), "tensor", scatter_dimension=1, tiled=True
    ).astype(jnp.float32)
    layer_out = (resid_one + sig_two * value_two).astype(jnp.bfloat16)
    upstream = upstream_sensitivity.astype(jnp.float32)
    g_value_two = (upstream * sig_two).astype(jnp.bfloat16)
    g_recept_two = (upstream * value_two * sig_two * (1.0 - sig_two)).astype(jnp.bfloat16)
    grad_recept_two = outer_sum(in_recept_two, g_recept_two)
    g_mix_r2 = project_back(g_recept_two, gate_coefficients_later)
    row_grads = lax.all_gather(g_value_two, "tensor", axis=1, tiled=True)
    partial_grad, grad_key_two, grad_value_two = ffn_grads(
        row_inputs,
        hidden_pre,
        hidden,
        row_grads,
        lookup_coefficients_later,
        payload_coefficients_later,
    )
    g_mix_k2 = lax.psum_scatter(
        partial_grad.astype(jnp.bfloat16), "tensor", scatter_dimension=1, tiled=True
    ).astype(jnp.float32)
    sum_key_two, sum_value_two = (
        lax.psum_scatter(
            grad_key_two.astype(jnp.bfloat16), "dp", scatter_dimension=0, tiled=True
        ).astype(jnp.float32),
        lax.psum_scatter(
            grad_value_two.astype(jnp.bfloat16), "dp", scatter_dimension=1, tiled=True
        ).astype(jnp.float32),
    )
    g_normed_two, shares_two = mix_back(
        (g_mix_k2, g_mix_r2), (share_k2, share_r2), differ_two, persist_indicator
    )
    g_resid_part, grad_gain_two, grad_bias_two = wide_norm_back(
        g_normed_two, unit_two, inverse_two, later_scaling_coords
    )
    g_resid = upstream + g_resid_part
    g_branch = g_resid.astype(jnp.bfloat16)
    grad_out_one = outer_sum(mixed_att, g_branch)
    g_mixed = project_back(g_branch, emit_coefficients_initial)
    g_weighted = g_mixed * sig_one
    g_recept_one = (g_mixed * blended_mean_state * sig_one * (1.0 - sig_one)).astype(jnp.bfloat16)
    reaching = pieces_list[2]
    g_in_num = jnp.sum(g_weighted * reaching / below_total, axis=1)
    g_in_den = -jnp.sum(g_weighted * reaching * blended_mean_state / below_total, axis=1)
    unused_item, back_num, back_den = entering(
        (passing, g_in_num, g_in_den), "tensor", chain_combine, identity
    )
    g_passing = back_num * incoming_num + back_den * incoming_den

    def device_fragment(lookup_wide, payload_wide, fading_coords, reward_power):
        shard_pieces = scan_fragments(
            lookup_wide, payload_wide, fading_coords, reward_power, text_boundary_indicators
        )
        local_out, unused_item = recurrence_finish(shard_pieces, incoming_num, incoming_den)
        return (local_out, shard_pieces[3], shard_pieces[4], shard_pieces[5])

    unused_item, reverse_pass_rule = jax.vjp(
        device_fragment, initial_lookup_lines, initial_payload_lines, fading_power, reward_coords
    )
    derivative_lookup_wide, derivative_payload_wide, fading_derivative, reward_derivative = (
        reverse_pass_rule((g_weighted, back_num, back_den, g_passing))
    )
    g_key_one = derivative_lookup_wide.astype(jnp.bfloat16)
    g_value_one = derivative_payload_wide.astype(jnp.bfloat16)
    grad_key_one = outer_sum(in_key, g_key_one)
    grad_value_one = outer_sum(in_value, g_value_one)
    grad_recept_one = outer_sum(in_recept, g_recept_one)
    g_mix_k1 = project_back(g_key_one, lookup_coefficients_initial)
    g_mix_v1 = project_back(g_value_one, payload_coefficients_initial)
    g_mix_r1 = project_back(g_recept_one, gate_coefficients_initial)
    g_normed_one, shares_one = mix_back(
        (g_mix_k1, g_mix_v1, g_mix_r1),
        (share_k1, share_v1, share_r1),
        differ_one,
        persist_indicator,
    )
    g_input_part, grad_gain_one, grad_bias_one = wide_norm_back(
        g_normed_one, unit_one, inverse_one, initial_scaling_coords
    )
    grad_tokens = g_resid + g_input_part
    summed = (
        lax.psum_scatter(grad_gain_one, ("dp", "tensor"), scatter_dimension=0, tiled=True),
        lax.psum_scatter(grad_bias_one, ("dp", "tensor"), scatter_dimension=0, tiled=True),
        lax.psum_scatter(grad_gain_two, ("dp", "tensor"), scatter_dimension=0, tiled=True),
        lax.psum_scatter(grad_bias_two, ("dp", "tensor"), scatter_dimension=0, tiled=True),
        lax.psum_scatter(fading_derivative, ("dp", "tensor"), scatter_dimension=0, tiled=True),
        lax.psum_scatter(reward_derivative, ("dp", "tensor"), scatter_dimension=0, tiled=True),
        lax.psum_scatter(shares_one[0], ("dp", "tensor"), scatter_dimension=0, tiled=True),
        lax.psum_scatter(shares_one[1], ("dp", "tensor"), scatter_dimension=0, tiled=True),
        lax.psum_scatter(shares_one[2], ("dp", "tensor"), scatter_dimension=0, tiled=True),
        lax.psum_scatter(grad_key_one, ("dp", "tensor"), scatter_dimension=0, tiled=True),
        lax.psum_scatter(grad_value_one, ("dp", "tensor"), scatter_dimension=0, tiled=True),
        lax.psum_scatter(grad_recept_one, ("dp", "tensor"), scatter_dimension=0, tiled=True),
        lax.psum_scatter(grad_out_one, ("dp", "tensor"), scatter_dimension=0, tiled=True),
        lax.psum_scatter(shares_two[0], ("dp", "tensor"), scatter_dimension=0, tiled=True),
        lax.psum_scatter(shares_two[1], ("dp", "tensor"), scatter_dimension=0, tiled=True),
        lax.psum_scatter(grad_recept_two, ("dp", "tensor"), scatter_dimension=0, tiled=True),
    )
    return (
        layer_out,
        grad_tokens,
        summed[0],
        summed[1],
        summed[2],
        summed[3],
        summed[4],
        summed[5],
        summed[6],
        summed[7],
        summed[8],
        summed[9],
        summed[10],
        summed[11],
        summed[12],
        summed[13],
        summed[14],
        summed[15],
        sum_key_two,
        sum_value_two,
    )


def split_columns(w, parts):
    rows, width = w.shape
    return w.reshape(rows, parts, 2, width // (2 * parts)).transpose(2, 0, 1, 3).reshape(2, rows, width // 2)


def join_columns(own, other, c, parts):
    rows, half = own.shape[-2:]
    a = jnp.where(c == 0, own, other).reshape(own.shape[:-1] + (parts, half // parts))
    b = jnp.where(c == 0, other, own).reshape(own.shape[:-1] + (parts, half // parts))
    return jnp.stack([a, b], axis=-2).reshape(own.shape[:-1] + (2 * half,))


def pack(tokens, starts, upstream, gain1, bias1, gain2, bias2, fading, reward, mk1, mv1, mr1, wk, wv, wr, wo, mk2, mr2, wg, fk, fv):
    i, c, count = lax.axis_index("dp"), lax.axis_index("tensor"), lax.axis_size("dp")
    own_rows, width = wk.shape
    half, hidden = width // 2, fk.shape[1]
    by_core = jnp.stack([split_columns(wk, count), split_columns(wv, count), split_columns(wr, count), split_columns(wg, 1)])
    own4 = lax.dynamic_index_in_dim(by_core, c, 1, False)
    other4 = lax.dynamic_index_in_dim(by_core, 1 - c, 1, False)
    emit = wo.reshape(own_rows, 2, half).transpose(1, 0, 2).reshape(1, 2 * own_rows, half)
    key4 = fk.reshape(2 * own_rows, 4, hidden // 4).transpose(1, 0, 2)
    value4 = fv.reshape(4, hidden // 4, 2 * own_rows).transpose(0, 2, 1)
    ffn = jnp.stack([key4, value4], axis=1).reshape(8, 2 * own_rows, hidden // 4)
    rest = jnp.concatenate([emit, ffn])
    slots = 128 // own_rows
    everywhere = jnp.stack([gain1, bias1, gain2, bias2, fading, reward, mk1, mv1, mr1, mk2, mr2])
    own = jnp.stack([fading, reward, jnp.zeros_like(fading), jnp.zeros_like(fading), jnp.zeros_like(fading)])
    lane = jnp.arange(128)[None, :] // own_rows
    vec = jnp.concatenate([
        jnp.where(lane == (2 * i + c) % slots, jnp.tile(everywhere, (1, slots)), 0),
        jnp.where(lane == i % slots, jnp.tile(own, (1, slots)), 0),
    ]).astype(BF16)
    keep = jnp.broadcast_to((1 - starts[0]).astype(F32)[:, None], (starts.shape[1], 128))
    return own4, other4, rest, vec, tokens[0], upstream[0], keep


def shards(*args):
    tokens = args[0]
    c = lax.axis_index("tensor")
    i = lax.axis_index("dp")
    count = lax.axis_size("dp")
    own_rows, width = args[12].shape
    hidden = args[19].shape[1]
    half = width // 2
    (
        g, layer_out, x, up, ins, kvr, sn, sd, mixed, resid, ins2, pre, act, g_value, g_recept2, vec, rows, keep,
    ) = forward_call(*pack(*args))

    total, recv4, vtotal, grad_tokens = backward_call(
        g, x, up, ins, kvr, sn, sd, mixed, resid, ins2, pre, act, g_value, g_recept2, vec, rows, keep
    )
    own_scan = lax.dynamic_slice_in_dim(vtotal, c * half + i * own_rows, own_rows, 1)
    vtotal = lax.dynamic_slice_in_dim(vtotal, (2 * i + c) * own_rows, own_rows, 1)
    own = lax.dynamic_slice_in_dim(total[R_GATE2:], c * own_rows, own_rows, 1)
    out_k, out_v, out_r = (join_columns(own[2 + n], recv4[n], c, count) for n in range(3))
    out_g = join_columns(own[0], recv4[3], c, 1)
    out_o = total[R_EMIT].reshape(2, own_rows, half).transpose(1, 0, 2).reshape(own_rows, width)
    out_fk = total[R_KEY : R_KEY + 4].transpose(1, 0, 2).reshape(2 * own_rows, hidden)
    out_fv = total[R_VALUE : R_VALUE + 4].transpose(0, 2, 1).reshape(hidden, 2 * own_rows)
    return (
        layer_out[None], grad_tokens[None], *(vtotal[n] for n in range(4)), own_scan[4], own_scan[5],
        *(vtotal[n] for n in range(6, 9)), out_k, out_v, out_r, out_o, vtotal[9], vtotal[10], out_g, out_fk, out_fv,
    )


def solution(mesh):
    row, vector, matrix_ = P("dp", "tensor", None), P(("dp", "tensor")), P(("dp", "tensor"), None)
    key, value = P("dp", "tensor"), P("tensor", "dp")
    in_specs = (row, P("dp", "tensor"), row) + (vector,) * 9 + (matrix_,) * 4 + (vector,) * 2 + (matrix_, key, value)
    out_specs = (row, row) + (vector,) * 9 + (matrix_,) * 4 + (vector,) * 2 + (matrix_, key, value)
    body = shards if (mesh.shape["dp"], mesh.shape["tensor"]) == (16, 2) else wide_shards
    return jax.shard_map(body, mesh=mesh, in_specs=in_specs, out_specs=out_specs, check_vma=False)
```

```python
import functools

import jax
import jax.numpy as jnp
from jax import lax
from jax.experimental import pallas as pl
from jax.experimental.pallas import tpu as pltpu
from jax.sharding import PartitionSpec as P

F32, BF16 = jnp.float32, jnp.bfloat16
MESH_ID = pl.DeviceIdType.MESH
MIB = 1 << 20
PARTS = 10
PIECES = 13


def place():
    i, c = lax.axis_index("dp"), lax.axis_index("tensor")
    return i // 4, i % 4, c


def neighbours(z, yx):
    x = yx + 1 - 2 * (yx % 2)
    y = (yx + 2) % 4
    d = (x + 2) % 4
    zs = (z + 1 - 2 * (z % 2), (z + 2) % 4, 3 - z)
    return x, y, d, zs


def enter(z, yx, c):
    x, y, d, zs = neighbours(z, yx)
    barrier = pltpu.get_barrier_semaphore()
    targets = [(z * 4 + yx, 1 - c), (z * 4 + x, c), (z * 4 + y, c)]
    targets += [(peer * 4 + yx, c) for peer in zs]
    for target in targets:
        pl.semaphore_signal(barrier, inc=1, device_id=target, device_id_type=MESH_ID)
    pl.semaphore_wait(barrier, len(targets))


def remote(src, dst, send, recv, target):
    return pltpu.make_async_remote_copy(
        src_ref=src, dst_ref=dst, send_sem=send, recv_sem=recv,
        device_id=target, device_id_type=MESH_ID,
    )


class Gather:
    def __init__(self, view, sends, recvs, first=0):
        self.view, self.sends, self.recvs, self.first = view, sends, recvs, first
        self.z, self.yx, self.c = place()
        self.x, self.y, self.d, self.zs = neighbours(self.z, self.yx)

    def to(self, z, yx):
        return (z * 4 + yx, self.c)

    def copy(self, p, k, ref, target):
        return remote(ref, ref, self.sends.at[p, k], self.recvs.at[p, k], target)

    def along(self, p):
        own = self.view(p).at[self.z, self.yx]
        return [self.copy(p, k, own, self.to(peer, self.yx)) for k, peer in enumerate(self.zs)]

    def plane(self, p):
        own = self.view(p).at[:, self.yx]
        return [self.copy(p, 3, own, self.to(self.z, self.x)), self.copy(p, 4, own, self.to(self.z, self.y))]

    def onward(self, p):
        return [
            self.copy(p, 5, self.view(p).at[0:2, self.x], self.to(self.z, self.y)),
            self.copy(p, 6, self.view(p).at[2:4, self.y], self.to(self.z, self.x)),
        ]

    def start(self, copies):
        for copy in copies:
            copy.start()

    def arrive(self, copies):
        for copy in copies:
            copy.wait_recv()

    def step(self, p):
        self.arrive(self.along(p))
        self.start(self.plane(p))

    def forward(self, p):
        self.arrive(self.plane(p))
        self.start(self.onward(p))

    def finish(self, p):
        for copy in self.along(p) + self.plane(p) + self.onward(p):
            copy.wait_send()


class GatherLine(Gather):
    def ring(self, p):
        own = self.view(p).at[self.z, self.yx]
        return [self.copy(p, 0, own, self.to(self.z, self.x)), self.copy(p, 1, own, self.to(self.z, self.y))]

    def onward(self, p):
        half = self.view(p).shape[2] // 2
        return [
            self.copy(p, 2, self.view(p).at[self.z, self.x, 0:half], self.to(self.z, self.y)),
            self.copy(p, 3, self.view(p).at[self.z, self.y, half:], self.to(self.z, self.x)),
        ]

    def climb(self, p, k, up, arriving):
        behind = k if arriving else k - 1
        plane = self.z - behind if up else self.z + behind
        beyond = self.z + 1 if up != arriving else self.z - 1
        real = (plane >= 0) & (plane <= 3) & (beyond >= 0) & (beyond <= 3)
        plane, beyond = jnp.clip(plane, 0, 3), jnp.clip(beyond, 0, 3)
        k = (4 if up else 7) + k - 1
        return real, self.copy(p, k, self.view(p).at[plane], self.to(beyond, self.yx))

    def each(self, p, k, arriving, action):
        for up in (True, False):
            real, copy = self.climb(p, k, up, arriving)
            pl.when(real)(functools.partial(action, copy))

    def line(self, p, k):
        if k > 1:
            self.each(p, k - 1, True, lambda copy: copy.wait_recv())
        self.each(p, k, False, lambda copy: copy.start())

    def ready(self, p):
        self.each(p, 3, True, lambda copy: copy.wait_recv())

    def finish(self, p):
        for copy in self.ring(p) + self.onward(p):
            copy.wait_send()
        for k in (1, 2, 3):
            self.each(p, k, False, lambda copy: copy.wait_send())


class Reduce:
    def __init__(self, part, slot, ring1, ring2, line, out, sends, recvs):
        self.parts, self.slot, self.ring1, self.ring2, self.line, self.out = part, slot, ring1, ring2, line, out
        self.sends, self.recvs = sends, recvs
        self.z, self.yx, self.c = place()
        self.x, self.y, self.d, self.zs = neighbours(self.z, self.yx)

    def copy(self, k, src, dst, z, yx):
        return remote(src, dst, self.sends.at[k], self.recvs.at[k], (z * 4 + yx, self.c))

    def part(self):
        return self.parts.at[self.slot]

    def diagonal(self):
        return [
            self.copy(0, self.part().at[0:2, self.d], self.ring1.at[0], self.z, self.x),
            self.copy(1, self.part().at[2:4, self.d], self.ring1.at[1], self.z, self.y),
        ]

    def side(self):
        return [
            self.copy(2, self.part().at[:, self.x], self.ring2.at[0], self.z, self.x),
            self.copy(3, self.part().at[:, self.y], self.ring2.at[1], self.z, self.y),
        ]

    def down(self):
        return [
            self.copy(4 + k, self.part().at[peer, self.yx], self.line.at[k], peer, self.yx)
            for k, peer in enumerate(self.zs)
        ]

    def start(self, copies):
        for copy in copies:
            copy.start()

    def arrive(self, copies):
        for copy in copies:
            copy.wait_recv()

    def total(self, a, yx, pieces):
        return sum((piece.astype(F32) for piece in pieces), self.part()[a, yx].astype(F32))

    def add(self, a, yx, pieces):
        self.part()[a, yx] = self.total(a, yx, pieces).astype(self.parts.dtype)

    def stage1(self):
        self.start(self.diagonal())

    def stage2(self):
        self.arrive(self.diagonal())
        for a in range(2):
            self.add(a, self.y, [self.ring1[0, a]])
            self.add(a + 2, self.x, [self.ring1[1, a]])
        self.start(self.side())

    def stage3(self):
        self.arrive(self.side())
        for a in range(4):
            self.add(a, self.yx, [self.ring2[0, a], self.ring2[1, a]])
        self.start(self.down())

    def stage4(self):
        self.arrive(self.down())
        self.out[...] = self.total(self.z, self.yx, [self.line[k] for k in range(3)])

    def finish(self):
        for copy in self.diagonal() + self.side() + self.down():
            copy.wait_send()


class ReduceLine(Reduce):
    def step(self, k, up, arriving):
        z = self.z
        plane = (3 if arriving else 4) - k + z if up else k - (3 if arriving else 4) + z
        beyond = z + 1 if up != arriving else z - 1
        real = (plane >= 0) & (plane <= 3) & (beyond >= 0) & (beyond <= 3)
        plane, beyond = jnp.clip(plane, 0, 3), jnp.clip(beyond, 0, 3)
        place_in = plane + 1 if up else plane
        k = (3 if up else 0) + k - 1
        return real, plane, place_in, self.copy(k, self.part().at[plane], self.line.at[place_in], beyond, self.yx)

    def move(self, k):
        for up in (True, False):
            real, plane, _, leaving = self.step(k, up, False)
            if k > 1:
                came, _, place_in, arrived = self.step(k - 1, up, True)

                @pl.when(real & came)
                def _():
                    arrived.wait_recv()
                    for yx in range(4):
                        self.add(plane, yx, [self.line[place_in, yx]])

            pl.when(real)(leaving.start)

    def halves(self):
        half = self.ring1.shape[1]
        own = self.part().at[self.z, self.d]
        return [
            self.copy(6, own.at[0:half], self.ring1.at[0], self.z, self.x),
            self.copy(7, own.at[half:], self.ring1.at[1], self.z, self.y),
        ]

    def sides(self):
        return [
            self.copy(8, self.part().at[self.z, self.x], self.ring2.at[0], self.z, self.x),
            self.copy(9, self.part().at[self.z, self.y], self.ring2.at[1], self.z, self.y),
        ]

    def stage1(self):
        self.move(1)

    def stage2(self):
        self.move(2)

    def stage3(self):
        self.move(3)

    def stage4(self):
        for up in (True, False):
            came, plane, place_in, arrived = self.step(3, up, True)

            @pl.when(came)
            def _():
                arrived.wait_recv()
                for yx in range(4):
                    self.add(plane, yx, [self.line[place_in, yx]])

        self.start(self.halves())

    def stage5(self):
        self.arrive(self.halves())
        half = self.ring1.shape[1]
        for yx, at, piece in ((self.y, slice(0, half), 0), (self.x, slice(half, 2 * half), 1)):
            total = self.part()[self.z, yx, at].astype(F32) + self.ring1[piece].astype(F32)
            self.part()[self.z, yx, at] = total.astype(self.parts.dtype)
        self.start(self.sides())

    def stage6(self):
        self.arrive(self.sides())
        self.out[...] = self.total(self.z, self.yx, [self.ring2[0], self.ring2[1]])

    def finish(self):
        for k in (1, 2, 3):
            for up in (True, False):
                real, _, _, leaving = self.step(k, up, False)
                pl.when(real)(leaving.wait_send)
        for copy in self.halves() + self.sides():
            copy.wait_send()


def lanes(j):
    return slice(j * 128, (j + 1) * 128)


def bottom(v):
    return jnp.broadcast_to(v[7:8], v.shape)


def top(v):
    return jnp.broadcast_to(v[0:1], v.shape)


def masks_down(keep, place_in):
    m1 = jnp.where(place_in >= 1, keep, 0.0)
    m2 = m1 * pltpu.roll(m1, 1, 0)
    m4 = m2 * pltpu.roll(m2, 2, 0)
    for n in (1, 2, 4):
        keep = keep * jnp.where(place_in >= n, pltpu.roll(keep, n, 0), 1.0)
    return m1, m2, m4, keep


def masks_up(after, place_in):
    m1 = jnp.where(place_in <= 6, after, 0.0)
    m2 = m1 * pltpu.roll(m1, 7, 0)
    m4 = m2 * pltpu.roll(m2, 6, 0)
    for n in (1, 2, 4):
        after = after * jnp.where(place_in <= 7 - n, pltpu.roll(after, 8 - n, 0), 1.0)
    return m1, m2, m4, after


def wkv_forward(k_ref, v_ref, r_ref, keep_ref, rows_ref, mixed_ref, sn_ref, sd_ref):
    length, width = k_ref.shape
    tiles = width // 128
    place_in = lax.broadcasted_iota(jnp.int32, (8, 128), 0)
    first = place_in == 0
    zero = jnp.zeros((8, 128), F32)

    def pair(g, carry):
        carry = list(carry)
        base = pl.multiple_of(g * 16, 16)
        keeps = [keep_ref[pl.ds(base + 8 * h, 8), :] for h in range(2)]
        masks = [masks_down(keep, place_in) for keep in keeps]
        for j in range(tiles):
            d1, d2, d4, eu = (rows_ref[n : n + 1, lanes(j)] for n in range(4))
            dp = rows_ref[8:16, lanes(j)]
            made = []
            for h in range(2):
                at = pl.ds(base + 8 * h, 8)
                keep, (m1, m2, m4, mp) = keeps[h], masks[h]
                ek = jnp.exp(k_ref[at, lanes(j)])
                v = v_ref[at, lanes(j)]
                num, den = ek * v, ek
                x, b = num, eu * ek
                for n, coef in ((1, m1 * d1), (2, m2 * d2), (4, m4 * d4)):
                    num = num + coef * pltpu.roll(num, n, 0)
                    den = den + coef * pltpu.roll(den, n, 0)
                coef = mp * dp
                cn, cd = carry[2 * j], carry[2 * j + 1]
                num = num + coef * cn
                den = den + coef * cd
                sn = keep * jnp.where(first, cn, pltpu.roll(num, 1, 0))
                sd = keep * jnp.where(first, cd, pltpu.roll(den, 1, 0))
                carry[2 * j], carry[2 * j + 1] = bottom(num), bottom(den)
                sn_ref[at, lanes(j)] = sn
                sd_ref[at, lanes(j)] = sd
                weighted = (sn + eu * x) / (sd + b)
                made.append(jax.nn.sigmoid(r_ref[at, lanes(j)]) * weighted)
            mixed_ref[pl.ds(base, 16), lanes(j)] = jnp.concatenate(made, axis=0).astype(BF16)
        return tuple(carry)

    lax.fori_loop(0, length // 16, pair, (zero,) * (2 * tiles))


def wkv_backward(
    g_ref, k_ref, v_ref, r_ref, sn_ref, sd_ref, keep_ref, rows_ref, gk_ref, gv_ref, gr_ref, begin, end, carry
):
    length, width = k_ref.shape
    tiles = width // 128
    place_in = lax.broadcasted_iota(jnp.int32, (8, 128), 0)
    last = place_in == 7
    zero = jnp.zeros((8, 128), F32)
    pairs = length // 16

    def pair(step, carry):
        carry = list(carry)
        base = pl.multiple_of((pairs - 1 - step) * 16, 16)
        low, high = (keep_ref[pl.ds(base + 8 * h, 8), :] for h in range(2))
        afters = [
            jnp.where(last, top(high), pltpu.roll(low, 7, 0)),
            jnp.where(last, carry[4 * tiles], pltpu.roll(high, 7, 0)),
        ]
        masks = [masks_up(after, place_in) for after in afters]
        carry[4 * tiles] = top(low)
        for j in range(tiles):
            d1, d2, d4, eu = (rows_ref[n : n + 1, lanes(j)] for n in range(4))
            dp = rows_ref[16:24, lanes(j)]
            made = [None, None]
            for h in (1, 0):
                at = pl.ds(base + 8 * h, 8)
                after, (m1, m2, m4, mp) = afters[h], masks[h]
                ek = jnp.exp(k_ref[at, lanes(j)])
                v = v_ref[at, lanes(j)]
                sn, sd = sn_ref[at, lanes(j)], sd_ref[at, lanes(j)]
                s = jax.nn.sigmoid(r_ref[at, lanes(j)])
                b = eu * ek
                inverse = 1.0 / (sd + b)
                weighted = (sn + b * v) * inverse
                g = g_ref[at, lanes(j)]
                gs = g * s
                p = gs * inverse
                q = -p * weighted
                gr = gs * weighted * (1.0 - s)
                hp, hq = p, q
                for n, coef in ((1, m1 * d1), (2, m2 * d2), (4, m4 * d4)):
                    hp = hp + coef * pltpu.roll(hp, 8 - n, 0)
                    hq = hq + coef * pltpu.roll(hq, 8 - n, 0)
                coef = mp * dp
                cp, cq = carry[4 * j], carry[4 * j + 1]
                hp = hp + coef * cp
                hq = hq + coef * cq
                ap = after * jnp.where(last, cp, pltpu.roll(hp, 7, 0))
                aq = after * jnp.where(last, cq, pltpu.roll(hq, 7, 0))
                carry[4 * j], carry[4 * j + 1] = top(hp), top(hq)
                bonus = b * (v * p + q)
                gv = ek * ap + b * p
                gk = ek * (v * ap + aq) + bonus
                carry[4 * j + 2] = carry[4 * j + 2] + bonus
                carry[4 * j + 3] = carry[4 * j + 3] + (ap * sn + aq * sd)
                made[h] = (gk, gv, gr)
            both = pl.ds(base, 16)
            for n, ref in enumerate((gk_ref, gv_ref, gr_ref)):
                ref[both, lanes(j)] = jnp.concatenate([made[0][n], made[1][n]], axis=0).astype(BF16)
        return tuple(carry)

    return lax.fori_loop(begin, end, pair, (zero,) * (4 * tiles + 1) if carry is None else carry)


def wkv_sums(carry, rows_ref, decay_ref, bonus_ref):
    for j in range(decay_ref.shape[1] // 128):
        bonus_ref[0:1, lanes(j)] = jnp.sum(carry[4 * j + 2], axis=0, keepdims=True)
        decay_ref[0:1, lanes(j)] = -rows_ref[4:5, lanes(j)] * jnp.sum(carry[4 * j + 3], axis=0, keepdims=True)


NN, NT, TN = ((1,), (0,)), ((1,), (1,)), ((0,), (0,))
KEY, VALUE, GATE, EMIT, GATE2, FFN = 0, 1, 2, 3, 4, 5
KEYS, VALUES = (5, 7, 9, 11), (6, 8, 10, 12)
RINGS = 11
VECTORS = 11
TILE = 64
GAIN1, BIAS1, GAIN2, BIAS2, FADE, REWARD, MK1, MV1, MR1, MK2, MR2, OWN_FADE, OWN_REWARD = range(13)


def dot(a, b, dims):
    return lax.dot_general(a, b, (dims, ((), ())), preferred_element_type=F32)


def strip(i, size):
    return pl.ds(pl.multiple_of(i * size, size), size)


def over_rows(length, size, body):
    def step(i, carry):
        body(strip(i, size))
        return carry

    lax.fori_loop(0, length // size, step, 0)


def matrix(ref):
    return ref[...].reshape(16 * ref.shape[2], ref.shape[3])


def emit_half(ref, h):
    rows = ref.shape[2] // 2
    return ref[:, :, h * rows : (h + 1) * rows, :].reshape(16 * rows, ref.shape[3])


def wide(column, width):
    return jnp.concatenate([column] * (width // 128), axis=1)


def norm(x):
    center = x - jnp.mean(x, axis=-1, keepdims=True)
    inverse = lax.rsqrt(jnp.mean(center * center, axis=-1, keepdims=True) + 1e-05)
    return center * inverse, inverse


def norm_and_mix(length, width, load, gain, bias, keep_ref, mixes, outs):
    first = lax.broadcasted_iota(jnp.int32, (TILE, width), 0) == 0

    def step(i, before):
        at = strip(i, TILE)
        unit, _ = norm(load(at))
        normed = unit * gain + bias
        prev = jnp.where(first, before, pltpu.roll(normed, 1, 0)) * wide(keep_ref[at, :], width)
        differ = normed - prev
        for share, out in zip(mixes, outs):
            out[at, :] = (prev + differ * share).astype(BF16)
        return normed[TILE - 1 : TILE]

    lax.fori_loop(0, length // TILE, step, jnp.zeros((1, width), F32))


def forward_kernel(
    own4, other4, rest, vec, x_own, up_own, keep_own,
    g_out, out, x_out, up_out, ins_out, kvr_out, sn_out, sd_out, mixed_out, resid_out, ins2_out, pre_out, act_out,
    gv_out, gr_out, vec_out, rows_out, keep_out,
    gv, g, x, up, ins, kvr, sn, sd, mixed, sum_own, sum_other, resid, ins2, pre, act, v_send, v_other, gval, grec, low_half,
    local_sem, ex_send, ex_recv, sends, recvs, lsends, lrecvs, vsends, vrecvs, out_sem, sum_send, sum_recv, val_send, val_recv,
):
    z, yx, c = place()
    length, width = x.shape
    half = width // 2
    span = length // 2
    partner = (z * 4 + yx, 1 - c)
    enter(z, yx, c)

    block = own4.shape[1]
    mine = strip(c, block)
    rows_mine = strip(c, span)
    swaps = [
        (vec, gv.at[z, yx, c]),
        (other4.at[0:3], g.at[0:3, z, yx, mine]),
        (other4.at[3], g.at[GATE2, z, yx, mine]),
        (x_own, x.at[rows_mine]),
        (keep_own, keep_out.at[rows_mine]),
        (up_own, up.at[rows_mine]),
    ]
    swaps = [remote(a, b, ex_send.at[n], ex_recv.at[n], partner) for n, (a, b) in enumerate(swaps)]
    keeps = [
        (vec, gv.at[z, yx, c]),
        (own4.at[0:3], g.at[0:3, z, yx, mine]),
        (own4.at[3], g.at[GATE2, z, yx, mine]),
        (x_own, x.at[rows_mine]),
        (keep_own, keep_out.at[rows_mine]),
        (up_own, up.at[rows_mine]),
        (rest.at[0], g.at[EMIT, z, yx]),
        (rest.at[1:9], g.at[FFN : FFN + 8, z, yx]),
    ]
    keeps = [pltpu.make_async_copy(a, b, local_sem.at[n]) for n, (a, b) in enumerate(keeps)]
    for copy in swaps + keeps:
        copy.start()
    weights = Gather(lambda p: g.at[p], sends, recvs)
    lines = GatherLine(lambda p: g.at[RINGS + p], lsends, lrecvs)
    vectors = Gather(lambda p: gv, vsends, vrecvs)

    outs = []

    def put(src, dst):
        copy = pltpu.make_async_copy(src, dst, out_sem.at[len(outs)])
        copy.start()
        outs.append(copy)
        return copy

    along_z = {4: [(0, 1)], 5: [(1, 1)], 6: [(0, 2)], 7: [(1, 2)], 8: [(0, 3)], 9: [(1, 3)]}

    def turn(n):
        if n < RINGS:
            weights.step(n)
            if n + 2 < RINGS:
                weights.start(weights.along(n + 2))
        if 1 <= n <= RINGS:
            weights.forward(n - 1)
        for p, k in along_z.get(n, []):
            lines.line(p, k)
        if n >= 2:
            weights.arrive(weights.onward(n - 2))
            put(g.at[n - 2], g_out.at[n - 2])

    def lined(p):
        lines.ready(p - RINGS)
        put(g.at[p], g_out.at[p])

    for copy in keeps[6:]:
        copy.wait()
    for p in range(PIECES - RINGS):
        lines.start(lines.ring(p))
    for n in (0, 1, 2):
        swaps[n].wait()
        keeps[n].wait()
    vectors.start(vectors.along(0))
    weights.start(weights.along(0))
    weights.start(weights.along(1))
    for p in range(PIECES - RINGS):
        lines.arrive(lines.ring(p))
        lines.start(lines.onward(p))
    vectors.step(0)
    turn(0)
    vectors.forward(0)
    for n in (3, 4, 5):
        swaps[n].wait()
        keeps[n].wait()
    x_copy, up_copy = put(x, x_out), put(up, up_out)
    for p in range(PIECES - RINGS):
        lines.arrive(lines.onward(p))
    turn(1)
    vectors.arrive(vectors.onward(0))

    for t in range(width // 128):
        parts = [gv[(2 * t + k) // 4, (2 * t + k) % 4, core].astype(F32) for k in range(2) for core in range(2)]
        vec_out[:, lanes(t)] = functools.reduce(lambda a, b: a + b, parts)
    ramp = lax.broadcasted_iota(jnp.int32, (8, 128), 0).astype(F32)
    for t in range(half // 128):
        own = functools.reduce(lambda a, b: a + b, [gv[t, k, c].astype(F32) for k in range(4)])
        rate = jnp.exp(own[OWN_FADE : OWN_FADE + 1])
        head = [
            jnp.exp(-rate), jnp.exp(-2.0 * rate), jnp.exp(-4.0 * rate), jnp.exp(own[OWN_REWARD : OWN_REWARD + 1]),
            rate * jnp.exp(-rate),
        ]
        for n, row in enumerate(head):
            rows_out[n : n + 1, lanes(t)] = row
        rows_out[8:16, lanes(t)] = jnp.exp(-(ramp + 1.0) * rate)
        rows_out[16:24, lanes(t)] = jnp.exp(-(8.0 - ramp) * rate)

    def row(n):
        return vec_out[n : n + 1, :]

    norm_and_mix(
        length, width, lambda at: x[at, :].astype(F32), row(GAIN1), row(BIAS1), keep_out,
        [row(MK1), row(MV1), row(MR1)], [ins.at[n] for n in range(3)],
    )
    put(ins, ins_out)
    kvr_copies = []
    for n in range(3):
        turn(n + 2)
        weight = g.at[n]

        def project(at):
            kvr[n, at, :] = dot(ins[n, at, :], matrix(weight), NN)

        over_rows(length, 256, project)
        kvr_copies.append(put(kvr.at[n], kvr_out.at[n]))
    wkv_forward(kvr.at[0], kvr.at[1], kvr.at[2], keep_out, rows_out, mixed, sn, sd)
    put(mixed, mixed_out)
    put(sn, sn_out)
    put(sd, sd_out)
    turn(5)
    weight = g.at[EMIT]
    quarters = length // 4
    sums = []
    for n in range(4):
        at = pl.ds(n * quarters, quarters)
        for h in range(2):
            sum_own[at, h * half : (h + 1) * half] = dot(mixed[at, :], emit_half(weight, h), NN).astype(BF16)
        sums.append(remote(sum_own.at[at], sum_other.at[at], sum_send.at[n], sum_recv.at[n], partner))
        sums[-1].start()
    turn(6)
    for copy in sums:
        copy.wait()

    def add_up(at):
        total = x[at, :].astype(F32) + (sum_own[at, :].astype(F32) + sum_other[at, :].astype(F32))
        resid[0, at, :] = total[:, :half]
        resid[1, at, :] = total[:, half:]
        return total

    norm_and_mix(
        length, width, add_up, row(GAIN2), row(BIAS2), keep_out, [row(MK2), row(MR2)], [ins2.at[n] for n in range(2)]
    )
    put(resid, resid_out)
    put(ins2, ins2_out)
    for copy in kvr_copies:
        copy.wait()
    weight = g.at[GATE2]

    def gate(at):
        kvr[2, at, :] = jax.nn.sigmoid(dot(ins2[1, at, :], matrix(weight), NN))

    over_rows(length, 256, gate)
    pre_copies = []

    def expand_chunk(j):
        weight, slot = g.at[KEYS[j]], len(pre_copies) % 2
        if len(pre_copies) >= 2:
            pre_copies[-2].wait()

        def expand(at):
            positive = jnp.maximum(dot(ins2[0, at, :], matrix(weight), NN), 0.0)
            pre[slot, at, :] = positive.astype(BF16)
            act[j, at, :] = (positive * positive).astype(BF16)

        over_rows(length, 256, expand)
        pre_copies.append(put(pre.at[slot], pre_out.at[j]))
        put(act.at[j], act_out.at[j])

    def contract_chunk(j):
        weight = g.at[VALUES[j]]

        def contract(at):
            for h in range(2):
                part = dot(act[j, at, :], weight[2 * h : 2 * h + 2].reshape(half, -1), NT)
                kvr[h, at, :] = part if j == 0 else kvr[h, at, :] + part

        over_rows(length, 256, contract)

    turn(7)
    expand_chunk(0)
    turn(8)
    contract_chunk(0)
    turn(9)
    expand_chunk(1)
    turn(10)
    contract_chunk(1)
    lined(KEYS[3])
    expand_chunk(3)
    lined(VALUES[3])
    contract_chunk(3)
    turn(11)
    expand_chunk(2)
    turn(12)
    contract_chunk(2)

    vals = []
    for n in range(4):
        at = pl.ds(n * quarters, quarters)
        v_send[at, :] = kvr[1 - c, at, :].astype(BF16)
        vals.append(remote(v_send.at[at], v_other.at[at], val_send.at[n], val_recv.at[n], partner))
        vals[-1].start()
    columns = strip(c, half)
    backs = []
    for n in range(4):
        vals[n].wait()

        def finish(i, carry):
            at = strip(n * (quarters // 16) + i, 16)
            value = kvr[c, at, :] + v_other[at, :].astype(F32)
            s = kvr[2, at, :]
            low_half[at, :] = (resid[c, at, :] + s * value).astype(BF16)
            upstream = up[at, columns].astype(F32)
            gval[c, at, :] = (upstream * s).astype(BF16)
            grec[at, :] = (upstream * value * s * (1.0 - s)).astype(BF16)
            return carry

        lax.fori_loop(0, quarters // 16, finish, 0)
        at = pl.ds(n * quarters, quarters)
        backs.append(remote(gval.at[c, at], gval.at[c, at], val_send.at[4 + n], val_recv.at[4 + n], partner))
        backs[-1].start()
    give = remote(low_half.at[strip(1 - c, span)], out.at[:, columns], val_send.at[8], val_recv.at[8], partner)
    give.start()
    put(low_half.at[rows_mine], out.at[:, columns])
    put(grec, gr_out)
    for copy in backs:
        copy.wait()
    put(gval, gv_out)
    give.wait()

    def close(p, carry):
        weights.finish(p)
        return carry

    lax.fori_loop(0, RINGS, close, 0)
    for p in range(PIECES - RINGS):
        lines.finish(p)
    vectors.finish(0)
    waited = kvr_copies + pre_copies[:2]
    for copy in outs:
        if not any(copy is other for other in waited):
            copy.wait()


def forward_call(own4, other4, rest, vec, x_own, up_own, keep_own):
    span, width = x_own.shape
    length, half = 2 * span, width // 2
    block = rest.shape[1:]
    any_, vmem = pl.BlockSpec(memory_space=pl.ANY), pl.BlockSpec(memory_space=pltpu.VMEM)
    full, col = (length, width), (length, half)

    def shape(dims, kind):
        return jax.ShapeDtypeStruct(dims, kind)

    outs = (
        (shape((PIECES, 4, 4) + block, BF16), any_),
        (shape((span, width), BF16), any_),
        (shape(full, BF16), any_),
        (shape(full, BF16), any_),
        (shape((3,) + full, BF16), any_),
        (shape((3,) + col, F32), any_),
        (shape(col, F32), any_),
        (shape(col, F32), any_),
        (shape(col, BF16), any_),
        (shape((2,) + col, F32), any_),
        (shape((2,) + full, BF16), any_),
        (shape((4,) + col, BF16), any_),
        (shape((4,) + col, BF16), any_),
        (shape((2,) + col, BF16), any_),
        (shape(col, BF16), any_),
        (shape((16, width), F32), vmem),
        (shape((24, half), F32), vmem),
        (shape((length, 128), F32), vmem),
    )
    dma = pltpu.SemaphoreType.DMA
    return pl.pallas_call(
        forward_kernel,
        out_shape=tuple(o[0] for o in outs),
        in_specs=[vmem] * 7,
        out_specs=tuple(o[1] for o in outs),
        scratch_shapes=[
            pltpu.VMEM((4, 4, 2) + vec.shape, BF16),
            pltpu.VMEM((PIECES, 4, 4) + block, BF16),
            pltpu.VMEM(full, BF16),
            pltpu.VMEM(full, BF16),
            pltpu.VMEM((3,) + full, BF16),
            pltpu.VMEM((3,) + col, F32),
            pltpu.VMEM(col, F32),
            pltpu.VMEM(col, F32),
            pltpu.VMEM(col, BF16),
            pltpu.VMEM(full, BF16),
            pltpu.VMEM(full, BF16),
            pltpu.VMEM((2,) + col, F32),
            pltpu.VMEM((2,) + full, BF16),
            pltpu.VMEM((2,) + col, BF16),
            pltpu.VMEM((4,) + col, BF16),
            pltpu.VMEM(col, BF16),
            pltpu.VMEM(col, BF16),
            pltpu.VMEM((2,) + col, BF16),
            pltpu.VMEM(col, BF16),
            pltpu.VMEM(col, BF16),
            dma((8,)), dma((6,)), dma((6,)),
            dma((RINGS, 7)), dma((RINGS, 7)), dma((PIECES - RINGS, 10)), dma((PIECES - RINGS, 10)), dma((1, 7)), dma((1, 7)),
            dma((40,)), dma((4,)), dma((4,)), dma((9,)), dma((9,)),
        ],
        compiler_params=pltpu.CompilerParams(
            collective_id=0, has_side_effects=True, vmem_limit_bytes=63 * MIB
        ),
        name="forward",
    )(own4, other4, rest, vec, x_own, up_own, keep_own)


R_VALUE, R_KEY, R_GATE2, R_EMIT, R_TIME = 0, 4, 8, 9, 10
WEIGHT_ORDER = [p for j in range(4) for p in (VALUES[j], KEYS[j])] + [GATE2, EMIT, KEY, VALUE, GATE]
LINED = (1, 3)
SUMS = 11
S_GAIN1, S_BIAS1, S_GAIN2, S_BIAS2, S_DECAY, S_BONUS, S_MK1, S_MV1, S_MR1, S_MK2, S_MR2 = range(11)
SLOTS = 12


def whole(ref, at):
    return jnp.concatenate([ref[0, at, :], ref[1, at, :]], axis=1)


def halves(ref, at, value):
    half = value.shape[1] // 2
    ref[0, at, :] = value[:, :half].astype(ref.dtype)
    ref[1, at, :] = value[:, half:].astype(ref.dtype)


def fold(value):
    return sum(value[n : n + 8] for n in range(8, value.shape[0], 8)) + value[:8]


def back_through_norm(g, unit, inverse, gain):
    q = g * gain
    return inverse * (
        q - jnp.mean(q, axis=-1, keepdims=True) - unit * jnp.mean(q * unit, axis=-1, keepdims=True)
    )


def lifted(now, following, last):
    return jnp.where(last, following[0:1], pltpu.roll(now, now.shape[0] - 1, 0))


def backward_kernel(
    plan,
    g, x_in, up_in, ins_in, kvr_in, sn_in, sd_in, mixed_in, resid_in, ins2_in, pre_in, act_in, gv_in, gr_in,
    vec, rows, keep,
    out, recv4, vsum, vother, gtok,
    part, ring1, ring2, line, lring1, lring2, lline, vpart, vring1, vring2, vline,
    b, w, f, resid, sum_other, n1_other, acc, own_sums,
    load_sem, w_sem, sends, recvs, lsends, lrecvs, vsends, vrecvs, ex_send, ex_recv, sum_send, sum_recv,
):
    z, yx, c = place()
    nx, ny, nd, zs = neighbours(z, yx)
    length, half = b.shape[1:]
    width = 2 * half
    span = length // 2
    quarter = length // 4
    partner = (z * 4 + yx, 1 - c)
    loads = {}

    def load(name, src, dst):
        copy = pltpu.make_async_copy(src, dst, load_sem.at[len(loads)])
        copy.start()
        loads[name] = copy

    def loaded(*names):
        for name in names:
            loads[name].wait()

    def pair(n):
        return b.at[n : n + 2]

    def load_pair(name, src, n):
        for h in range(2):
            load((name, h), src.at[:, h * half : (h + 1) * half], b.at[n + h])

    def loaded_pair(name):
        loaded((name, 0), (name, 1))

    def weight_copy(n):
        return pltpu.make_async_copy(g.at[WEIGHT_ORDER[n]], w.at[n % 3], w_sem.at[n])

    def weight(n):
        weight_copy(n).wait()
        return w.at[n % 3]

    GVAL, ACT, PRE, IN_K2, IN_R2, GREC, GPRE = 0, 2, 4, 6, 8, 10, 11
    load("gv0", gv_in.at[0], b.at[GVAL])
    load("gv1", gv_in.at[1], b.at[GVAL + 1])
    for j in range(2):
        load(("act", j), act_in.at[j], b.at[ACT + j])
    load_pair("in_k2", ins2_in.at[0], IN_K2)
    for j in range(2):
        load(("pre", j), pre_in.at[j], b.at[PRE + j])
    for n in range(3):
        weight_copy(n).start()
    load_pair("in_r2", ins2_in.at[1], IN_R2)
    load("gr", gr_in, b.at[GREC])
    load("resid", resid_in, resid)
    enter(z, yx, c)

    sums = []
    for p in range(PIECES):
        if p in LINED:
            n = LINED.index(p)
            sums.append(
                ReduceLine(
                    part, p % PARTS, lring1.at[n], lring2.at[n], lline.at[n], out.at[p], lsends.at[n], lrecvs.at[n]
                )
            )
        else:
            n = p - sum(q < p for q in LINED)
            sums.append(
                Reduce(part, p % PARTS, ring1.at[n], ring2.at[n], line.at[n], out.at[p], sends.at[n], recvs.at[n])
            )
    vector_sums = Reduce(vpart, 0, vring1, vring2, vline, vsum, vsends, vrecvs)
    final = []
    rows4 = recv4.shape[1]
    others = strip(1 - c, rows4)

    def pump(name):
        for stage, p in plan[name]:
            if p == "v":
                getattr(vector_sums, "stage%d" % stage)()
                continue
            getattr(sums[p], "stage%d" % stage)()
            if stage == 4 and p in (R_GATE2, R_TIME, R_TIME + 1, R_TIME + 2):
                n = len(final)
                slot = 3 if p == R_GATE2 else p - R_TIME
                final.append(remote(out.at[p, others], recv4.at[slot], ex_send.at[n], ex_recv.at[n], partner))
                final[-1].start()

    def gradient(p, lhs, rhs):
        for a in range(4):
            block = lhs[a // 2, :, (a % 2) * (half // 2) : (a % 2 + 1) * (half // 2)]
            part[p % PARTS, a] = dot(block, rhs[...], TN).astype(BF16).reshape(part.shape[2:])

    def thirds(ref, h):
        return ref[2 * h : 2 * h + 2].reshape(half, half)

    loaded("gv0", "gv1")
    for j in range(4):
        loaded(("act", j))
        gradient(R_VALUE + j, pair(GVAL), b.at[ACT + j % 2])
        if j < 2:
            load(("act", j + 2), act_in.at[j + 2], b.at[ACT + j])
        pump("fv%d" % j)
    loaded_pair("in_k2")
    for j in range(4):
        loaded(("pre", j))
        value_w = weight(2 * j)

        def through(at):
            g_hidden = sum(dot(b[GVAL + h, at, :], thirds(value_w, h), NN) for h in range(2))
            b[GPRE, at, :] = (2.0 * b[PRE + j % 2, at, :].astype(F32) * g_hidden).astype(BF16)

        over_rows(length, 256, through)
        pump("th%d" % j)
        if j < 2:
            load(("pre", j + 2), pre_in.at[j + 2], b.at[PRE + j])
        weight_copy(2 * j + 3).start()
        gradient(R_KEY + j, pair(IN_K2), b.at[GPRE])
        pump("fk%d" % j)
        key_w = weight(2 * j + 1)

        def collect(at):
            for h in range(2):
                piece = dot(b[GPRE, at, :], thirds(key_w, h), NT)
                f[h, at, :] = piece if j == 0 else f[h, at, :] + piece

        over_rows(length, 256, collect)
        pump("co%d" % j)
        weight_copy(2 * j + 4).start()
    loaded_pair("in_r2")
    loaded("gr")
    gradient(R_GATE2, pair(IN_R2), b.at[GREC])
    pump("g2")
    gate_w = weight(8)

    def gate_back(at):
        for h in range(2):
            f[2 + h, at, :] = dot(b[GREC, at, :], thirds(gate_w, h), NT)

    over_rows(length, 256, gate_back)
    pump("gb")
    weight_copy(11).start()
    loaded("resid")

    SUM_OWN, UP, BRANCH, MIXED, G3, X, IN_K, IN_V, IN_R, SEND = 0, 2, 4, 6, 7, 4, 10, 0, 2, 6
    load_pair("up", up_in, UP)
    load("mixed", mixed_in, b.at[MIXED])
    acc[...] = jnp.zeros_like(acc)
    last = lax.broadcasted_iota(jnp.int32, (TILE, width), 0) == TILE - 1

    def row(n):
        return vec[n : n + 1, :]

    def kept(at, n):
        return wide(keep[at, :], width) if n is None else wide(keep[n, :], width)

    gain2, bias2, mk2, mr2 = (GAIN2, BIAS2, MK2, MR2)
    sum_copies = []
    for q in range(4):

        def tile(i, carry):
            base = q * quarter + i * TILE
            at = pl.ds(pl.multiple_of(base, TILE), TILE)
            after = pl.ds(pl.multiple_of(jnp.minimum(base + TILE, length - 8), 8), 8)
            inside = jnp.where(base + TILE < length, 1.0, 0.0)
            keep_at, keep_after = wide(keep[at, :], width), wide(keep[after, :], width) * inside
            unit, _ = norm(whole(resid, at))
            normed = unit * row(gain2) + row(bias2)
            total = jnp.zeros_like(unit)
            for n, share in enumerate((mk2, mr2)):
                back = whole(f.at[2 * n : 2 * n + 2], at)
                ahead = lifted(back * keep_at, whole(f.at[2 * n : 2 * n + 2], after) * keep_after, last)
                total = total + ahead + (back - ahead) * row(share)
                acc[S_MK2 + n] = acc[S_MK2 + n] + fold(normed * (back - ahead))
            acc[S_GAIN2] = acc[S_GAIN2] + fold(total * unit)
            acc[S_BIAS2] = acc[S_BIAS2] + fold(total)
            halves(b.at[SUM_OWN : SUM_OWN + 2], at, total)
            return carry

        lax.fori_loop(0, quarter // TILE, tile, 0)
        at = pl.ds(q * quarter, quarter)
        sum_copies.append(
            remote(b.at[SUM_OWN : SUM_OWN + 2, at], sum_other.at[:, at], sum_send.at[q], sum_recv.at[q], partner)
        )
        sum_copies[-1].start()
        pump("a%d" % q)
    for n in range(3):
        load(("kvr", n), kvr_in.at[n], f.at[n])
    load("sn", sn_in, f.at[3])
    load("sd", sd_in, f.at[4])
    load_pair("in_k", ins_in.at[0], IN_K)

    loaded_pair("up")
    for q in range(4):
        sum_copies[q].wait_recv()

        def tile(i, carry):
            at = pl.ds(pl.multiple_of(q * quarter + i * TILE, TILE), TILE)
            unit, inverse = norm(whole(resid, at))
            total = whole(b.at[SUM_OWN : SUM_OWN + 2], at).astype(F32) + whole(sum_other, at).astype(F32)
            back = whole(pair(UP), at).astype(F32) + back_through_norm(total, unit, inverse, row(gain2))
            halves(pair(BRANCH), at, back)

            @pl.when(c == q // 2)
            def _():
                gtok[pl.ds(pl.multiple_of((q % 2) * quarter + i * TILE, TILE), TILE), :] = back

            return carry

        lax.fori_loop(0, quarter // TILE, tile, 0)
        pump("b%d" % q)
    for copy in sum_copies:
        copy.wait_send()
    load_pair("in_v", ins_in.at[1], IN_V)
    load_pair("in_r", ins_in.at[2], IN_R)

    loaded("mixed")
    for h in range(2):
        for a in range(2):
            block = dot(b[MIXED, :, a * (half // 2) : (a + 1) * (half // 2)], b[BRANCH + h], TN).astype(BF16)
            rows_h = part.shape[3] // 2
            part[R_EMIT, 2 * a : 2 * a + 2, :, h * rows_h : (h + 1) * rows_h, :] = block.reshape(2, 4, rows_h, half)
    pump("em")
    emit_w = weight(9)

    def emit_back(at):
        resid[0, at, :] = sum(dot(b[BRANCH + h, at, :], emit_half(emit_w, h), NT) for h in range(2))

    over_rows(length, 256, emit_back)
    pump("eb")
    weight_copy(12).start()
    load_pair("x", x_in, X)

    loaded(("kvr", 0), ("kvr", 1), ("kvr", 2), "sn", "sd")
    carry = None
    for q in range(4):
        carry = wkv_backward(
            resid.at[0], f.at[0], f.at[1], f.at[2], f.at[3], f.at[4], keep, rows, b.at[G3], b.at[G3 + 1], b.at[G3 + 2],
            q * (length // 64), (q + 1) * (length // 64), carry,
        )
        pump("w%d" % q)
    wkv_sums(carry, rows, own_sums.at[0:1], own_sums.at[1:2])

    for n, (name, slot) in enumerate((("in_k", IN_K), ("in_v", IN_V), ("in_r", IN_R))):
        loaded_pair(name)
        sums[R_TIME + n - PARTS].finish()
        gradient(R_TIME + n, pair(slot), b.at[G3 + n])
        pump("t%d" % n)
    loaded_pair("x")
    time_w = [weight(10 + n) for n in range(3)]
    for n in range(3):
        for h in range(2):
            f[n, pl.ds(h * span + quarter, 8), :] = jnp.zeros((8, half), F32)
    n1_copies = []
    for q in (3, 2, 1, 0):
        for n in range(3):
            for h in range(2):
                if q < 3:
                    f[n, pl.ds(h * span + quarter, 8), :] = f[n, pl.ds(h * span, 8), :]
                f[n, pl.ds(h * span, quarter), :] = dot(
                    b[G3 + n, pl.ds(q * quarter, quarter), :], thirds(time_w[n], h), NT
                )

        def tile(i, carry):
            base = q * quarter + i * TILE
            at = pl.ds(pl.multiple_of(base, TILE), TILE)
            after = pl.ds(pl.multiple_of(jnp.minimum(base + TILE, length - 8), 8), 8)
            keep_at, keep_after = wide(keep[at, :], width), wide(keep[after, :], width)

            def take(n, start, size):
                return jnp.concatenate(
                    [f[n, pl.ds(pl.multiple_of(h * span + start, 8), size), :] for h in range(2)], axis=1
                )

            unit, _ = norm(whole(pair(X), at).astype(F32))
            normed = unit * row(GAIN1) + row(BIAS1)
            total = jnp.zeros_like(unit)
            for n, share in enumerate((MK1, MV1, MR1)):
                back = take(n, i * TILE, TILE)
                ahead = lifted(back * keep_at, take(n, i * TILE + TILE, 8) * keep_after, last)
                total = total + ahead + (back - ahead) * row(share)
                acc[S_MK1 + n] = acc[S_MK1 + n] + fold(normed * (back - ahead))
            acc[S_GAIN1] = acc[S_GAIN1] + fold(total * unit)
            acc[S_BIAS1] = acc[S_BIAS1] + fold(total)
            rows_q = [pl.ds(pl.multiple_of(h * span + (q % 2) * quarter + i * TILE, TILE), TILE) for h in range(2)]

            @pl.when(c == q // 2)
            def _():
                for h in range(2):
                    f[3, rows_q[h], :] = total[:, h * half : (h + 1) * half]

            @pl.when(c != q // 2)
            def _():
                for h in range(2):
                    b[SEND, rows_q[h], :] = total[:, h * half : (h + 1) * half].astype(BF16)

            return carry

        lax.fori_loop(0, quarter // TILE, tile, 0)
        pump("c%d" % q)
    swap_n1 = remote(b.at[SEND], n1_other, sum_send.at[4], sum_recv.at[4], partner)
    swap_n1.start()

    for n in (S_GAIN1, S_BIAS1, S_GAIN2, S_BIAS2, S_MK1, S_MV1, S_MR1, S_MK2, S_MR2):
        acc[n, 0:1, :] = jnp.sum(acc[n], axis=0, keepdims=True)
    for i in range(16):
        vpart[0, i // 4, i % 4] = jnp.concatenate(
            [acc[n, 0:1, lanes(i // 2)] for n in range(SUMS)]
            + [own_sums[n : n + 1, lanes(i // 4)] for n in range(2)]
            + [jnp.zeros((3, 128), F32)]
        )
    pump("v0")
    swap_n1.wait()

    def tokens(i, carry):
        at = strip(i, TILE)
        spans = [pl.ds(pl.multiple_of(h * span + i * TILE, TILE), TILE) for h in range(2)]
        unit, inverse = norm(whole(pair(X), pl.ds(pl.multiple_of(c * span + i * TILE, TILE), TILE)).astype(F32))
        total = jnp.concatenate([f[3, s, :] + n1_other[s, :].astype(F32) for s in spans], axis=1)
        gtok[at, :] = gtok[at, :] + back_through_norm(total, unit, inverse, row(GAIN1))
        return carry

    lax.fori_loop(0, span // TILE, tokens, 0)
    for n in range(1, 4):
        pump("v%d" % n)
    swap = remote(vsum, vother, ex_send.at[4], ex_recv.at[4], partner)
    swap.start()
    pump("end")
    for p in range(PIECES - PARTS, PIECES):
        sums[p].finish()
    vector_sums.finish()
    for copy in final + [swap]:
        copy.wait()


PLAN = {
    "fv0": [(1, 0)], "fv1": [(1, 1)], "fv2": [(1, 2), (2, 0)], "fv3": [(1, 3)],
    "th0": [(2, 2), (2, 1)], "fk0": [(1, 4), (3, 0)], "co0": [(2, 3)],
    "th1": [(2, 4)], "fk1": [(1, 5), (3, 1)], "co1": [(3, 2)],
    "th2": [(2, 5)], "fk2": [(1, 6), (3, 3)], "co2": [(4, 1)],
    "th3": [(2, 6), (3, 4)], "fk3": [(1, 7), (4, 3)], "co3": [(5, 1), (3, 5)],
    "g2": [(1, 8), (2, 7)], "gb": [(4, 0), (4, 2)],
    "a0": [(5, 3)], "a1": [(2, 8)], "a2": [(6, 1), (3, 6)], "a3": [(6, 3)],
    "b0": [(4, 4)], "b1": [(3, 7)], "b2": [(4, 5)], "b3": [(4, 6)],
    "em": [(1, 9), (3, 8)], "eb": [(4, 7)], "w0": [(2, 9)], "w1": [(4, 8)], "w2": [(3, 9)], "w3": [],
    "t0": [(1, 10)], "t1": [(1, 11)], "t2": [(1, 12), (2, 10)],
    "c0": [(2, 11), (4, 9)], "c1": [(2, 12)], "c2": [(3, 10)], "c3": [],
    "v0": [(1, "v"), (3, 11)], "v1": [(2, "v"), (4, 10), (3, 12)], "v2": [(3, "v"), (4, 11)], "v3": [(4, "v")],
    "end": [(4, 12)],
}


def backward_call(g, x, up, ins, kvr, sn, sd, mixed, resid, ins2, pre, act, g_value, g_recept, vec, rows, keep):
    block = g.shape[3:]
    length, half = sn.shape
    lined = len(LINED)
    rings = PIECES - lined
    any_, vmem = pl.BlockSpec(memory_space=pl.ANY), pl.BlockSpec(memory_space=pltpu.VMEM)
    dma = pltpu.SemaphoreType.DMA

    def shape(*dims):
        return jax.ShapeDtypeStruct(dims, F32)

    return pl.pallas_call(
        functools.partial(backward_kernel, PLAN),
        out_shape=(
            shape(PIECES, *block), shape(4, block[0] // 2, block[1]), shape(16, 128), shape(16, 128),
            shape(length // 2, 2 * half),
        ),
        in_specs=[any_] * 14 + [vmem] * 3,
        out_specs=(vmem,) * 5,
        scratch_shapes=[
            pltpu.VMEM((PARTS, 4, 4) + block, BF16),
            pltpu.VMEM((rings, 2, 2) + block, BF16),
            pltpu.VMEM((rings, 2, 4) + block, BF16),
            pltpu.VMEM((rings, 3) + block, BF16),
            pltpu.VMEM((lined, 2, block[0] // 2, block[1]), BF16),
            pltpu.VMEM((lined, 2) + block, BF16),
            pltpu.VMEM((lined, 5, 4) + block, BF16),
            pltpu.VMEM((1, 4, 4, 16, 128), F32),
            pltpu.VMEM((2, 2, 16, 128), F32),
            pltpu.VMEM((2, 4, 16, 128), F32),
            pltpu.VMEM((3, 16, 128), F32),
            pltpu.VMEM((SLOTS, length, half), BF16),
            pltpu.VMEM((3, 4, 4) + block, BF16),
            pltpu.VMEM((5, length, half), F32),
            pltpu.VMEM((2, length, half), F32),
            pltpu.VMEM((2, length, half), BF16),
            pltpu.VMEM((length, half), BF16),
            pltpu.VMEM((SUMS, 8, 2 * half), F32),
            pltpu.VMEM((8, half), F32),
            dma((40,)), dma((PIECES,)), dma((rings, 7)), dma((rings, 7)), dma((lined, 10)), dma((lined, 10)),
            dma((7,)), dma((7,)), dma((5,)), dma((5,)), dma((5,)), dma((5,)),
        ],
        compiler_params=pltpu.CompilerParams(collective_id=1, has_side_effects=True, vmem_limit_bytes=63 * MIB),
        name="backward",
    )(g, x, up, ins, kvr, sn, sd, mixed, resid, ins2, pre, act, g_value, g_recept, vec, rows, keep)


def shifted(value, axis, steps):
    count = lax.axis_size(axis)
    first, last = (max(0, -steps), min(count, count - steps))
    return lax.ppermute(value, axis, [(source, source + steps) for source in range(first, last)])


def carried_in(array, axis, join, neutral):
    place = lax.axis_index(axis)
    gathered = jax.tree.map(
        lambda a, kind: lax.all_gather(a.astype(kind), axis),
        array,
        (jnp.bfloat16, jnp.bfloat16, jnp.bfloat16),
    )
    state = jax.tree.map(lambda a, e: jnp.zeros_like(a) + jnp.asarray(e, a.dtype), array, neutral)

    def one(turn, state):
        return join(
            state,
            jax.tree.map(
                lambda a, own: lax.dynamic_index_in_dim(a, turn, 0, False).astype(own.dtype),
                gathered,
                array,
            ),
        )

    return lax.fori_loop(0, place, one, state)


def entering(array, axis, combine, identity):
    count, place = (lax.axis_size(axis), lax.axis_index(axis))
    everything = jax.tree.map(
        lambda part, kind: lax.all_gather(part.astype(kind), axis),
        array,
        jax.tree.map(lambda a: jnp.bfloat16 if a.dtype == jnp.float32 else a.dtype, array),
    )
    start = jax.tree.map(
        lambda part, zero: jnp.broadcast_to(jnp.asarray(zero, part.dtype), part.shape),
        array,
        identity,
    )

    def turn(k, before):
        at = count - 1 - k
        reached = at > place
        new = combine(
            before, jax.tree.map(lambda part, own: part[at].astype(own.dtype), everything, array)
        )
        return jax.tree.map(lambda a, b: jnp.where(reached, a, b), new, before)

    return lax.fori_loop(0, count, turn, start)


def wide_layer_norm(values, scale_vec, shift_vec):
    center = values - jnp.mean(values, axis=-1, keepdims=True)
    inverse = lax.rsqrt(jnp.mean(center * center, axis=-1, keepdims=True) + 1e-05)
    normed = center * inverse
    return (normed * scale_vec + shift_vec, normed, inverse)


def wide_norm_back(upstream, normed, inverse, scale_vec):
    scaled = upstream * scale_vec
    inner = (
        scaled
        - jnp.mean(scaled, axis=-1, keepdims=True)
        - normed * jnp.mean(scaled * normed, axis=-1, keepdims=True)
    )
    return (
        inverse * inner,
        jnp.sum(upstream * normed, axis=(0, 1)),
        jnp.sum(upstream, axis=(0, 1)),
    )


def shift_prev(values, persist_indicator):
    arrived = shifted(values[:, -1:, :], "tensor", 1)
    return jnp.concatenate([arrived, values[:, :-1]], axis=1) * persist_indicator[:, :, None]


def shift_back(upstream, persist_indicator):
    masked = upstream * persist_indicator[:, :, None]
    arrived = shifted(masked[:, :1, :], "tensor", -1)
    return jnp.concatenate([masked[:, 1:], arrived], axis=1)


def project(values, matrix):
    return jnp.einsum("rtd,de->rte", values, matrix, preferred_element_type=jnp.float32)


def project_back(upstream, matrix):
    return jnp.einsum("rte,de->rtd", upstream, matrix, preferred_element_type=jnp.float32)


def outer_sum(values, upstream):
    return jnp.einsum("rtd,rte->de", values, upstream, preferred_element_type=jnp.float32)


def mix_back(upstreams, shares, differ, persist_indicator):
    toward = jnp.zeros_like(differ)
    behind = jnp.zeros_like(differ)
    share_grads = []
    for upstream, share in zip(upstreams, shares):
        toward = toward + upstream * share
        behind = behind + upstream * (1.0 - share)
        share_grads.append(jnp.sum(upstream * differ, axis=(0, 1)))
    return (toward + shift_back(behind, persist_indicator), share_grads)


def chain_combine(earlier, later):
    return (
        earlier[0] * later[0],
        later[0] * earlier[1] + later[1],
        later[0] * earlier[2] + later[2],
    )


def scan_fragments(
    lookup_wide, payload_wide, fading_power, reward_coords, text_boundary_indicators
):
    decay_rate = jnp.exp(fading_power)
    row_count, span_len, width_len = lookup_wide.shape
    block_len = min(32, span_len)
    block_count = span_len // block_len
    places = jnp.arange(block_len, dtype=jnp.float32)
    rising = jnp.exp(places[:, None] * decay_rate)
    falling = jnp.exp(-(places[:, None] - 1.0) * decay_rate)
    trailing = jnp.exp(-(block_len - 1.0 - places)[:, None] * decay_rate)
    leading = jnp.exp(-places[:, None] * decay_rate)
    settle = jnp.exp(-block_len * decay_rate)
    before = places[:, None] > places[None, :]

    def split_blocks(values):
        return jnp.swapaxes(
            values.reshape((row_count, block_count, block_len) + values.shape[2:]), 0, 1
        )

    def advance(state_pair, scanned):
        accrued_dividend_sum, accrued_divisor_sum = state_pair
        lookup_narrow, payload_narrow, reset_b = scanned
        tree_levels = jnp.cumsum(reset_b, axis=1)
        linked = ((tree_levels[:, :, None] == tree_levels[:, None, :]) & before).astype(jnp.float32)
        key_term = jnp.exp(lookup_narrow)
        keyed_value = key_term * payload_narrow
        inside_numerator = falling * jnp.einsum(
            "rti,rid->rtd", linked, rising * keyed_value, precision=lax.Precision.HIGHEST
        )
        interior_divisor_sum = falling * jnp.einsum(
            "rti,rid->rtd", linked, rising * key_term, precision=lax.Precision.HIGHEST
        )
        leftover_multiplier = (tree_levels == 0).astype(jnp.float32)[:, :, None] * leading
        reward_multiplier = jnp.exp(reward_coords + lookup_narrow)
        above_total = (
            inside_numerator
            + reward_multiplier * payload_narrow
            + leftover_multiplier * accrued_dividend_sum[:, None, :]
        )
        below_total = (
            interior_divisor_sum
            + reward_multiplier
            + leftover_multiplier * accrued_divisor_sum[:, None, :]
        )
        ending = (tree_levels == tree_levels[:, -1:]).astype(jnp.float32)[:, :, None] * trailing
        intact = (tree_levels[:, -1] == 0).astype(jnp.float32)[:, None] * settle
        new_num = intact * accrued_dividend_sum + jnp.sum(ending * keyed_value, axis=1)
        new_den = intact * accrued_divisor_sum + jnp.sum(ending * key_term, axis=1)
        return ((new_num, new_den), (above_total, below_total))

    initial = jnp.zeros((row_count, width_len), jnp.float32)
    (total_num, total_den), (uppers, lowers) = lax.scan(
        advance,
        (initial, initial),
        (
            split_blocks(lookup_wide),
            split_blocks(payload_wide),
            split_blocks(text_boundary_indicators),
        ),
    )

    def join_blocks(values):
        return jnp.swapaxes(values, 0, 1).reshape(row_count, span_len, width_len)

    tree_levels = jnp.cumsum(text_boundary_indicators, axis=1)
    reaching = (tree_levels == 0).astype(jnp.float32)[:, :, None] * jnp.exp(
        -jnp.arange(span_len, dtype=jnp.float32)[:, None] * decay_rate
    )
    passing = (tree_levels[:, -1] == 0).astype(jnp.float32)[:, None] * jnp.exp(
        -span_len * decay_rate
    )
    return (join_blocks(uppers), join_blocks(lowers), reaching, total_num, total_den, passing)


def recurrence_finish(pieces_list, incoming_num, incoming_den):
    above_total = pieces_list[0] + pieces_list[2] * incoming_num[:, None, :]
    below_total = pieces_list[1] + pieces_list[2] * incoming_den[:, None, :]
    return (above_total / below_total, below_total)


def ffn_apply(inputs, key_weight, value_weight):
    hidden_pre = project(inputs, key_weight)
    hidden = jnp.square(jax.nn.relu(hidden_pre)).astype(jnp.bfloat16)
    return (hidden_pre, hidden, project(hidden, value_weight))


def ffn_grads(inputs, hidden_pre, hidden, upstream, key_weight, value_weight):
    g_hidden = jnp.einsum("rtd,fd->rtf", upstream, value_weight, preferred_element_type=jnp.float32)
    grad_value = jnp.einsum("rtf,rtd->fd", hidden, upstream, preferred_element_type=jnp.float32)
    g_pre = (2.0 * jax.nn.relu(hidden_pre) * g_hidden).astype(jnp.bfloat16)
    grad_key = jnp.einsum("rtd,rtf->df", inputs, g_pre, preferred_element_type=jnp.float32)
    g_inputs = jnp.einsum("rtf,df->rtd", g_pre, key_weight, preferred_element_type=jnp.float32)
    return (g_inputs, grad_key, grad_value)


def wide_shards(
    incoming_embeddings,
    text_boundary_indicators,
    upstream_sensitivity,
    primary_standardize_scaling,
    primary_standardize_offset,
    secondary_standardize_scaling,
    secondary_standardize_offset,
    feature_fading_logarithms,
    present_symbol_reward,
    timemix_lookup_blend,
    timemix_payload_blend,
    timemix_gate_blend,
    timemix_lookup_proj,
    timemix_payload_proj,
    timemix_gate_proj,
    timemix_emit_proj,
    feedmix_lookup_blend,
    feedmix_gate_blend,
    feedmix_gate_proj,
    feedmix_lookup_proj,
    feedmix_payload_proj,
):
    gathered_portions = (
        lax.all_gather(primary_standardize_scaling, ("dp", "tensor"), axis=0, tiled=True),
        lax.all_gather(primary_standardize_offset, ("dp", "tensor"), axis=0, tiled=True),
        lax.all_gather(secondary_standardize_scaling, ("dp", "tensor"), axis=0, tiled=True),
        lax.all_gather(secondary_standardize_offset, ("dp", "tensor"), axis=0, tiled=True),
        lax.all_gather(feature_fading_logarithms, ("dp", "tensor"), axis=0, tiled=True),
        lax.all_gather(present_symbol_reward, ("dp", "tensor"), axis=0, tiled=True),
        lax.all_gather(timemix_lookup_blend, ("dp", "tensor"), axis=0, tiled=True),
        lax.all_gather(timemix_payload_blend, ("dp", "tensor"), axis=0, tiled=True),
        lax.all_gather(timemix_gate_blend, ("dp", "tensor"), axis=0, tiled=True),
        lax.all_gather(timemix_lookup_proj, ("dp", "tensor"), axis=0, tiled=True),
        lax.all_gather(timemix_payload_proj, ("dp", "tensor"), axis=0, tiled=True),
        lax.all_gather(timemix_gate_proj, ("dp", "tensor"), axis=0, tiled=True),
        lax.all_gather(timemix_emit_proj, ("dp", "tensor"), axis=0, tiled=True),
        lax.all_gather(feedmix_lookup_blend, ("dp", "tensor"), axis=0, tiled=True),
        lax.all_gather(feedmix_gate_blend, ("dp", "tensor"), axis=0, tiled=True),
        lax.all_gather(feedmix_gate_proj, ("dp", "tensor"), axis=0, tiled=True),
    )
    initial_scaling_coords = gathered_portions[0].astype(jnp.float32)
    initial_offset_coords = gathered_portions[1].astype(jnp.float32)
    later_scaling_coords = gathered_portions[2].astype(jnp.float32)
    later_offset_coords = gathered_portions[3].astype(jnp.float32)
    fading_power = gathered_portions[4].astype(jnp.float32)
    reward_coords = gathered_portions[5].astype(jnp.float32)
    share_k1 = gathered_portions[6].astype(jnp.float32)
    share_v1 = gathered_portions[7].astype(jnp.float32)
    share_r1 = gathered_portions[8].astype(jnp.float32)
    lookup_coefficients_initial = gathered_portions[9]
    payload_coefficients_initial = gathered_portions[10]
    gate_coefficients_initial = gathered_portions[11]
    emit_coefficients_initial = gathered_portions[12]
    share_k2 = gathered_portions[13].astype(jnp.float32)
    share_r2 = gathered_portions[14].astype(jnp.float32)
    gate_coefficients_later = gathered_portions[15]
    lookup_coefficients_later, payload_coefficients_later = (
        lax.all_gather(feedmix_lookup_proj, "dp", axis=0, tiled=True),
        lax.all_gather(feedmix_payload_proj, "dp", axis=1, tiled=True),
    )
    persist_indicator = (1 - text_boundary_indicators).astype(jnp.float32)
    inputs = incoming_embeddings.astype(jnp.float32)
    normed_one, unit_one, inverse_one = wide_layer_norm(
        inputs, initial_scaling_coords, initial_offset_coords
    )
    prev_one = shift_prev(normed_one, persist_indicator)
    differ_one = normed_one - prev_one
    in_key = (prev_one + differ_one * share_k1).astype(jnp.bfloat16)
    in_value = (prev_one + differ_one * share_v1).astype(jnp.bfloat16)
    in_recept = (prev_one + differ_one * share_r1).astype(jnp.bfloat16)
    initial_lookup_lines = project(in_key, lookup_coefficients_initial)
    initial_payload_lines = project(in_value, payload_coefficients_initial)
    recept_one = project(in_recept, gate_coefficients_initial)
    pieces_list = scan_fragments(
        initial_lookup_lines,
        initial_payload_lines,
        fading_power,
        reward_coords,
        text_boundary_indicators,
    )
    passing = pieces_list[5]
    identity = (jnp.ones_like(passing), jnp.zeros_like(passing), jnp.zeros_like(passing))
    unused_item, incoming_num, incoming_den = carried_in(
        (passing, pieces_list[3], pieces_list[4]), "tensor", chain_combine, identity
    )
    blended_mean_state, below_total = recurrence_finish(pieces_list, incoming_num, incoming_den)
    sig_one = jax.nn.sigmoid(recept_one)
    mixed_att = (sig_one * blended_mean_state).astype(jnp.bfloat16)
    resid_one = inputs + project(mixed_att, emit_coefficients_initial)
    normed_two, unit_two, inverse_two = wide_layer_norm(
        resid_one, later_scaling_coords, later_offset_coords
    )
    prev_two = shift_prev(normed_two, persist_indicator)
    differ_two = normed_two - prev_two
    in_key_two = (prev_two + differ_two * share_k2).astype(jnp.bfloat16)
    in_recept_two = (prev_two + differ_two * share_r2).astype(jnp.bfloat16)
    recept_two = project(in_recept_two, gate_coefficients_later)
    sig_two = jax.nn.sigmoid(recept_two)
    row_inputs = lax.all_gather(in_key_two, "tensor", axis=1, tiled=True)
    hidden_pre, hidden, partial_value = ffn_apply(
        row_inputs, lookup_coefficients_later, payload_coefficients_later
    )
    value_two = lax.psum_scatter(
        partial_value.astype(jnp.bfloat16), "tensor", scatter_dimension=1, tiled=True
    ).astype(jnp.float32)
    layer_out = (resid_one + sig_two * value_two).astype(jnp.bfloat16)
    upstream = upstream_sensitivity.astype(jnp.float32)
    g_value_two = (upstream * sig_two).astype(jnp.bfloat16)
    g_recept_two = (upstream * value_two * sig_two * (1.0 - sig_two)).astype(jnp.bfloat16)
    grad_recept_two = outer_sum(in_recept_two, g_recept_two)
    g_mix_r2 = project_back(g_recept_two, gate_coefficients_later)
    row_grads = lax.all_gather(g_value_two, "tensor", axis=1, tiled=True)
    partial_grad, grad_key_two, grad_value_two = ffn_grads(
        row_inputs,
        hidden_pre,
        hidden,
        row_grads,
        lookup_coefficients_later,
        payload_coefficients_later,
    )
    g_mix_k2 = lax.psum_scatter(
        partial_grad.astype(jnp.bfloat16), "tensor", scatter_dimension=1, tiled=True
    ).astype(jnp.float32)
    sum_key_two, sum_value_two = (
        lax.psum_scatter(
            grad_key_two.astype(jnp.bfloat16), "dp", scatter_dimension=0, tiled=True
        ).astype(jnp.float32),
        lax.psum_scatter(
            grad_value_two.astype(jnp.bfloat16), "dp", scatter_dimension=1, tiled=True
        ).astype(jnp.float32),
    )
    g_normed_two, shares_two = mix_back(
        (g_mix_k2, g_mix_r2), (share_k2, share_r2), differ_two, persist_indicator
    )
    g_resid_part, grad_gain_two, grad_bias_two = wide_norm_back(
        g_normed_two, unit_two, inverse_two, later_scaling_coords
    )
    g_resid = upstream + g_resid_part
    g_branch = g_resid.astype(jnp.bfloat16)
    grad_out_one = outer_sum(mixed_att, g_branch)
    g_mixed = project_back(g_branch, emit_coefficients_initial)
    g_weighted = g_mixed * sig_one
    g_recept_one = (g_mixed * blended_mean_state * sig_one * (1.0 - sig_one)).astype(jnp.bfloat16)
    reaching = pieces_list[2]
    g_in_num = jnp.sum(g_weighted * reaching / below_total, axis=1)
    g_in_den = -jnp.sum(g_weighted * reaching * blended_mean_state / below_total, axis=1)
    unused_item, back_num, back_den = entering(
        (passing, g_in_num, g_in_den), "tensor", chain_combine, identity
    )
    g_passing = back_num * incoming_num + back_den * incoming_den

    def device_fragment(lookup_wide, payload_wide, fading_coords, reward_power):
        shard_pieces = scan_fragments(
            lookup_wide, payload_wide, fading_coords, reward_power, text_boundary_indicators
        )
        local_out, unused_item = recurrence_finish(shard_pieces, incoming_num, incoming_den)
        return (local_out, shard_pieces[3], shard_pieces[4], shard_pieces[5])

    unused_item, reverse_pass_rule = jax.vjp(
        device_fragment, initial_lookup_lines, initial_payload_lines, fading_power, reward_coords
    )
    derivative_lookup_wide, derivative_payload_wide, fading_derivative, reward_derivative = (
        reverse_pass_rule((g_weighted, back_num, back_den, g_passing))
    )
    g_key_one = derivative_lookup_wide.astype(jnp.bfloat16)
    g_value_one = derivative_payload_wide.astype(jnp.bfloat16)
    grad_key_one = outer_sum(in_key, g_key_one)
    grad_value_one = outer_sum(in_value, g_value_one)
    grad_recept_one = outer_sum(in_recept, g_recept_one)
    g_mix_k1 = project_back(g_key_one, lookup_coefficients_initial)
    g_mix_v1 = project_back(g_value_one, payload_coefficients_initial)
    g_mix_r1 = project_back(g_recept_one, gate_coefficients_initial)
    g_normed_one, shares_one = mix_back(
        (g_mix_k1, g_mix_v1, g_mix_r1),
        (share_k1, share_v1, share_r1),
        differ_one,
        persist_indicator,
    )
    g_input_part, grad_gain_one, grad_bias_one = wide_norm_back(
        g_normed_one, unit_one, inverse_one, initial_scaling_coords
    )
    grad_tokens = g_resid + g_input_part
    summed = (
        lax.psum_scatter(grad_gain_one, ("dp", "tensor"), scatter_dimension=0, tiled=True),
        lax.psum_scatter(grad_bias_one, ("dp", "tensor"), scatter_dimension=0, tiled=True),
        lax.psum_scatter(grad_gain_two, ("dp", "tensor"), scatter_dimension=0, tiled=True),
        lax.psum_scatter(grad_bias_two, ("dp", "tensor"), scatter_dimension=0, tiled=True),
        lax.psum_scatter(fading_derivative, ("dp", "tensor"), scatter_dimension=0, tiled=True),
        lax.psum_scatter(reward_derivative, ("dp", "tensor"), scatter_dimension=0, tiled=True),
        lax.psum_scatter(shares_one[0], ("dp", "tensor"), scatter_dimension=0, tiled=True),
        lax.psum_scatter(shares_one[1], ("dp", "tensor"), scatter_dimension=0, tiled=True),
        lax.psum_scatter(shares_one[2], ("dp", "tensor"), scatter_dimension=0, tiled=True),
        lax.psum_scatter(grad_key_one, ("dp", "tensor"), scatter_dimension=0, tiled=True),
        lax.psum_scatter(grad_value_one, ("dp", "tensor"), scatter_dimension=0, tiled=True),
        lax.psum_scatter(grad_recept_one, ("dp", "tensor"), scatter_dimension=0, tiled=True),
        lax.psum_scatter(grad_out_one, ("dp", "tensor"), scatter_dimension=0, tiled=True),
        lax.psum_scatter(shares_two[0], ("dp", "tensor"), scatter_dimension=0, tiled=True),
        lax.psum_scatter(shares_two[1], ("dp", "tensor"), scatter_dimension=0, tiled=True),
        lax.psum_scatter(grad_recept_two, ("dp", "tensor"), scatter_dimension=0, tiled=True),
    )
    return (
        layer_out,
        grad_tokens,
        summed[0],
        summed[1],
        summed[2],
        summed[3],
        summed[4],
        summed[5],
        summed[6],
        summed[7],
        summed[8],
        summed[9],
        summed[10],
        summed[11],
        summed[12],
        summed[13],
        summed[14],
        summed[15],
        sum_key_two,
        sum_value_two,
    )


def split_columns(w, parts):
    rows, width = w.shape
    return w.reshape(rows, parts, 2, width // (2 * parts)).transpose(2, 0, 1, 3).reshape(2, rows, width // 2)


def join_columns(own, other, c, parts):
    rows, half = own.shape[-2:]
    a = jnp.where(c == 0, own, other).reshape(own.shape[:-1] + (parts, half // parts))
    b = jnp.where(c == 0, other, own).reshape(own.shape[:-1] + (parts, half // parts))
    return jnp.stack([a, b], axis=-2).reshape(own.shape[:-1] + (2 * half,))


def pack(tokens, starts, upstream, gain1, bias1, gain2, bias2, fading, reward, mk1, mv1, mr1, wk, wv, wr, wo, mk2, mr2, wg, fk, fv):
    i, c, count = lax.axis_index("dp"), lax.axis_index("tensor"), lax.axis_size("dp")
    own_rows, width = wk.shape
    half, hidden = width // 2, fk.shape[1]
    by_core = jnp.stack([split_columns(wk, count), split_columns(wv, count), split_columns(wr, count), split_columns(wg, 1)])
    own4 = lax.dynamic_index_in_dim(by_core, c, 1, False)
    other4 = lax.dynamic_index_in_dim(by_core, 1 - c, 1, False)
    emit = wo.reshape(own_rows, 2, half).transpose(1, 0, 2).reshape(1, 2 * own_rows, half)
    key4 = fk.reshape(2 * own_rows, 4, hidden // 4).transpose(1, 0, 2)
    value4 = fv.reshape(4, hidden // 4, 2 * own_rows).transpose(0, 2, 1)
    chunks = {**{p: key4[j] for j, p in enumerate(KEYS)}, **{p: value4[j] for j, p in enumerate(VALUES)}}
    rest = jnp.concatenate([emit, jnp.stack([chunks[p] for p in range(FFN, PIECES)])])
    slots = 128 // own_rows
    everywhere = jnp.stack([gain1, bias1, gain2, bias2, fading, reward, mk1, mv1, mr1, mk2, mr2])
    own = jnp.stack([fading, reward, jnp.zeros_like(fading), jnp.zeros_like(fading), jnp.zeros_like(fading)])
    lane = jnp.arange(128)[None, :] // own_rows
    vec = jnp.concatenate([
        jnp.where(lane == (2 * i + c) % slots, jnp.tile(everywhere, (1, slots)), 0),
        jnp.where(lane == i % slots, jnp.tile(own, (1, slots)), 0),
    ]).astype(BF16)
    keep = jnp.broadcast_to((1 - starts[0]).astype(F32)[:, None], (starts.shape[1], 128))
    return own4, other4, rest, vec, tokens[0], upstream[0], keep


def shards(*args):
    tokens = args[0]
    c = lax.axis_index("tensor")
    i = lax.axis_index("dp")
    count = lax.axis_size("dp")
    own_rows, width = args[12].shape
    hidden = args[19].shape[1]
    half = width // 2
    (
        g, layer_out, x, up, ins, kvr, sn, sd, mixed, resid, ins2, pre, act, g_value, g_recept2, vec, rows, keep,
    ) = forward_call(*pack(*args))

    total, recv4, vsum, vother, grad_tokens = backward_call(
        g, x, up, ins, kvr, sn, sd, mixed, resid, ins2, pre, act, g_value, g_recept2, vec, rows, keep
    )
    slots = 128 // own_rows
    vtotal = lax.dynamic_slice_in_dim(vsum + vother, (2 * i + c) % slots * own_rows, own_rows, 1)
    own_scan = lax.dynamic_slice_in_dim(vsum, i % slots * own_rows, own_rows, 1)
    own = lax.dynamic_slice_in_dim(total[R_GATE2:], c * own_rows, own_rows, 1)
    out_k, out_v, out_r = (join_columns(own[2 + n], recv4[n], c, count) for n in range(3))
    out_g = join_columns(own[0], recv4[3], c, 1)
    out_o = total[R_EMIT].reshape(2, own_rows, half).transpose(1, 0, 2).reshape(own_rows, width)
    out_fk = total[R_KEY : R_KEY + 4].transpose(1, 0, 2).reshape(2 * own_rows, hidden)
    out_fv = total[R_VALUE : R_VALUE + 4].transpose(0, 2, 1).reshape(hidden, 2 * own_rows)
    return (
        layer_out[None], grad_tokens[None], *(vtotal[n] for n in range(4)), own_scan[SUMS], own_scan[SUMS + 1],
        *(vtotal[n] for n in range(6, 9)), out_k, out_v, out_r, out_o, vtotal[9], vtotal[10], out_g, out_fk, out_fv,
    )


def solution(mesh):
    row, vector, matrix_ = P("dp", "tensor", None), P(("dp", "tensor")), P(("dp", "tensor"), None)
    key, value = P("dp", "tensor"), P("tensor", "dp")
    in_specs = (row, P("dp", "tensor"), row) + (vector,) * 9 + (matrix_,) * 4 + (vector,) * 2 + (matrix_, key, value)
    out_specs = (row, row) + (vector,) * 9 + (matrix_,) * 4 + (vector,) * 2 + (matrix_, key, value)
    body = shards if (mesh.shape["dp"], mesh.shape["tensor"]) == (16, 2) else wide_shards
    return jax.shard_map(body, mesh=mesh, in_specs=in_specs, out_specs=out_specs, check_vma=False)
```

```python
import functools

import jax
import jax.numpy as jnp
from jax import lax
from jax.experimental import pallas as pl
from jax.experimental.pallas import tpu as pltpu
from jax.sharding import PartitionSpec as P

F32, BF16 = jnp.float32, jnp.bfloat16
MESH_ID = pl.DeviceIdType.MESH
MIB = 1 << 20
PARTS = 10
PIECES = 13


def place():
    i, c = lax.axis_index("dp"), lax.axis_index("tensor")
    return i // 4, i % 4, c


def neighbours(z, yx):
    x = yx + 1 - 2 * (yx % 2)
    y = (yx + 2) % 4
    d = (x + 2) % 4
    zs = (z + 1 - 2 * (z % 2), (z + 2) % 4, 3 - z)
    return x, y, d, zs


def enter(z, yx, c):
    x, y, d, zs = neighbours(z, yx)
    barrier = pltpu.get_barrier_semaphore()
    targets = [(z * 4 + yx, 1 - c), (z * 4 + x, c), (z * 4 + y, c)]
    targets += [(peer * 4 + yx, c) for peer in zs]
    for target in targets:
        pl.semaphore_signal(barrier, inc=1, device_id=target, device_id_type=MESH_ID)
    pl.semaphore_wait(barrier, len(targets))


def remote(src, dst, send, recv, target):
    return pltpu.make_async_remote_copy(
        src_ref=src, dst_ref=dst, send_sem=send, recv_sem=recv,
        device_id=target, device_id_type=MESH_ID,
    )


def strip(i, size):
    return pl.ds(pl.multiple_of(i * size, size), size)


class Gather:
    def __init__(self, view, sends, recvs, first=0):
        self.view, self.sends, self.recvs, self.first = view, sends, recvs, first
        self.z, self.yx, self.c = place()
        self.x, self.y, self.d, self.zs = neighbours(self.z, self.yx)

    def to(self, z, yx):
        return (z * 4 + yx, self.c)

    def copy(self, p, k, ref, target):
        return remote(ref, ref, self.sends.at[p, k], self.recvs.at[p, k], target)

    def along(self, p):
        own = self.view(p).at[self.z, self.yx]
        return [self.copy(p, k, own, self.to(peer, self.yx)) for k, peer in enumerate(self.zs)]

    def plane(self, p):
        own = self.view(p).at[:, self.yx]
        return [self.copy(p, 3, own, self.to(self.z, self.x)), self.copy(p, 4, own, self.to(self.z, self.y))]

    def onward(self, p):
        return [
            self.copy(p, 5, self.view(p).at[0:2, self.x], self.to(self.z, self.y)),
            self.copy(p, 6, self.view(p).at[2:4, self.y], self.to(self.z, self.x)),
        ]

    def start(self, copies):
        for copy in copies:
            copy.start()

    def arrive(self, copies):
        for copy in copies:
            copy.wait_recv()

    def step(self, p):
        self.arrive(self.along(p))
        self.start(self.plane(p))

    def forward(self, p):
        self.arrive(self.plane(p))
        self.start(self.onward(p))

    def finish(self, p):
        for copy in self.along(p) + self.plane(p) + self.onward(p):
            copy.wait_send()


class GatherLine(Gather):
    def ring(self, p):
        own = self.view(p).at[self.z, self.yx]
        return [self.copy(p, 0, own, self.to(self.z, self.x)), self.copy(p, 1, own, self.to(self.z, self.y))]

    def onward(self, p):
        half = self.view(p).shape[2] // 2
        return [
            self.copy(p, 2, self.view(p).at[self.z, self.x, 0:half], self.to(self.z, self.y)),
            self.copy(p, 3, self.view(p).at[self.z, self.y, half:], self.to(self.z, self.x)),
        ]

    def climb(self, p, k, up, arriving):
        behind = k if arriving else k - 1
        plane = self.z - behind if up else self.z + behind
        beyond = self.z + 1 if up != arriving else self.z - 1
        real = (plane >= 0) & (plane <= 3) & (beyond >= 0) & (beyond <= 3)
        plane, beyond = jnp.clip(plane, 0, 3), jnp.clip(beyond, 0, 3)
        k = (4 if up else 7) + k - 1
        return real, self.copy(p, k, self.view(p).at[plane], self.to(beyond, self.yx))

    def each(self, p, k, arriving, action):
        for up in (True, False):
            real, copy = self.climb(p, k, up, arriving)
            pl.when(real)(functools.partial(action, copy))

    def line(self, p, k):
        if k > 1:
            self.each(p, k - 1, True, lambda copy: copy.wait_recv())
        self.each(p, k, False, lambda copy: copy.start())

    def ready(self, p):
        self.each(p, 3, True, lambda copy: copy.wait_recv())

    def finish(self, p):
        for copy in self.ring(p) + self.onward(p):
            copy.wait_send()
        for k in (1, 2, 3):
            self.each(p, k, False, lambda copy: copy.wait_send())


class Reduce:
    def __init__(self, part, slot, ring1, ring2, line, out, sends, recvs):
        self.parts, self.slot, self.ring1, self.ring2, self.line, self.out = part, slot, ring1, ring2, line, out
        self.sends, self.recvs = sends, recvs
        self.z, self.yx, self.c = place()
        self.x, self.y, self.d, self.zs = neighbours(self.z, self.yx)

    def copy(self, k, src, dst, z, yx):
        return remote(src, dst, self.sends.at[k], self.recvs.at[k], (z * 4 + yx, self.c))

    def part(self):
        return self.parts.at[self.slot]

    def diagonal(self):
        return [
            self.copy(0, self.part().at[0:2, self.d], self.ring1.at[0], self.z, self.x),
            self.copy(1, self.part().at[2:4, self.d], self.ring1.at[1], self.z, self.y),
        ]

    def side(self):
        return [
            self.copy(2, self.part().at[:, self.x], self.ring2.at[0], self.z, self.x),
            self.copy(3, self.part().at[:, self.y], self.ring2.at[1], self.z, self.y),
        ]

    def down(self):
        return [
            self.copy(4 + k, self.part().at[peer, self.yx], self.line.at[k], peer, self.yx)
            for k, peer in enumerate(self.zs)
        ]

    def start(self, copies):
        for copy in copies:
            copy.start()

    def arrive(self, copies):
        for copy in copies:
            copy.wait_recv()

    def add_up(self, own, others, result):
        def step(i, carry):
            at = strip(i, 16)
            total = own[at, :].astype(F32)
            for other in others:
                total = total + other[at, :].astype(F32)
            result[at, :] = total.astype(result.dtype)
            return carry

        lax.fori_loop(0, own.shape[0] // 16, step, 0)

    def add(self, a, yx, others):
        own = self.part().at[a, yx]
        self.add_up(own, others, own)

    def stage1(self):
        self.start(self.diagonal())

    def stage2(self):
        self.arrive(self.diagonal())

        def planes(a, carry):
            self.add(a, self.y, [self.ring1.at[0, a]])
            self.add(a + 2, self.x, [self.ring1.at[1, a]])
            return carry

        lax.fori_loop(0, 2, planes, 0)
        self.start(self.side())

    def stage3(self):
        self.arrive(self.side())

        def planes(a, carry):
            self.add(a, self.yx, [self.ring2.at[0, a], self.ring2.at[1, a]])
            return carry

        lax.fori_loop(0, 4, planes, 0)
        self.start(self.down())

    def stage4(self):
        self.arrive(self.down())
        self.add_up(self.part().at[self.z, self.yx], [self.line.at[k] for k in range(3)], self.out)

    def finish(self):
        for copy in self.diagonal() + self.side() + self.down():
            copy.wait_send()


class ReduceLine(Reduce):
    def step(self, k, up, arriving):
        z = self.z
        plane = (3 if arriving else 4) - k + z if up else k - (3 if arriving else 4) + z
        beyond = z + 1 if up != arriving else z - 1
        real = (plane >= 0) & (plane <= 3) & (beyond >= 0) & (beyond <= 3)
        plane, beyond = jnp.clip(plane, 0, 3), jnp.clip(beyond, 0, 3)
        place_in = plane + 1 if up else plane
        k = (3 if up else 0) + k - 1
        return real, plane, place_in, self.copy(k, self.part().at[plane], self.line.at[place_in], beyond, self.yx)

    def take(self, arrived, plane, place_in):
        arrived.wait_recv()

        def blocks(yx, carry):
            self.add(plane, yx, [self.line.at[place_in, yx]])
            return carry

        lax.fori_loop(0, 4, blocks, 0)

    def move(self, k):
        for up in (True, False):
            real, plane, _, leaving = self.step(k, up, False)
            if k > 1:
                came, _, place_in, arrived = self.step(k - 1, up, True)

                pl.when(real & came)(functools.partial(self.take, arrived, plane, place_in))

            pl.when(real)(leaving.start)

    def halves(self):
        half = self.ring1.shape[1]
        own = self.part().at[self.z, self.d]
        return [
            self.copy(6, own.at[0:half], self.ring1.at[0], self.z, self.x),
            self.copy(7, own.at[half:], self.ring1.at[1], self.z, self.y),
        ]

    def sides(self):
        return [
            self.copy(8, self.part().at[self.z, self.x], self.ring2.at[0], self.z, self.x),
            self.copy(9, self.part().at[self.z, self.y], self.ring2.at[1], self.z, self.y),
        ]

    def stage1(self):
        self.move(1)

    def stage2(self):
        self.move(2)

    def stage3(self):
        self.move(3)

    def stage4(self):
        for up in (True, False):
            came, plane, place_in, arrived = self.step(3, up, True)
            pl.when(came)(functools.partial(self.take, arrived, plane, place_in))

        self.start(self.halves())

    def stage5(self):
        self.arrive(self.halves())
        half = self.ring1.shape[1]
        for yx, start, piece in ((self.y, 0, 0), (self.x, half, 1)):
            own = self.part().at[self.z, yx, start : start + half]
            self.add_up(own, [self.ring1.at[piece]], own)
        self.start(self.sides())

    def stage6(self):
        self.arrive(self.sides())
        self.add_up(self.part().at[self.z, self.yx], [self.ring2.at[0], self.ring2.at[1]], self.out)

    def finish(self):
        for k in (1, 2, 3):
            for up in (True, False):
                real, _, _, leaving = self.step(k, up, False)
                pl.when(real)(leaving.wait_send)
        for copy in self.halves() + self.sides():
            copy.wait_send()


def lanes(j):
    return slice(j * 128, (j + 1) * 128)


def bottom(v):
    return jnp.broadcast_to(v[7:8], v.shape)


def top(v):
    return jnp.broadcast_to(v[0:1], v.shape)


def masks_down(keep, place_in):
    m1 = jnp.where(place_in >= 1, keep, 0.0)
    m2 = m1 * pltpu.roll(m1, 1, 0)
    m4 = m2 * pltpu.roll(m2, 2, 0)
    for n in (1, 2, 4):
        keep = keep * jnp.where(place_in >= n, pltpu.roll(keep, n, 0), 1.0)
    return m1, m2, m4, keep


def masks_up(after, place_in):
    m1 = jnp.where(place_in <= 6, after, 0.0)
    m2 = m1 * pltpu.roll(m1, 7, 0)
    m4 = m2 * pltpu.roll(m2, 6, 0)
    for n in (1, 2, 4):
        after = after * jnp.where(place_in <= 7 - n, pltpu.roll(after, 8 - n, 0), 1.0)
    return m1, m2, m4, after


def wkv_forward(k_ref, v_ref, r_ref, keep_ref, rows_ref, mixed_ref, sn_ref, sd_ref):
    length, width = k_ref.shape
    tiles = width // 128
    place_in = lax.broadcasted_iota(jnp.int32, (8, 128), 0)
    first = place_in == 0
    zero = jnp.zeros((8, 128), F32)

    def pair(g, carry):
        carry = list(carry)
        base = pl.multiple_of(g * 16, 16)
        keeps = [keep_ref[pl.ds(base + 8 * h, 8), :] for h in range(2)]
        masks = [masks_down(keep, place_in) for keep in keeps]
        for j in range(tiles):
            d1, d2, d4, eu = (rows_ref[n : n + 1, lanes(j)] for n in range(4))
            dp = rows_ref[8:16, lanes(j)]
            made = []
            for h in range(2):
                at = pl.ds(base + 8 * h, 8)
                keep, (m1, m2, m4, mp) = keeps[h], masks[h]
                ek = jnp.exp(k_ref[at, lanes(j)])
                v = v_ref[at, lanes(j)]
                num, den = ek * v, ek
                x, b = num, eu * ek
                for n, coef in ((1, m1 * d1), (2, m2 * d2), (4, m4 * d4)):
                    num = num + coef * pltpu.roll(num, n, 0)
                    den = den + coef * pltpu.roll(den, n, 0)
                coef = mp * dp
                cn, cd = carry[2 * j], carry[2 * j + 1]
                num = num + coef * cn
                den = den + coef * cd
                sn = keep * jnp.where(first, cn, pltpu.roll(num, 1, 0))
                sd = keep * jnp.where(first, cd, pltpu.roll(den, 1, 0))
                carry[2 * j], carry[2 * j + 1] = bottom(num), bottom(den)
                sn_ref[at, lanes(j)] = sn
                sd_ref[at, lanes(j)] = sd
                weighted = (sn + eu * x) / (sd + b)
                made.append(jax.nn.sigmoid(r_ref[at, lanes(j)]) * weighted)
            mixed_ref[pl.ds(base, 16), lanes(j)] = jnp.concatenate(made, axis=0).astype(BF16)
        return tuple(carry)

    lax.fori_loop(0, length // 16, pair, (zero,) * (2 * tiles))


def wkv_backward(
    g_ref, k_ref, v_ref, r_ref, sn_ref, sd_ref, keep_ref, rows_ref, gk_ref, gv_ref, gr_ref, begin, end, carry
):
    length, width = k_ref.shape
    tiles = width // 128
    place_in = lax.broadcasted_iota(jnp.int32, (8, 128), 0)
    last = place_in == 7
    zero = jnp.zeros((8, 128), F32)
    pairs = length // 16

    def pair(step, carry):
        carry = list(carry)
        base = pl.multiple_of((pairs - 1 - step) * 16, 16)
        low, high = (keep_ref[pl.ds(base + 8 * h, 8), :] for h in range(2))
        afters = [
            jnp.where(last, top(high), pltpu.roll(low, 7, 0)),
            jnp.where(last, carry[4 * tiles], pltpu.roll(high, 7, 0)),
        ]
        masks = [masks_up(after, place_in) for after in afters]
        carry[4 * tiles] = top(low)
        for j in range(tiles):
            d1, d2, d4, eu = (rows_ref[n : n + 1, lanes(j)] for n in range(4))
            dp = rows_ref[16:24, lanes(j)]
            made = [None, None]
            for h in (1, 0):
                at = pl.ds(base + 8 * h, 8)
                after, (m1, m2, m4, mp) = afters[h], masks[h]
                ek = jnp.exp(k_ref[at, lanes(j)])
                v = v_ref[at, lanes(j)]
                sn, sd = sn_ref[at, lanes(j)], sd_ref[at, lanes(j)]
                s = jax.nn.sigmoid(r_ref[at, lanes(j)])
                b = eu * ek
                inverse = 1.0 / (sd + b)
                weighted = (sn + b * v) * inverse
                g = g_ref[at, lanes(j)]
                gs = g * s
                p = gs * inverse
                q = -p * weighted
                gr = gs * weighted * (1.0 - s)
                hp, hq = p, q
                for n, coef in ((1, m1 * d1), (2, m2 * d2), (4, m4 * d4)):
                    hp = hp + coef * pltpu.roll(hp, 8 - n, 0)
                    hq = hq + coef * pltpu.roll(hq, 8 - n, 0)
                coef = mp * dp
                cp, cq = carry[4 * j], carry[4 * j + 1]
                hp = hp + coef * cp
                hq = hq + coef * cq
                ap = after * jnp.where(last, cp, pltpu.roll(hp, 7, 0))
                aq = after * jnp.where(last, cq, pltpu.roll(hq, 7, 0))
                carry[4 * j], carry[4 * j + 1] = top(hp), top(hq)
                bonus = b * (v * p + q)
                gv = ek * ap + b * p
                gk = ek * (v * ap + aq) + bonus
                carry[4 * j + 2] = carry[4 * j + 2] + bonus
                carry[4 * j + 3] = carry[4 * j + 3] + (ap * sn + aq * sd)
                made[h] = (gk, gv, gr)
            both = pl.ds(base, 16)
            for n, ref in enumerate((gk_ref, gv_ref, gr_ref)):
                ref[both, lanes(j)] = jnp.concatenate([made[0][n], made[1][n]], axis=0).astype(BF16)
        return tuple(carry)

    return lax.fori_loop(begin, end, pair, (zero,) * (4 * tiles + 1) if carry is None else carry)


def wkv_sums(carry, rows_ref, decay_ref, bonus_ref):
    for j in range(decay_ref.shape[1] // 128):
        bonus_ref[0:1, lanes(j)] = jnp.sum(carry[4 * j + 2], axis=0, keepdims=True)
        decay_ref[0:1, lanes(j)] = -rows_ref[4:5, lanes(j)] * jnp.sum(carry[4 * j + 3], axis=0, keepdims=True)


NN, NT, TN = ((1,), (0,)), ((1,), (1,)), ((0,), (0,))
KEY, VALUE, GATE, EMIT, GATE2, FFN = 0, 1, 2, 3, 4, 5
KEYS, VALUES = (5, 7, 9, 11), (6, 8, 10, 12)
RINGS = 11
VECTORS = 11
TILE = 64
GAIN1, BIAS1, GAIN2, BIAS2, FADE, REWARD, MK1, MV1, MR1, MK2, MR2, OWN_FADE, OWN_REWARD = range(13)


def dot(a, b, dims):
    return lax.dot_general(a, b, (dims, ((), ())), preferred_element_type=F32)


def over_rows(length, size, body):
    def step(i, carry):
        body(strip(i, size))
        return carry

    lax.fori_loop(0, length // size, step, 0)


def matrix(ref):
    return ref[...].reshape(16 * ref.shape[2], ref.shape[3])


def emit_half(ref, h):
    rows = ref.shape[2] // 2
    return ref[:, :, h * rows : (h + 1) * rows, :].reshape(16 * rows, ref.shape[3])


def wide(column, width):
    return jnp.concatenate([column] * (width // 128), axis=1)


def norm(x):
    center = x - jnp.mean(x, axis=-1, keepdims=True)
    inverse = lax.rsqrt(jnp.mean(center * center, axis=-1, keepdims=True) + 1e-05)
    return center * inverse, inverse


def norm_and_mix(length, width, load, gain, bias, keep_ref, mixes, outs):
    first = lax.broadcasted_iota(jnp.int32, (TILE, width), 0) == 0

    def step(i, before):
        at = strip(i, TILE)
        unit, _ = norm(load(at))
        normed = unit * gain + bias
        prev = jnp.where(first, before, pltpu.roll(normed, 1, 0)) * wide(keep_ref[at, :], width)
        differ = normed - prev
        for share, out in zip(mixes, outs):
            out[at, :] = (prev + differ * share).astype(BF16)
        return normed[TILE - 1 : TILE]

    lax.fori_loop(0, length // TILE, step, jnp.zeros((1, width), F32))


def forward_kernel(
    own4, other4, rest, vec, x_own, up_own, keep_own,
    g_out, out, x_out, up_out, ins_out, kvr_out, sn_out, sd_out, mixed_out, resid_out, ins2_out, pre_out, act_out,
    gv_out, gr_out, vec_out, rows_out, keep_out,
    gv, g, x, up, ins, kvr, sn, sd, mixed, sum_own, sum_other, resid, ins2, pre, act, v_send, v_other, gval, grec, low_half,
    local_sem, ex_send, ex_recv, sends, recvs, lsends, lrecvs, vsends, vrecvs, out_sem, sum_send, sum_recv, val_send, val_recv,
):
    z, yx, c = place()
    length, width = x.shape
    half = width // 2
    span = length // 2
    partner = (z * 4 + yx, 1 - c)
    enter(z, yx, c)

    block = own4.shape[1]
    mine = strip(c, block)
    rows_mine = strip(c, span)
    swaps = [
        (vec, gv.at[z, yx, c]),
        (other4.at[0:3], g.at[0:3, z, yx, mine]),
        (other4.at[3], g.at[GATE2, z, yx, mine]),
        (x_own, x.at[rows_mine]),
        (keep_own, keep_out.at[rows_mine]),
        (up_own, up.at[rows_mine]),
    ]
    swaps = [remote(a, b, ex_send.at[n], ex_recv.at[n], partner) for n, (a, b) in enumerate(swaps)]
    keeps = [
        (vec, gv.at[z, yx, c]),
        (own4.at[0:3], g.at[0:3, z, yx, mine]),
        (own4.at[3], g.at[GATE2, z, yx, mine]),
        (x_own, x.at[rows_mine]),
        (keep_own, keep_out.at[rows_mine]),
        (up_own, up.at[rows_mine]),
        (rest.at[0], g.at[EMIT, z, yx]),
        (rest.at[1:9], g.at[FFN : FFN + 8, z, yx]),
    ]
    keeps = [pltpu.make_async_copy(a, b, local_sem.at[n]) for n, (a, b) in enumerate(keeps)]
    for copy in swaps + keeps:
        copy.start()
    weights = Gather(lambda p: g.at[p], sends, recvs)
    lines = GatherLine(lambda p: g.at[RINGS + p], lsends, lrecvs)
    vectors = Gather(lambda p: gv, vsends, vrecvs)

    outs = []

    def put(src, dst):
        copy = pltpu.make_async_copy(src, dst, out_sem.at[len(outs)])
        copy.start()
        outs.append(copy)
        return copy

    along_z = {4: [(0, 1)], 5: [(1, 1)], 6: [(0, 2)], 7: [(1, 2)], 8: [(0, 3)], 9: [(1, 3)]}

    def turn(n):
        if n < RINGS:
            weights.step(n)
            if n + 2 < RINGS:
                weights.start(weights.along(n + 2))
        if 1 <= n <= RINGS:
            weights.forward(n - 1)
        for p, k in along_z.get(n, []):
            lines.line(p, k)
        if n >= 2:
            weights.arrive(weights.onward(n - 2))
            put(g.at[n - 2], g_out.at[n - 2])

    def lined(p):
        lines.ready(p - RINGS)
        put(g.at[p], g_out.at[p])

    for copy in keeps[6:]:
        copy.wait()
    for p in range(PIECES - RINGS):
        lines.start(lines.ring(p))
    for n in (0, 1, 2):
        swaps[n].wait()
        keeps[n].wait()
    vectors.start(vectors.along(0))
    weights.start(weights.along(0))
    weights.start(weights.along(1))
    for p in range(PIECES - RINGS):
        lines.arrive(lines.ring(p))
        lines.start(lines.onward(p))
    vectors.step(0)
    turn(0)
    vectors.forward(0)
    for n in (3, 4, 5):
        swaps[n].wait()
        keeps[n].wait()
    x_copy, up_copy = put(x, x_out), put(up, up_out)
    for p in range(PIECES - RINGS):
        lines.arrive(lines.onward(p))
    turn(1)
    vectors.arrive(vectors.onward(0))

    for t in range(width // 128):
        parts = [gv[(2 * t + k) // 4, (2 * t + k) % 4, core].astype(F32) for k in range(2) for core in range(2)]
        vec_out[:, lanes(t)] = functools.reduce(lambda a, b: a + b, parts)
    ramp = lax.broadcasted_iota(jnp.int32, (8, 128), 0).astype(F32)
    for t in range(half // 128):
        own = functools.reduce(lambda a, b: a + b, [gv[t, k, c].astype(F32) for k in range(4)])
        rate = jnp.exp(own[OWN_FADE : OWN_FADE + 1])
        head = [
            jnp.exp(-rate), jnp.exp(-2.0 * rate), jnp.exp(-4.0 * rate), jnp.exp(own[OWN_REWARD : OWN_REWARD + 1]),
            rate * jnp.exp(-rate),
        ]
        for n, row in enumerate(head):
            rows_out[n : n + 1, lanes(t)] = row
        rows_out[8:16, lanes(t)] = jnp.exp(-(ramp + 1.0) * rate)
        rows_out[16:24, lanes(t)] = jnp.exp(-(8.0 - ramp) * rate)

    def row(n):
        return vec_out[n : n + 1, :]

    norm_and_mix(
        length, width, lambda at: x[at, :].astype(F32), row(GAIN1), row(BIAS1), keep_out,
        [row(MK1), row(MV1), row(MR1)], [ins.at[n] for n in range(3)],
    )
    put(ins, ins_out)
    kvr_copies = []
    for n in range(3):
        turn(n + 2)
        weight = g.at[n]

        def project(at):
            kvr[n, at, :] = dot(ins[n, at, :], matrix(weight), NN)

        over_rows(length, 256, project)
        kvr_copies.append(put(kvr.at[n], kvr_out.at[n]))
    wkv_forward(kvr.at[0], kvr.at[1], kvr.at[2], keep_out, rows_out, mixed, sn, sd)
    put(mixed, mixed_out)
    put(sn, sn_out)
    put(sd, sd_out)
    turn(5)
    weight = g.at[EMIT]
    quarters = length // 4

    def emitted(n):
        at = strip(n, quarters)
        return remote(sum_own.at[at], sum_other.at[at], sum_send.at[n], sum_recv.at[n], partner)

    def emit(n, carry):
        at = strip(n, quarters)
        for h in range(2):
            sum_own[at, h * half : (h + 1) * half] = dot(mixed[at, :], emit_half(weight, h), NN).astype(BF16)
        emitted(n).start()
        return carry

    lax.fori_loop(0, 4, emit, 0)
    turn(6)
    for n in range(4):
        emitted(n).wait()

    def add_up(at):
        total = x[at, :].astype(F32) + (sum_own[at, :].astype(F32) + sum_other[at, :].astype(F32))
        resid[0, at, :] = total[:, :half]
        resid[1, at, :] = total[:, half:]
        return total

    norm_and_mix(
        length, width, add_up, row(GAIN2), row(BIAS2), keep_out, [row(MK2), row(MR2)], [ins2.at[n] for n in range(2)]
    )
    put(resid, resid_out)
    put(ins2, ins2_out)
    for copy in kvr_copies:
        copy.wait()
    weight = g.at[GATE2]

    def gate(at):
        kvr[2, at, :] = jax.nn.sigmoid(dot(ins2[1, at, :], matrix(weight), NN))

    over_rows(length, 256, gate)
    pre_copies = []

    def expand_chunk(j):
        weight, slot = g.at[KEYS[j]], len(pre_copies) % 2
        if len(pre_copies) >= 2:
            pre_copies[-2].wait()

        def expand(at):
            positive = jnp.maximum(dot(ins2[0, at, :], matrix(weight), NN), 0.0)
            pre[slot, at, :] = positive.astype(BF16)
            act[j, at, :] = (positive * positive).astype(BF16)

        over_rows(length, 256, expand)
        pre_copies.append(put(pre.at[slot], pre_out.at[j]))
        put(act.at[j], act_out.at[j])

    def contract_chunk(j):
        weight = g.at[VALUES[j]]

        def contract(at):
            for h in range(2):
                part = dot(act[j, at, :], weight[2 * h : 2 * h + 2].reshape(half, -1), NT)
                kvr[h, at, :] = part if j == 0 else kvr[h, at, :] + part

        over_rows(length, 256, contract)

    turn(7)
    expand_chunk(0)
    turn(8)
    contract_chunk(0)
    turn(9)
    expand_chunk(1)
    turn(10)
    contract_chunk(1)
    lined(KEYS[3])
    expand_chunk(3)
    lined(VALUES[3])
    contract_chunk(3)
    turn(11)
    expand_chunk(2)
    turn(12)
    contract_chunk(2)

    columns = strip(c, half)

    def value_copy(n):
        at = strip(n, quarters)
        return remote(v_send.at[at], v_other.at[at], val_send.at[n], val_recv.at[n], partner)

    def back_copy(n):
        at = strip(n, quarters)
        return remote(gval.at[c, at], gval.at[c, at], val_send.at[4 + n], val_recv.at[4 + n], partner)

    def send_values(n, carry):
        def narrow(i, carry):
            at = strip(n * (quarters // 32) + i, 32)
            v_send[at, :] = kvr[1 - c, at, :].astype(BF16)
            return carry

        lax.fori_loop(0, quarters // 32, narrow, 0)
        value_copy(n).start()
        return carry

    def finish_values(n, carry):
        value_copy(n).wait()

        def finish(i, carry):
            at = strip(n * (quarters // 32) + i, 32)
            value = kvr[c, at, :] + v_other[at, :].astype(F32)
            s = kvr[2, at, :]
            low_half[at, :] = (resid[c, at, :] + s * value).astype(BF16)
            upstream = up[at, columns].astype(F32)
            gval[c, at, :] = (upstream * s).astype(BF16)
            grec[at, :] = (upstream * value * s * (1.0 - s)).astype(BF16)
            return carry

        lax.fori_loop(0, quarters // 32, finish, 0)
        back_copy(n).start()
        return carry

    lax.fori_loop(0, 4, send_values, 0)
    lax.fori_loop(0, 4, finish_values, 0)
    give = remote(low_half.at[strip(1 - c, span)], out.at[:, columns], val_send.at[8], val_recv.at[8], partner)
    give.start()
    put(low_half.at[rows_mine], out.at[:, columns])
    put(grec, gr_out)
    for n in range(4):
        back_copy(n).wait()
    put(gval, gv_out)
    give.wait()

    def close(p, carry):
        weights.finish(p)
        return carry

    lax.fori_loop(0, RINGS, close, 0)
    for p in range(PIECES - RINGS):
        lines.finish(p)
    vectors.finish(0)
    waited = kvr_copies + pre_copies[:2]
    for copy in outs:
        if not any(copy is other for other in waited):
            copy.wait()


def forward_call(own4, other4, rest, vec, x_own, up_own, keep_own):
    span, width = x_own.shape
    length, half = 2 * span, width // 2
    block = rest.shape[1:]
    any_, vmem = pl.BlockSpec(memory_space=pl.ANY), pl.BlockSpec(memory_space=pltpu.VMEM)
    full, col = (length, width), (length, half)

    def shape(dims, kind):
        return jax.ShapeDtypeStruct(dims, kind)

    outs = (
        (shape((PIECES, 4, 4) + block, BF16), any_),
        (shape((span, width), BF16), any_),
        (shape(full, BF16), any_),
        (shape(full, BF16), any_),
        (shape((3,) + full, BF16), any_),
        (shape((3,) + col, F32), any_),
        (shape(col, F32), any_),
        (shape(col, F32), any_),
        (shape(col, BF16), any_),
        (shape((2,) + col, F32), any_),
        (shape((2,) + full, BF16), any_),
        (shape((4,) + col, BF16), any_),
        (shape((4,) + col, BF16), any_),
        (shape((2,) + col, BF16), any_),
        (shape(col, BF16), any_),
        (shape((16, width), F32), vmem),
        (shape((24, half), F32), vmem),
        (shape((length, 128), F32), vmem),
    )
    dma = pltpu.SemaphoreType.DMA
    return pl.pallas_call(
        forward_kernel,
        out_shape=tuple(o[0] for o in outs),
        in_specs=[vmem] * 7,
        out_specs=tuple(o[1] for o in outs),
        scratch_shapes=[
            pltpu.VMEM((4, 4, 2) + vec.shape, BF16),
            pltpu.VMEM((PIECES, 4, 4) + block, BF16),
            pltpu.VMEM(full, BF16),
            pltpu.VMEM(full, BF16),
            pltpu.VMEM((3,) + full, BF16),
            pltpu.VMEM((3,) + col, F32),
            pltpu.VMEM(col, F32),
            pltpu.VMEM(col, F32),
            pltpu.VMEM(col, BF16),
            pltpu.VMEM(full, BF16),
            pltpu.VMEM(full, BF16),
            pltpu.VMEM((2,) + col, F32),
            pltpu.VMEM((2,) + full, BF16),
            pltpu.VMEM((2,) + col, BF16),
            pltpu.VMEM((4,) + col, BF16),
            pltpu.VMEM(col, BF16),
            pltpu.VMEM(col, BF16),
            pltpu.VMEM((2,) + col, BF16),
            pltpu.VMEM(col, BF16),
            pltpu.VMEM(col, BF16),
            dma((8,)), dma((6,)), dma((6,)),
            dma((RINGS, 7)), dma((RINGS, 7)), dma((PIECES - RINGS, 10)), dma((PIECES - RINGS, 10)), dma((1, 7)), dma((1, 7)),
            dma((40,)), dma((4,)), dma((4,)), dma((9,)), dma((9,)),
        ],
        compiler_params=pltpu.CompilerParams(
            collective_id=0, has_side_effects=True, vmem_limit_bytes=63 * MIB
        ),
        name="forward",
    )(own4, other4, rest, vec, x_own, up_own, keep_own)


R_VALUE, R_KEY, R_GATE2, R_EMIT, R_TIME = 0, 4, 8, 9, 10
WEIGHT_ORDER = [p for j in range(4) for p in (VALUES[j], KEYS[j])] + [GATE2, EMIT, KEY, VALUE, GATE]
LINED = (1, 3, 5)
SUMS = 11
S_GAIN1, S_BIAS1, S_GAIN2, S_BIAS2, S_DECAY, S_BONUS, S_MK1, S_MV1, S_MR1, S_MK2, S_MR2 = range(11)
SLOTS = 12


def whole(ref, at):
    return jnp.concatenate([ref[0, at, :], ref[1, at, :]], axis=1)


def halves(ref, at, value):
    half = value.shape[1] // 2
    ref[0, at, :] = value[:, :half].astype(ref.dtype)
    ref[1, at, :] = value[:, half:].astype(ref.dtype)


def fold(value):
    return sum(value[n : n + 8] for n in range(8, value.shape[0], 8)) + value[:8]


def back_through_norm(g, unit, inverse, gain):
    q = g * gain
    return inverse * (
        q - jnp.mean(q, axis=-1, keepdims=True) - unit * jnp.mean(q * unit, axis=-1, keepdims=True)
    )


def lifted(now, following, last):
    return jnp.where(last, following[0:1], pltpu.roll(now, now.shape[0] - 1, 0))


def backward_kernel(
    plan,
    g, x_in, up_in, ins_in, kvr_in, sn_in, sd_in, mixed_in, resid_in, ins2_in, pre_in, act_in, gv_in, gr_in,
    vec, rows, keep,
    out, recv4, vsum, vother, gtok,
    part, ring1, ring2, line, lring1, lring2, lline, vpart, vring1, vring2, vline,
    b, w, f, resid, sum_other, n1_other, acc, own_sums,
    load_sem, w_sem, sends, recvs, lsends, lrecvs, vsends, vrecvs, ex_send, ex_recv, sum_send, sum_recv,
):
    z, yx, c = place()
    nx, ny, nd, zs = neighbours(z, yx)
    length, half = b.shape[1:]
    width = 2 * half
    span = length // 2
    quarter = length // 4
    partner = (z * 4 + yx, 1 - c)
    loads = {}

    def load(name, src, dst):
        copy = pltpu.make_async_copy(src, dst, load_sem.at[len(loads)])
        copy.start()
        loads[name] = copy

    def loaded(*names):
        for name in names:
            loads[name].wait()

    def pair(n):
        return b.at[n : n + 2]

    def load_pair(name, src, n):
        for h in range(2):
            load((name, h), src.at[:, h * half : (h + 1) * half], b.at[n + h])

    def loaded_pair(name):
        loaded((name, 0), (name, 1))

    def weight_copy(n):
        return pltpu.make_async_copy(g.at[WEIGHT_ORDER[n]], w.at[n % 3], w_sem.at[n])

    def weight(n):
        weight_copy(n).wait()
        return w.at[n % 3]

    GVAL, ACT, PRE, IN_K2, IN_R2, GREC, GPRE = 0, 2, 4, 6, 8, 10, 11
    load("gv0", gv_in.at[0], b.at[GVAL])
    load("gv1", gv_in.at[1], b.at[GVAL + 1])
    for j in range(2):
        load(("act", j), act_in.at[j], b.at[ACT + j])
    load_pair("in_k2", ins2_in.at[0], IN_K2)
    for j in range(2):
        load(("pre", j), pre_in.at[j], b.at[PRE + j])
    for n in range(3):
        weight_copy(n).start()
    load_pair("in_r2", ins2_in.at[1], IN_R2)
    load("gr", gr_in, b.at[GREC])
    load("resid", resid_in, resid)
    enter(z, yx, c)

    sums = []
    for p in range(PIECES):
        if p in LINED:
            n = LINED.index(p)
            sums.append(
                ReduceLine(
                    part, p % PARTS, lring1.at[n], lring2.at[n], lline.at[n], out.at[p], lsends.at[n], lrecvs.at[n]
                )
            )
        else:
            n = p - sum(q < p for q in LINED)
            sums.append(
                Reduce(part, p % PARTS, ring1.at[n], ring2.at[n], line.at[n], out.at[p], sends.at[n], recvs.at[n])
            )
    vector_sums = Reduce(vpart, 0, vring1, vring2, vline, vsum, vsends, vrecvs)
    final = []
    rows4 = recv4.shape[1]
    others = strip(1 - c, rows4)

    def pump(name):
        for stage, p in plan[name]:
            if p == "v":
                getattr(vector_sums, "stage%d" % stage)()
                continue
            getattr(sums[p], "stage%d" % stage)()
            if stage == 4 and p in (R_GATE2, R_TIME, R_TIME + 1, R_TIME + 2):
                n = len(final)
                slot = 3 if p == R_GATE2 else p - R_TIME
                final.append(remote(out.at[p, others], recv4.at[slot], ex_send.at[n], ex_recv.at[n], partner))
                final[-1].start()

    def gradient(p, lhs, rhs):
        def block(a, carry):
            rows_a = dot(lhs[a // 2, :, strip(a % 2, half // 2)], rhs[...], TN)
            part[p % PARTS, a] = rows_a.astype(BF16).reshape(part.shape[2:])
            return carry

        lax.fori_loop(0, 4, block, 0)

    def thirds(ref, h):
        return ref[2 * h : 2 * h + 2].reshape(half, half)

    loaded("gv0", "gv1")
    for j in range(4):
        loaded(("act", j))
        gradient(R_VALUE + j, pair(GVAL), b.at[ACT + j % 2])
        if j < 2:
            load(("act", j + 2), act_in.at[j + 2], b.at[ACT + j])
        pump("fv%d" % j)
    loaded_pair("in_k2")
    for j in range(4):
        loaded(("pre", j))
        value_w = weight(2 * j)

        def through(at):
            g_hidden = sum(dot(b[GVAL + h, at, :], thirds(value_w, h), NN) for h in range(2))
            b[GPRE, at, :] = (2.0 * b[PRE + j % 2, at, :].astype(F32) * g_hidden).astype(BF16)

        over_rows(length, 256, through)
        pump("th%d" % j)
        if j < 2:
            load(("pre", j + 2), pre_in.at[j + 2], b.at[PRE + j])
        weight_copy(2 * j + 3).start()
        gradient(R_KEY + j, pair(IN_K2), b.at[GPRE])
        pump("fk%d" % j)
        key_w = weight(2 * j + 1)

        def collect(at):
            for h in range(2):
                piece = dot(b[GPRE, at, :], thirds(key_w, h), NT)
                f[h, at, :] = piece if j == 0 else f[h, at, :] + piece

        over_rows(length, 256, collect)
        pump("co%d" % j)
        weight_copy(2 * j + 4).start()
    loaded_pair("in_r2")
    loaded("gr")
    gradient(R_GATE2, pair(IN_R2), b.at[GREC])
    pump("g2")
    gate_w = weight(8)

    def gate_back(at):
        for h in range(2):
            f[2 + h, at, :] = dot(b[GREC, at, :], thirds(gate_w, h), NT)

    over_rows(length, 256, gate_back)
    pump("gb")
    weight_copy(11).start()
    loaded("resid")

    SUM_OWN, UP, BRANCH, MIXED, G3, X, IN_K, IN_V, IN_R, SEND = 0, 2, 4, 6, 7, 4, 10, 0, 2, 6
    load_pair("up", up_in, UP)
    load("mixed", mixed_in, b.at[MIXED])
    acc[...] = jnp.zeros_like(acc)
    last = lax.broadcasted_iota(jnp.int32, (TILE, width), 0) == TILE - 1

    def row(n):
        return vec[n : n + 1, :]

    def kept(at, n):
        return wide(keep[at, :], width) if n is None else wide(keep[n, :], width)

    gain2, bias2, mk2, mr2 = (GAIN2, BIAS2, MK2, MR2)
    sum_copies = []
    for q in range(4):

        def tile(i, carry):
            base = q * quarter + i * TILE
            at = pl.ds(pl.multiple_of(base, TILE), TILE)
            after = pl.ds(pl.multiple_of(jnp.minimum(base + TILE, length - 8), 8), 8)
            inside = jnp.where(base + TILE < length, 1.0, 0.0)
            keep_at, keep_after = wide(keep[at, :], width), wide(keep[after, :], width) * inside
            unit, _ = norm(whole(resid, at))
            normed = unit * row(gain2) + row(bias2)
            total = jnp.zeros_like(unit)
            for n, share in enumerate((mk2, mr2)):
                back = whole(f.at[2 * n : 2 * n + 2], at)
                ahead = lifted(back * keep_at, whole(f.at[2 * n : 2 * n + 2], after) * keep_after, last)
                total = total + ahead + (back - ahead) * row(share)
                acc[S_MK2 + n] = acc[S_MK2 + n] + fold(normed * (back - ahead))
            acc[S_GAIN2] = acc[S_GAIN2] + fold(total * unit)
            acc[S_BIAS2] = acc[S_BIAS2] + fold(total)
            halves(b.at[SUM_OWN : SUM_OWN + 2], at, total)
            return carry

        lax.fori_loop(0, quarter // TILE, tile, 0)
        at = pl.ds(q * quarter, quarter)
        sum_copies.append(
            remote(b.at[SUM_OWN : SUM_OWN + 2, at], sum_other.at[:, at], sum_send.at[q], sum_recv.at[q], partner)
        )
        sum_copies[-1].start()
        pump("a%d" % q)
    for n in range(3):
        load(("kvr", n), kvr_in.at[n], f.at[n])
    load("sn", sn_in, f.at[3])
    load("sd", sd_in, f.at[4])
    load_pair("in_k", ins_in.at[0], IN_K)

    loaded_pair("up")
    for q in range(4):
        sum_copies[q].wait_recv()

        def tile(i, carry):
            at = pl.ds(pl.multiple_of(q * quarter + i * TILE, TILE), TILE)
            unit, inverse = norm(whole(resid, at))
            total = whole(b.at[SUM_OWN : SUM_OWN + 2], at).astype(F32) + whole(sum_other, at).astype(F32)
            back = whole(pair(UP), at).astype(F32) + back_through_norm(total, unit, inverse, row(gain2))
            halves(pair(BRANCH), at, back)

            @pl.when(c == q // 2)
            def _():
                gtok[pl.ds(pl.multiple_of((q % 2) * quarter + i * TILE, TILE), TILE), :] = back

            return carry

        lax.fori_loop(0, quarter // TILE, tile, 0)
        pump("b%d" % q)
    for copy in sum_copies:
        copy.wait_send()
    load_pair("in_v", ins_in.at[1], IN_V)
    load_pair("in_r", ins_in.at[2], IN_R)

    loaded("mixed")
    rows_h = part.shape[3] // 2
    for h in range(2):

        def emit_rows(a, carry):
            block = dot(b[MIXED, :, strip(a, half // 2)], b[BRANCH + h], TN).astype(BF16)
            part[R_EMIT, pl.ds(2 * a, 2), :, h * rows_h : (h + 1) * rows_h, :] = block.reshape(2, 4, rows_h, half)
            return carry

        lax.fori_loop(0, 2, emit_rows, 0)
    pump("em")
    emit_w = weight(9)

    def emit_back(at):
        resid[0, at, :] = sum(dot(b[BRANCH + h, at, :], emit_half(emit_w, h), NT) for h in range(2))

    over_rows(length, 256, emit_back)
    pump("eb")
    weight_copy(12).start()
    load_pair("x", x_in, X)

    loaded(("kvr", 0), ("kvr", 1), ("kvr", 2), "sn", "sd")
    carry = None
    for q in range(4):
        carry = wkv_backward(
            resid.at[0], f.at[0], f.at[1], f.at[2], f.at[3], f.at[4], keep, rows, b.at[G3], b.at[G3 + 1], b.at[G3 + 2],
            q * (length // 64), (q + 1) * (length // 64), carry,
        )
        pump("w%d" % q)
    wkv_sums(carry, rows, own_sums.at[0:1], own_sums.at[1:2])

    for n, (name, slot) in enumerate((("in_k", IN_K), ("in_v", IN_V), ("in_r", IN_R))):
        loaded_pair(name)
        sums[R_TIME + n - PARTS].finish()
        gradient(R_TIME + n, pair(slot), b.at[G3 + n])
        pump("t%d" % n)
    loaded_pair("x")
    for n in range(3):
        weight(10 + n)
    for n in range(3):
        for h in range(2):
            f[n, pl.ds(h * span + quarter, 8), :] = jnp.zeros((8, half), F32)
    n1_copies = []
    for q in (3, 2, 1, 0):
        def back_rows(n, carry):
            for h in range(2):
                if q < 3:
                    f[n, pl.ds(h * span + quarter, 8), :] = f[n, pl.ds(h * span, 8), :]
                f[n, pl.ds(h * span, quarter), :] = dot(
                    b[G3 + n, pl.ds(q * quarter, quarter), :], thirds(w.at[(n + 1) % 3], h), NT
                )
            return carry

        lax.fori_loop(0, 3, back_rows, 0)

        def tile(i, carry):
            base = q * quarter + i * TILE
            at = pl.ds(pl.multiple_of(base, TILE), TILE)
            after = pl.ds(pl.multiple_of(jnp.minimum(base + TILE, length - 8), 8), 8)
            keep_at, keep_after = wide(keep[at, :], width), wide(keep[after, :], width)

            def take(n, start, size):
                return jnp.concatenate(
                    [f[n, pl.ds(pl.multiple_of(h * span + start, 8), size), :] for h in range(2)], axis=1
                )

            unit, _ = norm(whole(pair(X), at).astype(F32))
            normed = unit * row(GAIN1) + row(BIAS1)
            total = jnp.zeros_like(unit)
            for n, share in enumerate((MK1, MV1, MR1)):
                back = take(n, i * TILE, TILE)
                ahead = lifted(back * keep_at, take(n, i * TILE + TILE, 8) * keep_after, last)
                total = total + ahead + (back - ahead) * row(share)
                acc[S_MK1 + n] = acc[S_MK1 + n] + fold(normed * (back - ahead))
            acc[S_GAIN1] = acc[S_GAIN1] + fold(total * unit)
            acc[S_BIAS1] = acc[S_BIAS1] + fold(total)
            rows_q = [pl.ds(pl.multiple_of(h * span + (q % 2) * quarter + i * TILE, TILE), TILE) for h in range(2)]

            @pl.when(c == q // 2)
            def _():
                for h in range(2):
                    f[3, rows_q[h], :] = total[:, h * half : (h + 1) * half]

            @pl.when(c != q // 2)
            def _():
                for h in range(2):
                    b[SEND, rows_q[h], :] = total[:, h * half : (h + 1) * half].astype(BF16)

            return carry

        lax.fori_loop(0, quarter // TILE, tile, 0)
        pump("c%d" % (3 - q))
    swap_n1 = remote(b.at[SEND], n1_other, sum_send.at[4], sum_recv.at[4], partner)
    swap_n1.start()

    for n in (S_GAIN1, S_BIAS1, S_GAIN2, S_BIAS2, S_MK1, S_MV1, S_MR1, S_MK2, S_MR2):
        acc[n, 0:1, :] = jnp.sum(acc[n], axis=0, keepdims=True)
    for i in range(16):
        vpart[0, i // 4, i % 4] = jnp.concatenate(
            [acc[n, 0:1, lanes(i // 2)] for n in range(SUMS)]
            + [own_sums[n : n + 1, lanes(i // 4)] for n in range(2)]
            + [jnp.zeros((3, 128), F32)]
        )
    pump("v0")
    swap_n1.wait()

    def tokens(i, carry):
        at = strip(i, TILE)
        spans = [pl.ds(pl.multiple_of(h * span + i * TILE, TILE), TILE) for h in range(2)]
        unit, inverse = norm(whole(pair(X), pl.ds(pl.multiple_of(c * span + i * TILE, TILE), TILE)).astype(F32))
        total = jnp.concatenate([f[3, s, :] + n1_other[s, :].astype(F32) for s in spans], axis=1)
        gtok[at, :] = gtok[at, :] + back_through_norm(total, unit, inverse, row(GAIN1))
        return carry

    lax.fori_loop(0, span // TILE, tokens, 0)
    for n in range(1, 4):
        pump("v%d" % n)
    swap = remote(vsum, vother, ex_send.at[4], ex_recv.at[4], partner)
    swap.start()
    pump("end")
    for p in range(PIECES - PARTS, PIECES):
        sums[p].finish()
    vector_sums.finish()
    for copy in final + [swap]:
        copy.wait()


PLAN = {
    "fv0": [(1, 0)],
    "fv1": [(1, 1)],
    "fv2": [(1, 2)],
    "fv3": [(1, 3), (2, 0)],
    "th0": [],
    "fk0": [(1, 4), (2, 2), (2, 1)],
    "co0": [],
    "th1": [],
    "fk1": [(1, 5), (3, 0), (2, 3)],
    "co1": [(2, 4)],
    "th2": [(3, 1)],
    "fk2": [(1, 6), (3, 2)],
    "co2": [],
    "th3": [(2, 5)],
    "fk3": [(1, 7), (3, 4)],
    "co3": [(2, 6), (4, 0)],
    "g2": [(1, 8), (2, 7)],
    "gb": [],
    "a0": [(3, 3)],
    "a1": [],
    "a2": [(3, 6)],
    "a3": [(4, 1), (2, 8)],
    "b0": [(3, 7), (5, 1), (4, 2)],
    "b1": [],
    "b2": [],
    "b3": [(3, 5), (3, 8)],
    "em": [(1, 9), (6, 1)],
    "eb": [],
    "w0": [(4, 4)],
    "w1": [(2, 9)],
    "w2": [(4, 3)],
    "w3": [],
    "t0": [(1, 10)],
    "t1": [(1, 11), (5, 3), (3, 9), (4, 6)],
    "t2": [(1, 12)],
    "c0": [(2, 10), (2, 11), (6, 3), (4, 7)],
    "c1": [(4, 5), (2, 12)],
    "c2": [(3, 10), (4, 8)],
    "c3": [],
    "v0": [(1, "v"), (3, 11), (5, 5)],
    "v1": [(2, "v"), (4, 9), (4, 10), (3, 12)],
    "v2": [(3, "v"), (6, 5), (4, 11)],
    "v3": [(4, "v")],
    "end": [(4, 12)],
}


def backward_call(g, x, up, ins, kvr, sn, sd, mixed, resid, ins2, pre, act, g_value, g_recept, vec, rows, keep):
    block = g.shape[3:]
    length, half = sn.shape
    lined = len(LINED)
    rings = PIECES - lined
    any_, vmem = pl.BlockSpec(memory_space=pl.ANY), pl.BlockSpec(memory_space=pltpu.VMEM)
    dma = pltpu.SemaphoreType.DMA

    def shape(*dims):
        return jax.ShapeDtypeStruct(dims, F32)

    return pl.pallas_call(
        functools.partial(backward_kernel, PLAN),
        out_shape=(
            shape(PIECES, *block), shape(4, block[0] // 2, block[1]), shape(16, 128), shape(16, 128),
            shape(length // 2, 2 * half),
        ),
        in_specs=[any_] * 14 + [vmem] * 3,
        out_specs=(vmem,) * 5,
        scratch_shapes=[
            pltpu.VMEM((PARTS, 4, 4) + block, BF16),
            pltpu.VMEM((rings, 2, 2) + block, BF16),
            pltpu.VMEM((rings, 2, 4) + block, BF16),
            pltpu.VMEM((rings, 3) + block, BF16),
            pltpu.VMEM((lined, 2, block[0] // 2, block[1]), BF16),
            pltpu.VMEM((lined, 2) + block, BF16),
            pltpu.VMEM((lined, 5, 4) + block, BF16),
            pltpu.VMEM((1, 4, 4, 16, 128), F32),
            pltpu.VMEM((2, 2, 16, 128), F32),
            pltpu.VMEM((2, 4, 16, 128), F32),
            pltpu.VMEM((3, 16, 128), F32),
            pltpu.VMEM((SLOTS, length, half), BF16),
            pltpu.VMEM((3, 4, 4) + block, BF16),
            pltpu.VMEM((5, length, half), F32),
            pltpu.VMEM((2, length, half), F32),
            pltpu.VMEM((2, length, half), BF16),
            pltpu.VMEM((length, half), BF16),
            pltpu.VMEM((SUMS, 8, 2 * half), F32),
            pltpu.VMEM((8, half), F32),
            dma((40,)), dma((PIECES,)), dma((rings, 7)), dma((rings, 7)), dma((lined, 10)), dma((lined, 10)),
            dma((7,)), dma((7,)), dma((5,)), dma((5,)), dma((5,)), dma((5,)),
        ],
        compiler_params=pltpu.CompilerParams(collective_id=1, has_side_effects=True, vmem_limit_bytes=63 * MIB),
        name="backward",
    )(g, x, up, ins, kvr, sn, sd, mixed, resid, ins2, pre, act, g_value, g_recept, vec, rows, keep)


def shifted(value, axis, steps):
    count = lax.axis_size(axis)
    first, last = (max(0, -steps), min(count, count - steps))
    return lax.ppermute(value, axis, [(source, source + steps) for source in range(first, last)])


def carried_in(array, axis, join, neutral):
    place = lax.axis_index(axis)
    gathered = jax.tree.map(
        lambda a, kind: lax.all_gather(a.astype(kind), axis),
        array,
        (jnp.bfloat16, jnp.bfloat16, jnp.bfloat16),
    )
    state = jax.tree.map(lambda a, e: jnp.zeros_like(a) + jnp.asarray(e, a.dtype), array, neutral)

    def one(turn, state):
        return join(
            state,
            jax.tree.map(
                lambda a, own: lax.dynamic_index_in_dim(a, turn, 0, False).astype(own.dtype),
                gathered,
                array,
            ),
        )

    return lax.fori_loop(0, place, one, state)


def entering(array, axis, combine, identity):
    count, place = (lax.axis_size(axis), lax.axis_index(axis))
    everything = jax.tree.map(
        lambda part, kind: lax.all_gather(part.astype(kind), axis),
        array,
        jax.tree.map(lambda a: jnp.bfloat16 if a.dtype == jnp.float32 else a.dtype, array),
    )
    start = jax.tree.map(
        lambda part, zero: jnp.broadcast_to(jnp.asarray(zero, part.dtype), part.shape),
        array,
        identity,
    )

    def turn(k, before):
        at = count - 1 - k
        reached = at > place
        new = combine(
            before, jax.tree.map(lambda part, own: part[at].astype(own.dtype), everything, array)
        )
        return jax.tree.map(lambda a, b: jnp.where(reached, a, b), new, before)

    return lax.fori_loop(0, count, turn, start)


def wide_layer_norm(values, scale_vec, shift_vec):
    center = values - jnp.mean(values, axis=-1, keepdims=True)
    inverse = lax.rsqrt(jnp.mean(center * center, axis=-1, keepdims=True) + 1e-05)
    normed = center * inverse
    return (normed * scale_vec + shift_vec, normed, inverse)


def wide_norm_back(upstream, normed, inverse, scale_vec):
    scaled = upstream * scale_vec
    inner = (
        scaled
        - jnp.mean(scaled, axis=-1, keepdims=True)
        - normed * jnp.mean(scaled * normed, axis=-1, keepdims=True)
    )
    return (
        inverse * inner,
        jnp.sum(upstream * normed, axis=(0, 1)),
        jnp.sum(upstream, axis=(0, 1)),
    )


def shift_prev(values, persist_indicator):
    arrived = shifted(values[:, -1:, :], "tensor", 1)
    return jnp.concatenate([arrived, values[:, :-1]], axis=1) * persist_indicator[:, :, None]


def shift_back(upstream, persist_indicator):
    masked = upstream * persist_indicator[:, :, None]
    arrived = shifted(masked[:, :1, :], "tensor", -1)
    return jnp.concatenate([masked[:, 1:], arrived], axis=1)


def project(values, matrix):
    return jnp.einsum("rtd,de->rte", values, matrix, preferred_element_type=jnp.float32)


def project_back(upstream, matrix):
    return jnp.einsum("rte,de->rtd", upstream, matrix, preferred_element_type=jnp.float32)


def outer_sum(values, upstream):
    return jnp.einsum("rtd,rte->de", values, upstream, preferred_element_type=jnp.float32)


def mix_back(upstreams, shares, differ, persist_indicator):
    toward = jnp.zeros_like(differ)
    behind = jnp.zeros_like(differ)
    share_grads = []
    for upstream, share in zip(upstreams, shares):
        toward = toward + upstream * share
        behind = behind + upstream * (1.0 - share)
        share_grads.append(jnp.sum(upstream * differ, axis=(0, 1)))
    return (toward + shift_back(behind, persist_indicator), share_grads)


def chain_combine(earlier, later):
    return (
        earlier[0] * later[0],
        later[0] * earlier[1] + later[1],
        later[0] * earlier[2] + later[2],
    )


def scan_fragments(
    lookup_wide, payload_wide, fading_power, reward_coords, text_boundary_indicators
):
    decay_rate = jnp.exp(fading_power)
    row_count, span_len, width_len = lookup_wide.shape
    block_len = min(32, span_len)
    block_count = span_len // block_len
    places = jnp.arange(block_len, dtype=jnp.float32)
    rising = jnp.exp(places[:, None] * decay_rate)
    falling = jnp.exp(-(places[:, None] - 1.0) * decay_rate)
    trailing = jnp.exp(-(block_len - 1.0 - places)[:, None] * decay_rate)
    leading = jnp.exp(-places[:, None] * decay_rate)
    settle = jnp.exp(-block_len * decay_rate)
    before = places[:, None] > places[None, :]

    def split_blocks(values):
        return jnp.swapaxes(
            values.reshape((row_count, block_count, block_len) + values.shape[2:]), 0, 1
        )

    def advance(state_pair, scanned):
        accrued_dividend_sum, accrued_divisor_sum = state_pair
        lookup_narrow, payload_narrow, reset_b = scanned
        tree_levels = jnp.cumsum(reset_b, axis=1)
        linked = ((tree_levels[:, :, None] == tree_levels[:, None, :]) & before).astype(jnp.float32)
        key_term = jnp.exp(lookup_narrow)
        keyed_value = key_term * payload_narrow
        inside_numerator = falling * jnp.einsum(
            "rti,rid->rtd", linked, rising * keyed_value, precision=lax.Precision.HIGHEST
        )
        interior_divisor_sum = falling * jnp.einsum(
            "rti,rid->rtd", linked, rising * key_term, precision=lax.Precision.HIGHEST
        )
        leftover_multiplier = (tree_levels == 0).astype(jnp.float32)[:, :, None] * leading
        reward_multiplier = jnp.exp(reward_coords + lookup_narrow)
        above_total = (
            inside_numerator
            + reward_multiplier * payload_narrow
            + leftover_multiplier * accrued_dividend_sum[:, None, :]
        )
        below_total = (
            interior_divisor_sum
            + reward_multiplier
            + leftover_multiplier * accrued_divisor_sum[:, None, :]
        )
        ending = (tree_levels == tree_levels[:, -1:]).astype(jnp.float32)[:, :, None] * trailing
        intact = (tree_levels[:, -1] == 0).astype(jnp.float32)[:, None] * settle
        new_num = intact * accrued_dividend_sum + jnp.sum(ending * keyed_value, axis=1)
        new_den = intact * accrued_divisor_sum + jnp.sum(ending * key_term, axis=1)
        return ((new_num, new_den), (above_total, below_total))

    initial = jnp.zeros((row_count, width_len), jnp.float32)
    (total_num, total_den), (uppers, lowers) = lax.scan(
        advance,
        (initial, initial),
        (
            split_blocks(lookup_wide),
            split_blocks(payload_wide),
            split_blocks(text_boundary_indicators),
        ),
    )

    def join_blocks(values):
        return jnp.swapaxes(values, 0, 1).reshape(row_count, span_len, width_len)

    tree_levels = jnp.cumsum(text_boundary_indicators, axis=1)
    reaching = (tree_levels == 0).astype(jnp.float32)[:, :, None] * jnp.exp(
        -jnp.arange(span_len, dtype=jnp.float32)[:, None] * decay_rate
    )
    passing = (tree_levels[:, -1] == 0).astype(jnp.float32)[:, None] * jnp.exp(
        -span_len * decay_rate
    )
    return (join_blocks(uppers), join_blocks(lowers), reaching, total_num, total_den, passing)


def recurrence_finish(pieces_list, incoming_num, incoming_den):
    above_total = pieces_list[0] + pieces_list[2] * incoming_num[:, None, :]
    below_total = pieces_list[1] + pieces_list[2] * incoming_den[:, None, :]
    return (above_total / below_total, below_total)


def ffn_apply(inputs, key_weight, value_weight):
    hidden_pre = project(inputs, key_weight)
    hidden = jnp.square(jax.nn.relu(hidden_pre)).astype(jnp.bfloat16)
    return (hidden_pre, hidden, project(hidden, value_weight))


def ffn_grads(inputs, hidden_pre, hidden, upstream, key_weight, value_weight):
    g_hidden = jnp.einsum("rtd,fd->rtf", upstream, value_weight, preferred_element_type=jnp.float32)
    grad_value = jnp.einsum("rtf,rtd->fd", hidden, upstream, preferred_element_type=jnp.float32)
    g_pre = (2.0 * jax.nn.relu(hidden_pre) * g_hidden).astype(jnp.bfloat16)
    grad_key = jnp.einsum("rtd,rtf->df", inputs, g_pre, preferred_element_type=jnp.float32)
    g_inputs = jnp.einsum("rtf,df->rtd", g_pre, key_weight, preferred_element_type=jnp.float32)
    return (g_inputs, grad_key, grad_value)


def wide_shards(
    incoming_embeddings,
    text_boundary_indicators,
    upstream_sensitivity,
    primary_standardize_scaling,
    primary_standardize_offset,
    secondary_standardize_scaling,
    secondary_standardize_offset,
    feature_fading_logarithms,
    present_symbol_reward,
    timemix_lookup_blend,
    timemix_payload_blend,
    timemix_gate_blend,
    timemix_lookup_proj,
    timemix_payload_proj,
    timemix_gate_proj,
    timemix_emit_proj,
    feedmix_lookup_blend,
    feedmix_gate_blend,
    feedmix_gate_proj,
    feedmix_lookup_proj,
    feedmix_payload_proj,
):
    gathered_portions = (
        lax.all_gather(primary_standardize_scaling, ("dp", "tensor"), axis=0, tiled=True),
        lax.all_gather(primary_standardize_offset, ("dp", "tensor"), axis=0, tiled=True),
        lax.all_gather(secondary_standardize_scaling, ("dp", "tensor"), axis=0, tiled=True),
        lax.all_gather(secondary_standardize_offset, ("dp", "tensor"), axis=0, tiled=True),
        lax.all_gather(feature_fading_logarithms, ("dp", "tensor"), axis=0, tiled=True),
        lax.all_gather(present_symbol_reward, ("dp", "tensor"), axis=0, tiled=True),
        lax.all_gather(timemix_lookup_blend, ("dp", "tensor"), axis=0, tiled=True),
        lax.all_gather(timemix_payload_blend, ("dp", "tensor"), axis=0, tiled=True),
        lax.all_gather(timemix_gate_blend, ("dp", "tensor"), axis=0, tiled=True),
        lax.all_gather(timemix_lookup_proj, ("dp", "tensor"), axis=0, tiled=True),
        lax.all_gather(timemix_payload_proj, ("dp", "tensor"), axis=0, tiled=True),
        lax.all_gather(timemix_gate_proj, ("dp", "tensor"), axis=0, tiled=True),
        lax.all_gather(timemix_emit_proj, ("dp", "tensor"), axis=0, tiled=True),
        lax.all_gather(feedmix_lookup_blend, ("dp", "tensor"), axis=0, tiled=True),
        lax.all_gather(feedmix_gate_blend, ("dp", "tensor"), axis=0, tiled=True),
        lax.all_gather(feedmix_gate_proj, ("dp", "tensor"), axis=0, tiled=True),
    )
    initial_scaling_coords = gathered_portions[0].astype(jnp.float32)
    initial_offset_coords = gathered_portions[1].astype(jnp.float32)
    later_scaling_coords = gathered_portions[2].astype(jnp.float32)
    later_offset_coords = gathered_portions[3].astype(jnp.float32)
    fading_power = gathered_portions[4].astype(jnp.float32)
    reward_coords = gathered_portions[5].astype(jnp.float32)
    share_k1 = gathered_portions[6].astype(jnp.float32)
    share_v1 = gathered_portions[7].astype(jnp.float32)
    share_r1 = gathered_portions[8].astype(jnp.float32)
    lookup_coefficients_initial = gathered_portions[9]
    payload_coefficients_initial = gathered_portions[10]
    gate_coefficients_initial = gathered_portions[11]
    emit_coefficients_initial = gathered_portions[12]
    share_k2 = gathered_portions[13].astype(jnp.float32)
    share_r2 = gathered_portions[14].astype(jnp.float32)
    gate_coefficients_later = gathered_portions[15]
    lookup_coefficients_later, payload_coefficients_later = (
        lax.all_gather(feedmix_lookup_proj, "dp", axis=0, tiled=True),
        lax.all_gather(feedmix_payload_proj, "dp", axis=1, tiled=True),
    )
    persist_indicator = (1 - text_boundary_indicators).astype(jnp.float32)
    inputs = incoming_embeddings.astype(jnp.float32)
    normed_one, unit_one, inverse_one = wide_layer_norm(
        inputs, initial_scaling_coords, initial_offset_coords
    )
    prev_one = shift_prev(normed_one, persist_indicator)
    differ_one = normed_one - prev_one
    in_key = (prev_one + differ_one * share_k1).astype(jnp.bfloat16)
    in_value = (prev_one + differ_one * share_v1).astype(jnp.bfloat16)
    in_recept = (prev_one + differ_one * share_r1).astype(jnp.bfloat16)
    initial_lookup_lines = project(in_key, lookup_coefficients_initial)
    initial_payload_lines = project(in_value, payload_coefficients_initial)
    recept_one = project(in_recept, gate_coefficients_initial)
    pieces_list = scan_fragments(
        initial_lookup_lines,
        initial_payload_lines,
        fading_power,
        reward_coords,
        text_boundary_indicators,
    )
    passing = pieces_list[5]
    identity = (jnp.ones_like(passing), jnp.zeros_like(passing), jnp.zeros_like(passing))
    unused_item, incoming_num, incoming_den = carried_in(
        (passing, pieces_list[3], pieces_list[4]), "tensor", chain_combine, identity
    )
    blended_mean_state, below_total = recurrence_finish(pieces_list, incoming_num, incoming_den)
    sig_one = jax.nn.sigmoid(recept_one)
    mixed_att = (sig_one * blended_mean_state).astype(jnp.bfloat16)
    resid_one = inputs + project(mixed_att, emit_coefficients_initial)
    normed_two, unit_two, inverse_two = wide_layer_norm(
        resid_one, later_scaling_coords, later_offset_coords
    )
    prev_two = shift_prev(normed_two, persist_indicator)
    differ_two = normed_two - prev_two
    in_key_two = (prev_two + differ_two * share_k2).astype(jnp.bfloat16)
    in_recept_two = (prev_two + differ_two * share_r2).astype(jnp.bfloat16)
    recept_two = project(in_recept_two, gate_coefficients_later)
    sig_two = jax.nn.sigmoid(recept_two)
    row_inputs = lax.all_gather(in_key_two, "tensor", axis=1, tiled=True)
    hidden_pre, hidden, partial_value = ffn_apply(
        row_inputs, lookup_coefficients_later, payload_coefficients_later
    )
    value_two = lax.psum_scatter(
        partial_value.astype(jnp.bfloat16), "tensor", scatter_dimension=1, tiled=True
    ).astype(jnp.float32)
    layer_out = (resid_one + sig_two * value_two).astype(jnp.bfloat16)
    upstream = upstream_sensitivity.astype(jnp.float32)
    g_value_two = (upstream * sig_two).astype(jnp.bfloat16)
    g_recept_two = (upstream * value_two * sig_two * (1.0 - sig_two)).astype(jnp.bfloat16)
    grad_recept_two = outer_sum(in_recept_two, g_recept_two)
    g_mix_r2 = project_back(g_recept_two, gate_coefficients_later)
    row_grads = lax.all_gather(g_value_two, "tensor", axis=1, tiled=True)
    partial_grad, grad_key_two, grad_value_two = ffn_grads(
        row_inputs,
        hidden_pre,
        hidden,
        row_grads,
        lookup_coefficients_later,
        payload_coefficients_later,
    )
    g_mix_k2 = lax.psum_scatter(
        partial_grad.astype(jnp.bfloat16), "tensor", scatter_dimension=1, tiled=True
    ).astype(jnp.float32)
    sum_key_two, sum_value_two = (
        lax.psum_scatter(
            grad_key_two.astype(jnp.bfloat16), "dp", scatter_dimension=0, tiled=True
        ).astype(jnp.float32),
        lax.psum_scatter(
            grad_value_two.astype(jnp.bfloat16), "dp", scatter_dimension=1, tiled=True
        ).astype(jnp.float32),
    )
    g_normed_two, shares_two = mix_back(
        (g_mix_k2, g_mix_r2), (share_k2, share_r2), differ_two, persist_indicator
    )
    g_resid_part, grad_gain_two, grad_bias_two = wide_norm_back(
        g_normed_two, unit_two, inverse_two, later_scaling_coords
    )
    g_resid = upstream + g_resid_part
    g_branch = g_resid.astype(jnp.bfloat16)
    grad_out_one = outer_sum(mixed_att, g_branch)
    g_mixed = project_back(g_branch, emit_coefficients_initial)
    g_weighted = g_mixed * sig_one
    g_recept_one = (g_mixed * blended_mean_state * sig_one * (1.0 - sig_one)).astype(jnp.bfloat16)
    reaching = pieces_list[2]
    g_in_num = jnp.sum(g_weighted * reaching / below_total, axis=1)
    g_in_den = -jnp.sum(g_weighted * reaching * blended_mean_state / below_total, axis=1)
    unused_item, back_num, back_den = entering(
        (passing, g_in_num, g_in_den), "tensor", chain_combine, identity
    )
    g_passing = back_num * incoming_num + back_den * incoming_den

    def device_fragment(lookup_wide, payload_wide, fading_coords, reward_power):
        shard_pieces = scan_fragments(
            lookup_wide, payload_wide, fading_coords, reward_power, text_boundary_indicators
        )
        local_out, unused_item = recurrence_finish(shard_pieces, incoming_num, incoming_den)
        return (local_out, shard_pieces[3], shard_pieces[4], shard_pieces[5])

    unused_item, reverse_pass_rule = jax.vjp(
        device_fragment, initial_lookup_lines, initial_payload_lines, fading_power, reward_coords
    )
    derivative_lookup_wide, derivative_payload_wide, fading_derivative, reward_derivative = (
        reverse_pass_rule((g_weighted, back_num, back_den, g_passing))
    )
    g_key_one = derivative_lookup_wide.astype(jnp.bfloat16)
    g_value_one = derivative_payload_wide.astype(jnp.bfloat16)
    grad_key_one = outer_sum(in_key, g_key_one)
    grad_value_one = outer_sum(in_value, g_value_one)
    grad_recept_one = outer_sum(in_recept, g_recept_one)
    g_mix_k1 = project_back(g_key_one, lookup_coefficients_initial)
    g_mix_v1 = project_back(g_value_one, payload_coefficients_initial)
    g_mix_r1 = project_back(g_recept_one, gate_coefficients_initial)
    g_normed_one, shares_one = mix_back(
        (g_mix_k1, g_mix_v1, g_mix_r1),
        (share_k1, share_v1, share_r1),
        differ_one,
        persist_indicator,
    )
    g_input_part, grad_gain_one, grad_bias_one = wide_norm_back(
        g_normed_one, unit_one, inverse_one, initial_scaling_coords
    )
    grad_tokens = g_resid + g_input_part
    summed = (
        lax.psum_scatter(grad_gain_one, ("dp", "tensor"), scatter_dimension=0, tiled=True),
        lax.psum_scatter(grad_bias_one, ("dp", "tensor"), scatter_dimension=0, tiled=True),
        lax.psum_scatter(grad_gain_two, ("dp", "tensor"), scatter_dimension=0, tiled=True),
        lax.psum_scatter(grad_bias_two, ("dp", "tensor"), scatter_dimension=0, tiled=True),
        lax.psum_scatter(fading_derivative, ("dp", "tensor"), scatter_dimension=0, tiled=True),
        lax.psum_scatter(reward_derivative, ("dp", "tensor"), scatter_dimension=0, tiled=True),
        lax.psum_scatter(shares_one[0], ("dp", "tensor"), scatter_dimension=0, tiled=True),
        lax.psum_scatter(shares_one[1], ("dp", "tensor"), scatter_dimension=0, tiled=True),
        lax.psum_scatter(shares_one[2], ("dp", "tensor"), scatter_dimension=0, tiled=True),
        lax.psum_scatter(grad_key_one, ("dp", "tensor"), scatter_dimension=0, tiled=True),
        lax.psum_scatter(grad_value_one, ("dp", "tensor"), scatter_dimension=0, tiled=True),
        lax.psum_scatter(grad_recept_one, ("dp", "tensor"), scatter_dimension=0, tiled=True),
        lax.psum_scatter(grad_out_one, ("dp", "tensor"), scatter_dimension=0, tiled=True),
        lax.psum_scatter(shares_two[0], ("dp", "tensor"), scatter_dimension=0, tiled=True),
        lax.psum_scatter(shares_two[1], ("dp", "tensor"), scatter_dimension=0, tiled=True),
        lax.psum_scatter(grad_recept_two, ("dp", "tensor"), scatter_dimension=0, tiled=True),
    )
    return (
        layer_out,
        grad_tokens,
        summed[0],
        summed[1],
        summed[2],
        summed[3],
        summed[4],
        summed[5],
        summed[6],
        summed[7],
        summed[8],
        summed[9],
        summed[10],
        summed[11],
        summed[12],
        summed[13],
        summed[14],
        summed[15],
        sum_key_two,
        sum_value_two,
    )


def split_columns(w, parts):
    rows, width = w.shape
    return w.reshape(rows, parts, 2, width // (2 * parts)).transpose(2, 0, 1, 3).reshape(2, rows, width // 2)


def join_columns(own, other, c, parts):
    rows, half = own.shape[-2:]
    a = jnp.where(c == 0, own, other).reshape(own.shape[:-1] + (parts, half // parts))
    b = jnp.where(c == 0, other, own).reshape(own.shape[:-1] + (parts, half // parts))
    return jnp.stack([a, b], axis=-2).reshape(own.shape[:-1] + (2 * half,))


def pack(tokens, starts, upstream, gain1, bias1, gain2, bias2, fading, reward, mk1, mv1, mr1, wk, wv, wr, wo, mk2, mr2, wg, fk, fv):
    i, c, count = lax.axis_index("dp"), lax.axis_index("tensor"), lax.axis_size("dp")
    own_rows, width = wk.shape
    half, hidden = width // 2, fk.shape[1]
    by_core = jnp.stack([split_columns(wk, count), split_columns(wv, count), split_columns(wr, count), split_columns(wg, 1)])
    own4 = lax.dynamic_index_in_dim(by_core, c, 1, False)
    other4 = lax.dynamic_index_in_dim(by_core, 1 - c, 1, False)
    emit = wo.reshape(own_rows, 2, half).transpose(1, 0, 2).reshape(1, 2 * own_rows, half)
    key4 = fk.reshape(2 * own_rows, 4, hidden // 4).transpose(1, 0, 2)
    value4 = fv.reshape(4, hidden // 4, 2 * own_rows).transpose(0, 2, 1)
    chunks = {**{p: key4[j] for j, p in enumerate(KEYS)}, **{p: value4[j] for j, p in enumerate(VALUES)}}
    rest = jnp.concatenate([emit, jnp.stack([chunks[p] for p in range(FFN, PIECES)])])
    slots = 128 // own_rows
    everywhere = jnp.stack([gain1, bias1, gain2, bias2, fading, reward, mk1, mv1, mr1, mk2, mr2])
    own = jnp.stack([fading, reward, jnp.zeros_like(fading), jnp.zeros_like(fading), jnp.zeros_like(fading)])
    lane = jnp.arange(128)[None, :] // own_rows
    vec = jnp.concatenate([
        jnp.where(lane == (2 * i + c) % slots, jnp.tile(everywhere, (1, slots)), 0),
        jnp.where(lane == i % slots, jnp.tile(own, (1, slots)), 0),
    ]).astype(BF16)
    keep = jnp.broadcast_to((1 - starts[0]).astype(F32)[:, None], (starts.shape[1], 128))
    return own4, other4, rest, vec, tokens[0], upstream[0], keep


def shards(*args):
    tokens = args[0]
    c = lax.axis_index("tensor")
    i = lax.axis_index("dp")
    count = lax.axis_size("dp")
    own_rows, width = args[12].shape
    hidden = args[19].shape[1]
    half = width // 2
    (
        g, layer_out, x, up, ins, kvr, sn, sd, mixed, resid, ins2, pre, act, g_value, g_recept2, vec, rows, keep,
    ) = forward_call(*pack(*args))

    total, recv4, vsum, vother, grad_tokens = backward_call(
        g, x, up, ins, kvr, sn, sd, mixed, resid, ins2, pre, act, g_value, g_recept2, vec, rows, keep
    )
    slots = 128 // own_rows
    vtotal = lax.dynamic_slice_in_dim(vsum + vother, (2 * i + c) % slots * own_rows, own_rows, 1)
    own_scan = lax.dynamic_slice_in_dim(vsum, i % slots * own_rows, own_rows, 1)
    own = lax.dynamic_slice_in_dim(total[R_GATE2:], c * own_rows, own_rows, 1)
    out_k, out_v, out_r = (join_columns(own[2 + n], recv4[n], c, count) for n in range(3))
    out_g = join_columns(own[0], recv4[3], c, 1)
    out_o = total[R_EMIT].reshape(2, own_rows, half).transpose(1, 0, 2).reshape(own_rows, width)
    out_fk = total[R_KEY : R_KEY + 4].transpose(1, 0, 2).reshape(2 * own_rows, hidden)
    out_fv = total[R_VALUE : R_VALUE + 4].transpose(0, 2, 1).reshape(hidden, 2 * own_rows)
    return (
        layer_out[None], grad_tokens[None], *(vtotal[n] for n in range(4)), own_scan[SUMS], own_scan[SUMS + 1],
        *(vtotal[n] for n in range(6, 9)), out_k, out_v, out_r, out_o, vtotal[9], vtotal[10], out_g, out_fk, out_fv,
    )


def solution(mesh):
    row, vector, matrix_ = P("dp", "tensor", None), P(("dp", "tensor")), P(("dp", "tensor"), None)
    key, value = P("dp", "tensor"), P("tensor", "dp")
    in_specs = (row, P("dp", "tensor"), row) + (vector,) * 9 + (matrix_,) * 4 + (vector,) * 2 + (matrix_, key, value)
    out_specs = (row, row) + (vector,) * 9 + (matrix_,) * 4 + (vector,) * 2 + (matrix_, key, value)
    body = shards if (mesh.shape["dp"], mesh.shape["tensor"]) == (16, 2) else wide_shards
    return jax.shard_map(body, mesh=mesh, in_specs=in_specs, out_specs=out_specs, check_vma=False)
```

```python
import functools

import jax
import jax.numpy as jnp
from jax import lax
from jax.experimental import pallas as pl
from jax.experimental.pallas import tpu as pltpu
from jax.sharding import PartitionSpec as P

F32, BF16 = jnp.float32, jnp.bfloat16
MESH_ID = pl.DeviceIdType.MESH
MIB = 1 << 20
PARTS = 10
PIECES = 13


def place():
    i, c = lax.axis_index("dp"), lax.axis_index("tensor")
    return i // 4, i % 4, c


def neighbours(z, yx):
    x = yx + 1 - 2 * (yx % 2)
    y = (yx + 2) % 4
    d = (x + 2) % 4
    zs = (z + 1 - 2 * (z % 2), (z + 2) % 4, 3 - z)
    return x, y, d, zs


def enter(z, yx, c):
    x, y, d, zs = neighbours(z, yx)
    barrier = pltpu.get_barrier_semaphore()
    targets = [(z * 4 + yx, 1 - c), (z * 4 + x, c), (z * 4 + y, c)]
    targets += [(peer * 4 + yx, c) for peer in zs]
    for target in targets:
        pl.semaphore_signal(barrier, inc=1, device_id=target, device_id_type=MESH_ID)
    pl.semaphore_wait(barrier, len(targets))


def remote(src, dst, send, recv, target):
    return pltpu.make_async_remote_copy(
        src_ref=src, dst_ref=dst, send_sem=send, recv_sem=recv,
        device_id=target, device_id_type=MESH_ID,
    )


def strip(i, size):
    return pl.ds(pl.multiple_of(i * size, size), size)


class Gather:
    def __init__(self, view, sends, recvs, first=0):
        self.view, self.sends, self.recvs, self.first = view, sends, recvs, first
        self.z, self.yx, self.c = place()
        self.x, self.y, self.d, self.zs = neighbours(self.z, self.yx)

    def to(self, z, yx):
        return (z * 4 + yx, self.c)

    def copy(self, p, k, ref, target):
        return remote(ref, ref, self.sends.at[p, k], self.recvs.at[p, k], target)

    def along(self, p):
        own = self.view(p).at[self.z, self.yx]
        return [self.copy(p, k, own, self.to(peer, self.yx)) for k, peer in enumerate(self.zs)]

    def plane(self, p):
        own = self.view(p).at[:, self.yx]
        return [self.copy(p, 3, own, self.to(self.z, self.x)), self.copy(p, 4, own, self.to(self.z, self.y))]

    def onward(self, p):
        return [
            self.copy(p, 5, self.view(p).at[0:2, self.x], self.to(self.z, self.y)),
            self.copy(p, 6, self.view(p).at[2:4, self.y], self.to(self.z, self.x)),
        ]

    def start(self, copies):
        for copy in copies:
            copy.start()

    def arrive(self, copies):
        for copy in copies:
            copy.wait_recv()

    def step(self, p):
        self.arrive(self.along(p))
        self.start(self.plane(p))

    def forward(self, p):
        self.arrive(self.plane(p))
        self.start(self.onward(p))

    def finish(self, p):
        for copy in self.along(p) + self.plane(p) + self.onward(p):
            copy.wait_send()


class GatherLine(Gather):
    def ring(self, p):
        own = self.view(p).at[self.z, self.yx]
        return [self.copy(p, 0, own, self.to(self.z, self.x)), self.copy(p, 1, own, self.to(self.z, self.y))]

    def onward(self, p):
        half = self.view(p).shape[2] // 2
        return [
            self.copy(p, 2, self.view(p).at[self.z, self.x, 0:half], self.to(self.z, self.y)),
            self.copy(p, 3, self.view(p).at[self.z, self.y, half:], self.to(self.z, self.x)),
        ]

    def climb(self, p, k, up, arriving):
        behind = k if arriving else k - 1
        plane = self.z - behind if up else self.z + behind
        beyond = self.z + 1 if up != arriving else self.z - 1
        real = (plane >= 0) & (plane <= 3) & (beyond >= 0) & (beyond <= 3)
        plane, beyond = jnp.clip(plane, 0, 3), jnp.clip(beyond, 0, 3)
        k = (4 if up else 7) + k - 1
        return real, self.copy(p, k, self.view(p).at[plane], self.to(beyond, self.yx))

    def each(self, p, k, arriving, action):
        for up in (True, False):
            real, copy = self.climb(p, k, up, arriving)
            pl.when(real)(functools.partial(action, copy))

    def line(self, p, k):
        if k > 1:
            self.each(p, k - 1, True, lambda copy: copy.wait_recv())
        self.each(p, k, False, lambda copy: copy.start())

    def ready(self, p):
        self.each(p, 3, True, lambda copy: copy.wait_recv())

    def finish(self, p):
        for copy in self.ring(p) + self.onward(p):
            copy.wait_send()
        for k in (1, 2, 3):
            self.each(p, k, False, lambda copy: copy.wait_send())


class Reduce:
    def __init__(self, part, slot, ring1, ring2, line, out, sends, recvs):
        self.parts, self.slot, self.ring1, self.ring2, self.line, self.out = part, slot, ring1, ring2, line, out
        self.sends, self.recvs = sends, recvs
        self.z, self.yx, self.c = place()
        self.x, self.y, self.d, self.zs = neighbours(self.z, self.yx)

    def copy(self, k, src, dst, z, yx):
        return remote(src, dst, self.sends.at[k], self.recvs.at[k], (z * 4 + yx, self.c))

    def part(self):
        return self.parts.at[self.slot]

    def diagonal(self):
        return [
            self.copy(0, self.part().at[0:2, self.d], self.ring1.at[0], self.z, self.x),
            self.copy(1, self.part().at[2:4, self.d], self.ring1.at[1], self.z, self.y),
        ]

    def side(self):
        return [
            self.copy(2, self.part().at[:, self.x], self.ring2.at[0], self.z, self.x),
            self.copy(3, self.part().at[:, self.y], self.ring2.at[1], self.z, self.y),
        ]

    def down(self):
        return [
            self.copy(4 + k, self.part().at[peer, self.yx], self.line.at[k], peer, self.yx)
            for k, peer in enumerate(self.zs)
        ]

    def start(self, copies):
        for copy in copies:
            copy.start()

    def arrive(self, copies):
        for copy in copies:
            copy.wait_recv()

    def add_up(self, own, others, result):
        def step(i, carry):
            at = strip(i, 16)
            total = own[at, :].astype(F32)
            for other in others:
                total = total + other[at, :].astype(F32)
            result[at, :] = total.astype(result.dtype)
            return carry

        lax.fori_loop(0, own.shape[0] // 16, step, 0)

    def add(self, a, yx, others):
        own = self.part().at[a, yx]
        self.add_up(own, others, own)

    def give(self, others):
        start = 0
        for out in self.out:
            rows = pl.ds(start, out.shape[0])
            own = self.part().at[self.z, self.yx, rows]
            self.add_up(own, [other.at[rows] for other in others], out)
            start += out.shape[0]

    def stage1(self):
        self.start(self.diagonal())

    def stage2(self):
        self.arrive(self.diagonal())

        def planes(a, carry):
            self.add(a, self.y, [self.ring1.at[0, a]])
            self.add(a + 2, self.x, [self.ring1.at[1, a]])
            return carry

        lax.fori_loop(0, 2, planes, 0)
        self.start(self.side())

    def stage3(self):
        self.arrive(self.side())

        def planes(a, carry):
            self.add(a, self.yx, [self.ring2.at[0, a], self.ring2.at[1, a]])
            return carry

        lax.fori_loop(0, 4, planes, 0)
        self.start(self.down())

    def stage4(self):
        self.arrive(self.down())
        self.give([self.line.at[k] for k in range(3)])

    def finish(self):
        for copy in self.diagonal() + self.side() + self.down():
            copy.wait_send()


class ReduceLine(Reduce):
    def step(self, k, up, arriving):
        z = self.z
        plane = (3 if arriving else 4) - k + z if up else k - (3 if arriving else 4) + z
        beyond = z + 1 if up != arriving else z - 1
        real = (plane >= 0) & (plane <= 3) & (beyond >= 0) & (beyond <= 3)
        plane, beyond = jnp.clip(plane, 0, 3), jnp.clip(beyond, 0, 3)
        place_in = plane + 1 if up else plane
        k = (3 if up else 0) + k - 1
        return real, plane, place_in, self.copy(k, self.part().at[plane], self.line.at[place_in], beyond, self.yx)

    def take(self, arrived, plane, place_in):
        arrived.wait_recv()

        def blocks(yx, carry):
            self.add(plane, yx, [self.line.at[place_in, yx]])
            return carry

        lax.fori_loop(0, 4, blocks, 0)

    def move(self, k):
        for up in (True, False):
            real, plane, _, leaving = self.step(k, up, False)
            if k > 1:
                came, _, place_in, arrived = self.step(k - 1, up, True)

                pl.when(real & came)(functools.partial(self.take, arrived, plane, place_in))

            pl.when(real)(leaving.start)

    def halves(self):
        half = self.ring1.shape[1]
        own = self.part().at[self.z, self.d]
        return [
            self.copy(6, own.at[0:half], self.ring1.at[0], self.z, self.x),
            self.copy(7, own.at[half:], self.ring1.at[1], self.z, self.y),
        ]

    def sides(self):
        return [
            self.copy(8, self.part().at[self.z, self.x], self.ring2.at[0], self.z, self.x),
            self.copy(9, self.part().at[self.z, self.y], self.ring2.at[1], self.z, self.y),
        ]

    def stage1(self):
        self.move(1)

    def stage2(self):
        self.move(2)

    def stage3(self):
        self.move(3)

    def stage4(self):
        for up in (True, False):
            came, plane, place_in, arrived = self.step(3, up, True)
            pl.when(came)(functools.partial(self.take, arrived, plane, place_in))

        self.start(self.halves())

    def stage5(self):
        self.arrive(self.halves())
        half = self.ring1.shape[1]
        for yx, start, piece in ((self.y, 0, 0), (self.x, half, 1)):
            own = self.part().at[self.z, yx, start : start + half]
            self.add_up(own, [self.ring1.at[piece]], own)
        self.start(self.sides())

    def stage6(self):
        self.arrive(self.sides())
        self.give([self.ring2.at[0], self.ring2.at[1]])

    def finish(self):
        for k in (1, 2, 3):
            for up in (True, False):
                real, _, _, leaving = self.step(k, up, False)
                pl.when(real)(leaving.wait_send)
        for copy in self.halves() + self.sides():
            copy.wait_send()


def lanes(j):
    return slice(j * 128, (j + 1) * 128)


def bottom(v):
    return jnp.broadcast_to(v[7:8], v.shape)


def top(v):
    return jnp.broadcast_to(v[0:1], v.shape)


def masks_down(keep, place_in):
    m1 = jnp.where(place_in >= 1, keep, 0.0)
    m2 = m1 * pltpu.roll(m1, 1, 0)
    m4 = m2 * pltpu.roll(m2, 2, 0)
    for n in (1, 2, 4):
        keep = keep * jnp.where(place_in >= n, pltpu.roll(keep, n, 0), 1.0)
    return m1, m2, m4, keep


def masks_up(after, place_in):
    m1 = jnp.where(place_in <= 6, after, 0.0)
    m2 = m1 * pltpu.roll(m1, 7, 0)
    m4 = m2 * pltpu.roll(m2, 6, 0)
    for n in (1, 2, 4):
        after = after * jnp.where(place_in <= 7 - n, pltpu.roll(after, 8 - n, 0), 1.0)
    return m1, m2, m4, after


def wkv_forward(k_ref, v_ref, r_ref, keep_ref, rows_ref, mixed_ref, sn_ref, sd_ref):
    length, width = k_ref.shape
    tiles = width // 128
    place_in = lax.broadcasted_iota(jnp.int32, (8, 128), 0)
    first = place_in == 0
    zero = jnp.zeros((8, 128), F32)

    def pair(g, carry):
        carry = list(carry)
        base = pl.multiple_of(g * 16, 16)
        keeps = [keep_ref[pl.ds(base + 8 * h, 8), :] for h in range(2)]
        masks = [masks_down(keep, place_in) for keep in keeps]
        for j in range(tiles):
            d1, d2, d4, eu = (rows_ref[n : n + 1, lanes(j)] for n in range(4))
            dp = rows_ref[8:16, lanes(j)]
            made = []
            for h in range(2):
                at = pl.ds(base + 8 * h, 8)
                keep, (m1, m2, m4, mp) = keeps[h], masks[h]
                ek = jnp.exp(k_ref[at, lanes(j)])
                v = v_ref[at, lanes(j)]
                num, den = ek * v, ek
                x, b = num, eu * ek
                for n, coef in ((1, m1 * d1), (2, m2 * d2), (4, m4 * d4)):
                    num = num + coef * pltpu.roll(num, n, 0)
                    den = den + coef * pltpu.roll(den, n, 0)
                coef = mp * dp
                cn, cd = carry[2 * j], carry[2 * j + 1]
                num = num + coef * cn
                den = den + coef * cd
                sn = keep * jnp.where(first, cn, pltpu.roll(num, 1, 0))
                sd = keep * jnp.where(first, cd, pltpu.roll(den, 1, 0))
                carry[2 * j], carry[2 * j + 1] = bottom(num), bottom(den)
                sn_ref[at, lanes(j)] = sn
                sd_ref[at, lanes(j)] = sd
                weighted = (sn + eu * x) / (sd + b)
                made.append(jax.nn.sigmoid(r_ref[at, lanes(j)]) * weighted)
            mixed_ref[pl.ds(base, 16), lanes(j)] = jnp.concatenate(made, axis=0).astype(BF16)
        return tuple(carry)

    lax.fori_loop(0, length // 16, pair, (zero,) * (2 * tiles))


def wkv_backward(
    g_ref, k_ref, v_ref, r_ref, sn_ref, sd_ref, keep_ref, rows_ref, gk_ref, gv_ref, gr_ref, begin, end, carry
):
    length, width = k_ref.shape
    tiles = width // 128
    place_in = lax.broadcasted_iota(jnp.int32, (8, 128), 0)
    last = place_in == 7
    zero = jnp.zeros((8, 128), F32)
    pairs = length // 16

    def pair(step, carry):
        carry = list(carry)
        base = pl.multiple_of((pairs - 1 - step) * 16, 16)
        low, high = (keep_ref[pl.ds(base + 8 * h, 8), :] for h in range(2))
        afters = [
            jnp.where(last, top(high), pltpu.roll(low, 7, 0)),
            jnp.where(last, carry[4 * tiles], pltpu.roll(high, 7, 0)),
        ]
        masks = [masks_up(after, place_in) for after in afters]
        carry[4 * tiles] = top(low)
        for j in range(tiles):
            d1, d2, d4, eu = (rows_ref[n : n + 1, lanes(j)] for n in range(4))
            dp = rows_ref[16:24, lanes(j)]
            made = [None, None]
            for h in (1, 0):
                at = pl.ds(base + 8 * h, 8)
                after, (m1, m2, m4, mp) = afters[h], masks[h]
                ek = jnp.exp(k_ref[at, lanes(j)])
                v = v_ref[at, lanes(j)]
                sn, sd = sn_ref[at, lanes(j)], sd_ref[at, lanes(j)]
                s = jax.nn.sigmoid(r_ref[at, lanes(j)])
                b = eu * ek
                inverse = 1.0 / (sd + b)
                weighted = (sn + b * v) * inverse
                g = g_ref[at, lanes(j)]
                gs = g * s
                p = gs * inverse
                q = -p * weighted
                gr = gs * weighted * (1.0 - s)
                hp, hq = p, q
                for n, coef in ((1, m1 * d1), (2, m2 * d2), (4, m4 * d4)):
                    hp = hp + coef * pltpu.roll(hp, 8 - n, 0)
                    hq = hq + coef * pltpu.roll(hq, 8 - n, 0)
                coef = mp * dp
                cp, cq = carry[4 * j], carry[4 * j + 1]
                hp = hp + coef * cp
                hq = hq + coef * cq
                ap = after * jnp.where(last, cp, pltpu.roll(hp, 7, 0))
                aq = after * jnp.where(last, cq, pltpu.roll(hq, 7, 0))
                carry[4 * j], carry[4 * j + 1] = top(hp), top(hq)
                bonus = b * (v * p + q)
                gv = ek * ap + b * p
                gk = ek * (v * ap + aq) + bonus
                carry[4 * j + 2] = carry[4 * j + 2] + bonus
                carry[4 * j + 3] = carry[4 * j + 3] + (ap * sn + aq * sd)
                made[h] = (gk, gv, gr)
            both = pl.ds(base, 16)
            for n, ref in enumerate((gk_ref, gv_ref, gr_ref)):
                ref[both, lanes(j)] = jnp.concatenate([made[0][n], made[1][n]], axis=0).astype(BF16)
        return tuple(carry)

    return lax.fori_loop(begin, end, pair, (zero,) * (4 * tiles + 1) if carry is None else carry)


def wkv_sums(carry, rows_ref, decay_ref, bonus_ref):
    for j in range(decay_ref.shape[1] // 128):
        bonus_ref[0:1, lanes(j)] = jnp.sum(carry[4 * j + 2], axis=0, keepdims=True)
        decay_ref[0:1, lanes(j)] = -rows_ref[4:5, lanes(j)] * jnp.sum(carry[4 * j + 3], axis=0, keepdims=True)


NN, NT, TN = ((1,), (0,)), ((1,), (1,)), ((0,), (0,))
KEY, VALUE, GATE, EMIT, GATE2, FFN = 0, 1, 2, 3, 4, 5
KEYS, VALUES = (5, 7, 9, 11), (6, 8, 10, 12)
RINGS = 11
VECTORS = 11
TILE = 64
GAIN1, BIAS1, GAIN2, BIAS2, FADE, REWARD, MK1, MV1, MR1, MK2, MR2, OWN_FADE, OWN_REWARD = range(13)


def dot(a, b, dims):
    return lax.dot_general(a, b, (dims, ((), ())), preferred_element_type=F32)


def over_rows(length, size, body):
    def step(i, carry):
        body(strip(i, size))
        return carry

    lax.fori_loop(0, length // size, step, 0)


def matrix(ref):
    return ref[...].reshape(16 * ref.shape[2], ref.shape[3])


def emit_half(ref, h):
    rows = ref.shape[2] // 2
    return ref[:, :, h * rows : (h + 1) * rows, :].reshape(16 * rows, ref.shape[3])


def wide(column, width):
    return jnp.concatenate([column] * (width // 128), axis=1)


def norm(x):
    center = x - jnp.mean(x, axis=-1, keepdims=True)
    inverse = lax.rsqrt(jnp.mean(center * center, axis=-1, keepdims=True) + 1e-05)
    return center * inverse, inverse


def norm_and_mix(length, width, load, gain, bias, keep_ref, mixes, outs):
    first = lax.broadcasted_iota(jnp.int32, (TILE, width), 0) == 0

    def step(i, before):
        at = strip(i, TILE)
        unit, _ = norm(load(at))
        normed = unit * gain + bias
        prev = jnp.where(first, before, pltpu.roll(normed, 1, 0)) * wide(keep_ref[at, :], width)
        differ = normed - prev
        for share, out in zip(mixes, outs):
            out[at, :] = (prev + differ * share).astype(BF16)
        return normed[TILE - 1 : TILE]

    lax.fori_loop(0, length // TILE, step, jnp.zeros((1, width), F32))


def unweave(ref, own, other, c):
    at = lax.broadcasted_iota(jnp.int32, (ref.shape[0], 128), 1) // 32
    for t in range(own.shape[1] // 128):
        a, b = ref[:, lanes(2 * t)].astype(F32), ref[:, lanes(2 * t + 1)].astype(F32)
        a3, a2, b2, b1 = pltpu.roll(a, 96, 1), pltpu.roll(a, 64, 1), pltpu.roll(b, 64, 1), pltpu.roll(b, 32, 1)
        first = jnp.where(at == 0, a, jnp.where(at == 1, a3, jnp.where(at == 2, b2, b1)))
        second = jnp.where(at == 0, a3, jnp.where(at == 1, a2, jnp.where(at == 2, b1, b)))
        own[:, lanes(t)] = jnp.where(c == 0, first, second).astype(BF16)
        other[:, lanes(t)] = jnp.where(c == 0, second, first).astype(BF16)


def weave(a, b, out):
    at = lax.broadcasted_iota(jnp.int32, (out.shape[0], 128), 1) // 32
    for t in range(out.shape[1] // 128):
        p, q = a[:, lanes(t // 2)], b[:, lanes(t // 2)]
        if t % 2 == 0:
            turned = (p, pltpu.roll(q, 32, 1), pltpu.roll(p, 32, 1), pltpu.roll(q, 64, 1))
        else:
            turned = (pltpu.roll(p, 64, 1), pltpu.roll(q, 96, 1), pltpu.roll(p, 96, 1), q)
        out[:, lanes(t)] = jnp.where(
            at == 0, turned[0], jnp.where(at == 1, turned[1], jnp.where(at == 2, turned[2], turned[3]))
        )


def forward_kernel(
    wk, wv, wr, wg, wo, fk, fvt, vec, x_own, up_own, keep_own,
    g_out, out, x_out, up_out, ins_out, kvr_out, sn_out, sd_out, mixed_out, resid_out, ins2_out, pre_out, act_out,
    gv_out, gr_out, vec_out, rows_out, keep_out,
    own3, other3, gv, g, x, up, ins, kvr, sn, sd, mixed, sum_own, sum_other, resid, ins2, pre, act, v_send, v_other, gval, grec, low_half,
    local_sem, ex_send, ex_recv, sends, recvs, lsends, lrecvs, vsends, vrecvs, out_sem, sum_send, sum_recv, val_send, val_recv,
):
    z, yx, c = place()
    length, width = x.shape
    half = width // 2
    span = length // 2
    partner = (z * 4 + yx, 1 - c)
    for n, ref in enumerate((wk, wv, wr)):
        unweave(ref, own3.at[n], other3.at[n], c)
    enter(z, yx, c)

    block = wk.shape[0]
    mine = strip(c, block)
    rows_mine = strip(c, span)
    swaps = [
        (vec, gv.at[z, yx, c]),
        (other3, g.at[0:3, z, yx, mine]),
        (wg.at[:, strip(1 - c, half)], g.at[GATE2, z, yx, mine]),
        (x_own, x.at[rows_mine]),
        (keep_own, keep_out.at[rows_mine]),
        (up_own, up.at[rows_mine]),
    ]
    swaps = [remote(a, b, ex_send.at[n], ex_recv.at[n], partner) for n, (a, b) in enumerate(swaps)]
    keeps = [
        (vec, gv.at[z, yx, c]),
        (own3, g.at[0:3, z, yx, mine]),
        (wg.at[:, strip(c, half)], g.at[GATE2, z, yx, mine]),
        (x_own, x.at[rows_mine]),
        (keep_own, keep_out.at[rows_mine]),
        (up_own, up.at[rows_mine]),
    ]
    for h in range(2):
        keeps.append((wo.at[:, h * half : (h + 1) * half], g.at[EMIT, z, yx, h * block : (h + 1) * block]))
    for n in range(4):
        chunk = slice(n * half, (n + 1) * half)
        keeps.append((fk.at[:, chunk], g.at[KEYS[n], z, yx]))
        keeps.append((fvt.at[:, chunk], g.at[VALUES[n], z, yx]))
    keeps = [pltpu.make_async_copy(a, b, local_sem.at[n]) for n, (a, b) in enumerate(keeps)]
    for copy in swaps + keeps:
        copy.start()
    weights = Gather(lambda p: g.at[p], sends, recvs)
    lines = GatherLine(lambda p: g.at[RINGS + p], lsends, lrecvs)
    vectors = Gather(lambda p: gv, vsends, vrecvs)

    outs = []

    def put(src, dst):
        copy = pltpu.make_async_copy(src, dst, out_sem.at[len(outs)])
        copy.start()
        outs.append(copy)
        return copy

    along_z = {4: [(0, 1)], 5: [(1, 1)], 6: [(0, 2)], 7: [(1, 2)], 8: [(0, 3)], 9: [(1, 3)]}

    def turn(n):
        if n < RINGS:
            weights.step(n)
            if n + 2 < RINGS:
                weights.start(weights.along(n + 2))
        if 1 <= n <= RINGS:
            weights.forward(n - 1)
        for p, k in along_z.get(n, []):
            lines.line(p, k)
        if n >= 2:
            weights.arrive(weights.onward(n - 2))
            put(g.at[n - 2], g_out.at[n - 2])

    def lined(p):
        lines.ready(p - RINGS)
        put(g.at[p], g_out.at[p])

    for copy in keeps[6:]:
        copy.wait()
    for p in range(PIECES - RINGS):
        lines.start(lines.ring(p))
    for n in (0, 1, 2):
        swaps[n].wait()
        keeps[n].wait()
    vectors.start(vectors.along(0))
    weights.start(weights.along(0))
    weights.start(weights.along(1))
    for p in range(PIECES - RINGS):
        lines.arrive(lines.ring(p))
        lines.start(lines.onward(p))
    vectors.step(0)
    turn(0)
    vectors.forward(0)
    for n in (3, 4, 5):
        swaps[n].wait()
        keeps[n].wait()
    x_copy, up_copy = put(x, x_out), put(up, up_out)
    for p in range(PIECES - RINGS):
        lines.arrive(lines.onward(p))
    turn(1)
    vectors.arrive(vectors.onward(0))

    for t in range(width // 128):
        parts = [gv[(2 * t + k) // 4, (2 * t + k) % 4, core].astype(F32) for k in range(2) for core in range(2)]
        vec_out[:, lanes(t)] = functools.reduce(lambda a, b: a + b, parts)
    ramp = lax.broadcasted_iota(jnp.int32, (8, 128), 0).astype(F32)
    for t in range(half // 128):
        own = functools.reduce(lambda a, b: a + b, [gv[t, k, c].astype(F32) for k in range(4)])
        rate = jnp.exp(own[OWN_FADE : OWN_FADE + 1])
        head = [
            jnp.exp(-rate), jnp.exp(-2.0 * rate), jnp.exp(-4.0 * rate), jnp.exp(own[OWN_REWARD : OWN_REWARD + 1]),
            rate * jnp.exp(-rate),
        ]
        for n, row in enumerate(head):
            rows_out[n : n + 1, lanes(t)] = row
        rows_out[8:16, lanes(t)] = jnp.exp(-(ramp + 1.0) * rate)
        rows_out[16:24, lanes(t)] = jnp.exp(-(8.0 - ramp) * rate)

    def row(n):
        return vec_out[n : n + 1, :]

    norm_and_mix(
        length, width, lambda at: x[at, :].astype(F32), row(GAIN1), row(BIAS1), keep_out,
        [row(MK1), row(MV1), row(MR1)], [ins.at[n] for n in range(3)],
    )
    put(ins, ins_out)
    kvr_copies = []
    for n in range(3):
        turn(n + 2)
        weight = g.at[n]

        def project(at):
            kvr[n, at, :] = dot(ins[n, at, :], matrix(weight), NN)

        over_rows(length, 256, project)
        kvr_copies.append(put(kvr.at[n], kvr_out.at[n]))
    wkv_forward(kvr.at[0], kvr.at[1], kvr.at[2], keep_out, rows_out, mixed, sn, sd)
    put(mixed, mixed_out)
    put(sn, sn_out)
    put(sd, sd_out)
    turn(5)
    weight = g.at[EMIT]
    quarters = length // 4

    def emitted(n):
        at = strip(n, quarters)
        return remote(sum_own.at[at], sum_other.at[at], sum_send.at[n], sum_recv.at[n], partner)

    def emit(n, carry):
        at = strip(n, quarters)
        for h in range(2):
            sum_own[at, h * half : (h + 1) * half] = dot(mixed[at, :], emit_half(weight, h), NN).astype(BF16)
        emitted(n).start()
        return carry

    lax.fori_loop(0, 4, emit, 0)
    turn(6)
    for n in range(4):
        emitted(n).wait()

    def add_up(at):
        total = x[at, :].astype(F32) + (sum_own[at, :].astype(F32) + sum_other[at, :].astype(F32))
        resid[0, at, :] = total[:, :half]
        resid[1, at, :] = total[:, half:]
        return total

    norm_and_mix(
        length, width, add_up, row(GAIN2), row(BIAS2), keep_out, [row(MK2), row(MR2)], [ins2.at[n] for n in range(2)]
    )
    put(resid, resid_out)
    put(ins2, ins2_out)
    for copy in kvr_copies:
        copy.wait()
    weight = g.at[GATE2]

    def gate(at):
        kvr[2, at, :] = jax.nn.sigmoid(dot(ins2[1, at, :], matrix(weight), NN))

    over_rows(length, 256, gate)
    pre_copies = []

    def expand_chunk(j):
        weight, slot = g.at[KEYS[j]], len(pre_copies) % 2
        if len(pre_copies) >= 2:
            pre_copies[-2].wait()

        def expand(at):
            positive = jnp.maximum(dot(ins2[0, at, :], matrix(weight), NN), 0.0)
            pre[slot, at, :] = positive.astype(BF16)
            act[j, at, :] = (positive * positive).astype(BF16)

        over_rows(length, 256, expand)
        pre_copies.append(put(pre.at[slot], pre_out.at[j]))
        put(act.at[j], act_out.at[j])

    def contract_chunk(j):
        weight = g.at[VALUES[j]]

        def contract(at):
            for h in range(2):
                part = dot(act[j, at, :], weight[2 * h : 2 * h + 2].reshape(half, -1), NT)
                kvr[h, at, :] = part if j == 0 else kvr[h, at, :] + part

        over_rows(length, 256, contract)

    turn(7)
    expand_chunk(0)
    turn(8)
    contract_chunk(0)
    turn(9)
    expand_chunk(1)
    turn(10)
    contract_chunk(1)
    lined(KEYS[3])
    expand_chunk(3)
    lined(VALUES[3])
    contract_chunk(3)
    turn(11)
    expand_chunk(2)
    turn(12)
    contract_chunk(2)

    columns = strip(c, half)

    def value_copy(n):
        at = strip(n, quarters)
        return remote(v_send.at[at], v_other.at[at], val_send.at[n], val_recv.at[n], partner)

    def back_copy(n):
        at = strip(n, quarters)
        return remote(gval.at[c, at], gval.at[c, at], val_send.at[4 + n], val_recv.at[4 + n], partner)

    def send_values(n, carry):
        def narrow(i, carry):
            at = strip(n * (quarters // 32) + i, 32)
            v_send[at, :] = kvr[1 - c, at, :].astype(BF16)
            return carry

        lax.fori_loop(0, quarters // 32, narrow, 0)
        value_copy(n).start()
        return carry

    def finish_values(n, carry):
        value_copy(n).wait()

        def finish(i, carry):
            at = strip(n * (quarters // 32) + i, 32)
            value = kvr[c, at, :] + v_other[at, :].astype(F32)
            s = kvr[2, at, :]
            low_half[at, :] = (resid[c, at, :] + s * value).astype(BF16)
            upstream = up[at, columns].astype(F32)
            gval[c, at, :] = (upstream * s).astype(BF16)
            grec[at, :] = (upstream * value * s * (1.0 - s)).astype(BF16)
            return carry

        lax.fori_loop(0, quarters // 32, finish, 0)
        back_copy(n).start()
        return carry

    lax.fori_loop(0, 4, send_values, 0)
    lax.fori_loop(0, 4, finish_values, 0)
    give = remote(low_half.at[strip(1 - c, span)], out.at[:, columns], val_send.at[8], val_recv.at[8], partner)
    give.start()
    put(low_half.at[rows_mine], out.at[:, columns])
    put(grec, gr_out)
    for n in range(4):
        back_copy(n).wait()
    put(gval, gv_out)
    give.wait()

    def close(p, carry):
        weights.finish(p)
        return carry

    lax.fori_loop(0, RINGS, close, 0)
    for p in range(PIECES - RINGS):
        lines.finish(p)
    vectors.finish(0)
    waited = kvr_copies + pre_copies[:2]
    for copy in outs:
        if not any(copy is other for other in waited):
            copy.wait()


def forward_call(wk, wv, wr, wg, wo, fk, fvt, vec, x_own, up_own, keep_own):
    span, width = x_own.shape
    length, half = 2 * span, width // 2
    block = (fk.shape[0], half)
    any_, vmem = pl.BlockSpec(memory_space=pl.ANY), pl.BlockSpec(memory_space=pltpu.VMEM)
    full, col = (length, width), (length, half)

    def shape(dims, kind):
        return jax.ShapeDtypeStruct(dims, kind)

    outs = (
        (shape((PIECES, 4, 4) + block, BF16), any_),
        (shape((span, width), BF16), any_),
        (shape(full, BF16), any_),
        (shape(full, BF16), any_),
        (shape((3,) + full, BF16), any_),
        (shape((3,) + col, F32), any_),
        (shape(col, F32), any_),
        (shape(col, F32), any_),
        (shape(col, BF16), any_),
        (shape((2,) + col, F32), any_),
        (shape((2,) + full, BF16), any_),
        (shape((4,) + col, BF16), any_),
        (shape((4,) + col, BF16), any_),
        (shape((2,) + col, BF16), any_),
        (shape(col, BF16), any_),
        (shape((16, width), F32), vmem),
        (shape((24, half), F32), vmem),
        (shape((length, 128), F32), vmem),
    )
    dma = pltpu.SemaphoreType.DMA
    return pl.pallas_call(
        forward_kernel,
        out_shape=tuple(o[0] for o in outs),
        in_specs=[vmem] * 11,
        out_specs=tuple(o[1] for o in outs),
        scratch_shapes=[
            pltpu.VMEM((3, block[0] // 2, half), BF16),
            pltpu.VMEM((3, block[0] // 2, half), BF16),
            pltpu.VMEM((4, 4, 2) + vec.shape, BF16),
            pltpu.VMEM((PIECES, 4, 4) + block, BF16),
            pltpu.VMEM(full, BF16),
            pltpu.VMEM(full, BF16),
            pltpu.VMEM((3,) + full, BF16),
            pltpu.VMEM((3,) + col, F32),
            pltpu.VMEM(col, F32),
            pltpu.VMEM(col, F32),
            pltpu.VMEM(col, BF16),
            pltpu.VMEM(full, BF16),
            pltpu.VMEM(full, BF16),
            pltpu.VMEM((2,) + col, F32),
            pltpu.VMEM((2,) + full, BF16),
            pltpu.VMEM((2,) + col, BF16),
            pltpu.VMEM((4,) + col, BF16),
            pltpu.VMEM(col, BF16),
            pltpu.VMEM(col, BF16),
            pltpu.VMEM((2,) + col, BF16),
            pltpu.VMEM(col, BF16),
            pltpu.VMEM(col, BF16),
            dma((16,)), dma((6,)), dma((6,)),
            dma((RINGS, 7)), dma((RINGS, 7)), dma((PIECES - RINGS, 10)), dma((PIECES - RINGS, 10)), dma((1, 7)), dma((1, 7)),
            dma((40,)), dma((4,)), dma((4,)), dma((9,)), dma((9,)),
        ],
        compiler_params=pltpu.CompilerParams(
            collective_id=0, has_side_effects=True, vmem_limit_bytes=63 * MIB
        ),
        name="forward",
    )(wk, wv, wr, wg, wo, fk, fvt, vec, x_own, up_own, keep_own)


R_VALUE, R_KEY, R_GATE2, R_EMIT, R_TIME = 0, 4, 8, 9, 10
WEIGHT_ORDER = [p for j in range(4) for p in (VALUES[j], KEYS[j])] + [GATE2, EMIT, KEY, VALUE, GATE]
LINED = (1, 3, 5)
SUMS = 11
S_GAIN1, S_BIAS1, S_GAIN2, S_BIAS2, S_DECAY, S_BONUS, S_MK1, S_MV1, S_MR1, S_MK2, S_MR2 = range(11)
SLOTS = 12


def whole(ref, at):
    return jnp.concatenate([ref[0, at, :], ref[1, at, :]], axis=1)


def halves(ref, at, value):
    half = value.shape[1] // 2
    ref[0, at, :] = value[:, :half].astype(ref.dtype)
    ref[1, at, :] = value[:, half:].astype(ref.dtype)


def fold(value):
    return sum(value[n : n + 8] for n in range(8, value.shape[0], 8)) + value[:8]


def back_through_norm(g, unit, inverse, gain):
    q = g * gain
    return inverse * (
        q - jnp.mean(q, axis=-1, keepdims=True) - unit * jnp.mean(q * unit, axis=-1, keepdims=True)
    )


def lifted(now, following, last):
    return jnp.where(last, following[0:1], pltpu.roll(now, now.shape[0] - 1, 0))


def backward_kernel(
    plan,
    g, x_in, up_in, ins_in, kvr_in, sn_in, sd_in, mixed_in, resid_in, ins2_in, pre_in, act_in, gv_in, gr_in,
    vec, rows, keep,
    out_k, out_v, out_r, out_g, out_o, out_fk, out_fv, vsum, vother, gtok,
    own_t, recv_t, own_g,
    part, ring1, ring2, line, lring1, lring2, lline, vpart, vring1, vring2, vline,
    b, w, f, resid, sum_other, n1_other, acc, own_sums,
    load_sem, w_sem, sends, recvs, lsends, lrecvs, vsends, vrecvs, ex_send, ex_recv, sum_send, sum_recv,
):
    z, yx, c = place()
    nx, ny, nd, zs = neighbours(z, yx)
    length, half = b.shape[1:]
    width = 2 * half
    span = length // 2
    quarter = length // 4
    partner = (z * 4 + yx, 1 - c)
    loads = {}

    def load(name, src, dst):
        copy = pltpu.make_async_copy(src, dst, load_sem.at[len(loads)])
        copy.start()
        loads[name] = copy

    def loaded(*names):
        for name in names:
            loads[name].wait()

    def pair(n):
        return b.at[n : n + 2]

    def load_pair(name, src, n):
        for h in range(2):
            load((name, h), src.at[:, h * half : (h + 1) * half], b.at[n + h])

    def loaded_pair(name):
        loaded((name, 0), (name, 1))

    def weight_copy(n):
        return pltpu.make_async_copy(g.at[WEIGHT_ORDER[n]], w.at[n % 3], w_sem.at[n])

    def weight(n):
        weight_copy(n).wait()
        return w.at[n % 3]

    GVAL, ACT, PRE, IN_K2, IN_R2, GREC, GPRE = 0, 2, 4, 6, 8, 10, 11
    load("gv0", gv_in.at[0], b.at[GVAL])
    load("gv1", gv_in.at[1], b.at[GVAL + 1])
    for j in range(2):
        load(("act", j), act_in.at[j], b.at[ACT + j])
    load_pair("in_k2", ins2_in.at[0], IN_K2)
    for j in range(2):
        load(("pre", j), pre_in.at[j], b.at[PRE + j])
    for n in range(3):
        weight_copy(n).start()
    load_pair("in_r2", ins2_in.at[1], IN_R2)
    load("gr", gr_in, b.at[GREC])
    load("resid", resid_in, resid)
    enter(z, yx, c)

    columns = strip(c, half)
    outs = {R_GATE2: [own_g], R_EMIT: [out_o.at[:, h * half : (h + 1) * half] for h in range(2)]}
    for n in range(4):
        chunk = slice(n * half, (n + 1) * half)
        outs[R_VALUE + n], outs[R_KEY + n] = [out_fv.at[:, chunk]], [out_fk.at[:, chunk]]
    for n in range(3):
        outs[R_TIME + n] = [own_t.at[n]]
    sums = []
    for p in range(PIECES):
        if p in LINED:
            n = LINED.index(p)
            sums.append(
                ReduceLine(
                    part, p % PARTS, lring1.at[n], lring2.at[n], lline.at[n], outs[p], lsends.at[n], lrecvs.at[n]
                )
            )
        else:
            n = p - sum(q < p for q in LINED)
            sums.append(
                Reduce(part, p % PARTS, ring1.at[n], ring2.at[n], line.at[n], outs[p], sends.at[n], recvs.at[n])
            )
    vector_sums = Reduce(vpart, 0, vring1, vring2, vline, [vsum], vsends, vrecvs)
    final = []
    rows4 = recv_t.shape[1]
    mine, others = strip(c, rows4), strip(1 - c, rows4)

    def pump(name):
        for stage, p in plan[name]:
            if p == "v":
                getattr(vector_sums, "stage%d" % stage)()
                continue
            getattr(sums[p], "stage%d" % stage)()
            if stage == 4 and p in (R_GATE2, R_TIME, R_TIME + 1, R_TIME + 2):
                n = len(final)
                if p == R_GATE2:
                    src, dst = own_g.at[others], out_g.at[:, columns]
                else:
                    src, dst = own_t.at[p - R_TIME, others], recv_t.at[p - R_TIME]
                final.append(remote(src, dst, ex_send.at[n], ex_recv.at[n], partner))
                final[-1].start()

    def gradient(p, lhs, rhs):
        def block(a, carry):
            rows_a = dot(lhs[a // 2, :, strip(a % 2, half // 2)], rhs[...], TN)
            part[p % PARTS, a] = rows_a.astype(BF16).reshape(part.shape[2:])
            return carry

        lax.fori_loop(0, 4, block, 0)

    def thirds(ref, h):
        return ref[2 * h : 2 * h + 2].reshape(half, half)

    loaded("gv0", "gv1")
    for j in range(4):
        loaded(("act", j))
        gradient(R_VALUE + j, pair(GVAL), b.at[ACT + j % 2])
        if j < 2:
            load(("act", j + 2), act_in.at[j + 2], b.at[ACT + j])
        pump("fv%d" % j)
    loaded_pair("in_k2")
    for j in range(4):
        loaded(("pre", j))
        value_w = weight(2 * j)

        def through(at):
            g_hidden = sum(dot(b[GVAL + h, at, :], thirds(value_w, h), NN) for h in range(2))
            b[GPRE, at, :] = (2.0 * b[PRE + j % 2, at, :].astype(F32) * g_hidden).astype(BF16)

        over_rows(length, 256, through)
        pump("th%d" % j)
        if j < 2:
            load(("pre", j + 2), pre_in.at[j + 2], b.at[PRE + j])
        weight_copy(2 * j + 3).start()
        gradient(R_KEY + j, pair(IN_K2), b.at[GPRE])
        pump("fk%d" % j)
        key_w = weight(2 * j + 1)

        def collect(at):
            for h in range(2):
                piece = dot(b[GPRE, at, :], thirds(key_w, h), NT)
                f[h, at, :] = piece if j == 0 else f[h, at, :] + piece

        over_rows(length, 256, collect)
        pump("co%d" % j)
        weight_copy(2 * j + 4).start()
    loaded_pair("in_r2")
    loaded("gr")
    gradient(R_GATE2, pair(IN_R2), b.at[GREC])
    pump("g2")
    gate_w = weight(8)

    def gate_back(at):
        for h in range(2):
            f[2 + h, at, :] = dot(b[GREC, at, :], thirds(gate_w, h), NT)

    over_rows(length, 256, gate_back)
    pump("gb")
    weight_copy(11).start()
    loaded("resid")

    SUM_OWN, UP, BRANCH, MIXED, G3, X, IN_K, IN_V, IN_R, SEND = 0, 2, 4, 6, 7, 4, 10, 0, 2, 6
    load_pair("up", up_in, UP)
    load("mixed", mixed_in, b.at[MIXED])
    acc[...] = jnp.zeros_like(acc)
    last = lax.broadcasted_iota(jnp.int32, (TILE, width), 0) == TILE - 1

    def row(n):
        return vec[n : n + 1, :]

    def kept(at, n):
        return wide(keep[at, :], width) if n is None else wide(keep[n, :], width)

    gain2, bias2, mk2, mr2 = (GAIN2, BIAS2, MK2, MR2)
    sum_copies = []
    for q in range(4):

        def tile(i, carry):
            base = q * quarter + i * TILE
            at = pl.ds(pl.multiple_of(base, TILE), TILE)
            after = pl.ds(pl.multiple_of(jnp.minimum(base + TILE, length - 8), 8), 8)
            inside = jnp.where(base + TILE < length, 1.0, 0.0)
            keep_at, keep_after = wide(keep[at, :], width), wide(keep[after, :], width) * inside
            unit, _ = norm(whole(resid, at))
            normed = unit * row(gain2) + row(bias2)
            total = jnp.zeros_like(unit)
            for n, share in enumerate((mk2, mr2)):
                back = whole(f.at[2 * n : 2 * n + 2], at)
                ahead = lifted(back * keep_at, whole(f.at[2 * n : 2 * n + 2], after) * keep_after, last)
                total = total + ahead + (back - ahead) * row(share)
                acc[S_MK2 + n] = acc[S_MK2 + n] + fold(normed * (back - ahead))
            acc[S_GAIN2] = acc[S_GAIN2] + fold(total * unit)
            acc[S_BIAS2] = acc[S_BIAS2] + fold(total)
            halves(b.at[SUM_OWN : SUM_OWN + 2], at, total)
            return carry

        lax.fori_loop(0, quarter // TILE, tile, 0)
        at = pl.ds(q * quarter, quarter)
        sum_copies.append(
            remote(b.at[SUM_OWN : SUM_OWN + 2, at], sum_other.at[:, at], sum_send.at[q], sum_recv.at[q], partner)
        )
        sum_copies[-1].start()
        pump("a%d" % q)
    for n in range(3):
        load(("kvr", n), kvr_in.at[n], f.at[n])
    load("sn", sn_in, f.at[3])
    load("sd", sd_in, f.at[4])
    load_pair("in_k", ins_in.at[0], IN_K)

    loaded_pair("up")
    for q in range(4):
        sum_copies[q].wait_recv()

        def tile(i, carry):
            at = pl.ds(pl.multiple_of(q * quarter + i * TILE, TILE), TILE)
            unit, inverse = norm(whole(resid, at))
            total = whole(b.at[SUM_OWN : SUM_OWN + 2], at).astype(F32) + whole(sum_other, at).astype(F32)
            back = whole(pair(UP), at).astype(F32) + back_through_norm(total, unit, inverse, row(gain2))
            halves(pair(BRANCH), at, back)

            @pl.when(c == q // 2)
            def _():
                gtok[pl.ds(pl.multiple_of((q % 2) * quarter + i * TILE, TILE), TILE), :] = back

            return carry

        lax.fori_loop(0, quarter // TILE, tile, 0)
        pump("b%d" % q)
    for copy in sum_copies:
        copy.wait_send()
    load_pair("in_v", ins_in.at[1], IN_V)
    load_pair("in_r", ins_in.at[2], IN_R)

    loaded("mixed")
    rows_h = part.shape[3] // 2
    for h in range(2):

        def emit_rows(a, carry):
            block = dot(b[MIXED, :, strip(a, half // 2)], b[BRANCH + h], TN).astype(BF16)
            part[R_EMIT, pl.ds(2 * a, 2), :, h * rows_h : (h + 1) * rows_h, :] = block.reshape(2, 4, rows_h, half)
            return carry

        lax.fori_loop(0, 2, emit_rows, 0)
    pump("em")
    emit_w = weight(9)

    def emit_back(at):
        resid[0, at, :] = sum(dot(b[BRANCH + h, at, :], emit_half(emit_w, h), NT) for h in range(2))

    over_rows(length, 256, emit_back)
    pump("eb")
    weight_copy(12).start()
    load_pair("x", x_in, X)

    loaded(("kvr", 0), ("kvr", 1), ("kvr", 2), "sn", "sd")
    carry = None
    for q in range(4):
        carry = wkv_backward(
            resid.at[0], f.at[0], f.at[1], f.at[2], f.at[3], f.at[4], keep, rows, b.at[G3], b.at[G3 + 1], b.at[G3 + 2],
            q * (length // 64), (q + 1) * (length // 64), carry,
        )
        pump("w%d" % q)
    wkv_sums(carry, rows, own_sums.at[0:1], own_sums.at[1:2])

    for n, (name, slot) in enumerate((("in_k", IN_K), ("in_v", IN_V), ("in_r", IN_R))):
        loaded_pair(name)
        sums[R_TIME + n - PARTS].finish()
        gradient(R_TIME + n, pair(slot), b.at[G3 + n])
        pump("t%d" % n)
    loaded_pair("x")
    for n in range(3):
        weight(10 + n)
    for n in range(3):
        for h in range(2):
            f[n, pl.ds(h * span + quarter, 8), :] = jnp.zeros((8, half), F32)
    n1_copies = []
    for q in (3, 2, 1, 0):
        def back_rows(n, carry):
            for h in range(2):
                if q < 3:
                    f[n, pl.ds(h * span + quarter, 8), :] = f[n, pl.ds(h * span, 8), :]
                f[n, pl.ds(h * span, quarter), :] = dot(
                    b[G3 + n, pl.ds(q * quarter, quarter), :], thirds(w.at[(n + 1) % 3], h), NT
                )
            return carry

        lax.fori_loop(0, 3, back_rows, 0)

        def tile(i, carry):
            base = q * quarter + i * TILE
            at = pl.ds(pl.multiple_of(base, TILE), TILE)
            after = pl.ds(pl.multiple_of(jnp.minimum(base + TILE, length - 8), 8), 8)
            keep_at, keep_after = wide(keep[at, :], width), wide(keep[after, :], width)

            def take(n, start, size):
                return jnp.concatenate(
                    [f[n, pl.ds(pl.multiple_of(h * span + start, 8), size), :] for h in range(2)], axis=1
                )

            unit, _ = norm(whole(pair(X), at).astype(F32))
            normed = unit * row(GAIN1) + row(BIAS1)
            total = jnp.zeros_like(unit)
            for n, share in enumerate((MK1, MV1, MR1)):
                back = take(n, i * TILE, TILE)
                ahead = lifted(back * keep_at, take(n, i * TILE + TILE, 8) * keep_after, last)
                total = total + ahead + (back - ahead) * row(share)
                acc[S_MK1 + n] = acc[S_MK1 + n] + fold(normed * (back - ahead))
            acc[S_GAIN1] = acc[S_GAIN1] + fold(total * unit)
            acc[S_BIAS1] = acc[S_BIAS1] + fold(total)
            rows_q = [pl.ds(pl.multiple_of(h * span + (q % 2) * quarter + i * TILE, TILE), TILE) for h in range(2)]

            @pl.when(c == q // 2)
            def _():
                for h in range(2):
                    f[3, rows_q[h], :] = total[:, h * half : (h + 1) * half]

            @pl.when(c != q // 2)
            def _():
                for h in range(2):
                    b[SEND, rows_q[h], :] = total[:, h * half : (h + 1) * half].astype(BF16)

            return carry

        lax.fori_loop(0, quarter // TILE, tile, 0)
        pump("c%d" % (3 - q))
    swap_n1 = remote(b.at[SEND], n1_other, sum_send.at[4], sum_recv.at[4], partner)
    swap_n1.start()

    for n in (S_GAIN1, S_BIAS1, S_GAIN2, S_BIAS2, S_MK1, S_MV1, S_MR1, S_MK2, S_MR2):
        acc[n, 0:1, :] = jnp.sum(acc[n], axis=0, keepdims=True)
    for i in range(16):
        vpart[0, i // 4, i % 4] = jnp.concatenate(
            [acc[n, 0:1, lanes(i // 2)] for n in range(SUMS)]
            + [own_sums[n : n + 1, lanes(i // 4)] for n in range(2)]
            + [jnp.zeros((3, 128), F32)]
        )
    pump("v0")
    swap_n1.wait()

    def tokens(i, carry):
        at = strip(i, TILE)
        spans = [pl.ds(pl.multiple_of(h * span + i * TILE, TILE), TILE) for h in range(2)]
        unit, inverse = norm(whole(pair(X), pl.ds(pl.multiple_of(c * span + i * TILE, TILE), TILE)).astype(F32))
        total = jnp.concatenate([f[3, s, :] + n1_other[s, :].astype(F32) for s in spans], axis=1)
        gtok[at, :] = gtok[at, :] + back_through_norm(total, unit, inverse, row(GAIN1))
        return carry

    lax.fori_loop(0, span // TILE, tokens, 0)
    for n in range(1, 4):
        pump("v%d" % n)
    swap = remote(vsum, vother, ex_send.at[4], ex_recv.at[4], partner)
    swap.start()
    pump("end")
    for p in range(PIECES - PARTS, PIECES):
        sums[p].finish()
    vector_sums.finish()
    out_g[:, columns] = own_g[mine, :]
    for copy in final + [swap]:
        copy.wait()
    for n, out in enumerate((out_k, out_v, out_r)):
        own, other = own_t[n, mine, :], recv_t[n]
        weave(jnp.where(c == 0, own, other), jnp.where(c == 0, other, own), out)


PLAN = {
    "fv0": [(1, 0)],
    "fv1": [(1, 1)],
    "fv2": [(1, 2)],
    "fv3": [(1, 3), (2, 0)],
    "th0": [],
    "fk0": [(1, 4), (2, 2), (2, 1)],
    "co0": [],
    "th1": [],
    "fk1": [(1, 5), (3, 0), (2, 3)],
    "co1": [(2, 4)],
    "th2": [(3, 1)],
    "fk2": [(1, 6), (3, 2)],
    "co2": [],
    "th3": [(2, 5)],
    "fk3": [(1, 7), (3, 4)],
    "co3": [(2, 6), (4, 0)],
    "g2": [(1, 8), (2, 7)],
    "gb": [],
    "a0": [(3, 3)],
    "a1": [],
    "a2": [(3, 6)],
    "a3": [(4, 1), (2, 8)],
    "b0": [(3, 7), (5, 1), (4, 2)],
    "b1": [],
    "b2": [],
    "b3": [(3, 5), (3, 8)],
    "em": [(1, 9), (6, 1)],
    "eb": [],
    "w0": [(4, 4)],
    "w1": [(2, 9)],
    "w2": [(4, 3)],
    "w3": [],
    "t0": [(1, 10)],
    "t1": [(1, 11), (5, 3), (3, 9), (4, 6)],
    "t2": [(1, 12)],
    "c0": [(2, 10), (2, 11), (6, 3), (4, 7)],
    "c1": [(4, 5), (2, 12)],
    "c2": [(3, 10), (4, 8)],
    "c3": [],
    "v0": [(1, "v"), (3, 11), (5, 5)],
    "v1": [(2, "v"), (4, 9), (4, 10), (3, 12)],
    "v2": [(3, "v"), (6, 5), (4, 11)],
    "v3": [(4, "v")],
    "end": [(4, 12)],
}


def backward_call(g, x, up, ins, kvr, sn, sd, mixed, resid, ins2, pre, act, g_value, g_recept, vec, rows, keep):
    block = g.shape[3:]
    length, half = sn.shape
    lined = len(LINED)
    rings = PIECES - lined
    any_, vmem = pl.BlockSpec(memory_space=pl.ANY), pl.BlockSpec(memory_space=pltpu.VMEM)
    dma = pltpu.SemaphoreType.DMA

    def shape(*dims):
        return jax.ShapeDtypeStruct(dims, F32)

    return pl.pallas_call(
        functools.partial(backward_kernel, PLAN),
        out_shape=(
            *[shape(block[0] // 2, 2 * half)] * 5, *[shape(block[0], 4 * half)] * 2, shape(16, 128), shape(16, 128),
            shape(length // 2, 2 * half),
        ),
        in_specs=[any_] * 14 + [vmem] * 3,
        out_specs=(vmem,) * 10,
        scratch_shapes=[
            pltpu.VMEM((3,) + block, F32),
            pltpu.VMEM((3, block[0] // 2, block[1]), F32),
            pltpu.VMEM(block, F32),
            pltpu.VMEM((PARTS, 4, 4) + block, BF16),
            pltpu.VMEM((rings, 2, 2) + block, BF16),
            pltpu.VMEM((rings, 2, 4) + block, BF16),
            pltpu.VMEM((rings, 3) + block, BF16),
            pltpu.VMEM((lined, 2, block[0] // 2, block[1]), BF16),
            pltpu.VMEM((lined, 2) + block, BF16),
            pltpu.VMEM((lined, 5, 4) + block, BF16),
            pltpu.VMEM((1, 4, 4, 16, 128), F32),
            pltpu.VMEM((2, 2, 16, 128), F32),
            pltpu.VMEM((2, 4, 16, 128), F32),
            pltpu.VMEM((3, 16, 128), F32),
            pltpu.VMEM((SLOTS, length, half), BF16),
            pltpu.VMEM((3, 4, 4) + block, BF16),
            pltpu.VMEM((5, length, half), F32),
            pltpu.VMEM((2, length, half), F32),
            pltpu.VMEM((2, length, half), BF16),
            pltpu.VMEM((length, half), BF16),
            pltpu.VMEM((SUMS, 8, 2 * half), F32),
            pltpu.VMEM((8, half), F32),
            dma((40,)), dma((PIECES,)), dma((rings, 7)), dma((rings, 7)), dma((lined, 10)), dma((lined, 10)),
            dma((7,)), dma((7,)), dma((5,)), dma((5,)), dma((5,)), dma((5,)),
        ],
        compiler_params=pltpu.CompilerParams(collective_id=1, has_side_effects=True, vmem_limit_bytes=63 * MIB),
        name="backward",
    )(g, x, up, ins, kvr, sn, sd, mixed, resid, ins2, pre, act, g_value, g_recept, vec, rows, keep)


def shifted(value, axis, steps):
    count = lax.axis_size(axis)
    first, last = (max(0, -steps), min(count, count - steps))
    return lax.ppermute(value, axis, [(source, source + steps) for source in range(first, last)])


def carried_in(array, axis, join, neutral):
    place = lax.axis_index(axis)
    gathered = jax.tree.map(
        lambda a, kind: lax.all_gather(a.astype(kind), axis),
        array,
        (jnp.bfloat16, jnp.bfloat16, jnp.bfloat16),
    )
    state = jax.tree.map(lambda a, e: jnp.zeros_like(a) + jnp.asarray(e, a.dtype), array, neutral)

    def one(turn, state):
        return join(
            state,
            jax.tree.map(
                lambda a, own: lax.dynamic_index_in_dim(a, turn, 0, False).astype(own.dtype),
                gathered,
                array,
            ),
        )

    return lax.fori_loop(0, place, one, state)


def entering(array, axis, combine, identity):
    count, place = (lax.axis_size(axis), lax.axis_index(axis))
    everything = jax.tree.map(
        lambda part, kind: lax.all_gather(part.astype(kind), axis),
        array,
        jax.tree.map(lambda a: jnp.bfloat16 if a.dtype == jnp.float32 else a.dtype, array),
    )
    start = jax.tree.map(
        lambda part, zero: jnp.broadcast_to(jnp.asarray(zero, part.dtype), part.shape),
        array,
        identity,
    )

    def turn(k, before):
        at = count - 1 - k
        reached = at > place
        new = combine(
            before, jax.tree.map(lambda part, own: part[at].astype(own.dtype), everything, array)
        )
        return jax.tree.map(lambda a, b: jnp.where(reached, a, b), new, before)

    return lax.fori_loop(0, count, turn, start)


def wide_layer_norm(values, scale_vec, shift_vec):
    center = values - jnp.mean(values, axis=-1, keepdims=True)
    inverse = lax.rsqrt(jnp.mean(center * center, axis=-1, keepdims=True) + 1e-05)
    normed = center * inverse
    return (normed * scale_vec + shift_vec, normed, inverse)


def wide_norm_back(upstream, normed, inverse, scale_vec):
    scaled = upstream * scale_vec
    inner = (
        scaled
        - jnp.mean(scaled, axis=-1, keepdims=True)
        - normed * jnp.mean(scaled * normed, axis=-1, keepdims=True)
    )
    return (
        inverse * inner,
        jnp.sum(upstream * normed, axis=(0, 1)),
        jnp.sum(upstream, axis=(0, 1)),
    )


def shift_prev(values, persist_indicator):
    arrived = shifted(values[:, -1:, :], "tensor", 1)
    return jnp.concatenate([arrived, values[:, :-1]], axis=1) * persist_indicator[:, :, None]


def shift_back(upstream, persist_indicator):
    masked = upstream * persist_indicator[:, :, None]
    arrived = shifted(masked[:, :1, :], "tensor", -1)
    return jnp.concatenate([masked[:, 1:], arrived], axis=1)


def project(values, matrix):
    return jnp.einsum("rtd,de->rte", values, matrix, preferred_element_type=jnp.float32)


def project_back(upstream, matrix):
    return jnp.einsum("rte,de->rtd", upstream, matrix, preferred_element_type=jnp.float32)


def outer_sum(values, upstream):
    return jnp.einsum("rtd,rte->de", values, upstream, preferred_element_type=jnp.float32)


def mix_back(upstreams, shares, differ, persist_indicator):
    toward = jnp.zeros_like(differ)
    behind = jnp.zeros_like(differ)
    share_grads = []
    for upstream, share in zip(upstreams, shares):
        toward = toward + upstream * share
        behind = behind + upstream * (1.0 - share)
        share_grads.append(jnp.sum(upstream * differ, axis=(0, 1)))
    return (toward + shift_back(behind, persist_indicator), share_grads)


def chain_combine(earlier, later):
    return (
        earlier[0] * later[0],
        later[0] * earlier[1] + later[1],
        later[0] * earlier[2] + later[2],
    )


def scan_fragments(
    lookup_wide, payload_wide, fading_power, reward_coords, text_boundary_indicators
):
    decay_rate = jnp.exp(fading_power)
    row_count, span_len, width_len = lookup_wide.shape
    block_len = min(32, span_len)
    block_count = span_len // block_len
    places = jnp.arange(block_len, dtype=jnp.float32)
    rising = jnp.exp(places[:, None] * decay_rate)
    falling = jnp.exp(-(places[:, None] - 1.0) * decay_rate)
    trailing = jnp.exp(-(block_len - 1.0 - places)[:, None] * decay_rate)
    leading = jnp.exp(-places[:, None] * decay_rate)
    settle = jnp.exp(-block_len * decay_rate)
    before = places[:, None] > places[None, :]

    def split_blocks(values):
        return jnp.swapaxes(
            values.reshape((row_count, block_count, block_len) + values.shape[2:]), 0, 1
        )

    def advance(state_pair, scanned):
        accrued_dividend_sum, accrued_divisor_sum = state_pair
        lookup_narrow, payload_narrow, reset_b = scanned
        tree_levels = jnp.cumsum(reset_b, axis=1)
        linked = ((tree_levels[:, :, None] == tree_levels[:, None, :]) & before).astype(jnp.float32)
        key_term = jnp.exp(lookup_narrow)
        keyed_value = key_term * payload_narrow
        inside_numerator = falling * jnp.einsum(
            "rti,rid->rtd", linked, rising * keyed_value, precision=lax.Precision.HIGHEST
        )
        interior_divisor_sum = falling * jnp.einsum(
            "rti,rid->rtd", linked, rising * key_term, precision=lax.Precision.HIGHEST
        )
        leftover_multiplier = (tree_levels == 0).astype(jnp.float32)[:, :, None] * leading
        reward_multiplier = jnp.exp(reward_coords + lookup_narrow)
        above_total = (
            inside_numerator
            + reward_multiplier * payload_narrow
            + leftover_multiplier * accrued_dividend_sum[:, None, :]
        )
        below_total = (
            interior_divisor_sum
            + reward_multiplier
            + leftover_multiplier * accrued_divisor_sum[:, None, :]
        )
        ending = (tree_levels == tree_levels[:, -1:]).astype(jnp.float32)[:, :, None] * trailing
        intact = (tree_levels[:, -1] == 0).astype(jnp.float32)[:, None] * settle
        new_num = intact * accrued_dividend_sum + jnp.sum(ending * keyed_value, axis=1)
        new_den = intact * accrued_divisor_sum + jnp.sum(ending * key_term, axis=1)
        return ((new_num, new_den), (above_total, below_total))

    initial = jnp.zeros((row_count, width_len), jnp.float32)
    (total_num, total_den), (uppers, lowers) = lax.scan(
        advance,
        (initial, initial),
        (
            split_blocks(lookup_wide),
            split_blocks(payload_wide),
            split_blocks(text_boundary_indicators),
        ),
    )

    def join_blocks(values):
        return jnp.swapaxes(values, 0, 1).reshape(row_count, span_len, width_len)

    tree_levels = jnp.cumsum(text_boundary_indicators, axis=1)
    reaching = (tree_levels == 0).astype(jnp.float32)[:, :, None] * jnp.exp(
        -jnp.arange(span_len, dtype=jnp.float32)[:, None] * decay_rate
    )
    passing = (tree_levels[:, -1] == 0).astype(jnp.float32)[:, None] * jnp.exp(
        -span_len * decay_rate
    )
    return (join_blocks(uppers), join_blocks(lowers), reaching, total_num, total_den, passing)


def recurrence_finish(pieces_list, incoming_num, incoming_den):
    above_total = pieces_list[0] + pieces_list[2] * incoming_num[:, None, :]
    below_total = pieces_list[1] + pieces_list[2] * incoming_den[:, None, :]
    return (above_total / below_total, below_total)


def ffn_apply(inputs, key_weight, value_weight):
    hidden_pre = project(inputs, key_weight)
    hidden = jnp.square(jax.nn.relu(hidden_pre)).astype(jnp.bfloat16)
    return (hidden_pre, hidden, project(hidden, value_weight))


def ffn_grads(inputs, hidden_pre, hidden, upstream, key_weight, value_weight):
    g_hidden = jnp.einsum("rtd,fd->rtf", upstream, value_weight, preferred_element_type=jnp.float32)
    grad_value = jnp.einsum("rtf,rtd->fd", hidden, upstream, preferred_element_type=jnp.float32)
    g_pre = (2.0 * jax.nn.relu(hidden_pre) * g_hidden).astype(jnp.bfloat16)
    grad_key = jnp.einsum("rtd,rtf->df", inputs, g_pre, preferred_element_type=jnp.float32)
    g_inputs = jnp.einsum("rtf,df->rtd", g_pre, key_weight, preferred_element_type=jnp.float32)
    return (g_inputs, grad_key, grad_value)


def wide_shards(
    incoming_embeddings,
    text_boundary_indicators,
    upstream_sensitivity,
    primary_standardize_scaling,
    primary_standardize_offset,
    secondary_standardize_scaling,
    secondary_standardize_offset,
    feature_fading_logarithms,
    present_symbol_reward,
    timemix_lookup_blend,
    timemix_payload_blend,
    timemix_gate_blend,
    timemix_lookup_proj,
    timemix_payload_proj,
    timemix_gate_proj,
    timemix_emit_proj,
    feedmix_lookup_blend,
    feedmix_gate_blend,
    feedmix_gate_proj,
    feedmix_lookup_proj,
    feedmix_payload_proj,
):
    gathered_portions = (
        lax.all_gather(primary_standardize_scaling, ("dp", "tensor"), axis=0, tiled=True),
        lax.all_gather(primary_standardize_offset, ("dp", "tensor"), axis=0, tiled=True),
        lax.all_gather(secondary_standardize_scaling, ("dp", "tensor"), axis=0, tiled=True),
        lax.all_gather(secondary_standardize_offset, ("dp", "tensor"), axis=0, tiled=True),
        lax.all_gather(feature_fading_logarithms, ("dp", "tensor"), axis=0, tiled=True),
        lax.all_gather(present_symbol_reward, ("dp", "tensor"), axis=0, tiled=True),
        lax.all_gather(timemix_lookup_blend, ("dp", "tensor"), axis=0, tiled=True),
        lax.all_gather(timemix_payload_blend, ("dp", "tensor"), axis=0, tiled=True),
        lax.all_gather(timemix_gate_blend, ("dp", "tensor"), axis=0, tiled=True),
        lax.all_gather(timemix_lookup_proj, ("dp", "tensor"), axis=0, tiled=True),
        lax.all_gather(timemix_payload_proj, ("dp", "tensor"), axis=0, tiled=True),
        lax.all_gather(timemix_gate_proj, ("dp", "tensor"), axis=0, tiled=True),
        lax.all_gather(timemix_emit_proj, ("dp", "tensor"), axis=0, tiled=True),
        lax.all_gather(feedmix_lookup_blend, ("dp", "tensor"), axis=0, tiled=True),
        lax.all_gather(feedmix_gate_blend, ("dp", "tensor"), axis=0, tiled=True),
        lax.all_gather(feedmix_gate_proj, ("dp", "tensor"), axis=0, tiled=True),
    )
    initial_scaling_coords = gathered_portions[0].astype(jnp.float32)
    initial_offset_coords = gathered_portions[1].astype(jnp.float32)
    later_scaling_coords = gathered_portions[2].astype(jnp.float32)
    later_offset_coords = gathered_portions[3].astype(jnp.float32)
    fading_power = gathered_portions[4].astype(jnp.float32)
    reward_coords = gathered_portions[5].astype(jnp.float32)
    share_k1 = gathered_portions[6].astype(jnp.float32)
    share_v1 = gathered_portions[7].astype(jnp.float32)
    share_r1 = gathered_portions[8].astype(jnp.float32)
    lookup_coefficients_initial = gathered_portions[9]
    payload_coefficients_initial = gathered_portions[10]
    gate_coefficients_initial = gathered_portions[11]
    emit_coefficients_initial = gathered_portions[12]
    share_k2 = gathered_portions[13].astype(jnp.float32)
    share_r2 = gathered_portions[14].astype(jnp.float32)
    gate_coefficients_later = gathered_portions[15]
    lookup_coefficients_later, payload_coefficients_later = (
        lax.all_gather(feedmix_lookup_proj, "dp", axis=0, tiled=True),
        lax.all_gather(feedmix_payload_proj, "dp", axis=1, tiled=True),
    )
    persist_indicator = (1 - text_boundary_indicators).astype(jnp.float32)
    inputs = incoming_embeddings.astype(jnp.float32)
    normed_one, unit_one, inverse_one = wide_layer_norm(
        inputs, initial_scaling_coords, initial_offset_coords
    )
    prev_one = shift_prev(normed_one, persist_indicator)
    differ_one = normed_one - prev_one
    in_key = (prev_one + differ_one * share_k1).astype(jnp.bfloat16)
    in_value = (prev_one + differ_one * share_v1).astype(jnp.bfloat16)
    in_recept = (prev_one + differ_one * share_r1).astype(jnp.bfloat16)
    initial_lookup_lines = project(in_key, lookup_coefficients_initial)
    initial_payload_lines = project(in_value, payload_coefficients_initial)
    recept_one = project(in_recept, gate_coefficients_initial)
    pieces_list = scan_fragments(
        initial_lookup_lines,
        initial_payload_lines,
        fading_power,
        reward_coords,
        text_boundary_indicators,
    )
    passing = pieces_list[5]
    identity = (jnp.ones_like(passing), jnp.zeros_like(passing), jnp.zeros_like(passing))
    unused_item, incoming_num, incoming_den = carried_in(
        (passing, pieces_list[3], pieces_list[4]), "tensor", chain_combine, identity
    )
    blended_mean_state, below_total = recurrence_finish(pieces_list, incoming_num, incoming_den)
    sig_one = jax.nn.sigmoid(recept_one)
    mixed_att = (sig_one * blended_mean_state).astype(jnp.bfloat16)
    resid_one = inputs + project(mixed_att, emit_coefficients_initial)
    normed_two, unit_two, inverse_two = wide_layer_norm(
        resid_one, later_scaling_coords, later_offset_coords
    )
    prev_two = shift_prev(normed_two, persist_indicator)
    differ_two = normed_two - prev_two
    in_key_two = (prev_two + differ_two * share_k2).astype(jnp.bfloat16)
    in_recept_two = (prev_two + differ_two * share_r2).astype(jnp.bfloat16)
    recept_two = project(in_recept_two, gate_coefficients_later)
    sig_two = jax.nn.sigmoid(recept_two)
    row_inputs = lax.all_gather(in_key_two, "tensor", axis=1, tiled=True)
    hidden_pre, hidden, partial_value = ffn_apply(
        row_inputs, lookup_coefficients_later, payload_coefficients_later
    )
    value_two = lax.psum_scatter(
        partial_value.astype(jnp.bfloat16), "tensor", scatter_dimension=1, tiled=True
    ).astype(jnp.float32)
    layer_out = (resid_one + sig_two * value_two).astype(jnp.bfloat16)
    upstream = upstream_sensitivity.astype(jnp.float32)
    g_value_two = (upstream * sig_two).astype(jnp.bfloat16)
    g_recept_two = (upstream * value_two * sig_two * (1.0 - sig_two)).astype(jnp.bfloat16)
    grad_recept_two = outer_sum(in_recept_two, g_recept_two)
    g_mix_r2 = project_back(g_recept_two, gate_coefficients_later)
    row_grads = lax.all_gather(g_value_two, "tensor", axis=1, tiled=True)
    partial_grad, grad_key_two, grad_value_two = ffn_grads(
        row_inputs,
        hidden_pre,
        hidden,
        row_grads,
        lookup_coefficients_later,
        payload_coefficients_later,
    )
    g_mix_k2 = lax.psum_scatter(
        partial_grad.astype(jnp.bfloat16), "tensor", scatter_dimension=1, tiled=True
    ).astype(jnp.float32)
    sum_key_two, sum_value_two = (
        lax.psum_scatter(
            grad_key_two.astype(jnp.bfloat16), "dp", scatter_dimension=0, tiled=True
        ).astype(jnp.float32),
        lax.psum_scatter(
            grad_value_two.astype(jnp.bfloat16), "dp", scatter_dimension=1, tiled=True
        ).astype(jnp.float32),
    )
    g_normed_two, shares_two = mix_back(
        (g_mix_k2, g_mix_r2), (share_k2, share_r2), differ_two, persist_indicator
    )
    g_resid_part, grad_gain_two, grad_bias_two = wide_norm_back(
        g_normed_two, unit_two, inverse_two, later_scaling_coords
    )
    g_resid = upstream + g_resid_part
    g_branch = g_resid.astype(jnp.bfloat16)
    grad_out_one = outer_sum(mixed_att, g_branch)
    g_mixed = project_back(g_branch, emit_coefficients_initial)
    g_weighted = g_mixed * sig_one
    g_recept_one = (g_mixed * blended_mean_state * sig_one * (1.0 - sig_one)).astype(jnp.bfloat16)
    reaching = pieces_list[2]
    g_in_num = jnp.sum(g_weighted * reaching / below_total, axis=1)
    g_in_den = -jnp.sum(g_weighted * reaching * blended_mean_state / below_total, axis=1)
    unused_item, back_num, back_den = entering(
        (passing, g_in_num, g_in_den), "tensor", chain_combine, identity
    )
    g_passing = back_num * incoming_num + back_den * incoming_den

    def device_fragment(lookup_wide, payload_wide, fading_coords, reward_power):
        shard_pieces = scan_fragments(
            lookup_wide, payload_wide, fading_coords, reward_power, text_boundary_indicators
        )
        local_out, unused_item = recurrence_finish(shard_pieces, incoming_num, incoming_den)
        return (local_out, shard_pieces[3], shard_pieces[4], shard_pieces[5])

    unused_item, reverse_pass_rule = jax.vjp(
        device_fragment, initial_lookup_lines, initial_payload_lines, fading_power, reward_coords
    )
    derivative_lookup_wide, derivative_payload_wide, fading_derivative, reward_derivative = (
        reverse_pass_rule((g_weighted, back_num, back_den, g_passing))
    )
    g_key_one = derivative_lookup_wide.astype(jnp.bfloat16)
    g_value_one = derivative_payload_wide.astype(jnp.bfloat16)
    grad_key_one = outer_sum(in_key, g_key_one)
    grad_value_one = outer_sum(in_value, g_value_one)
    grad_recept_one = outer_sum(in_recept, g_recept_one)
    g_mix_k1 = project_back(g_key_one, lookup_coefficients_initial)
    g_mix_v1 = project_back(g_value_one, payload_coefficients_initial)
    g_mix_r1 = project_back(g_recept_one, gate_coefficients_initial)
    g_normed_one, shares_one = mix_back(
        (g_mix_k1, g_mix_v1, g_mix_r1),
        (share_k1, share_v1, share_r1),
        differ_one,
        persist_indicator,
    )
    g_input_part, grad_gain_one, grad_bias_one = wide_norm_back(
        g_normed_one, unit_one, inverse_one, initial_scaling_coords
    )
    grad_tokens = g_resid + g_input_part
    summed = (
        lax.psum_scatter(grad_gain_one, ("dp", "tensor"), scatter_dimension=0, tiled=True),
        lax.psum_scatter(grad_bias_one, ("dp", "tensor"), scatter_dimension=0, tiled=True),
        lax.psum_scatter(grad_gain_two, ("dp", "tensor"), scatter_dimension=0, tiled=True),
        lax.psum_scatter(grad_bias_two, ("dp", "tensor"), scatter_dimension=0, tiled=True),
        lax.psum_scatter(fading_derivative, ("dp", "tensor"), scatter_dimension=0, tiled=True),
        lax.psum_scatter(reward_derivative, ("dp", "tensor"), scatter_dimension=0, tiled=True),
        lax.psum_scatter(shares_one[0], ("dp", "tensor"), scatter_dimension=0, tiled=True),
        lax.psum_scatter(shares_one[1], ("dp", "tensor"), scatter_dimension=0, tiled=True),
        lax.psum_scatter(shares_one[2], ("dp", "tensor"), scatter_dimension=0, tiled=True),
        lax.psum_scatter(grad_key_one, ("dp", "tensor"), scatter_dimension=0, tiled=True),
        lax.psum_scatter(grad_value_one, ("dp", "tensor"), scatter_dimension=0, tiled=True),
        lax.psum_scatter(grad_recept_one, ("dp", "tensor"), scatter_dimension=0, tiled=True),
        lax.psum_scatter(grad_out_one, ("dp", "tensor"), scatter_dimension=0, tiled=True),
        lax.psum_scatter(shares_two[0], ("dp", "tensor"), scatter_dimension=0, tiled=True),
        lax.psum_scatter(shares_two[1], ("dp", "tensor"), scatter_dimension=0, tiled=True),
        lax.psum_scatter(grad_recept_two, ("dp", "tensor"), scatter_dimension=0, tiled=True),
    )
    return (
        layer_out,
        grad_tokens,
        summed[0],
        summed[1],
        summed[2],
        summed[3],
        summed[4],
        summed[5],
        summed[6],
        summed[7],
        summed[8],
        summed[9],
        summed[10],
        summed[11],
        summed[12],
        summed[13],
        summed[14],
        summed[15],
        sum_key_two,
        sum_value_two,
    )


def pack(tokens, starts, upstream, gain1, bias1, gain2, bias2, fading, reward, mk1, mv1, mr1, wk, wv, wr, wo, mk2, mr2, wg, fk, fv):
    i, c = lax.axis_index("dp"), lax.axis_index("tensor")
    own_rows = wk.shape[0]
    slots = 128 // own_rows
    everywhere = jnp.stack([gain1, bias1, gain2, bias2, fading, reward, mk1, mv1, mr1, mk2, mr2])
    own = jnp.stack([fading, reward, jnp.zeros_like(fading), jnp.zeros_like(fading), jnp.zeros_like(fading)])
    lane = jnp.arange(128)[None, :] // own_rows
    vec = jnp.concatenate([
        jnp.where(lane == (2 * i + c) % slots, jnp.tile(everywhere, (1, slots)), 0),
        jnp.where(lane == i % slots, jnp.tile(own, (1, slots)), 0),
    ]).astype(BF16)
    keep = jnp.broadcast_to((1 - starts[0]).astype(F32)[:, None], (starts.shape[1], 128))
    return wk, wv, wr, wg, wo, fk, fv.T, vec, tokens[0], upstream[0], keep


def shards(*args):
    c = lax.axis_index("tensor")
    i = lax.axis_index("dp")
    own_rows = args[12].shape[0]
    (
        g, layer_out, x, up, ins, kvr, sn, sd, mixed, resid, ins2, pre, act, g_value, g_recept2, vec, rows, keep,
    ) = forward_call(*pack(*args))

    out_k, out_v, out_r, out_g, out_o, out_fk, out_fv, vsum, vother, grad_tokens = backward_call(
        g, x, up, ins, kvr, sn, sd, mixed, resid, ins2, pre, act, g_value, g_recept2, vec, rows, keep
    )
    slots = 128 // own_rows
    vtotal = lax.dynamic_slice_in_dim(vsum + vother, (2 * i + c) % slots * own_rows, own_rows, 1)
    own_scan = lax.dynamic_slice_in_dim(vsum, i % slots * own_rows, own_rows, 1)
    return (
        layer_out[None], grad_tokens[None], *(vtotal[n] for n in range(4)), own_scan[SUMS], own_scan[SUMS + 1],
        *(vtotal[n] for n in range(6, 9)), out_k, out_v, out_r, out_o, vtotal[9], vtotal[10], out_g, out_fk, out_fv.T,
    )


def solution(mesh):
    row, vector, matrix_ = P("dp", "tensor", None), P(("dp", "tensor")), P(("dp", "tensor"), None)
    key, value = P("dp", "tensor"), P("tensor", "dp")
    in_specs = (row, P("dp", "tensor"), row) + (vector,) * 9 + (matrix_,) * 4 + (vector,) * 2 + (matrix_, key, value)
    out_specs = (row, row) + (vector,) * 9 + (matrix_,) * 4 + (vector,) * 2 + (matrix_, key, value)
    body = shards if (mesh.shape["dp"], mesh.shape["tensor"]) == (16, 2) else wide_shards
    return jax.shard_map(body, mesh=mesh, in_specs=in_specs, out_specs=out_specs, check_vma=False)
```

```python
import functools

import jax
import jax.numpy as jnp
from jax import lax
from jax.experimental import pallas as pl
from jax.experimental.pallas import tpu as pltpu
from jax.sharding import PartitionSpec as P

F32, BF16 = jnp.float32, jnp.bfloat16
MESH_ID = pl.DeviceIdType.MESH
MIB = 1 << 20
PARTS = 10
PIECES = 13


def place():
    i, c = lax.axis_index("dp"), lax.axis_index("tensor")
    return i // 4, i % 4, c


def neighbours(z, yx):
    x = yx + 1 - 2 * (yx % 2)
    y = (yx + 2) % 4
    d = (x + 2) % 4
    zs = (z + 1 - 2 * (z % 2), (z + 2) % 4, 3 - z)
    return x, y, d, zs


def enter(z, yx, c):
    x, y, d, zs = neighbours(z, yx)
    barrier = pltpu.get_barrier_semaphore()
    targets = [(z * 4 + yx, 1 - c), (z * 4 + x, c), (z * 4 + y, c)]
    targets += [(peer * 4 + yx, c) for peer in zs]
    for target in targets:
        pl.semaphore_signal(barrier, inc=1, device_id=target, device_id_type=MESH_ID)
    pl.semaphore_wait(barrier, len(targets))


def remote(src, dst, send, recv, target):
    return pltpu.make_async_remote_copy(
        src_ref=src, dst_ref=dst, send_sem=send, recv_sem=recv,
        device_id=target, device_id_type=MESH_ID,
    )


def strip(i, size):
    return pl.ds(pl.multiple_of(i * size, size), size)


class Gather:
    def __init__(self, view, sends, recvs, first=0):
        self.view, self.sends, self.recvs, self.first = view, sends, recvs, first
        self.z, self.yx, self.c = place()
        self.x, self.y, self.d, self.zs = neighbours(self.z, self.yx)

    def to(self, z, yx):
        return (z * 4 + yx, self.c)

    def copy(self, p, k, ref, target):
        return remote(ref, ref, self.sends.at[p, k], self.recvs.at[p, k], target)

    def along(self, p):
        own = self.view(p).at[self.z, self.yx]
        return [self.copy(p, k, own, self.to(peer, self.yx)) for k, peer in enumerate(self.zs)]

    def plane(self, p):
        own = self.view(p).at[:, self.yx]
        return [self.copy(p, 3, own, self.to(self.z, self.x)), self.copy(p, 4, own, self.to(self.z, self.y))]

    def onward(self, p):
        return [
            self.copy(p, 5, self.view(p).at[0:2, self.x], self.to(self.z, self.y)),
            self.copy(p, 6, self.view(p).at[2:4, self.y], self.to(self.z, self.x)),
        ]

    def start(self, copies):
        for copy in copies:
            copy.start()

    def arrive(self, copies):
        for copy in copies:
            copy.wait_recv()

    def step(self, p):
        self.arrive(self.along(p))
        self.start(self.plane(p))

    def forward(self, p):
        self.arrive(self.plane(p))
        self.start(self.onward(p))

    def finish(self, p):
        for copy in self.along(p) + self.plane(p) + self.onward(p):
            copy.wait_send()


class GatherLine(Gather):
    def ring(self, p):
        own = self.view(p).at[self.z, self.yx]
        return [self.copy(p, 0, own, self.to(self.z, self.x)), self.copy(p, 1, own, self.to(self.z, self.y))]

    def onward(self, p):
        half = self.view(p).shape[2] // 2
        return [
            self.copy(p, 2, self.view(p).at[self.z, self.x, 0:half], self.to(self.z, self.y)),
            self.copy(p, 3, self.view(p).at[self.z, self.y, half:], self.to(self.z, self.x)),
        ]

    def climb(self, p, k, up, arriving):
        behind = k if arriving else k - 1
        plane = self.z - behind if up else self.z + behind
        beyond = self.z + 1 if up != arriving else self.z - 1
        real = (plane >= 0) & (plane <= 3) & (beyond >= 0) & (beyond <= 3)
        plane, beyond = jnp.clip(plane, 0, 3), jnp.clip(beyond, 0, 3)
        k = (4 if up else 7) + k - 1
        return real, self.copy(p, k, self.view(p).at[plane], self.to(beyond, self.yx))

    def each(self, p, k, arriving, action):
        for up in (True, False):
            real, copy = self.climb(p, k, up, arriving)
            pl.when(real)(functools.partial(action, copy))

    def line(self, p, k):
        if k > 1:
            self.each(p, k - 1, True, lambda copy: copy.wait_recv())
        self.each(p, k, False, lambda copy: copy.start())

    def ready(self, p):
        self.each(p, 3, True, lambda copy: copy.wait_recv())

    def finish(self, p):
        for copy in self.ring(p) + self.onward(p):
            copy.wait_send()
        for k in (1, 2, 3):
            self.each(p, k, False, lambda copy: copy.wait_send())


class Reduce:
    def __init__(self, part, slot, ring1, ring2, line, out, sends, recvs):
        self.parts, self.slot, self.ring1, self.ring2, self.line, self.out = part, slot, ring1, ring2, line, out
        self.sends, self.recvs = sends, recvs
        self.z, self.yx, self.c = place()
        self.x, self.y, self.d, self.zs = neighbours(self.z, self.yx)

    def copy(self, k, src, dst, z, yx):
        return remote(src, dst, self.sends.at[k], self.recvs.at[k], (z * 4 + yx, self.c))

    def part(self):
        return self.parts.at[self.slot]

    def diagonal(self):
        return [
            self.copy(0, self.part().at[0:2, self.d], self.ring1.at[0], self.z, self.x),
            self.copy(1, self.part().at[2:4, self.d], self.ring1.at[1], self.z, self.y),
        ]

    def side(self):
        return [
            self.copy(2, self.part().at[:, self.x], self.ring2.at[0], self.z, self.x),
            self.copy(3, self.part().at[:, self.y], self.ring2.at[1], self.z, self.y),
        ]

    def down(self):
        return [
            self.copy(4 + k, self.part().at[peer, self.yx], self.line.at[k], peer, self.yx)
            for k, peer in enumerate(self.zs)
        ]

    def start(self, copies):
        for copy in copies:
            copy.start()

    def arrive(self, copies):
        for copy in copies:
            copy.wait_recv()

    def add_up(self, own, others, result):
        def step(i, carry):
            at = strip(i, 16)
            total = own[at, :].astype(F32)
            for other in others:
                total = total + other[at, :].astype(F32)
            result[at, :] = total.astype(result.dtype)
            return carry

        lax.fori_loop(0, own.shape[0] // 16, step, 0)

    def add(self, a, yx, others):
        own = self.part().at[a, yx]
        self.add_up(own, others, own)

    def give(self, others):
        start = 0
        for out in self.out:
            rows = pl.ds(start, out.shape[0])
            own = self.part().at[self.z, self.yx, rows]
            self.add_up(own, [other.at[rows] for other in others], out)
            start += out.shape[0]

    def stage1(self):
        self.start(self.diagonal())

    def stage2(self):
        self.arrive(self.diagonal())

        def planes(a, carry):
            self.add(a, self.y, [self.ring1.at[0, a]])
            self.add(a + 2, self.x, [self.ring1.at[1, a]])
            return carry

        lax.fori_loop(0, 2, planes, 0)
        self.start(self.side())

    def stage3(self):
        self.arrive(self.side())

        def planes(a, carry):
            self.add(a, self.yx, [self.ring2.at[0, a], self.ring2.at[1, a]])
            return carry

        lax.fori_loop(0, 4, planes, 0)
        self.start(self.down())

    def stage4(self):
        self.arrive(self.down())
        self.give([self.line.at[k] for k in range(3)])

    def finish(self):
        for copy in self.diagonal() + self.side() + self.down():
            copy.wait_send()


class ReduceLine(Reduce):
    def step(self, k, up, arriving):
        z = self.z
        plane = (3 if arriving else 4) - k + z if up else k - (3 if arriving else 4) + z
        beyond = z + 1 if up != arriving else z - 1
        real = (plane >= 0) & (plane <= 3) & (beyond >= 0) & (beyond <= 3)
        plane, beyond = jnp.clip(plane, 0, 3), jnp.clip(beyond, 0, 3)
        place_in = plane + 1 if up else plane
        k = (3 if up else 0) + k - 1
        return real, plane, place_in, self.copy(k, self.part().at[plane], self.line.at[place_in], beyond, self.yx)

    def take(self, arrived, plane, place_in):
        arrived.wait_recv()

        def blocks(yx, carry):
            self.add(plane, yx, [self.line.at[place_in, yx]])
            return carry

        lax.fori_loop(0, 4, blocks, 0)

    def move(self, k):
        for up in (True, False):
            real, plane, _, leaving = self.step(k, up, False)
            if k > 1:
                came, _, place_in, arrived = self.step(k - 1, up, True)

                pl.when(real & came)(functools.partial(self.take, arrived, plane, place_in))

            pl.when(real)(leaving.start)

    def halves(self):
        half = self.ring1.shape[1]
        own = self.part().at[self.z, self.d]
        return [
            self.copy(6, own.at[0:half], self.ring1.at[0], self.z, self.x),
            self.copy(7, own.at[half:], self.ring1.at[1], self.z, self.y),
        ]

    def sides(self):
        return [
            self.copy(8, self.part().at[self.z, self.x], self.ring2.at[0], self.z, self.x),
            self.copy(9, self.part().at[self.z, self.y], self.ring2.at[1], self.z, self.y),
        ]

    def stage1(self):
        self.move(1)

    def stage2(self):
        self.move(2)

    def stage3(self):
        self.move(3)

    def stage4(self):
        for up in (True, False):
            came, plane, place_in, arrived = self.step(3, up, True)
            pl.when(came)(functools.partial(self.take, arrived, plane, place_in))

        self.start(self.halves())

    def stage5(self):
        self.arrive(self.halves())
        half = self.ring1.shape[1]
        for yx, start, piece in ((self.y, 0, 0), (self.x, half, 1)):
            own = self.part().at[self.z, yx, start : start + half]
            self.add_up(own, [self.ring1.at[piece]], own)
        self.start(self.sides())

    def stage6(self):
        self.arrive(self.sides())
        self.give([self.ring2.at[0], self.ring2.at[1]])

    def finish(self):
        for k in (1, 2, 3):
            for up in (True, False):
                real, _, _, leaving = self.step(k, up, False)
                pl.when(real)(leaving.wait_send)
        for copy in self.halves() + self.sides():
            copy.wait_send()


def lanes(j):
    return slice(j * 128, (j + 1) * 128)


def bottom(v):
    return jnp.broadcast_to(v[7:8], v.shape)


def top(v):
    return jnp.broadcast_to(v[0:1], v.shape)


def masks_down(keep, place_in):
    m1 = jnp.where(place_in >= 1, keep, 0.0)
    m2 = m1 * pltpu.roll(m1, 1, 0)
    m4 = m2 * pltpu.roll(m2, 2, 0)
    for n in (1, 2, 4):
        keep = keep * jnp.where(place_in >= n, pltpu.roll(keep, n, 0), 1.0)
    return m1, m2, m4, keep


def masks_up(after, place_in):
    m1 = jnp.where(place_in <= 6, after, 0.0)
    m2 = m1 * pltpu.roll(m1, 7, 0)
    m4 = m2 * pltpu.roll(m2, 6, 0)
    for n in (1, 2, 4):
        after = after * jnp.where(place_in <= 7 - n, pltpu.roll(after, 8 - n, 0), 1.0)
    return m1, m2, m4, after


def wkv_forward(k_ref, v_ref, r_ref, keep_ref, rows_ref, mixed_ref, sn_ref, sd_ref):
    length, width = k_ref.shape
    tiles = width // 128
    place_in = lax.broadcasted_iota(jnp.int32, (8, 128), 0)
    first = place_in == 0
    zero = jnp.zeros((8, 128), F32)

    def pair(g, carry):
        carry = list(carry)
        base = pl.multiple_of(g * 16, 16)
        keeps = [keep_ref[pl.ds(base + 8 * h, 8), :] for h in range(2)]
        masks = [masks_down(keep, place_in) for keep in keeps]
        for j in range(tiles):
            d1, d2, d4, eu = (rows_ref[n : n + 1, lanes(j)] for n in range(4))
            dp = rows_ref[8:16, lanes(j)]
            made = []
            for h in range(2):
                at = pl.ds(base + 8 * h, 8)
                keep, (m1, m2, m4, mp) = keeps[h], masks[h]
                ek = jnp.exp(k_ref[at, lanes(j)])
                v = v_ref[at, lanes(j)]
                num, den = ek * v, ek
                x, b = num, eu * ek
                for n, coef in ((1, m1 * d1), (2, m2 * d2), (4, m4 * d4)):
                    num = num + coef * pltpu.roll(num, n, 0)
                    den = den + coef * pltpu.roll(den, n, 0)
                coef = mp * dp
                cn, cd = carry[2 * j], carry[2 * j + 1]
                num = num + coef * cn
                den = den + coef * cd
                sn = keep * jnp.where(first, cn, pltpu.roll(num, 1, 0))
                sd = keep * jnp.where(first, cd, pltpu.roll(den, 1, 0))
                carry[2 * j], carry[2 * j + 1] = bottom(num), bottom(den)
                sn_ref[at, lanes(j)] = sn
                sd_ref[at, lanes(j)] = sd
                weighted = (sn + eu * x) / (sd + b)
                made.append(jax.nn.sigmoid(r_ref[at, lanes(j)]) * weighted)
            mixed_ref[pl.ds(base, 16), lanes(j)] = jnp.concatenate(made, axis=0).astype(BF16)
        return tuple(carry)

    lax.fori_loop(0, length // 16, pair, (zero,) * (2 * tiles))


def wkv_backward(
    g_ref, k_ref, v_ref, r_ref, sn_ref, sd_ref, keep_ref, rows_ref, gk_ref, gv_ref, gr_ref, begin, end, carry
):
    length, width = k_ref.shape
    tiles = width // 128
    place_in = lax.broadcasted_iota(jnp.int32, (8, 128), 0)
    last = place_in == 7
    zero = jnp.zeros((8, 128), F32)
    pairs = length // 16

    def pair(step, carry):
        carry = list(carry)
        base = pl.multiple_of((pairs - 1 - step) * 16, 16)
        low, high = (keep_ref[pl.ds(base + 8 * h, 8), :] for h in range(2))
        afters = [
            jnp.where(last, top(high), pltpu.roll(low, 7, 0)),
            jnp.where(last, carry[4 * tiles], pltpu.roll(high, 7, 0)),
        ]
        masks = [masks_up(after, place_in) for after in afters]
        carry[4 * tiles] = top(low)
        for j in range(tiles):
            d1, d2, d4, eu = (rows_ref[n : n + 1, lanes(j)] for n in range(4))
            dp = rows_ref[16:24, lanes(j)]
            made = [None, None]
            for h in (1, 0):
                at = pl.ds(base + 8 * h, 8)
                after, (m1, m2, m4, mp) = afters[h], masks[h]
                ek = jnp.exp(k_ref[at, lanes(j)])
                v = v_ref[at, lanes(j)]
                sn, sd = sn_ref[at, lanes(j)], sd_ref[at, lanes(j)]
                s = jax.nn.sigmoid(r_ref[at, lanes(j)])
                b = eu * ek
                inverse = 1.0 / (sd + b)
                weighted = (sn + b * v) * inverse
                g = g_ref[at, lanes(j)]
                gs = g * s
                p = gs * inverse
                q = -p * weighted
                gr = gs * weighted * (1.0 - s)
                hp, hq = p, q
                for n, coef in ((1, m1 * d1), (2, m2 * d2), (4, m4 * d4)):
                    hp = hp + coef * pltpu.roll(hp, 8 - n, 0)
                    hq = hq + coef * pltpu.roll(hq, 8 - n, 0)
                coef = mp * dp
                cp, cq = carry[4 * j], carry[4 * j + 1]
                hp = hp + coef * cp
                hq = hq + coef * cq
                ap = after * jnp.where(last, cp, pltpu.roll(hp, 7, 0))
                aq = after * jnp.where(last, cq, pltpu.roll(hq, 7, 0))
                carry[4 * j], carry[4 * j + 1] = top(hp), top(hq)
                bonus = b * (v * p + q)
                gv = ek * ap + b * p
                gk = ek * (v * ap + aq) + bonus
                carry[4 * j + 2] = carry[4 * j + 2] + bonus
                carry[4 * j + 3] = carry[4 * j + 3] + (ap * sn + aq * sd)
                made[h] = (gk, gv, gr)
            both = pl.ds(base, 16)
            for n, ref in enumerate((gk_ref, gv_ref, gr_ref)):
                ref[both, lanes(j)] = jnp.concatenate([made[0][n], made[1][n]], axis=0).astype(BF16)
        return tuple(carry)

    return lax.fori_loop(begin, end, pair, (zero,) * (4 * tiles + 1) if carry is None else carry)


def wkv_sums(carry, rows_ref, decay_ref, bonus_ref):
    for j in range(decay_ref.shape[1] // 128):
        bonus_ref[0:1, lanes(j)] = jnp.sum(carry[4 * j + 2], axis=0, keepdims=True)
        decay_ref[0:1, lanes(j)] = -rows_ref[4:5, lanes(j)] * jnp.sum(carry[4 * j + 3], axis=0, keepdims=True)


NN, NT, TN = ((1,), (0,)), ((1,), (1,)), ((0,), (0,))
KEY, VALUE, GATE, EMIT, GATE2, FFN = 0, 1, 2, 3, 4, 5
KEYS, VALUES = (5, 7, 9, 11), (6, 8, 10, 12)
RINGS = 11
VECTORS = 11
TILE = 64
GAIN1, BIAS1, GAIN2, BIAS2, FADE, REWARD, MK1, MV1, MR1, MK2, MR2, OWN_FADE, OWN_REWARD = range(13)


def dot(a, b, dims):
    return lax.dot_general(a, b, (dims, ((), ())), preferred_element_type=F32)


def over_rows(length, size, body):
    def step(i, carry):
        body(strip(i, size))
        return carry

    lax.fori_loop(0, length // size, step, 0)


def matrix(ref):
    return ref[...].reshape(16 * ref.shape[2], ref.shape[3])


def emit_half(ref, h):
    rows = ref.shape[2] // 2
    return ref[:, :, h * rows : (h + 1) * rows, :].reshape(16 * rows, ref.shape[3])


def wide(column, width):
    return jnp.concatenate([column] * (width // 128), axis=1)


def norm(x):
    center = x - jnp.mean(x, axis=-1, keepdims=True)
    inverse = lax.rsqrt(jnp.mean(center * center, axis=-1, keepdims=True) + 1e-05)
    return center * inverse, inverse


def norm_and_mix(length, width, load, gain, bias, keep_ref, mixes, outs):
    first = lax.broadcasted_iota(jnp.int32, (TILE, width), 0) == 0

    def step(i, before):
        at = strip(i, TILE)
        unit, _ = norm(load(at))
        normed = unit * gain + bias
        prev = jnp.where(first, before, pltpu.roll(normed, 1, 0)) * wide(keep_ref[at, :], width)
        differ = normed - prev
        for share, out in zip(mixes, outs):
            out[at, :] = (prev + differ * share).astype(BF16)
        return normed[TILE - 1 : TILE]

    lax.fori_loop(0, length // TILE, step, jnp.zeros((1, width), F32))


def unweave(ref, own, other, c):
    at = lax.broadcasted_iota(jnp.int32, (ref.shape[0], 128), 1) // 32
    for t in range(own.shape[1] // 128):
        a, b = ref[:, lanes(2 * t)].astype(F32), ref[:, lanes(2 * t + 1)].astype(F32)
        a3, a2, b2, b1 = pltpu.roll(a, 96, 1), pltpu.roll(a, 64, 1), pltpu.roll(b, 64, 1), pltpu.roll(b, 32, 1)
        first = jnp.where(at == 0, a, jnp.where(at == 1, a3, jnp.where(at == 2, b2, b1)))
        second = jnp.where(at == 0, a3, jnp.where(at == 1, a2, jnp.where(at == 2, b1, b)))
        own[:, lanes(t)] = jnp.where(c == 0, first, second).astype(BF16)
        other[:, lanes(t)] = jnp.where(c == 0, second, first).astype(BF16)


def weave(a, b, out):
    at = lax.broadcasted_iota(jnp.int32, (out.shape[0], 128), 1) // 32
    for t in range(out.shape[1] // 128):
        p, q = a[:, lanes(t // 2)], b[:, lanes(t // 2)]
        if t % 2 == 0:
            turned = (p, pltpu.roll(q, 32, 1), pltpu.roll(p, 32, 1), pltpu.roll(q, 64, 1))
        else:
            turned = (pltpu.roll(p, 64, 1), pltpu.roll(q, 96, 1), pltpu.roll(p, 96, 1), q)
        out[:, lanes(t)] = jnp.where(
            at == 0, turned[0], jnp.where(at == 1, turned[1], jnp.where(at == 2, turned[2], turned[3]))
        )


def forward_kernel(
    wk, wv, wr, wg, wo, fk, fvt, vec, x_own, up_own, starts,
    g_out, out, x_out, up_out, ins_out, kvr_out, sn_out, sd_out, mixed_out, resid_out, ins2_out, pre_out, act_out,
    gv_out, gr_out, vec_out, rows_out, keep_out,
    own3, other3, keep_own, gv, g, x, up, ins, kvr, sn, sd, mixed, sum_own, sum_other, resid, ins2, pre, act, v_send, v_other, gval, grec, low_half,
    local_sem, ex_send, ex_recv, sends, recvs, lsends, lrecvs, vsends, vrecvs, out_sem, sum_send, sum_recv, val_send, val_recv,
):
    z, yx, c = place()
    length, width = x.shape
    half = width // 2
    span = length // 2
    partner = (z * 4 + yx, 1 - c)
    keep_own[...] = jnp.broadcast_to(1.0 - starts[...].astype(F32), (128, span)).T
    for n, ref in enumerate((wk, wv, wr)):
        unweave(ref, own3.at[n], other3.at[n], c)
    enter(z, yx, c)

    block = wk.shape[0]
    mine = strip(c, block)
    rows_mine = strip(c, span)
    swaps = [
        (vec, gv.at[z, yx, c]),
        (other3, g.at[0:3, z, yx, mine]),
        (wg.at[:, strip(1 - c, half)], g.at[GATE2, z, yx, mine]),
        (x_own, x.at[rows_mine]),
        (keep_own, keep_out.at[rows_mine]),
        (up_own, up.at[rows_mine]),
    ]
    swaps = [remote(a, b, ex_send.at[n], ex_recv.at[n], partner) for n, (a, b) in enumerate(swaps)]
    keeps = [
        (vec, gv.at[z, yx, c]),
        (own3, g.at[0:3, z, yx, mine]),
        (wg.at[:, strip(c, half)], g.at[GATE2, z, yx, mine]),
        (x_own, x.at[rows_mine]),
        (keep_own, keep_out.at[rows_mine]),
        (up_own, up.at[rows_mine]),
    ]
    for h in range(2):
        keeps.append((wo.at[:, h * half : (h + 1) * half], g.at[EMIT, z, yx, h * block : (h + 1) * block]))
    for n in range(4):
        chunk = slice(n * half, (n + 1) * half)
        keeps.append((fk.at[:, chunk], g.at[KEYS[n], z, yx]))
        keeps.append((fvt.at[:, chunk], g.at[VALUES[n], z, yx]))
    keeps = [pltpu.make_async_copy(a, b, local_sem.at[n]) for n, (a, b) in enumerate(keeps)]
    for copy in swaps + keeps:
        copy.start()
    weights = Gather(lambda p: g.at[p], sends, recvs)
    lines = GatherLine(lambda p: g.at[RINGS + p], lsends, lrecvs)
    vectors = Gather(lambda p: gv, vsends, vrecvs)

    outs = []

    def put(src, dst):
        copy = pltpu.make_async_copy(src, dst, out_sem.at[len(outs)])
        copy.start()
        outs.append(copy)
        return copy

    along_z = {4: [(0, 1)], 5: [(1, 1)], 6: [(0, 2)], 7: [(1, 2)], 8: [(0, 3)], 9: [(1, 3)]}

    def turn(n):
        if n < RINGS:
            weights.step(n)
            if n + 2 < RINGS:
                weights.start(weights.along(n + 2))
        if 1 <= n <= RINGS:
            weights.forward(n - 1)
        for p, k in along_z.get(n, []):
            lines.line(p, k)
        if n >= 2:
            weights.arrive(weights.onward(n - 2))
            put(g.at[n - 2], g_out.at[n - 2])

    def lined(p):
        lines.ready(p - RINGS)
        put(g.at[p], g_out.at[p])

    for copy in keeps[6:]:
        copy.wait()
    for p in range(PIECES - RINGS):
        lines.start(lines.ring(p))
    for n in (0, 1, 2):
        swaps[n].wait()
        keeps[n].wait()
    vectors.start(vectors.along(0))
    weights.start(weights.along(0))
    weights.start(weights.along(1))
    for p in range(PIECES - RINGS):
        lines.arrive(lines.ring(p))
        lines.start(lines.onward(p))
    vectors.step(0)
    turn(0)
    vectors.forward(0)
    for n in (3, 4, 5):
        swaps[n].wait()
        keeps[n].wait()
    x_copy, up_copy = put(x, x_out), put(up, up_out)
    for p in range(PIECES - RINGS):
        lines.arrive(lines.onward(p))
    turn(1)
    vectors.arrive(vectors.onward(0))

    for t in range(width // 128):
        parts = [gv[(2 * t + k) // 4, (2 * t + k) % 4, core].astype(F32) for k in range(2) for core in range(2)]
        vec_out[:, lanes(t)] = functools.reduce(lambda a, b: a + b, parts)
    ramp = lax.broadcasted_iota(jnp.int32, (8, 128), 0).astype(F32)
    for t in range(half // 128):
        own = functools.reduce(lambda a, b: a + b, [gv[t, k, c].astype(F32) for k in range(4)])
        rate = jnp.exp(own[OWN_FADE : OWN_FADE + 1])
        head = [
            jnp.exp(-rate), jnp.exp(-2.0 * rate), jnp.exp(-4.0 * rate), jnp.exp(own[OWN_REWARD : OWN_REWARD + 1]),
            rate * jnp.exp(-rate),
        ]
        for n, row in enumerate(head):
            rows_out[n : n + 1, lanes(t)] = row
        rows_out[8:16, lanes(t)] = jnp.exp(-(ramp + 1.0) * rate)
        rows_out[16:24, lanes(t)] = jnp.exp(-(8.0 - ramp) * rate)

    def row(n):
        return vec_out[n : n + 1, :]

    norm_and_mix(
        length, width, lambda at: x[at, :].astype(F32), row(GAIN1), row(BIAS1), keep_out,
        [row(MK1), row(MV1), row(MR1)], [ins.at[n] for n in range(3)],
    )
    put(ins, ins_out)
    kvr_copies = []
    for n in range(3):
        turn(n + 2)
        weight = g.at[n]

        def project(at):
            kvr[n, at, :] = dot(ins[n, at, :], matrix(weight), NN)

        over_rows(length, 256, project)
        kvr_copies.append(put(kvr.at[n], kvr_out.at[n]))
    wkv_forward(kvr.at[0], kvr.at[1], kvr.at[2], keep_out, rows_out, mixed, sn, sd)
    put(mixed, mixed_out)
    put(sn, sn_out)
    put(sd, sd_out)
    turn(5)
    weight = g.at[EMIT]
    quarters = length // 4

    def emitted(n):
        at = strip(n, quarters)
        return remote(sum_own.at[at], sum_other.at[at], sum_send.at[n], sum_recv.at[n], partner)

    def emit(n, carry):
        at = strip(n, quarters)
        for h in range(2):
            sum_own[at, h * half : (h + 1) * half] = dot(mixed[at, :], emit_half(weight, h), NN).astype(BF16)
        emitted(n).start()
        return carry

    lax.fori_loop(0, 4, emit, 0)
    turn(6)
    for n in range(4):
        emitted(n).wait()

    def add_up(at):
        total = x[at, :].astype(F32) + (sum_own[at, :].astype(F32) + sum_other[at, :].astype(F32))
        resid[0, at, :] = total[:, :half]
        resid[1, at, :] = total[:, half:]
        return total

    norm_and_mix(
        length, width, add_up, row(GAIN2), row(BIAS2), keep_out, [row(MK2), row(MR2)], [ins2.at[n] for n in range(2)]
    )
    put(resid, resid_out)
    put(ins2, ins2_out)
    for copy in kvr_copies:
        copy.wait()
    weight = g.at[GATE2]

    def gate(at):
        kvr[2, at, :] = jax.nn.sigmoid(dot(ins2[1, at, :], matrix(weight), NN))

    over_rows(length, 256, gate)
    pre_copies = []

    def expand_chunk(j):
        weight, slot = g.at[KEYS[j]], len(pre_copies) % 2
        if len(pre_copies) >= 2:
            pre_copies[-2].wait()

        def expand(at):
            positive = jnp.maximum(dot(ins2[0, at, :], matrix(weight), NN), 0.0)
            pre[slot, at, :] = positive.astype(BF16)
            act[j, at, :] = (positive * positive).astype(BF16)

        over_rows(length, 256, expand)
        pre_copies.append(put(pre.at[slot], pre_out.at[j]))
        put(act.at[j], act_out.at[j])

    def contract_chunk(j):
        weight = g.at[VALUES[j]]

        def contract(at):
            for h in range(2):
                part = dot(act[j, at, :], weight[2 * h : 2 * h + 2].reshape(half, -1), NT)
                kvr[h, at, :] = part if j == 0 else kvr[h, at, :] + part

        over_rows(length, 256, contract)

    turn(7)
    expand_chunk(0)
    turn(8)
    contract_chunk(0)
    turn(9)
    expand_chunk(1)
    turn(10)
    contract_chunk(1)
    lined(KEYS[3])
    expand_chunk(3)
    lined(VALUES[3])
    contract_chunk(3)
    turn(11)
    expand_chunk(2)
    turn(12)
    contract_chunk(2)

    columns = strip(c, half)

    def value_copy(n):
        at = strip(n, quarters)
        return remote(v_send.at[at], v_other.at[at], val_send.at[n], val_recv.at[n], partner)

    def back_copy(n):
        at = strip(n, quarters)
        return remote(gval.at[c, at], gval.at[c, at], val_send.at[4 + n], val_recv.at[4 + n], partner)

    def send_values(n, carry):
        def narrow(i, carry):
            at = strip(n * (quarters // 32) + i, 32)
            v_send[at, :] = kvr[1 - c, at, :].astype(BF16)
            return carry

        lax.fori_loop(0, quarters // 32, narrow, 0)
        value_copy(n).start()
        return carry

    def finish_values(n, carry):
        value_copy(n).wait()

        def finish(i, carry):
            at = strip(n * (quarters // 32) + i, 32)
            value = kvr[c, at, :] + v_other[at, :].astype(F32)
            s = kvr[2, at, :]
            low_half[at, :] = (resid[c, at, :] + s * value).astype(BF16)
            upstream = up[at, columns].astype(F32)
            gval[c, at, :] = (upstream * s).astype(BF16)
            grec[at, :] = (upstream * value * s * (1.0 - s)).astype(BF16)
            return carry

        lax.fori_loop(0, quarters // 32, finish, 0)
        back_copy(n).start()
        return carry

    lax.fori_loop(0, 4, send_values, 0)
    lax.fori_loop(0, 4, finish_values, 0)
    give = remote(low_half.at[strip(1 - c, span)], out.at[:, columns], val_send.at[8], val_recv.at[8], partner)
    give.start()
    put(low_half.at[rows_mine], out.at[:, columns])
    put(grec, gr_out)
    for n in range(4):
        back_copy(n).wait()
    put(gval, gv_out)
    give.wait()

    def close(p, carry):
        weights.finish(p)
        return carry

    lax.fori_loop(0, RINGS, close, 0)
    for p in range(PIECES - RINGS):
        lines.finish(p)
    vectors.finish(0)
    waited = kvr_copies + pre_copies[:2]
    for copy in outs:
        if not any(copy is other for other in waited):
            copy.wait()


def forward_call(wk, wv, wr, wg, wo, fk, fvt, vec, x_own, up_own, starts):
    span, width = x_own.shape
    length, half = 2 * span, width // 2
    block = (fk.shape[0], half)
    any_, vmem = pl.BlockSpec(memory_space=pl.ANY), pl.BlockSpec(memory_space=pltpu.VMEM)
    full, col = (length, width), (length, half)

    def shape(dims, kind):
        return jax.ShapeDtypeStruct(dims, kind)

    outs = (
        (shape((PIECES, 4, 4) + block, BF16), any_),
        (shape((span, width), BF16), any_),
        (shape(full, BF16), any_),
        (shape(full, BF16), any_),
        (shape((3,) + full, BF16), any_),
        (shape((3,) + col, F32), any_),
        (shape(col, F32), any_),
        (shape(col, F32), any_),
        (shape(col, BF16), any_),
        (shape((2,) + col, F32), any_),
        (shape((2,) + full, BF16), any_),
        (shape((4,) + col, BF16), any_),
        (shape((4,) + col, BF16), any_),
        (shape((2,) + col, BF16), any_),
        (shape(col, BF16), any_),
        (shape((16, width), F32), vmem),
        (shape((24, half), F32), vmem),
        (shape((length, 128), F32), vmem),
    )
    dma = pltpu.SemaphoreType.DMA
    return pl.pallas_call(
        forward_kernel,
        out_shape=tuple(o[0] for o in outs),
        in_specs=[vmem] * 11,
        out_specs=tuple(o[1] for o in outs),
        scratch_shapes=[
            pltpu.VMEM((3, block[0] // 2, half), BF16),
            pltpu.VMEM((3, block[0] // 2, half), BF16),
            pltpu.VMEM((span, 128), F32),
            pltpu.VMEM((4, 4, 2) + vec.shape, BF16),
            pltpu.VMEM((PIECES, 4, 4) + block, BF16),
            pltpu.VMEM(full, BF16),
            pltpu.VMEM(full, BF16),
            pltpu.VMEM((3,) + full, BF16),
            pltpu.VMEM((3,) + col, F32),
            pltpu.VMEM(col, F32),
            pltpu.VMEM(col, F32),
            pltpu.VMEM(col, BF16),
            pltpu.VMEM(full, BF16),
            pltpu.VMEM(full, BF16),
            pltpu.VMEM((2,) + col, F32),
            pltpu.VMEM((2,) + full, BF16),
            pltpu.VMEM((2,) + col, BF16),
            pltpu.VMEM((4,) + col, BF16),
            pltpu.VMEM(col, BF16),
            pltpu.VMEM(col, BF16),
            pltpu.VMEM((2,) + col, BF16),
            pltpu.VMEM(col, BF16),
            pltpu.VMEM(col, BF16),
            dma((16,)), dma((6,)), dma((6,)),
            dma((RINGS, 7)), dma((RINGS, 7)), dma((PIECES - RINGS, 10)), dma((PIECES - RINGS, 10)), dma((1, 7)), dma((1, 7)),
            dma((40,)), dma((4,)), dma((4,)), dma((9,)), dma((9,)),
        ],
        compiler_params=pltpu.CompilerParams(
            collective_id=0, has_side_effects=True, vmem_limit_bytes=63 * MIB
        ),
        name="forward",
    )(wk, wv, wr, wg, wo, fk, fvt, vec, x_own, up_own, starts)


R_VALUE, R_KEY, R_GATE2, R_EMIT, R_TIME = 0, 4, 8, 9, 10
WEIGHT_ORDER = [p for j in range(4) for p in (VALUES[j], KEYS[j])] + [GATE2, EMIT, KEY, VALUE, GATE]
LINED = (1, 3, 5)
SUMS = 11
S_GAIN1, S_BIAS1, S_GAIN2, S_BIAS2, S_DECAY, S_BONUS, S_MK1, S_MV1, S_MR1, S_MK2, S_MR2 = range(11)
SLOTS = 12


def whole(ref, at):
    return jnp.concatenate([ref[0, at, :], ref[1, at, :]], axis=1)


def halves(ref, at, value):
    half = value.shape[1] // 2
    ref[0, at, :] = value[:, :half].astype(ref.dtype)
    ref[1, at, :] = value[:, half:].astype(ref.dtype)


def fold(value):
    return sum(value[n : n + 8] for n in range(8, value.shape[0], 8)) + value[:8]


def back_through_norm(g, unit, inverse, gain):
    q = g * gain
    return inverse * (
        q - jnp.mean(q, axis=-1, keepdims=True) - unit * jnp.mean(q * unit, axis=-1, keepdims=True)
    )


def lifted(now, following, last):
    return jnp.where(last, following[0:1], pltpu.roll(now, now.shape[0] - 1, 0))


def backward_kernel(
    plan,
    g, x_in, up_in, ins_in, kvr_in, sn_in, sd_in, mixed_in, resid_in, ins2_in, pre_in, act_in, gv_in, gr_in,
    vec, rows, keep,
    out_k, out_v, out_r, out_g, out_o, out_fk, out_fv, vsum, vother, gtok,
    own_t, recv_t, own_g,
    part, ring1, ring2, line, lring1, lring2, lline, vpart, vring1, vring2, vline,
    b, w, f, resid, sum_other, n1_other, acc, own_sums,
    load_sem, w_sem, sends, recvs, lsends, lrecvs, vsends, vrecvs, ex_send, ex_recv, sum_send, sum_recv,
):
    z, yx, c = place()
    nx, ny, nd, zs = neighbours(z, yx)
    length, half = b.shape[1:]
    width = 2 * half
    span = length // 2
    quarter = length // 4
    partner = (z * 4 + yx, 1 - c)
    loads = {}

    def load(name, src, dst):
        copy = pltpu.make_async_copy(src, dst, load_sem.at[len(loads)])
        copy.start()
        loads[name] = copy

    def loaded(*names):
        for name in names:
            loads[name].wait()

    def pair(n):
        return b.at[n : n + 2]

    def load_pair(name, src, n):
        for h in range(2):
            load((name, h), src.at[:, h * half : (h + 1) * half], b.at[n + h])

    def loaded_pair(name):
        loaded((name, 0), (name, 1))

    def weight_copy(n):
        return pltpu.make_async_copy(g.at[WEIGHT_ORDER[n]], w.at[n % 3], w_sem.at[n])

    def weight(n):
        weight_copy(n).wait()
        return w.at[n % 3]

    GVAL, ACT, PRE, IN_K2, IN_R2, GREC, GPRE = 0, 2, 4, 6, 8, 10, 11
    load("gv0", gv_in.at[0], b.at[GVAL])
    load("gv1", gv_in.at[1], b.at[GVAL + 1])
    for j in range(2):
        load(("act", j), act_in.at[j], b.at[ACT + j])
    load_pair("in_k2", ins2_in.at[0], IN_K2)
    for j in range(2):
        load(("pre", j), pre_in.at[j], b.at[PRE + j])
    for n in range(3):
        weight_copy(n).start()
    load_pair("in_r2", ins2_in.at[1], IN_R2)
    load("gr", gr_in, b.at[GREC])
    load("resid", resid_in, resid)
    enter(z, yx, c)

    columns = strip(c, half)
    outs = {R_GATE2: [own_g], R_EMIT: [out_o.at[:, h * half : (h + 1) * half] for h in range(2)]}
    for n in range(4):
        chunk = slice(n * half, (n + 1) * half)
        outs[R_VALUE + n], outs[R_KEY + n] = [out_fv.at[:, chunk]], [out_fk.at[:, chunk]]
    for n in range(3):
        outs[R_TIME + n] = [own_t.at[n]]
    sums = []
    for p in range(PIECES):
        if p in LINED:
            n = LINED.index(p)
            sums.append(
                ReduceLine(
                    part, p % PARTS, lring1.at[n], lring2.at[n], lline.at[n], outs[p], lsends.at[n], lrecvs.at[n]
                )
            )
        else:
            n = p - sum(q < p for q in LINED)
            sums.append(
                Reduce(part, p % PARTS, ring1.at[n], ring2.at[n], line.at[n], outs[p], sends.at[n], recvs.at[n])
            )
    vector_sums = Reduce(vpart, 0, vring1, vring2, vline, [vsum], vsends, vrecvs)
    final = []
    rows4 = recv_t.shape[1]
    mine, others = strip(c, rows4), strip(1 - c, rows4)

    def pump(name):
        for stage, p in plan[name]:
            if p == "v":
                getattr(vector_sums, "stage%d" % stage)()
                continue
            getattr(sums[p], "stage%d" % stage)()
            if stage == 4 and p in (R_GATE2, R_TIME, R_TIME + 1, R_TIME + 2):
                n = len(final)
                if p == R_GATE2:
                    src, dst = own_g.at[others], out_g.at[:, columns]
                else:
                    src, dst = own_t.at[p - R_TIME, others], recv_t.at[p - R_TIME]
                final.append(remote(src, dst, ex_send.at[n], ex_recv.at[n], partner))
                final[-1].start()

    def gradient(p, lhs, rhs):
        def block(a, carry):
            rows_a = dot(lhs[a // 2, :, strip(a % 2, half // 2)], rhs[...], TN)
            part[p % PARTS, a] = rows_a.astype(BF16).reshape(part.shape[2:])
            return carry

        lax.fori_loop(0, 4, block, 0)

    def thirds(ref, h):
        return ref[2 * h : 2 * h + 2].reshape(half, half)

    loaded("gv0", "gv1")
    for j in range(4):
        loaded(("act", j))
        gradient(R_VALUE + j, pair(GVAL), b.at[ACT + j % 2])
        if j < 2:
            load(("act", j + 2), act_in.at[j + 2], b.at[ACT + j])
        pump("fv%d" % j)
    loaded_pair("in_k2")
    for j in range(4):
        loaded(("pre", j))
        value_w = weight(2 * j)

        def through(at):
            g_hidden = sum(dot(b[GVAL + h, at, :], thirds(value_w, h), NN) for h in range(2))
            b[GPRE, at, :] = (2.0 * b[PRE + j % 2, at, :].astype(F32) * g_hidden).astype(BF16)

        over_rows(length, 256, through)
        pump("th%d" % j)
        if j < 2:
            load(("pre", j + 2), pre_in.at[j + 2], b.at[PRE + j])
        weight_copy(2 * j + 3).start()
        gradient(R_KEY + j, pair(IN_K2), b.at[GPRE])
        pump("fk%d" % j)
        key_w = weight(2 * j + 1)

        def collect(at):
            for h in range(2):
                piece = dot(b[GPRE, at, :], thirds(key_w, h), NT)
                f[h, at, :] = piece if j == 0 else f[h, at, :] + piece

        over_rows(length, 256, collect)
        pump("co%d" % j)
        weight_copy(2 * j + 4).start()
    loaded_pair("in_r2")
    loaded("gr")
    gradient(R_GATE2, pair(IN_R2), b.at[GREC])
    pump("g2")
    gate_w = weight(8)

    def gate_back(at):
        for h in range(2):
            f[2 + h, at, :] = dot(b[GREC, at, :], thirds(gate_w, h), NT)

    over_rows(length, 256, gate_back)
    pump("gb")
    weight_copy(11).start()
    loaded("resid")

    SUM_OWN, UP, BRANCH, MIXED, G3, X, IN_K, IN_V, IN_R, SEND = 0, 2, 4, 6, 7, 4, 10, 0, 2, 6
    load_pair("up", up_in, UP)
    load("mixed", mixed_in, b.at[MIXED])
    acc[...] = jnp.zeros_like(acc)
    last = lax.broadcasted_iota(jnp.int32, (TILE, width), 0) == TILE - 1

    def row(n):
        return vec[n : n + 1, :]

    def kept(at, n):
        return wide(keep[at, :], width) if n is None else wide(keep[n, :], width)

    gain2, bias2, mk2, mr2 = (GAIN2, BIAS2, MK2, MR2)
    sum_copies = []
    for q in range(4):

        def tile(i, carry):
            base = q * quarter + i * TILE
            at = pl.ds(pl.multiple_of(base, TILE), TILE)
            after = pl.ds(pl.multiple_of(jnp.minimum(base + TILE, length - 8), 8), 8)
            inside = jnp.where(base + TILE < length, 1.0, 0.0)
            keep_at, keep_after = wide(keep[at, :], width), wide(keep[after, :], width) * inside
            unit, _ = norm(whole(resid, at))
            normed = unit * row(gain2) + row(bias2)
            total = jnp.zeros_like(unit)
            for n, share in enumerate((mk2, mr2)):
                back = whole(f.at[2 * n : 2 * n + 2], at)
                ahead = lifted(back * keep_at, whole(f.at[2 * n : 2 * n + 2], after) * keep_after, last)
                total = total + ahead + (back - ahead) * row(share)
                acc[S_MK2 + n] = acc[S_MK2 + n] + fold(normed * (back - ahead))
            acc[S_GAIN2] = acc[S_GAIN2] + fold(total * unit)
            acc[S_BIAS2] = acc[S_BIAS2] + fold(total)
            halves(b.at[SUM_OWN : SUM_OWN + 2], at, total)
            return carry

        lax.fori_loop(0, quarter // TILE, tile, 0)
        at = pl.ds(q * quarter, quarter)
        sum_copies.append(
            remote(b.at[SUM_OWN : SUM_OWN + 2, at], sum_other.at[:, at], sum_send.at[q], sum_recv.at[q], partner)
        )
        sum_copies[-1].start()
        pump("a%d" % q)
    for n in range(3):
        load(("kvr", n), kvr_in.at[n], f.at[n])
    load("sn", sn_in, f.at[3])
    load("sd", sd_in, f.at[4])
    load_pair("in_k", ins_in.at[0], IN_K)

    loaded_pair("up")
    for q in range(4):
        sum_copies[q].wait_recv()

        def tile(i, carry):
            at = pl.ds(pl.multiple_of(q * quarter + i * TILE, TILE), TILE)
            unit, inverse = norm(whole(resid, at))
            total = whole(b.at[SUM_OWN : SUM_OWN + 2], at).astype(F32) + whole(sum_other, at).astype(F32)
            back = whole(pair(UP), at).astype(F32) + back_through_norm(total, unit, inverse, row(gain2))
            halves(pair(BRANCH), at, back)

            @pl.when(c == q // 2)
            def _():
                gtok[pl.ds(pl.multiple_of((q % 2) * quarter + i * TILE, TILE), TILE), :] = back

            return carry

        lax.fori_loop(0, quarter // TILE, tile, 0)
        pump("b%d" % q)
    for copy in sum_copies:
        copy.wait_send()
    load_pair("in_v", ins_in.at[1], IN_V)
    load_pair("in_r", ins_in.at[2], IN_R)

    loaded("mixed")
    rows_h = part.shape[3] // 2
    for h in range(2):

        def emit_rows(a, carry):
            block = dot(b[MIXED, :, strip(a, half // 2)], b[BRANCH + h], TN).astype(BF16)
            part[R_EMIT, pl.ds(2 * a, 2), :, h * rows_h : (h + 1) * rows_h, :] = block.reshape(2, 4, rows_h, half)
            return carry

        lax.fori_loop(0, 2, emit_rows, 0)
    pump("em")
    emit_w = weight(9)

    def emit_back(at):
        resid[0, at, :] = sum(dot(b[BRANCH + h, at, :], emit_half(emit_w, h), NT) for h in range(2))

    over_rows(length, 256, emit_back)
    pump("eb")
    weight_copy(12).start()
    load_pair("x", x_in, X)

    loaded(("kvr", 0), ("kvr", 1), ("kvr", 2), "sn", "sd")
    carry = None
    for q in range(4):
        carry = wkv_backward(
            resid.at[0], f.at[0], f.at[1], f.at[2], f.at[3], f.at[4], keep, rows, b.at[G3], b.at[G3 + 1], b.at[G3 + 2],
            q * (length // 64), (q + 1) * (length // 64), carry,
        )
        pump("w%d" % q)
    wkv_sums(carry, rows, own_sums.at[0:1], own_sums.at[1:2])

    for n, (name, slot) in enumerate((("in_k", IN_K), ("in_v", IN_V), ("in_r", IN_R))):
        loaded_pair(name)
        sums[R_TIME + n - PARTS].finish()
        gradient(R_TIME + n, pair(slot), b.at[G3 + n])
        pump("t%d" % n)
    loaded_pair("x")
    for n in range(3):
        weight(10 + n)
    for n in range(3):
        for h in range(2):
            f[n, pl.ds(h * span + quarter, 8), :] = jnp.zeros((8, half), F32)
    n1_copies = []
    for q in (3, 2, 1, 0):
        def back_rows(n, carry):
            for h in range(2):
                if q < 3:
                    f[n, pl.ds(h * span + quarter, 8), :] = f[n, pl.ds(h * span, 8), :]
                f[n, pl.ds(h * span, quarter), :] = dot(
                    b[G3 + n, pl.ds(q * quarter, quarter), :], thirds(w.at[(n + 1) % 3], h), NT
                )
            return carry

        lax.fori_loop(0, 3, back_rows, 0)

        def tile(i, carry):
            base = q * quarter + i * TILE
            at = pl.ds(pl.multiple_of(base, TILE), TILE)
            after = pl.ds(pl.multiple_of(jnp.minimum(base + TILE, length - 8), 8), 8)
            keep_at, keep_after = wide(keep[at, :], width), wide(keep[after, :], width)

            def take(n, start, size):
                return jnp.concatenate(
                    [f[n, pl.ds(pl.multiple_of(h * span + start, 8), size), :] for h in range(2)], axis=1
                )

            unit, _ = norm(whole(pair(X), at).astype(F32))
            normed = unit * row(GAIN1) + row(BIAS1)
            total = jnp.zeros_like(unit)
            for n, share in enumerate((MK1, MV1, MR1)):
                back = take(n, i * TILE, TILE)
                ahead = lifted(back * keep_at, take(n, i * TILE + TILE, 8) * keep_after, last)
                total = total + ahead + (back - ahead) * row(share)
                acc[S_MK1 + n] = acc[S_MK1 + n] + fold(normed * (back - ahead))
            acc[S_GAIN1] = acc[S_GAIN1] + fold(total * unit)
            acc[S_BIAS1] = acc[S_BIAS1] + fold(total)
            rows_q = [pl.ds(pl.multiple_of(h * span + (q % 2) * quarter + i * TILE, TILE), TILE) for h in range(2)]

            @pl.when(c == q // 2)
            def _():
                for h in range(2):
                    f[3, rows_q[h], :] = total[:, h * half : (h + 1) * half]

            @pl.when(c != q // 2)
            def _():
                for h in range(2):
                    b[SEND, rows_q[h], :] = total[:, h * half : (h + 1) * half].astype(BF16)

            return carry

        lax.fori_loop(0, quarter // TILE, tile, 0)
        pump("c%d" % (3 - q))
    swap_n1 = remote(b.at[SEND], n1_other, sum_send.at[4], sum_recv.at[4], partner)
    swap_n1.start()

    for n in (S_GAIN1, S_BIAS1, S_GAIN2, S_BIAS2, S_MK1, S_MV1, S_MR1, S_MK2, S_MR2):
        acc[n, 0:1, :] = jnp.sum(acc[n], axis=0, keepdims=True)
    for i in range(16):
        vpart[0, i // 4, i % 4] = jnp.concatenate(
            [acc[n, 0:1, lanes(i // 2)] for n in range(SUMS)]
            + [own_sums[n : n + 1, lanes(i // 4)] for n in range(2)]
            + [jnp.zeros((3, 128), F32)]
        )
    pump("v0")
    swap_n1.wait()

    def tokens(i, carry):
        at = strip(i, TILE)
        spans = [pl.ds(pl.multiple_of(h * span + i * TILE, TILE), TILE) for h in range(2)]
        unit, inverse = norm(whole(pair(X), pl.ds(pl.multiple_of(c * span + i * TILE, TILE), TILE)).astype(F32))
        total = jnp.concatenate([f[3, s, :] + n1_other[s, :].astype(F32) for s in spans], axis=1)
        gtok[at, :] = gtok[at, :] + back_through_norm(total, unit, inverse, row(GAIN1))
        return carry

    lax.fori_loop(0, span // TILE, tokens, 0)
    for n in range(1, 4):
        pump("v%d" % n)
    swap = remote(vsum, vother, ex_send.at[4], ex_recv.at[4], partner)
    swap.start()
    pump("end")
    for p in range(PIECES - PARTS, PIECES):
        sums[p].finish()
    vector_sums.finish()
    out_g[:, columns] = own_g[mine, :]
    for copy in final + [swap]:
        copy.wait()
    for n, out in enumerate((out_k, out_v, out_r)):
        own, other = own_t[n, mine, :], recv_t[n]
        weave(jnp.where(c == 0, own, other), jnp.where(c == 0, other, own), out)


PLAN = {
    "fv0": [(1, 0)],
    "fv1": [(1, 1)],
    "fv2": [(1, 2)],
    "fv3": [(1, 3), (2, 0)],
    "th0": [],
    "fk0": [(1, 4), (2, 2), (2, 1)],
    "co0": [],
    "th1": [],
    "fk1": [(1, 5), (3, 0), (2, 3)],
    "co1": [(2, 4)],
    "th2": [(3, 1)],
    "fk2": [(1, 6), (3, 2)],
    "co2": [],
    "th3": [(2, 5)],
    "fk3": [(1, 7), (3, 4)],
    "co3": [(2, 6), (4, 0)],
    "g2": [(1, 8), (2, 7)],
    "gb": [],
    "a0": [(3, 3)],
    "a1": [],
    "a2": [(3, 6)],
    "a3": [(4, 1), (2, 8)],
    "b0": [(3, 7), (5, 1), (4, 2)],
    "b1": [],
    "b2": [],
    "b3": [(3, 5), (3, 8)],
    "em": [(1, 9), (6, 1)],
    "eb": [],
    "w0": [(4, 4)],
    "w1": [(2, 9)],
    "w2": [(4, 3)],
    "w3": [],
    "t0": [(1, 10)],
    "t1": [(1, 11), (5, 3), (3, 9), (4, 6)],
    "t2": [(1, 12)],
    "c0": [(2, 10), (2, 11), (6, 3), (4, 7)],
    "c1": [(4, 5), (2, 12)],
    "c2": [(3, 10), (4, 8)],
    "c3": [],
    "v0": [(1, "v"), (3, 11), (5, 5)],
    "v1": [(2, "v"), (4, 9), (4, 10), (3, 12)],
    "v2": [(3, "v"), (6, 5), (4, 11)],
    "v3": [(4, "v")],
    "end": [(4, 12)],
}


def backward_call(g, x, up, ins, kvr, sn, sd, mixed, resid, ins2, pre, act, g_value, g_recept, vec, rows, keep):
    block = g.shape[3:]
    length, half = sn.shape
    lined = len(LINED)
    rings = PIECES - lined
    any_, vmem = pl.BlockSpec(memory_space=pl.ANY), pl.BlockSpec(memory_space=pltpu.VMEM)
    dma = pltpu.SemaphoreType.DMA

    def shape(*dims):
        return jax.ShapeDtypeStruct(dims, F32)

    return pl.pallas_call(
        functools.partial(backward_kernel, PLAN),
        out_shape=(
            *[shape(block[0] // 2, 2 * half)] * 5, *[shape(block[0], 4 * half)] * 2, shape(16, 128), shape(16, 128),
            shape(length // 2, 2 * half),
        ),
        in_specs=[any_] * 14 + [vmem] * 3,
        out_specs=(vmem,) * 10,
        scratch_shapes=[
            pltpu.VMEM((3,) + block, F32),
            pltpu.VMEM((3, block[0] // 2, block[1]), F32),
            pltpu.VMEM(block, F32),
            pltpu.VMEM((PARTS, 4, 4) + block, BF16),
            pltpu.VMEM((rings, 2, 2) + block, BF16),
            pltpu.VMEM((rings, 2, 4) + block, BF16),
            pltpu.VMEM((rings, 3) + block, BF16),
            pltpu.VMEM((lined, 2, block[0] // 2, block[1]), BF16),
            pltpu.VMEM((lined, 2) + block, BF16),
            pltpu.VMEM((lined, 5, 4) + block, BF16),
            pltpu.VMEM((1, 4, 4, 16, 128), F32),
            pltpu.VMEM((2, 2, 16, 128), F32),
            pltpu.VMEM((2, 4, 16, 128), F32),
            pltpu.VMEM((3, 16, 128), F32),
            pltpu.VMEM((SLOTS, length, half), BF16),
            pltpu.VMEM((3, 4, 4) + block, BF16),
            pltpu.VMEM((5, length, half), F32),
            pltpu.VMEM((2, length, half), F32),
            pltpu.VMEM((2, length, half), BF16),
            pltpu.VMEM((length, half), BF16),
            pltpu.VMEM((SUMS, 8, 2 * half), F32),
            pltpu.VMEM((8, half), F32),
            dma((40,)), dma((PIECES,)), dma((rings, 7)), dma((rings, 7)), dma((lined, 10)), dma((lined, 10)),
            dma((7,)), dma((7,)), dma((5,)), dma((5,)), dma((5,)), dma((5,)),
        ],
        compiler_params=pltpu.CompilerParams(collective_id=1, has_side_effects=True, vmem_limit_bytes=63 * MIB),
        name="backward",
    )(g, x, up, ins, kvr, sn, sd, mixed, resid, ins2, pre, act, g_value, g_recept, vec, rows, keep)


def shifted(value, axis, steps):
    count = lax.axis_size(axis)
    first, last = (max(0, -steps), min(count, count - steps))
    return lax.ppermute(value, axis, [(source, source + steps) for source in range(first, last)])


def carried_in(array, axis, join, neutral):
    place = lax.axis_index(axis)
    gathered = jax.tree.map(
        lambda a, kind: lax.all_gather(a.astype(kind), axis),
        array,
        (jnp.bfloat16, jnp.bfloat16, jnp.bfloat16),
    )
    state = jax.tree.map(lambda a, e: jnp.zeros_like(a) + jnp.asarray(e, a.dtype), array, neutral)

    def one(turn, state):
        return join(
            state,
            jax.tree.map(
                lambda a, own: lax.dynamic_index_in_dim(a, turn, 0, False).astype(own.dtype),
                gathered,
                array,
            ),
        )

    return lax.fori_loop(0, place, one, state)


def entering(array, axis, combine, identity):
    count, place = (lax.axis_size(axis), lax.axis_index(axis))
    everything = jax.tree.map(
        lambda part, kind: lax.all_gather(part.astype(kind), axis),
        array,
        jax.tree.map(lambda a: jnp.bfloat16 if a.dtype == jnp.float32 else a.dtype, array),
    )
    start = jax.tree.map(
        lambda part, zero: jnp.broadcast_to(jnp.asarray(zero, part.dtype), part.shape),
        array,
        identity,
    )

    def turn(k, before):
        at = count - 1 - k
        reached = at > place
        new = combine(
            before, jax.tree.map(lambda part, own: part[at].astype(own.dtype), everything, array)
        )
        return jax.tree.map(lambda a, b: jnp.where(reached, a, b), new, before)

    return lax.fori_loop(0, count, turn, start)


def wide_layer_norm(values, scale_vec, shift_vec):
    center = values - jnp.mean(values, axis=-1, keepdims=True)
    inverse = lax.rsqrt(jnp.mean(center * center, axis=-1, keepdims=True) + 1e-05)
    normed = center * inverse
    return (normed * scale_vec + shift_vec, normed, inverse)


def wide_norm_back(upstream, normed, inverse, scale_vec):
    scaled = upstream * scale_vec
    inner = (
        scaled
        - jnp.mean(scaled, axis=-1, keepdims=True)
        - normed * jnp.mean(scaled * normed, axis=-1, keepdims=True)
    )
    return (
        inverse * inner,
        jnp.sum(upstream * normed, axis=(0, 1)),
        jnp.sum(upstream, axis=(0, 1)),
    )


def shift_prev(values, persist_indicator):
    arrived = shifted(values[:, -1:, :], "tensor", 1)
    return jnp.concatenate([arrived, values[:, :-1]], axis=1) * persist_indicator[:, :, None]


def shift_back(upstream, persist_indicator):
    masked = upstream * persist_indicator[:, :, None]
    arrived = shifted(masked[:, :1, :], "tensor", -1)
    return jnp.concatenate([masked[:, 1:], arrived], axis=1)


def project(values, matrix):
    return jnp.einsum("rtd,de->rte", values, matrix, preferred_element_type=jnp.float32)


def project_back(upstream, matrix):
    return jnp.einsum("rte,de->rtd", upstream, matrix, preferred_element_type=jnp.float32)


def outer_sum(values, upstream):
    return jnp.einsum("rtd,rte->de", values, upstream, preferred_element_type=jnp.float32)


def mix_back(upstreams, shares, differ, persist_indicator):
    toward = jnp.zeros_like(differ)
    behind = jnp.zeros_like(differ)
    share_grads = []
    for upstream, share in zip(upstreams, shares):
        toward = toward + upstream * share
        behind = behind + upstream * (1.0 - share)
        share_grads.append(jnp.sum(upstream * differ, axis=(0, 1)))
    return (toward + shift_back(behind, persist_indicator), share_grads)


def chain_combine(earlier, later):
    return (
        earlier[0] * later[0],
        later[0] * earlier[1] + later[1],
        later[0] * earlier[2] + later[2],
    )


def scan_fragments(
    lookup_wide, payload_wide, fading_power, reward_coords, text_boundary_indicators
):
    decay_rate = jnp.exp(fading_power)
    row_count, span_len, width_len = lookup_wide.shape
    block_len = min(32, span_len)
    block_count = span_len // block_len
    places = jnp.arange(block_len, dtype=jnp.float32)
    rising = jnp.exp(places[:, None] * decay_rate)
    falling = jnp.exp(-(places[:, None] - 1.0) * decay_rate)
    trailing = jnp.exp(-(block_len - 1.0 - places)[:, None] * decay_rate)
    leading = jnp.exp(-places[:, None] * decay_rate)
    settle = jnp.exp(-block_len * decay_rate)
    before = places[:, None] > places[None, :]

    def split_blocks(values):
        return jnp.swapaxes(
            values.reshape((row_count, block_count, block_len) + values.shape[2:]), 0, 1
        )

    def advance(state_pair, scanned):
        accrued_dividend_sum, accrued_divisor_sum = state_pair
        lookup_narrow, payload_narrow, reset_b = scanned
        tree_levels = jnp.cumsum(reset_b, axis=1)
        linked = ((tree_levels[:, :, None] == tree_levels[:, None, :]) & before).astype(jnp.float32)
        key_term = jnp.exp(lookup_narrow)
        keyed_value = key_term * payload_narrow
        inside_numerator = falling * jnp.einsum(
            "rti,rid->rtd", linked, rising * keyed_value, precision=lax.Precision.HIGHEST
        )
        interior_divisor_sum = falling * jnp.einsum(
            "rti,rid->rtd", linked, rising * key_term, precision=lax.Precision.HIGHEST
        )
        leftover_multiplier = (tree_levels == 0).astype(jnp.float32)[:, :, None] * leading
        reward_multiplier = jnp.exp(reward_coords + lookup_narrow)
        above_total = (
            inside_numerator
            + reward_multiplier * payload_narrow
            + leftover_multiplier * accrued_dividend_sum[:, None, :]
        )
        below_total = (
            interior_divisor_sum
            + reward_multiplier
            + leftover_multiplier * accrued_divisor_sum[:, None, :]
        )
        ending = (tree_levels == tree_levels[:, -1:]).astype(jnp.float32)[:, :, None] * trailing
        intact = (tree_levels[:, -1] == 0).astype(jnp.float32)[:, None] * settle
        new_num = intact * accrued_dividend_sum + jnp.sum(ending * keyed_value, axis=1)
        new_den = intact * accrued_divisor_sum + jnp.sum(ending * key_term, axis=1)
        return ((new_num, new_den), (above_total, below_total))

    initial = jnp.zeros((row_count, width_len), jnp.float32)
    (total_num, total_den), (uppers, lowers) = lax.scan(
        advance,
        (initial, initial),
        (
            split_blocks(lookup_wide),
            split_blocks(payload_wide),
            split_blocks(text_boundary_indicators),
        ),
    )

    def join_blocks(values):
        return jnp.swapaxes(values, 0, 1).reshape(row_count, span_len, width_len)

    tree_levels = jnp.cumsum(text_boundary_indicators, axis=1)
    reaching = (tree_levels == 0).astype(jnp.float32)[:, :, None] * jnp.exp(
        -jnp.arange(span_len, dtype=jnp.float32)[:, None] * decay_rate
    )
    passing = (tree_levels[:, -1] == 0).astype(jnp.float32)[:, None] * jnp.exp(
        -span_len * decay_rate
    )
    return (join_blocks(uppers), join_blocks(lowers), reaching, total_num, total_den, passing)


def recurrence_finish(pieces_list, incoming_num, incoming_den):
    above_total = pieces_list[0] + pieces_list[2] * incoming_num[:, None, :]
    below_total = pieces_list[1] + pieces_list[2] * incoming_den[:, None, :]
    return (above_total / below_total, below_total)


def ffn_apply(inputs, key_weight, value_weight):
    hidden_pre = project(inputs, key_weight)
    hidden = jnp.square(jax.nn.relu(hidden_pre)).astype(jnp.bfloat16)
    return (hidden_pre, hidden, project(hidden, value_weight))


def ffn_grads(inputs, hidden_pre, hidden, upstream, key_weight, value_weight):
    g_hidden = jnp.einsum("rtd,fd->rtf", upstream, value_weight, preferred_element_type=jnp.float32)
    grad_value = jnp.einsum("rtf,rtd->fd", hidden, upstream, preferred_element_type=jnp.float32)
    g_pre = (2.0 * jax.nn.relu(hidden_pre) * g_hidden).astype(jnp.bfloat16)
    grad_key = jnp.einsum("rtd,rtf->df", inputs, g_pre, preferred_element_type=jnp.float32)
    g_inputs = jnp.einsum("rtf,df->rtd", g_pre, key_weight, preferred_element_type=jnp.float32)
    return (g_inputs, grad_key, grad_value)


def wide_shards(
    incoming_embeddings,
    text_boundary_indicators,
    upstream_sensitivity,
    primary_standardize_scaling,
    primary_standardize_offset,
    secondary_standardize_scaling,
    secondary_standardize_offset,
    feature_fading_logarithms,
    present_symbol_reward,
    timemix_lookup_blend,
    timemix_payload_blend,
    timemix_gate_blend,
    timemix_lookup_proj,
    timemix_payload_proj,
    timemix_gate_proj,
    timemix_emit_proj,
    feedmix_lookup_blend,
    feedmix_gate_blend,
    feedmix_gate_proj,
    feedmix_lookup_proj,
    feedmix_payload_proj,
):
    gathered_portions = (
        lax.all_gather(primary_standardize_scaling, ("dp", "tensor"), axis=0, tiled=True),
        lax.all_gather(primary_standardize_offset, ("dp", "tensor"), axis=0, tiled=True),
        lax.all_gather(secondary_standardize_scaling, ("dp", "tensor"), axis=0, tiled=True),
        lax.all_gather(secondary_standardize_offset, ("dp", "tensor"), axis=0, tiled=True),
        lax.all_gather(feature_fading_logarithms, ("dp", "tensor"), axis=0, tiled=True),
        lax.all_gather(present_symbol_reward, ("dp", "tensor"), axis=0, tiled=True),
        lax.all_gather(timemix_lookup_blend, ("dp", "tensor"), axis=0, tiled=True),
        lax.all_gather(timemix_payload_blend, ("dp", "tensor"), axis=0, tiled=True),
        lax.all_gather(timemix_gate_blend, ("dp", "tensor"), axis=0, tiled=True),
        lax.all_gather(timemix_lookup_proj, ("dp", "tensor"), axis=0, tiled=True),
        lax.all_gather(timemix_payload_proj, ("dp", "tensor"), axis=0, tiled=True),
        lax.all_gather(timemix_gate_proj, ("dp", "tensor"), axis=0, tiled=True),
        lax.all_gather(timemix_emit_proj, ("dp", "tensor"), axis=0, tiled=True),
        lax.all_gather(feedmix_lookup_blend, ("dp", "tensor"), axis=0, tiled=True),
        lax.all_gather(feedmix_gate_blend, ("dp", "tensor"), axis=0, tiled=True),
        lax.all_gather(feedmix_gate_proj, ("dp", "tensor"), axis=0, tiled=True),
    )
    initial_scaling_coords = gathered_portions[0].astype(jnp.float32)
    initial_offset_coords = gathered_portions[1].astype(jnp.float32)
    later_scaling_coords = gathered_portions[2].astype(jnp.float32)
    later_offset_coords = gathered_portions[3].astype(jnp.float32)
    fading_power = gathered_portions[4].astype(jnp.float32)
    reward_coords = gathered_portions[5].astype(jnp.float32)
    share_k1 = gathered_portions[6].astype(jnp.float32)
    share_v1 = gathered_portions[7].astype(jnp.float32)
    share_r1 = gathered_portions[8].astype(jnp.float32)
    lookup_coefficients_initial = gathered_portions[9]
    payload_coefficients_initial = gathered_portions[10]
    gate_coefficients_initial = gathered_portions[11]
    emit_coefficients_initial = gathered_portions[12]
    share_k2 = gathered_portions[13].astype(jnp.float32)
    share_r2 = gathered_portions[14].astype(jnp.float32)
    gate_coefficients_later = gathered_portions[15]
    lookup_coefficients_later, payload_coefficients_later = (
        lax.all_gather(feedmix_lookup_proj, "dp", axis=0, tiled=True),
        lax.all_gather(feedmix_payload_proj, "dp", axis=1, tiled=True),
    )
    persist_indicator = (1 - text_boundary_indicators).astype(jnp.float32)
    inputs = incoming_embeddings.astype(jnp.float32)
    normed_one, unit_one, inverse_one = wide_layer_norm(
        inputs, initial_scaling_coords, initial_offset_coords
    )
    prev_one = shift_prev(normed_one, persist_indicator)
    differ_one = normed_one - prev_one
    in_key = (prev_one + differ_one * share_k1).astype(jnp.bfloat16)
    in_value = (prev_one + differ_one * share_v1).astype(jnp.bfloat16)
    in_recept = (prev_one + differ_one * share_r1).astype(jnp.bfloat16)
    initial_lookup_lines = project(in_key, lookup_coefficients_initial)
    initial_payload_lines = project(in_value, payload_coefficients_initial)
    recept_one = project(in_recept, gate_coefficients_initial)
    pieces_list = scan_fragments(
        initial_lookup_lines,
        initial_payload_lines,
        fading_power,
        reward_coords,
        text_boundary_indicators,
    )
    passing = pieces_list[5]
    identity = (jnp.ones_like(passing), jnp.zeros_like(passing), jnp.zeros_like(passing))
    unused_item, incoming_num, incoming_den = carried_in(
        (passing, pieces_list[3], pieces_list[4]), "tensor", chain_combine, identity
    )
    blended_mean_state, below_total = recurrence_finish(pieces_list, incoming_num, incoming_den)
    sig_one = jax.nn.sigmoid(recept_one)
    mixed_att = (sig_one * blended_mean_state).astype(jnp.bfloat16)
    resid_one = inputs + project(mixed_att, emit_coefficients_initial)
    normed_two, unit_two, inverse_two = wide_layer_norm(
        resid_one, later_scaling_coords, later_offset_coords
    )
    prev_two = shift_prev(normed_two, persist_indicator)
    differ_two = normed_two - prev_two
    in_key_two = (prev_two + differ_two * share_k2).astype(jnp.bfloat16)
    in_recept_two = (prev_two + differ_two * share_r2).astype(jnp.bfloat16)
    recept_two = project(in_recept_two, gate_coefficients_later)
    sig_two = jax.nn.sigmoid(recept_two)
    row_inputs = lax.all_gather(in_key_two, "tensor", axis=1, tiled=True)
    hidden_pre, hidden, partial_value = ffn_apply(
        row_inputs, lookup_coefficients_later, payload_coefficients_later
    )
    value_two = lax.psum_scatter(
        partial_value.astype(jnp.bfloat16), "tensor", scatter_dimension=1, tiled=True
    ).astype(jnp.float32)
    layer_out = (resid_one + sig_two * value_two).astype(jnp.bfloat16)
    upstream = upstream_sensitivity.astype(jnp.float32)
    g_value_two = (upstream * sig_two).astype(jnp.bfloat16)
    g_recept_two = (upstream * value_two * sig_two * (1.0 - sig_two)).astype(jnp.bfloat16)
    grad_recept_two = outer_sum(in_recept_two, g_recept_two)
    g_mix_r2 = project_back(g_recept_two, gate_coefficients_later)
    row_grads = lax.all_gather(g_value_two, "tensor", axis=1, tiled=True)
    partial_grad, grad_key_two, grad_value_two = ffn_grads(
        row_inputs,
        hidden_pre,
        hidden,
        row_grads,
        lookup_coefficients_later,
        payload_coefficients_later,
    )
    g_mix_k2 = lax.psum_scatter(
        partial_grad.astype(jnp.bfloat16), "tensor", scatter_dimension=1, tiled=True
    ).astype(jnp.float32)
    sum_key_two, sum_value_two = (
        lax.psum_scatter(
            grad_key_two.astype(jnp.bfloat16), "dp", scatter_dimension=0, tiled=True
        ).astype(jnp.float32),
        lax.psum_scatter(
            grad_value_two.astype(jnp.bfloat16), "dp", scatter_dimension=1, tiled=True
        ).astype(jnp.float32),
    )
    g_normed_two, shares_two = mix_back(
        (g_mix_k2, g_mix_r2), (share_k2, share_r2), differ_two, persist_indicator
    )
    g_resid_part, grad_gain_two, grad_bias_two = wide_norm_back(
        g_normed_two, unit_two, inverse_two, later_scaling_coords
    )
    g_resid = upstream + g_resid_part
    g_branch = g_resid.astype(jnp.bfloat16)
    grad_out_one = outer_sum(mixed_att, g_branch)
    g_mixed = project_back(g_branch, emit_coefficients_initial)
    g_weighted = g_mixed * sig_one
    g_recept_one = (g_mixed * blended_mean_state * sig_one * (1.0 - sig_one)).astype(jnp.bfloat16)
    reaching = pieces_list[2]
    g_in_num = jnp.sum(g_weighted * reaching / below_total, axis=1)
    g_in_den = -jnp.sum(g_weighted * reaching * blended_mean_state / below_total, axis=1)
    unused_item, back_num, back_den = entering(
        (passing, g_in_num, g_in_den), "tensor", chain_combine, identity
    )
    g_passing = back_num * incoming_num + back_den * incoming_den

    def device_fragment(lookup_wide, payload_wide, fading_coords, reward_power):
        shard_pieces = scan_fragments(
            lookup_wide, payload_wide, fading_coords, reward_power, text_boundary_indicators
        )
        local_out, unused_item = recurrence_finish(shard_pieces, incoming_num, incoming_den)
        return (local_out, shard_pieces[3], shard_pieces[4], shard_pieces[5])

    unused_item, reverse_pass_rule = jax.vjp(
        device_fragment, initial_lookup_lines, initial_payload_lines, fading_power, reward_coords
    )
    derivative_lookup_wide, derivative_payload_wide, fading_derivative, reward_derivative = (
        reverse_pass_rule((g_weighted, back_num, back_den, g_passing))
    )
    g_key_one = derivative_lookup_wide.astype(jnp.bfloat16)
    g_value_one = derivative_payload_wide.astype(jnp.bfloat16)
    grad_key_one = outer_sum(in_key, g_key_one)
    grad_value_one = outer_sum(in_value, g_value_one)
    grad_recept_one = outer_sum(in_recept, g_recept_one)
    g_mix_k1 = project_back(g_key_one, lookup_coefficients_initial)
    g_mix_v1 = project_back(g_value_one, payload_coefficients_initial)
    g_mix_r1 = project_back(g_recept_one, gate_coefficients_initial)
    g_normed_one, shares_one = mix_back(
        (g_mix_k1, g_mix_v1, g_mix_r1),
        (share_k1, share_v1, share_r1),
        differ_one,
        persist_indicator,
    )
    g_input_part, grad_gain_one, grad_bias_one = wide_norm_back(
        g_normed_one, unit_one, inverse_one, initial_scaling_coords
    )
    grad_tokens = g_resid + g_input_part
    summed = (
        lax.psum_scatter(grad_gain_one, ("dp", "tensor"), scatter_dimension=0, tiled=True),
        lax.psum_scatter(grad_bias_one, ("dp", "tensor"), scatter_dimension=0, tiled=True),
        lax.psum_scatter(grad_gain_two, ("dp", "tensor"), scatter_dimension=0, tiled=True),
        lax.psum_scatter(grad_bias_two, ("dp", "tensor"), scatter_dimension=0, tiled=True),
        lax.psum_scatter(fading_derivative, ("dp", "tensor"), scatter_dimension=0, tiled=True),
        lax.psum_scatter(reward_derivative, ("dp", "tensor"), scatter_dimension=0, tiled=True),
        lax.psum_scatter(shares_one[0], ("dp", "tensor"), scatter_dimension=0, tiled=True),
        lax.psum_scatter(shares_one[1], ("dp", "tensor"), scatter_dimension=0, tiled=True),
        lax.psum_scatter(shares_one[2], ("dp", "tensor"), scatter_dimension=0, tiled=True),
        lax.psum_scatter(grad_key_one, ("dp", "tensor"), scatter_dimension=0, tiled=True),
        lax.psum_scatter(grad_value_one, ("dp", "tensor"), scatter_dimension=0, tiled=True),
        lax.psum_scatter(grad_recept_one, ("dp", "tensor"), scatter_dimension=0, tiled=True),
        lax.psum_scatter(grad_out_one, ("dp", "tensor"), scatter_dimension=0, tiled=True),
        lax.psum_scatter(shares_two[0], ("dp", "tensor"), scatter_dimension=0, tiled=True),
        lax.psum_scatter(shares_two[1], ("dp", "tensor"), scatter_dimension=0, tiled=True),
        lax.psum_scatter(grad_recept_two, ("dp", "tensor"), scatter_dimension=0, tiled=True),
    )
    return (
        layer_out,
        grad_tokens,
        summed[0],
        summed[1],
        summed[2],
        summed[3],
        summed[4],
        summed[5],
        summed[6],
        summed[7],
        summed[8],
        summed[9],
        summed[10],
        summed[11],
        summed[12],
        summed[13],
        summed[14],
        summed[15],
        sum_key_two,
        sum_value_two,
    )


def pack(tokens, starts, upstream, gain1, bias1, gain2, bias2, fading, reward, mk1, mv1, mr1, wk, wv, wr, wo, mk2, mr2, wg, fk, fv):
    i, c = lax.axis_index("dp"), lax.axis_index("tensor")
    own_rows = wk.shape[0]
    slots = 128 // own_rows
    everywhere = jnp.stack([gain1, bias1, gain2, bias2, fading, reward, mk1, mv1, mr1, mk2, mr2])
    own = jnp.stack([fading, reward, jnp.zeros_like(fading), jnp.zeros_like(fading), jnp.zeros_like(fading)])
    lane = jnp.arange(128)[None, :] // own_rows
    vec = jnp.concatenate([
        jnp.where(lane == (2 * i + c) % slots, jnp.tile(everywhere, (1, slots)), 0),
        jnp.where(lane == i % slots, jnp.tile(own, (1, slots)), 0),
    ]).astype(BF16)
    return wk, wv, wr, wg, wo, fk, fv.T, vec, tokens[0], upstream[0], starts


def land_kernel(*refs):
    count = (len(refs) - 2) // 3
    ins, outs, held = refs[:count], refs[count : 2 * count], refs[2 * count : 3 * count]
    came, left = refs[-2:]
    first = [pltpu.make_async_copy(ins[n], held[n], came.at[n]) for n in range(count)]
    second = [pltpu.make_async_copy(held[n], outs[n], left.at[n]) for n in range(count)]
    for copy in first:
        copy.start()
    for one, other in zip(first, second):
        one.wait()
        other.start()
    for copy in second:
        copy.wait()


def land(*arrays):
    any_, count = pl.BlockSpec(memory_space=pl.ANY), len(arrays)
    size = sum(a.size * a.dtype.itemsize for a in arrays)
    return pl.pallas_call(
        land_kernel,
        out_shape=tuple(jax.ShapeDtypeStruct(a.shape, a.dtype) for a in arrays),
        in_specs=[any_] * count,
        out_specs=(any_,) * count,
        scratch_shapes=[pltpu.VMEM(a.shape, a.dtype) for a in arrays] + [pltpu.SemaphoreType.DMA((count,))] * 2,
        compiler_params=pltpu.CompilerParams(vmem_limit_bytes=63 * MIB),
        cost_estimate=pl.CostEstimate(flops=0, transcendentals=0, bytes_accessed=2 * size),
        name="land",
    )(*arrays)


def shards(*args):
    c = lax.axis_index("tensor")
    i = lax.axis_index("dp")
    own_rows = args[12].shape[0]
    (
        g, layer_out, x, up, ins, kvr, sn, sd, mixed, resid, ins2, pre, act, g_value, g_recept2, vec, rows, keep,
    ) = forward_call(*pack(*args))

    out_k, out_v, out_r, out_g, out_o, out_fk, out_fv, vsum, vother, grad_tokens = backward_call(
        g, x, up, ins, kvr, sn, sd, mixed, resid, ins2, pre, act, g_value, g_recept2, vec, rows, keep
    )
    out_fv = out_fv.T
    layer_out, grad_tokens, out_k, out_v, out_r, out_g, out_o, out_fk = land(
        layer_out, grad_tokens, out_k, out_v, out_r, out_g, out_o, out_fk
    )
    slots = 128 // own_rows
    vtotal = lax.dynamic_slice_in_dim(vsum + vother, (2 * i + c) % slots * own_rows, own_rows, 1)
    own_scan = lax.dynamic_slice_in_dim(vsum, i % slots * own_rows, own_rows, 1)
    return (
        layer_out[None], grad_tokens[None], *(vtotal[n] for n in range(4)), own_scan[SUMS], own_scan[SUMS + 1],
        *(vtotal[n] for n in range(6, 9)), out_k, out_v, out_r, out_o, vtotal[9], vtotal[10], out_g, out_fk, out_fv,
    )


def solution(mesh):
    row, vector, matrix_ = P("dp", "tensor", None), P(("dp", "tensor")), P(("dp", "tensor"), None)
    key, value = P("dp", "tensor"), P("tensor", "dp")
    in_specs = (row, P("dp", "tensor"), row) + (vector,) * 9 + (matrix_,) * 4 + (vector,) * 2 + (matrix_, key, value)
    out_specs = (row, row) + (vector,) * 9 + (matrix_,) * 4 + (vector,) * 2 + (matrix_, key, value)
    body = shards if (mesh.shape["dp"], mesh.shape["tensor"]) == (16, 2) else wide_shards
    return jax.shard_map(body, mesh=mesh, in_specs=in_specs, out_specs=out_specs, check_vma=False)
```

```python
import functools

import jax
import jax.numpy as jnp
from jax import lax
from jax.experimental import pallas as pl
from jax.experimental.pallas import tpu as pltpu
from jax.sharding import PartitionSpec as P

F32, BF16 = jnp.float32, jnp.bfloat16
MESH_ID = pl.DeviceIdType.MESH
MIB = 1 << 20
PARTS = 10
PIECES = 13


def place():
    i, c = lax.axis_index("dp"), lax.axis_index("tensor")
    return i // 4, i % 4, c


def neighbours(z, yx):
    x = yx + 1 - 2 * (yx % 2)
    y = (yx + 2) % 4
    d = (x + 2) % 4
    zs = (z + 1 - 2 * (z % 2), (z + 2) % 4, 3 - z)
    return x, y, d, zs


def enter(z, yx, c):
    x, y, d, zs = neighbours(z, yx)
    barrier = pltpu.get_barrier_semaphore()
    targets = [(z * 4 + yx, 1 - c), (z * 4 + x, c), (z * 4 + y, c)]
    targets += [(peer * 4 + yx, c) for peer in zs]
    for target in targets:
        pl.semaphore_signal(barrier, inc=1, device_id=target, device_id_type=MESH_ID)
    pl.semaphore_wait(barrier, len(targets))


def remote(src, dst, send, recv, target):
    return pltpu.make_async_remote_copy(
        src_ref=src, dst_ref=dst, send_sem=send, recv_sem=recv,
        device_id=target, device_id_type=MESH_ID,
    )


def strip(i, size):
    return pl.ds(pl.multiple_of(i * size, size), size)


class Gather:
    def __init__(self, view, sends, recvs, first=0):
        self.view, self.sends, self.recvs, self.first = view, sends, recvs, first
        self.z, self.yx, self.c = place()
        self.x, self.y, self.d, self.zs = neighbours(self.z, self.yx)

    def to(self, z, yx):
        return (z * 4 + yx, self.c)

    def copy(self, p, k, ref, target):
        return remote(ref, ref, self.sends.at[p, k], self.recvs.at[p, k], target)

    def along(self, p):
        own = self.view(p).at[self.z, self.yx]
        return [self.copy(p, k, own, self.to(peer, self.yx)) for k, peer in enumerate(self.zs)]

    def plane(self, p):
        own = self.view(p).at[:, self.yx]
        return [self.copy(p, 3, own, self.to(self.z, self.x)), self.copy(p, 4, own, self.to(self.z, self.y))]

    def onward(self, p):
        return [
            self.copy(p, 5, self.view(p).at[0:2, self.x], self.to(self.z, self.y)),
            self.copy(p, 6, self.view(p).at[2:4, self.y], self.to(self.z, self.x)),
        ]

    def start(self, copies):
        for copy in copies:
            copy.start()

    def arrive(self, copies):
        for copy in copies:
            copy.wait_recv()

    def step(self, p):
        self.arrive(self.along(p))
        self.start(self.plane(p))

    def forward(self, p):
        self.arrive(self.plane(p))
        self.start(self.onward(p))

    def finish(self, p):
        for copy in self.along(p) + self.plane(p) + self.onward(p):
            copy.wait_send()


class GatherLine(Gather):
    def ring(self, p):
        own = self.view(p).at[self.z, self.yx]
        return [self.copy(p, 0, own, self.to(self.z, self.x)), self.copy(p, 1, own, self.to(self.z, self.y))]

    def onward(self, p):
        half = self.view(p).shape[2] // 2
        return [
            self.copy(p, 2, self.view(p).at[self.z, self.x, 0:half], self.to(self.z, self.y)),
            self.copy(p, 3, self.view(p).at[self.z, self.y, half:], self.to(self.z, self.x)),
        ]

    def climb(self, p, k, up, arriving):
        behind = k if arriving else k - 1
        plane = self.z - behind if up else self.z + behind
        beyond = self.z + 1 if up != arriving else self.z - 1
        real = (plane >= 0) & (plane <= 3) & (beyond >= 0) & (beyond <= 3)
        plane, beyond = jnp.clip(plane, 0, 3), jnp.clip(beyond, 0, 3)
        k = (4 if up else 7) + k - 1
        return real, self.copy(p, k, self.view(p).at[plane], self.to(beyond, self.yx))

    def each(self, p, k, arriving, action):
        for up in (True, False):
            real, copy = self.climb(p, k, up, arriving)
            pl.when(real)(functools.partial(action, copy))

    def line(self, p, k):
        if k > 1:
            self.each(p, k - 1, True, lambda copy: copy.wait_recv())
        self.each(p, k, False, lambda copy: copy.start())

    def ready(self, p):
        self.each(p, 3, True, lambda copy: copy.wait_recv())

    def finish(self, p):
        for copy in self.ring(p) + self.onward(p):
            copy.wait_send()
        for k in (1, 2, 3):
            self.each(p, k, False, lambda copy: copy.wait_send())


class Reduce:
    def __init__(self, part, slot, ring1, ring2, line, out, sends, recvs):
        self.parts, self.slot, self.ring1, self.ring2, self.line, self.out = part, slot, ring1, ring2, line, out
        self.sends, self.recvs = sends, recvs
        self.z, self.yx, self.c = place()
        self.x, self.y, self.d, self.zs = neighbours(self.z, self.yx)

    def copy(self, k, src, dst, z, yx):
        return remote(src, dst, self.sends.at[k], self.recvs.at[k], (z * 4 + yx, self.c))

    def part(self):
        return self.parts.at[self.slot]

    def diagonal(self):
        return [
            self.copy(0, self.part().at[0:2, self.d], self.ring1.at[0], self.z, self.x),
            self.copy(1, self.part().at[2:4, self.d], self.ring1.at[1], self.z, self.y),
        ]

    def side(self):
        return [
            self.copy(2, self.part().at[:, self.x], self.ring2.at[0], self.z, self.x),
            self.copy(3, self.part().at[:, self.y], self.ring2.at[1], self.z, self.y),
        ]

    def down(self):
        return [
            self.copy(4 + k, self.part().at[peer, self.yx], self.line.at[k], peer, self.yx)
            for k, peer in enumerate(self.zs)
        ]

    def start(self, copies):
        for copy in copies:
            copy.start()

    def arrive(self, copies):
        for copy in copies:
            copy.wait_recv()

    def add_up(self, own, others, result):
        size = min(64, own.shape[0])

        def step(i, carry):
            at = strip(i, size)
            total = own[at, :].astype(F32)
            for other in others:
                total = total + other[at, :].astype(F32)
            result[at, :] = total.astype(result.dtype)
            return carry

        lax.fori_loop(0, own.shape[0] // size, step, 0)

    def add(self, a, yx, others):
        own = self.part().at[a, yx]
        self.add_up(own, others, own)

    def give(self, others):
        start = 0
        for out in self.out:
            rows = pl.ds(start, out.shape[0])
            own = self.part().at[self.z, self.yx, rows]
            self.add_up(own, [other.at[rows] for other in others], out)
            start += out.shape[0]

    def stage1(self):
        self.start(self.diagonal())

    def stage2(self):
        self.arrive(self.diagonal())

        def planes(a, carry):
            self.add(a, self.y, [self.ring1.at[0, a]])
            self.add(a + 2, self.x, [self.ring1.at[1, a]])
            return carry

        lax.fori_loop(0, 2, planes, 0)
        self.start(self.side())

    def stage3(self):
        self.arrive(self.side())

        def planes(a, carry):
            self.add(a, self.yx, [self.ring2.at[0, a], self.ring2.at[1, a]])
            return carry

        lax.fori_loop(0, 4, planes, 0)
        self.start(self.down())

    def stage4(self):
        self.arrive(self.down())
        self.give([self.line.at[k] for k in range(3)])

    def finish(self):
        for copy in self.diagonal() + self.side() + self.down():
            copy.wait_send()


class ReduceLine(Reduce):
    def step(self, k, up, arriving):
        z = self.z
        plane = (3 if arriving else 4) - k + z if up else k - (3 if arriving else 4) + z
        beyond = z + 1 if up != arriving else z - 1
        real = (plane >= 0) & (plane <= 3) & (beyond >= 0) & (beyond <= 3)
        plane, beyond = jnp.clip(plane, 0, 3), jnp.clip(beyond, 0, 3)
        place_in = plane + 1 if up else plane
        k = (3 if up else 0) + k - 1
        return real, plane, place_in, self.copy(k, self.part().at[plane], self.line.at[place_in], beyond, self.yx)

    def take(self, arrived, plane, place_in):
        arrived.wait_recv()

        def blocks(yx, carry):
            self.add(plane, yx, [self.line.at[place_in, yx]])
            return carry

        lax.fori_loop(0, 4, blocks, 0)

    def move(self, k):
        for up in (True, False):
            real, plane, _, leaving = self.step(k, up, False)
            if k > 1:
                came, _, place_in, arrived = self.step(k - 1, up, True)

                pl.when(real & came)(functools.partial(self.take, arrived, plane, place_in))

            pl.when(real)(leaving.start)

    def halves(self):
        half = self.ring1.shape[1]
        own = self.part().at[self.z, self.d]
        return [
            self.copy(6, own.at[0:half], self.ring1.at[0], self.z, self.x),
            self.copy(7, own.at[half:], self.ring1.at[1], self.z, self.y),
        ]

    def sides(self):
        return [
            self.copy(8, self.part().at[self.z, self.x], self.ring2.at[0], self.z, self.x),
            self.copy(9, self.part().at[self.z, self.y], self.ring2.at[1], self.z, self.y),
        ]

    def stage1(self):
        self.move(1)

    def stage2(self):
        self.move(2)

    def stage3(self):
        self.move(3)

    def stage4(self):
        for up in (True, False):
            came, plane, place_in, arrived = self.step(3, up, True)
            pl.when(came)(functools.partial(self.take, arrived, plane, place_in))

        self.start(self.halves())

    def stage5(self):
        self.arrive(self.halves())
        half = self.ring1.shape[1]
        for yx, start, piece in ((self.y, 0, 0), (self.x, half, 1)):
            own = self.part().at[self.z, yx, start : start + half]
            self.add_up(own, [self.ring1.at[piece]], own)
        self.start(self.sides())

    def stage6(self):
        self.arrive(self.sides())
        self.give([self.ring2.at[0], self.ring2.at[1]])

    def finish(self):
        for k in (1, 2, 3):
            for up in (True, False):
                real, _, _, leaving = self.step(k, up, False)
                pl.when(real)(leaving.wait_send)
        for copy in self.halves() + self.sides():
            copy.wait_send()


def lanes(j):
    return slice(j * 128, (j + 1) * 128)


def bottom(v):
    return jnp.broadcast_to(v[7:8], v.shape)


def top(v):
    return jnp.broadcast_to(v[0:1], v.shape)


def masks_down(keep, place_in):
    m1 = jnp.where(place_in >= 1, keep, 0.0)
    m2 = m1 * pltpu.roll(m1, 1, 0)
    m4 = m2 * pltpu.roll(m2, 2, 0)
    for n in (1, 2, 4):
        keep = keep * jnp.where(place_in >= n, pltpu.roll(keep, n, 0), 1.0)
    return m1, m2, m4, keep


def masks_up(after, place_in):
    m1 = jnp.where(place_in <= 6, after, 0.0)
    m2 = m1 * pltpu.roll(m1, 7, 0)
    m4 = m2 * pltpu.roll(m2, 6, 0)
    for n in (1, 2, 4):
        after = after * jnp.where(place_in <= 7 - n, pltpu.roll(after, 8 - n, 0), 1.0)
    return m1, m2, m4, after


def wkv_forward(k_ref, v_ref, r_ref, keep_ref, rows_ref, mixed_ref, sn_ref, sd_ref):
    length, width = k_ref.shape
    tiles = width // 128
    place_in = lax.broadcasted_iota(jnp.int32, (8, 128), 0)
    first = place_in == 0
    zero = jnp.zeros((8, 128), F32)

    def pair(g, carry):
        carry = list(carry)
        base = pl.multiple_of(g * 16, 16)
        keeps = [keep_ref[pl.ds(base + 8 * h, 8), :] for h in range(2)]
        masks = [masks_down(keep, place_in) for keep in keeps]
        for j in range(tiles):
            d1, d2, d4, eu = (rows_ref[n : n + 1, lanes(j)] for n in range(4))
            dp = rows_ref[8:16, lanes(j)]
            made = []
            for h in range(2):
                at = pl.ds(base + 8 * h, 8)
                keep, (m1, m2, m4, mp) = keeps[h], masks[h]
                ek = jnp.exp(k_ref[at, lanes(j)])
                v = v_ref[at, lanes(j)]
                num, den = ek * v, ek
                x, b = num, eu * ek
                for n, coef in ((1, m1 * d1), (2, m2 * d2), (4, m4 * d4)):
                    num = num + coef * pltpu.roll(num, n, 0)
                    den = den + coef * pltpu.roll(den, n, 0)
                coef = mp * dp
                cn, cd = carry[2 * j], carry[2 * j + 1]
                num = num + coef * cn
                den = den + coef * cd
                sn = keep * jnp.where(first, cn, pltpu.roll(num, 1, 0))
                sd = keep * jnp.where(first, cd, pltpu.roll(den, 1, 0))
                carry[2 * j], carry[2 * j + 1] = bottom(num), bottom(den)
                sn_ref[at, lanes(j)] = sn
                sd_ref[at, lanes(j)] = sd
                weighted = (sn + eu * x) / (sd + b)
                made.append(jax.nn.sigmoid(r_ref[at, lanes(j)]) * weighted)
            mixed_ref[pl.ds(base, 16), lanes(j)] = jnp.concatenate(made, axis=0).astype(BF16)
        return tuple(carry)

    lax.fori_loop(0, length // 16, pair, (zero,) * (2 * tiles))


def wkv_backward(
    g_ref, k_ref, v_ref, r_ref, sn_ref, sd_ref, keep_ref, rows_ref, gk_ref, gv_ref, gr_ref, begin, end, carry
):
    length, width = k_ref.shape
    tiles = width // 128
    place_in = lax.broadcasted_iota(jnp.int32, (8, 128), 0)
    last = place_in == 7
    zero = jnp.zeros((8, 128), F32)
    pairs = length // 16

    def pair(step, carry):
        carry = list(carry)
        base = pl.multiple_of((pairs - 1 - step) * 16, 16)
        low, high = (keep_ref[pl.ds(base + 8 * h, 8), :] for h in range(2))
        afters = [
            jnp.where(last, top(high), pltpu.roll(low, 7, 0)),
            jnp.where(last, carry[4 * tiles], pltpu.roll(high, 7, 0)),
        ]
        masks = [masks_up(after, place_in) for after in afters]
        carry[4 * tiles] = top(low)
        for j in range(tiles):
            d1, d2, d4, eu = (rows_ref[n : n + 1, lanes(j)] for n in range(4))
            dp = rows_ref[16:24, lanes(j)]
            made = [None, None]
            for h in (1, 0):
                at = pl.ds(base + 8 * h, 8)
                after, (m1, m2, m4, mp) = afters[h], masks[h]
                ek = jnp.exp(k_ref[at, lanes(j)])
                v = v_ref[at, lanes(j)]
                sn, sd = sn_ref[at, lanes(j)], sd_ref[at, lanes(j)]
                s = jax.nn.sigmoid(r_ref[at, lanes(j)])
                b = eu * ek
                inverse = 1.0 / (sd + b)
                weighted = (sn + b * v) * inverse
                g = g_ref[at, lanes(j)]
                gs = g * s
                p = gs * inverse
                q = -p * weighted
                gr = gs * weighted * (1.0 - s)
                hp, hq = p, q
                for n, coef in ((1, m1 * d1), (2, m2 * d2), (4, m4 * d4)):
                    hp = hp + coef * pltpu.roll(hp, 8 - n, 0)
                    hq = hq + coef * pltpu.roll(hq, 8 - n, 0)
                coef = mp * dp
                cp, cq = carry[4 * j], carry[4 * j + 1]
                hp = hp + coef * cp
                hq = hq + coef * cq
                ap = after * jnp.where(last, cp, pltpu.roll(hp, 7, 0))
                aq = after * jnp.where(last, cq, pltpu.roll(hq, 7, 0))
                carry[4 * j], carry[4 * j + 1] = top(hp), top(hq)
                bonus = b * (v * p + q)
                gv = ek * ap + b * p
                gk = ek * (v * ap + aq) + bonus
                carry[4 * j + 2] = carry[4 * j + 2] + bonus
                carry[4 * j + 3] = carry[4 * j + 3] + (ap * sn + aq * sd)
                made[h] = (gk, gv, gr)
            both = pl.ds(base, 16)
            for n, ref in enumerate((gk_ref, gv_ref, gr_ref)):
                ref[both, lanes(j)] = jnp.concatenate([made[0][n], made[1][n]], axis=0).astype(BF16)
        return tuple(carry)

    return lax.fori_loop(begin, end, pair, (zero,) * (4 * tiles + 1) if carry is None else carry)


def wkv_sums(carry, rows_ref, decay_ref, bonus_ref):
    for j in range(decay_ref.shape[1] // 128):
        bonus_ref[0:1, lanes(j)] = jnp.sum(carry[4 * j + 2], axis=0, keepdims=True)
        decay_ref[0:1, lanes(j)] = -rows_ref[4:5, lanes(j)] * jnp.sum(carry[4 * j + 3], axis=0, keepdims=True)


NN, NT, TN = ((1,), (0,)), ((1,), (1,)), ((0,), (0,))
KEY, VALUE, GATE, EMIT, GATE2, FFN = 0, 1, 2, 3, 4, 5
KEYS, VALUES = (5, 7, 9, 11), (6, 8, 10, 12)
RINGS = 11
VECTORS = 11
TILE = 64
GAIN1, BIAS1, GAIN2, BIAS2, FADE, REWARD, MK1, MV1, MR1, MK2, MR2, OWN_FADE, OWN_REWARD = range(13)


def dot(a, b, dims):
    return lax.dot_general(a, b, (dims, ((), ())), preferred_element_type=F32)


def over_rows(length, size, body):
    def step(i, carry):
        body(strip(i, size))
        return carry

    lax.fori_loop(0, length // size, step, 0)


def matrix(ref):
    return ref[...].reshape(16 * ref.shape[2], ref.shape[3])


def emit_half(ref, h):
    rows = ref.shape[2] // 2
    return ref[:, :, h * rows : (h + 1) * rows, :].reshape(16 * rows, ref.shape[3])


def wide(column, width):
    return jnp.concatenate([column] * (width // 128), axis=1)


def norm(x):
    center = x - jnp.mean(x, axis=-1, keepdims=True)
    inverse = lax.rsqrt(jnp.mean(center * center, axis=-1, keepdims=True) + 1e-05)
    return center * inverse, inverse


def norm_and_mix(length, width, load, gain, bias, keep_ref, mixes, outs):
    first = lax.broadcasted_iota(jnp.int32, (TILE, width), 0) == 0

    def step(i, before):
        at = strip(i, TILE)
        unit, _ = norm(load(at))
        normed = unit * gain + bias
        prev = jnp.where(first, before, pltpu.roll(normed, 1, 0)) * wide(keep_ref[at, :], width)
        differ = normed - prev
        for share, out in zip(mixes, outs):
            out[at, :] = (prev + differ * share).astype(BF16)
        return normed[TILE - 1 : TILE]

    lax.fori_loop(0, length // TILE, step, jnp.zeros((1, width), F32))


def unweave(ref, own, other, c):
    at = lax.broadcasted_iota(jnp.int32, (ref.shape[0], 128), 1) // 32
    for t in range(own.shape[1] // 128):
        a, b = ref[:, lanes(2 * t)].astype(F32), ref[:, lanes(2 * t + 1)].astype(F32)
        a3, a2, b2, b1 = pltpu.roll(a, 96, 1), pltpu.roll(a, 64, 1), pltpu.roll(b, 64, 1), pltpu.roll(b, 32, 1)
        first = jnp.where(at == 0, a, jnp.where(at == 1, a3, jnp.where(at == 2, b2, b1)))
        second = jnp.where(at == 0, a3, jnp.where(at == 1, a2, jnp.where(at == 2, b1, b)))
        own[:, lanes(t)] = jnp.where(c == 0, first, second).astype(BF16)
        other[:, lanes(t)] = jnp.where(c == 0, second, first).astype(BF16)


def weave(a, b, out):
    at = lax.broadcasted_iota(jnp.int32, (out.shape[0], 128), 1) // 32
    for t in range(out.shape[1] // 128):
        p, q = a[:, lanes(t // 2)], b[:, lanes(t // 2)]
        if t % 2 == 0:
            turned = (p, pltpu.roll(q, 32, 1), pltpu.roll(p, 32, 1), pltpu.roll(q, 64, 1))
        else:
            turned = (pltpu.roll(p, 64, 1), pltpu.roll(q, 96, 1), pltpu.roll(p, 96, 1), q)
        out[:, lanes(t)] = jnp.where(
            at == 0, turned[0], jnp.where(at == 1, turned[1], jnp.where(at == 2, turned[2], turned[3]))
        )


def forward_kernel(
    wk, wv, wr, wg, wo, fk, fvt, vec, x_own, up_own, starts,
    g_out, out, x_out, up_out, ins_out, kvr_out, sn_out, sd_out, mixed_out, resid_out, ins2_out, pre_out, act_out,
    gv_out, gr_out, vec_out, rows_out, keep_out,
    own3, other3, keep_own, gv, g, x, up, ins, kvr, sn, sd, mixed, sum_own, sum_other, resid, ins2, pre, act, v_send, v_other, gval, grec, low_half,
    local_sem, ex_send, ex_recv, sends, recvs, lsends, lrecvs, vsends, vrecvs, out_sem, sum_send, sum_recv, val_send, val_recv,
):
    z, yx, c = place()
    length, width = x.shape
    half = width // 2
    span = length // 2
    partner = (z * 4 + yx, 1 - c)
    keep_own[...] = jnp.broadcast_to(1.0 - starts[...].astype(F32), (128, span)).T
    for n, ref in enumerate((wk, wv, wr)):
        unweave(ref, own3.at[n], other3.at[n], c)
    enter(z, yx, c)

    block = wk.shape[0]
    mine = strip(c, block)
    rows_mine = strip(c, span)
    swaps = [
        (vec, gv.at[z, yx, c]),
        (other3, g.at[0:3, z, yx, mine]),
        (wg.at[:, strip(1 - c, half)], g.at[GATE2, z, yx, mine]),
        (x_own, x.at[rows_mine]),
        (keep_own, keep_out.at[rows_mine]),
        (up_own, up.at[rows_mine]),
    ]
    swaps = [remote(a, b, ex_send.at[n], ex_recv.at[n], partner) for n, (a, b) in enumerate(swaps)]
    keeps = [
        (vec, gv.at[z, yx, c]),
        (own3, g.at[0:3, z, yx, mine]),
        (wg.at[:, strip(c, half)], g.at[GATE2, z, yx, mine]),
        (x_own, x.at[rows_mine]),
        (keep_own, keep_out.at[rows_mine]),
        (up_own, up.at[rows_mine]),
    ]
    for h in range(2):
        keeps.append((wo.at[:, h * half : (h + 1) * half], g.at[EMIT, z, yx, h * block : (h + 1) * block]))
    for n in range(4):
        chunk = slice(n * half, (n + 1) * half)
        keeps.append((fk.at[:, chunk], g.at[KEYS[n], z, yx]))
        keeps.append((fvt.at[:, chunk], g.at[VALUES[n], z, yx]))
    keeps = [pltpu.make_async_copy(a, b, local_sem.at[n]) for n, (a, b) in enumerate(keeps)]
    for copy in swaps + keeps:
        copy.start()
    weights = Gather(lambda p: g.at[p], sends, recvs)
    lines = GatherLine(lambda p: g.at[RINGS + p], lsends, lrecvs)
    vectors = Gather(lambda p: gv, vsends, vrecvs)

    outs = []

    def put(src, dst):
        copy = pltpu.make_async_copy(src, dst, out_sem.at[len(outs)])
        copy.start()
        outs.append(copy)
        return copy

    along_z = {3: [(0, 1)], 4: [(1, 1)], 5: [(0, 2)], 6: [(1, 2)], 7: [(0, 3)], 8: [(1, 3)]}

    def turn(n):
        if n < RINGS:
            weights.step(n)
            if n + 2 < RINGS:
                weights.start(weights.along(n + 2))
        if 1 <= n <= RINGS:
            weights.forward(n - 1)
        for p, k in along_z.get(n, []):
            lines.line(p, k)
        if n >= 2:
            weights.arrive(weights.onward(n - 2))
            put(g.at[n - 2], g_out.at[n - 2])

    def lined(p):
        lines.ready(p - RINGS)
        put(g.at[p], g_out.at[p])

    for copy in keeps[6:]:
        copy.wait()
    for p in range(PIECES - RINGS):
        lines.start(lines.ring(p))
    for n in (0, 1, 2):
        swaps[n].wait()
        keeps[n].wait()
    vectors.start(vectors.along(0))
    weights.start(weights.along(0))
    weights.start(weights.along(1))
    for p in range(PIECES - RINGS):
        lines.arrive(lines.ring(p))
        lines.start(lines.onward(p))
    vectors.step(0)
    turn(0)
    vectors.forward(0)
    for n in (3, 4, 5):
        swaps[n].wait()
        keeps[n].wait()
    x_copy, up_copy = put(x, x_out), put(up, up_out)
    for p in range(PIECES - RINGS):
        lines.arrive(lines.onward(p))
    turn(1)
    vectors.arrive(vectors.onward(0))

    for t in range(width // 128):
        parts = [gv[(2 * t + k) // 4, (2 * t + k) % 4, core].astype(F32) for k in range(2) for core in range(2)]
        vec_out[:, lanes(t)] = functools.reduce(lambda a, b: a + b, parts)
    ramp = lax.broadcasted_iota(jnp.int32, (8, 128), 0).astype(F32)
    for t in range(half // 128):
        own = functools.reduce(lambda a, b: a + b, [gv[t, k, c].astype(F32) for k in range(4)])
        rate = jnp.exp(own[OWN_FADE : OWN_FADE + 1])
        head = [
            jnp.exp(-rate), jnp.exp(-2.0 * rate), jnp.exp(-4.0 * rate), jnp.exp(own[OWN_REWARD : OWN_REWARD + 1]),
            rate * jnp.exp(-rate),
        ]
        for n, row in enumerate(head):
            rows_out[n : n + 1, lanes(t)] = row
        rows_out[8:16, lanes(t)] = jnp.exp(-(ramp + 1.0) * rate)
        rows_out[16:24, lanes(t)] = jnp.exp(-(8.0 - ramp) * rate)

    def row(n):
        return vec_out[n : n + 1, :]

    norm_and_mix(
        length, width, lambda at: x[at, :].astype(F32), row(GAIN1), row(BIAS1), keep_out,
        [row(MK1), row(MV1), row(MR1)], [ins.at[n] for n in range(3)],
    )
    put(ins, ins_out)
    kvr_copies = []
    for n in range(3):
        turn(n + 2)
        weight = g.at[n]

        def project(at):
            kvr[n, at, :] = dot(ins[n, at, :], matrix(weight), NN)

        over_rows(length, 256, project)
        kvr_copies.append(put(kvr.at[n], kvr_out.at[n]))
    wkv_forward(kvr.at[0], kvr.at[1], kvr.at[2], keep_out, rows_out, mixed, sn, sd)
    put(mixed, mixed_out)
    put(sn, sn_out)
    put(sd, sd_out)
    turn(5)
    weight = g.at[EMIT]
    quarters = length // 4

    def emitted(n):
        at = strip(n, quarters)
        return remote(sum_own.at[at], sum_other.at[at], sum_send.at[n], sum_recv.at[n], partner)

    def emit(n, carry):
        at = strip(n, quarters)
        for h in range(2):
            sum_own[at, h * half : (h + 1) * half] = dot(mixed[at, :], emit_half(weight, h), NN).astype(BF16)
        emitted(n).start()
        return carry

    lax.fori_loop(0, 4, emit, 0)
    turn(6)
    for n in range(4):
        emitted(n).wait()

    def add_up(at):
        total = x[at, :].astype(F32) + (sum_own[at, :].astype(F32) + sum_other[at, :].astype(F32))
        resid[0, at, :] = total[:, :half]
        resid[1, at, :] = total[:, half:]
        return total

    norm_and_mix(
        length, width, add_up, row(GAIN2), row(BIAS2), keep_out, [row(MK2), row(MR2)], [ins2.at[n] for n in range(2)]
    )
    put(resid, resid_out)
    put(ins2, ins2_out)
    for copy in kvr_copies:
        copy.wait()
    weight = g.at[GATE2]

    def gate(at):
        kvr[2, at, :] = jax.nn.sigmoid(dot(ins2[1, at, :], matrix(weight), NN))

    over_rows(length, 256, gate)
    pre_copies = []

    def expand_chunk(j):
        weight, slot = g.at[KEYS[j]], len(pre_copies) % 2
        if len(pre_copies) >= 2:
            pre_copies[-2].wait()

        def expand(at):
            positive = jnp.maximum(dot(ins2[0, at, :], matrix(weight), NN), 0.0)
            pre[slot, at, :] = positive.astype(BF16)
            act[j, at, :] = (positive * positive).astype(BF16)

        over_rows(length, 256, expand)
        pre_copies.append(put(pre.at[slot], pre_out.at[j]))
        put(act.at[j], act_out.at[j])

    def contract_chunk(j):
        weight = g.at[VALUES[j]]

        def contract(at):
            for h in range(2):
                part = dot(act[j, at, :], weight[2 * h : 2 * h + 2].reshape(half, -1), NT)
                kvr[h, at, :] = part if j == 0 else kvr[h, at, :] + part

        over_rows(length, 256, contract)

    turn(7)
    expand_chunk(0)
    turn(8)
    contract_chunk(0)
    turn(9)
    expand_chunk(1)
    turn(10)
    contract_chunk(1)
    lined(KEYS[3])
    expand_chunk(3)
    lined(VALUES[3])
    contract_chunk(3)
    turn(11)
    expand_chunk(2)
    turn(12)
    contract_chunk(2)

    columns = strip(c, half)

    def value_copy(n):
        at = strip(n, quarters)
        return remote(v_send.at[at], v_other.at[at], val_send.at[n], val_recv.at[n], partner)

    def back_copy(n):
        at = strip(n, quarters)
        return remote(gval.at[c, at], gval.at[c, at], val_send.at[4 + n], val_recv.at[4 + n], partner)

    def send_values(n, carry):
        def narrow(i, carry):
            at = strip(n * (quarters // 32) + i, 32)
            v_send[at, :] = kvr[1 - c, at, :].astype(BF16)
            return carry

        lax.fori_loop(0, quarters // 32, narrow, 0)
        value_copy(n).start()
        return carry

    def finish_values(n, carry):
        value_copy(n).wait()

        def finish(i, carry):
            at = strip(n * (quarters // 32) + i, 32)
            value = kvr[c, at, :] + v_other[at, :].astype(F32)
            s = kvr[2, at, :]
            low_half[at, :] = (resid[c, at, :] + s * value).astype(BF16)
            upstream = up[at, columns].astype(F32)
            gval[c, at, :] = (upstream * s).astype(BF16)
            grec[at, :] = (upstream * value * s * (1.0 - s)).astype(BF16)
            return carry

        lax.fori_loop(0, quarters // 32, finish, 0)
        back_copy(n).start()
        return carry

    lax.fori_loop(0, 4, send_values, 0)
    lax.fori_loop(0, 4, finish_values, 0)
    give = remote(low_half.at[strip(1 - c, span)], out.at[:, columns], val_send.at[8], val_recv.at[8], partner)
    give.start()
    put(low_half.at[rows_mine], out.at[:, columns])
    put(grec, gr_out)
    for n in range(4):
        back_copy(n).wait()
    put(gval, gv_out)
    give.wait()

    def close(p, carry):
        weights.finish(p)
        return carry

    lax.fori_loop(0, RINGS, close, 0)
    for p in range(PIECES - RINGS):
        lines.finish(p)
    vectors.finish(0)
    waited = kvr_copies + pre_copies[:2]
    for copy in outs:
        if not any(copy is other for other in waited):
            copy.wait()


def forward_call(wk, wv, wr, wg, wo, fk, fvt, vec, x_own, up_own, starts):
    span, width = x_own.shape
    length, half = 2 * span, width // 2
    block = (fk.shape[0], half)
    any_, vmem = pl.BlockSpec(memory_space=pl.ANY), pl.BlockSpec(memory_space=pltpu.VMEM)
    full, col = (length, width), (length, half)

    def shape(dims, kind):
        return jax.ShapeDtypeStruct(dims, kind)

    outs = (
        (shape((PIECES, 4, 4) + block, BF16), any_),
        (shape((span, width), BF16), any_),
        (shape(full, BF16), any_),
        (shape(full, BF16), any_),
        (shape((3,) + full, BF16), any_),
        (shape((3,) + col, F32), any_),
        (shape(col, F32), any_),
        (shape(col, F32), any_),
        (shape(col, BF16), any_),
        (shape((2,) + col, F32), any_),
        (shape((2,) + full, BF16), any_),
        (shape((4,) + col, BF16), any_),
        (shape((4,) + col, BF16), any_),
        (shape((2,) + col, BF16), any_),
        (shape(col, BF16), any_),
        (shape((16, width), F32), vmem),
        (shape((24, half), F32), vmem),
        (shape((length, 128), F32), vmem),
    )
    dma = pltpu.SemaphoreType.DMA
    return pl.pallas_call(
        forward_kernel,
        out_shape=tuple(o[0] for o in outs),
        in_specs=[vmem] * 11,
        out_specs=tuple(o[1] for o in outs),
        scratch_shapes=[
            pltpu.VMEM((3, block[0] // 2, half), BF16),
            pltpu.VMEM((3, block[0] // 2, half), BF16),
            pltpu.VMEM((span, 128), F32),
            pltpu.VMEM((4, 4, 2) + vec.shape, BF16),
            pltpu.VMEM((PIECES, 4, 4) + block, BF16),
            pltpu.VMEM(full, BF16),
            pltpu.VMEM(full, BF16),
            pltpu.VMEM((3,) + full, BF16),
            pltpu.VMEM((3,) + col, F32),
            pltpu.VMEM(col, F32),
            pltpu.VMEM(col, F32),
            pltpu.VMEM(col, BF16),
            pltpu.VMEM(full, BF16),
            pltpu.VMEM(full, BF16),
            pltpu.VMEM((2,) + col, F32),
            pltpu.VMEM((2,) + full, BF16),
            pltpu.VMEM((2,) + col, BF16),
            pltpu.VMEM((4,) + col, BF16),
            pltpu.VMEM(col, BF16),
            pltpu.VMEM(col, BF16),
            pltpu.VMEM((2,) + col, BF16),
            pltpu.VMEM(col, BF16),
            pltpu.VMEM(col, BF16),
            dma((16,)), dma((6,)), dma((6,)),
            dma((RINGS, 7)), dma((RINGS, 7)), dma((PIECES - RINGS, 10)), dma((PIECES - RINGS, 10)), dma((1, 7)), dma((1, 7)),
            dma((40,)), dma((4,)), dma((4,)), dma((9,)), dma((9,)),
        ],
        compiler_params=pltpu.CompilerParams(
            collective_id=0, has_side_effects=True, vmem_limit_bytes=63 * MIB
        ),
        name="forward",
    )(wk, wv, wr, wg, wo, fk, fvt, vec, x_own, up_own, starts)


R_VALUE, R_KEY, R_GATE2, R_EMIT, R_TIME = 0, 4, 8, 9, 10
WEIGHT_ORDER = [p for j in range(4) for p in (VALUES[j], KEYS[j])] + [GATE2, EMIT, KEY, VALUE, GATE]
LINED = (1, 3, 5)
SUMS = 11
S_GAIN1, S_BIAS1, S_GAIN2, S_BIAS2, S_DECAY, S_BONUS, S_MK1, S_MV1, S_MR1, S_MK2, S_MR2 = range(11)
SLOTS = 12


def whole(ref, at):
    return jnp.concatenate([ref[0, at, :], ref[1, at, :]], axis=1)


def halves(ref, at, value):
    half = value.shape[1] // 2
    ref[0, at, :] = value[:, :half].astype(ref.dtype)
    ref[1, at, :] = value[:, half:].astype(ref.dtype)


def fold(value):
    return sum(value[n : n + 8] for n in range(8, value.shape[0], 8)) + value[:8]


def back_through_norm(g, unit, inverse, gain):
    q = g * gain
    return inverse * (
        q - jnp.mean(q, axis=-1, keepdims=True) - unit * jnp.mean(q * unit, axis=-1, keepdims=True)
    )


def lifted(now, following, last):
    return jnp.where(last, following[0:1], pltpu.roll(now, now.shape[0] - 1, 0))


def backward_kernel(
    plan,
    g, x_in, up_in, ins_in, kvr_in, sn_in, sd_in, mixed_in, resid_in, ins2_in, pre_in, act_in, gv_in, gr_in,
    vec, rows, keep,
    out_k, out_v, out_r, out_g, out_o, out_fk, out_fv, vsum, vother, gtok,
    own_t, recv_t, own_g,
    part, ring1, ring2, line, lring1, lring2, lline, vpart, vring1, vring2, vline,
    b, w, f, resid, sum_other, n1_other, acc, own_sums,
    load_sem, w_sem, sends, recvs, lsends, lrecvs, vsends, vrecvs, ex_send, ex_recv, sum_send, sum_recv,
):
    z, yx, c = place()
    nx, ny, nd, zs = neighbours(z, yx)
    length, half = b.shape[1:]
    width = 2 * half
    span = length // 2
    quarter = length // 4
    partner = (z * 4 + yx, 1 - c)
    loads = {}

    def load(name, src, dst):
        copy = pltpu.make_async_copy(src, dst, load_sem.at[len(loads)])
        copy.start()
        loads[name] = copy

    def loaded(*names):
        for name in names:
            loads[name].wait()

    def pair(n):
        return b.at[n : n + 2]

    def load_pair(name, src, n):
        for h in range(2):
            load((name, h), src.at[:, h * half : (h + 1) * half], b.at[n + h])

    def loaded_pair(name):
        loaded((name, 0), (name, 1))

    def weight_copy(n):
        return pltpu.make_async_copy(g.at[WEIGHT_ORDER[n]], w.at[n % 3], w_sem.at[n])

    def weight(n):
        weight_copy(n).wait()
        return w.at[n % 3]

    GVAL, ACT, PRE, IN_K2, IN_R2, GREC, GPRE = 0, 2, 4, 6, 8, 10, 11
    load("gv0", gv_in.at[0], b.at[GVAL])
    load("gv1", gv_in.at[1], b.at[GVAL + 1])
    for j in range(2):
        load(("act", j), act_in.at[j], b.at[ACT + j])
    load_pair("in_k2", ins2_in.at[0], IN_K2)
    for j in range(2):
        load(("pre", j), pre_in.at[j], b.at[PRE + j])
    for n in range(3):
        weight_copy(n).start()
    load_pair("in_r2", ins2_in.at[1], IN_R2)
    load("gr", gr_in, b.at[GREC])
    load("resid", resid_in, resid)
    enter(z, yx, c)

    columns = strip(c, half)
    outs = {R_GATE2: [own_g], R_EMIT: [out_o.at[:, h * half : (h + 1) * half] for h in range(2)]}
    for n in range(4):
        chunk = slice(n * half, (n + 1) * half)
        outs[R_VALUE + n], outs[R_KEY + n] = [out_fv.at[:, chunk]], [out_fk.at[:, chunk]]
    for n in range(3):
        outs[R_TIME + n] = [own_t.at[n]]
    sums = []
    for p in range(PIECES):
        if p in LINED:
            n = LINED.index(p)
            sums.append(
                ReduceLine(
                    part, p % PARTS, lring1.at[n], lring2.at[n], lline.at[n], outs[p], lsends.at[n], lrecvs.at[n]
                )
            )
        else:
            n = p - sum(q < p for q in LINED)
            sums.append(
                Reduce(part, p % PARTS, ring1.at[n], ring2.at[n], line.at[n], outs[p], sends.at[n], recvs.at[n])
            )
    vector_sums = Reduce(vpart, 0, vring1, vring2, vline, [vsum], vsends, vrecvs)
    final = []
    rows4 = recv_t.shape[1]
    mine, others = strip(c, rows4), strip(1 - c, rows4)

    def pump(name):
        for stage, p in plan[name]:
            if p == "v":
                getattr(vector_sums, "stage%d" % stage)()
                continue
            getattr(sums[p], "stage%d" % stage)()
            if stage == 4 and p in (R_GATE2, R_TIME, R_TIME + 1, R_TIME + 2):
                n = len(final)
                if p == R_GATE2:
                    src, dst = own_g.at[others], out_g.at[:, columns]
                else:
                    src, dst = own_t.at[p - R_TIME, others], recv_t.at[p - R_TIME]
                final.append(remote(src, dst, ex_send.at[n], ex_recv.at[n], partner))
                final[-1].start()

    def gradient(p, lhs, rhs):
        def block(a, carry):
            rows_a = dot(lhs[a // 2, :, strip(a % 2, half // 2)], rhs[...], TN)
            part[p % PARTS, a] = rows_a.astype(BF16).reshape(part.shape[2:])
            return carry

        lax.fori_loop(0, 4, block, 0, unroll=True)

    def thirds(ref, h):
        return ref[2 * h : 2 * h + 2].reshape(half, half)

    loaded("gv0", "gv1")
    for j in range(4):
        loaded(("act", j))
        gradient(R_VALUE + j, pair(GVAL), b.at[ACT + j % 2])
        if j < 2:
            load(("act", j + 2), act_in.at[j + 2], b.at[ACT + j])
        pump("fv%d" % j)
    loaded_pair("in_k2")
    for j in range(4):
        loaded(("pre", j))
        value_w = weight(2 * j)

        def through(at):
            g_hidden = sum(dot(b[GVAL + h, at, :], thirds(value_w, h), NN) for h in range(2))
            b[GPRE, at, :] = (2.0 * b[PRE + j % 2, at, :].astype(F32) * g_hidden).astype(BF16)

        over_rows(length, 256, through)
        pump("th%d" % j)
        if j < 2:
            load(("pre", j + 2), pre_in.at[j + 2], b.at[PRE + j])
        weight_copy(2 * j + 3).start()
        gradient(R_KEY + j, pair(IN_K2), b.at[GPRE])
        pump("fk%d" % j)
        key_w = weight(2 * j + 1)

        def collect(at):
            for h in range(2):
                piece = dot(b[GPRE, at, :], thirds(key_w, h), NT)
                f[h, at, :] = piece if j == 0 else f[h, at, :] + piece

        over_rows(length, 256, collect)
        pump("co%d" % j)
        weight_copy(2 * j + 4).start()
    loaded_pair("in_r2")
    loaded("gr")
    gradient(R_GATE2, pair(IN_R2), b.at[GREC])
    pump("g2")
    gate_w = weight(8)

    def gate_back(at):
        for h in range(2):
            f[2 + h, at, :] = dot(b[GREC, at, :], thirds(gate_w, h), NT)

    over_rows(length, 256, gate_back)
    pump("gb")
    weight_copy(11).start()
    loaded("resid")

    SUM_OWN, UP, BRANCH, MIXED, G3, X, IN_K, IN_V, IN_R, SEND = 0, 2, 4, 6, 7, 4, 10, 0, 2, 6
    load_pair("up", up_in, UP)
    load("mixed", mixed_in, b.at[MIXED])
    acc[...] = jnp.zeros_like(acc)
    last = lax.broadcasted_iota(jnp.int32, (TILE, width), 0) == TILE - 1

    def row(n):
        return vec[n : n + 1, :]

    def kept(at, n):
        return wide(keep[at, :], width) if n is None else wide(keep[n, :], width)

    gain2, bias2, mk2, mr2 = (GAIN2, BIAS2, MK2, MR2)
    sum_copies = []
    for q in range(4):

        def tile(i, carry):
            base = q * quarter + i * TILE
            at = pl.ds(pl.multiple_of(base, TILE), TILE)
            after = pl.ds(pl.multiple_of(jnp.minimum(base + TILE, length - 8), 8), 8)
            inside = jnp.where(base + TILE < length, 1.0, 0.0)
            keep_at, keep_after = wide(keep[at, :], width), wide(keep[after, :], width) * inside
            unit, _ = norm(whole(resid, at))
            normed = unit * row(gain2) + row(bias2)
            total = jnp.zeros_like(unit)
            for n, share in enumerate((mk2, mr2)):
                back = whole(f.at[2 * n : 2 * n + 2], at)
                ahead = lifted(back * keep_at, whole(f.at[2 * n : 2 * n + 2], after) * keep_after, last)
                total = total + ahead + (back - ahead) * row(share)
                acc[S_MK2 + n] = acc[S_MK2 + n] + fold(normed * (back - ahead))
            acc[S_GAIN2] = acc[S_GAIN2] + fold(total * unit)
            acc[S_BIAS2] = acc[S_BIAS2] + fold(total)
            halves(b.at[SUM_OWN : SUM_OWN + 2], at, total)
            return carry

        lax.fori_loop(0, quarter // TILE, tile, 0)
        at = pl.ds(q * quarter, quarter)
        sum_copies.append(
            remote(b.at[SUM_OWN : SUM_OWN + 2, at], sum_other.at[:, at], sum_send.at[q], sum_recv.at[q], partner)
        )
        sum_copies[-1].start()
        pump("a%d" % q)
    for n in range(3):
        load(("kvr", n), kvr_in.at[n], f.at[n])
    load("sn", sn_in, f.at[3])
    load("sd", sd_in, f.at[4])
    load_pair("in_k", ins_in.at[0], IN_K)

    loaded_pair("up")
    for q in range(4):
        sum_copies[q].wait_recv()

        def tile(i, carry):
            at = pl.ds(pl.multiple_of(q * quarter + i * TILE, TILE), TILE)
            unit, inverse = norm(whole(resid, at))
            total = whole(b.at[SUM_OWN : SUM_OWN + 2], at).astype(F32) + whole(sum_other, at).astype(F32)
            back = whole(pair(UP), at).astype(F32) + back_through_norm(total, unit, inverse, row(gain2))
            halves(pair(BRANCH), at, back)

            @pl.when(c == q // 2)
            def _():
                gtok[pl.ds(pl.multiple_of((q % 2) * quarter + i * TILE, TILE), TILE), :] = back

            return carry

        lax.fori_loop(0, quarter // TILE, tile, 0)
        pump("b%d" % q)
    for copy in sum_copies:
        copy.wait_send()
    load_pair("in_v", ins_in.at[1], IN_V)
    load_pair("in_r", ins_in.at[2], IN_R)

    loaded("mixed")
    rows_h = part.shape[3] // 2
    for h in range(2):

        def emit_rows(a, carry):
            block = dot(b[MIXED, :, strip(a, half // 2)], b[BRANCH + h], TN).astype(BF16)
            part[R_EMIT, pl.ds(2 * a, 2), :, h * rows_h : (h + 1) * rows_h, :] = block.reshape(2, 4, rows_h, half)
            return carry

        lax.fori_loop(0, 2, emit_rows, 0)
    pump("em")
    emit_w = weight(9)

    def emit_back(at):
        resid[0, at, :] = sum(dot(b[BRANCH + h, at, :], emit_half(emit_w, h), NT) for h in range(2))

    over_rows(length, 256, emit_back)
    pump("eb")
    weight_copy(12).start()
    load_pair("x", x_in, X)

    loaded(("kvr", 0), ("kvr", 1), ("kvr", 2), "sn", "sd")
    carry = None
    for q in range(4):
        carry = wkv_backward(
            resid.at[0], f.at[0], f.at[1], f.at[2], f.at[3], f.at[4], keep, rows, b.at[G3], b.at[G3 + 1], b.at[G3 + 2],
            q * (length // 64), (q + 1) * (length // 64), carry,
        )
        pump("w%d" % q)
    wkv_sums(carry, rows, own_sums.at[0:1], own_sums.at[1:2])

    for n, (name, slot) in enumerate((("in_k", IN_K), ("in_v", IN_V), ("in_r", IN_R))):
        loaded_pair(name)
        sums[R_TIME + n - PARTS].finish()
        gradient(R_TIME + n, pair(slot), b.at[G3 + n])
        pump("t%d" % n)
    loaded_pair("x")
    for n in range(3):
        weight(10 + n)
    for n in range(3):
        for h in range(2):
            f[n, pl.ds(h * span + quarter, 8), :] = jnp.zeros((8, half), F32)
    n1_copies = []
    for q in (3, 2, 1, 0):
        def back_rows(n, carry):
            for h in range(2):
                if q < 3:
                    f[n, pl.ds(h * span + quarter, 8), :] = f[n, pl.ds(h * span, 8), :]
                f[n, pl.ds(h * span, quarter), :] = dot(
                    b[G3 + n, pl.ds(q * quarter, quarter), :], thirds(w.at[(n + 1) % 3], h), NT
                )
            return carry

        lax.fori_loop(0, 3, back_rows, 0)

        def tile(i, carry):
            base = q * quarter + i * TILE
            at = pl.ds(pl.multiple_of(base, TILE), TILE)
            after = pl.ds(pl.multiple_of(jnp.minimum(base + TILE, length - 8), 8), 8)
            keep_at, keep_after = wide(keep[at, :], width), wide(keep[after, :], width)

            def take(n, start, size):
                return jnp.concatenate(
                    [f[n, pl.ds(pl.multiple_of(h * span + start, 8), size), :] for h in range(2)], axis=1
                )

            unit, _ = norm(whole(pair(X), at).astype(F32))
            normed = unit * row(GAIN1) + row(BIAS1)
            total = jnp.zeros_like(unit)
            for n, share in enumerate((MK1, MV1, MR1)):
                back = take(n, i * TILE, TILE)
                ahead = lifted(back * keep_at, take(n, i * TILE + TILE, 8) * keep_after, last)
                total = total + ahead + (back - ahead) * row(share)
                acc[S_MK1 + n] = acc[S_MK1 + n] + fold(normed * (back - ahead))
            acc[S_GAIN1] = acc[S_GAIN1] + fold(total * unit)
            acc[S_BIAS1] = acc[S_BIAS1] + fold(total)
            rows_q = [pl.ds(pl.multiple_of(h * span + (q % 2) * quarter + i * TILE, TILE), TILE) for h in range(2)]

            @pl.when(c == q // 2)
            def _():
                for h in range(2):
                    f[3, rows_q[h], :] = total[:, h * half : (h + 1) * half]

            @pl.when(c != q // 2)
            def _():
                for h in range(2):
                    b[SEND, rows_q[h], :] = total[:, h * half : (h + 1) * half].astype(BF16)

            return carry

        lax.fori_loop(0, quarter // TILE, tile, 0)
        pump("c%d" % (3 - q))
    swap_n1 = remote(b.at[SEND], n1_other, sum_send.at[4], sum_recv.at[4], partner)
    swap_n1.start()

    for n in (S_GAIN1, S_BIAS1, S_GAIN2, S_BIAS2, S_MK1, S_MV1, S_MR1, S_MK2, S_MR2):
        acc[n, 0:1, :] = jnp.sum(acc[n], axis=0, keepdims=True)
    for i in range(16):
        vpart[0, i // 4, i % 4] = jnp.concatenate(
            [acc[n, 0:1, lanes(i // 2)] for n in range(SUMS)]
            + [own_sums[n : n + 1, lanes(i // 4)] for n in range(2)]
            + [jnp.zeros((3, 128), F32)]
        )
    pump("v0")
    swap_n1.wait()

    def tokens(i, carry):
        at = strip(i, TILE)
        spans = [pl.ds(pl.multiple_of(h * span + i * TILE, TILE), TILE) for h in range(2)]
        unit, inverse = norm(whole(pair(X), pl.ds(pl.multiple_of(c * span + i * TILE, TILE), TILE)).astype(F32))
        total = jnp.concatenate([f[3, s, :] + n1_other[s, :].astype(F32) for s in spans], axis=1)
        gtok[at, :] = gtok[at, :] + back_through_norm(total, unit, inverse, row(GAIN1))
        return carry

    lax.fori_loop(0, span // TILE, tokens, 0)
    for n in range(1, 4):
        pump("v%d" % n)
    swap = remote(vsum, vother, ex_send.at[4], ex_recv.at[4], partner)
    swap.start()
    pump("end")
    for p in range(PIECES - PARTS, PIECES):
        sums[p].finish()
    vector_sums.finish()
    out_g[:, columns] = own_g[mine, :]
    for copy in final + [swap]:
        copy.wait()
    for n, out in enumerate((out_k, out_v, out_r)):
        own, other = own_t[n, mine, :], recv_t[n]
        weave(jnp.where(c == 0, own, other), jnp.where(c == 0, other, own), out)


PLAN = {
    "fv0": [(1, 0)],
    "fv1": [(1, 1)],
    "fv2": [(1, 2)],
    "fv3": [(1, 3), (2, 0)],
    "th0": [],
    "fk0": [(1, 4), (2, 2), (2, 1)],
    "co0": [],
    "th1": [],
    "fk1": [(1, 5), (3, 0), (2, 3)],
    "co1": [(2, 4)],
    "th2": [(3, 1)],
    "fk2": [(1, 6), (3, 2)],
    "co2": [],
    "th3": [(2, 5)],
    "fk3": [(1, 7), (3, 4)],
    "co3": [(2, 6), (4, 0)],
    "g2": [(1, 8), (2, 7)],
    "gb": [],
    "a0": [(3, 3)],
    "a1": [],
    "a2": [(3, 6)],
    "a3": [(4, 1), (2, 8)],
    "b0": [(3, 7), (5, 1), (4, 2)],
    "b1": [],
    "b2": [],
    "b3": [(3, 5), (3, 8)],
    "em": [(1, 9), (6, 1)],
    "eb": [],
    "w0": [(4, 4)],
    "w1": [(2, 9)],
    "w2": [(4, 3)],
    "w3": [],
    "t0": [(1, 10)],
    "t1": [(1, 11), (5, 3), (3, 9), (4, 6)],
    "t2": [(1, 12)],
    "c0": [(2, 10), (2, 11), (6, 3), (4, 7)],
    "c1": [(4, 5), (2, 12)],
    "c2": [(3, 10), (4, 8)],
    "c3": [],
    "v0": [(1, "v"), (3, 11), (5, 5)],
    "v1": [(2, "v"), (4, 9), (4, 10), (3, 12)],
    "v2": [(3, "v"), (6, 5), (4, 11)],
    "v3": [(4, "v")],
    "end": [(4, 12)],
}


def backward_call(g, x, up, ins, kvr, sn, sd, mixed, resid, ins2, pre, act, g_value, g_recept, vec, rows, keep):
    block = g.shape[3:]
    length, half = sn.shape
    lined = len(LINED)
    rings = PIECES - lined
    any_, vmem = pl.BlockSpec(memory_space=pl.ANY), pl.BlockSpec(memory_space=pltpu.VMEM)
    dma = pltpu.SemaphoreType.DMA

    def shape(*dims):
        return jax.ShapeDtypeStruct(dims, F32)

    return pl.pallas_call(
        functools.partial(backward_kernel, PLAN),
        out_shape=(
            *[shape(block[0] // 2, 2 * half)] * 5, *[shape(block[0], 4 * half)] * 2, shape(16, 128), shape(16, 128),
            shape(length // 2, 2 * half),
        ),
        in_specs=[any_] * 14 + [vmem] * 3,
        out_specs=(vmem,) * 10,
        scratch_shapes=[
            pltpu.VMEM((3,) + block, F32),
            pltpu.VMEM((3, block[0] // 2, block[1]), F32),
            pltpu.VMEM(block, F32),
            pltpu.VMEM((PARTS, 4, 4) + block, BF16),
            pltpu.VMEM((rings, 2, 2) + block, BF16),
            pltpu.VMEM((rings, 2, 4) + block, BF16),
            pltpu.VMEM((rings, 3) + block, BF16),
            pltpu.VMEM((lined, 2, block[0] // 2, block[1]), BF16),
            pltpu.VMEM((lined, 2) + block, BF16),
            pltpu.VMEM((lined, 5, 4) + block, BF16),
            pltpu.VMEM((1, 4, 4, 16, 128), F32),
            pltpu.VMEM((2, 2, 16, 128), F32),
            pltpu.VMEM((2, 4, 16, 128), F32),
            pltpu.VMEM((3, 16, 128), F32),
            pltpu.VMEM((SLOTS, length, half), BF16),
            pltpu.VMEM((3, 4, 4) + block, BF16),
            pltpu.VMEM((5, length, half), F32),
            pltpu.VMEM((2, length, half), F32),
            pltpu.VMEM((2, length, half), BF16),
            pltpu.VMEM((length, half), BF16),
            pltpu.VMEM((SUMS, 8, 2 * half), F32),
            pltpu.VMEM((8, half), F32),
            dma((40,)), dma((PIECES,)), dma((rings, 7)), dma((rings, 7)), dma((lined, 10)), dma((lined, 10)),
            dma((7,)), dma((7,)), dma((5,)), dma((5,)), dma((5,)), dma((5,)),
        ],
        compiler_params=pltpu.CompilerParams(collective_id=1, has_side_effects=True, vmem_limit_bytes=63 * MIB),
        name="backward",
    )(g, x, up, ins, kvr, sn, sd, mixed, resid, ins2, pre, act, g_value, g_recept, vec, rows, keep)


def shifted(value, axis, steps):
    count = lax.axis_size(axis)
    first, last = (max(0, -steps), min(count, count - steps))
    return lax.ppermute(value, axis, [(source, source + steps) for source in range(first, last)])


def carried_in(array, axis, join, neutral):
    place = lax.axis_index(axis)
    gathered = jax.tree.map(
        lambda a, kind: lax.all_gather(a.astype(kind), axis),
        array,
        (jnp.bfloat16, jnp.bfloat16, jnp.bfloat16),
    )
    state = jax.tree.map(lambda a, e: jnp.zeros_like(a) + jnp.asarray(e, a.dtype), array, neutral)

    def one(turn, state):
        return join(
            state,
            jax.tree.map(
                lambda a, own: lax.dynamic_index_in_dim(a, turn, 0, False).astype(own.dtype),
                gathered,
                array,
            ),
        )

    return lax.fori_loop(0, place, one, state)


def entering(array, axis, combine, identity):
    count, place = (lax.axis_size(axis), lax.axis_index(axis))
    everything = jax.tree.map(
        lambda part, kind: lax.all_gather(part.astype(kind), axis),
        array,
        jax.tree.map(lambda a: jnp.bfloat16 if a.dtype == jnp.float32 else a.dtype, array),
    )
    start = jax.tree.map(
        lambda part, zero: jnp.broadcast_to(jnp.asarray(zero, part.dtype), part.shape),
        array,
        identity,
    )

    def turn(k, before):
        at = count - 1 - k
        reached = at > place
        new = combine(
            before, jax.tree.map(lambda part, own: part[at].astype(own.dtype), everything, array)
        )
        return jax.tree.map(lambda a, b: jnp.where(reached, a, b), new, before)

    return lax.fori_loop(0, count, turn, start)


def wide_layer_norm(values, scale_vec, shift_vec):
    center = values - jnp.mean(values, axis=-1, keepdims=True)
    inverse = lax.rsqrt(jnp.mean(center * center, axis=-1, keepdims=True) + 1e-05)
    normed = center * inverse
    return (normed * scale_vec + shift_vec, normed, inverse)


def wide_norm_back(upstream, normed, inverse, scale_vec):
    scaled = upstream * scale_vec
    inner = (
        scaled
        - jnp.mean(scaled, axis=-1, keepdims=True)
        - normed * jnp.mean(scaled * normed, axis=-1, keepdims=True)
    )
    return (
        inverse * inner,
        jnp.sum(upstream * normed, axis=(0, 1)),
        jnp.sum(upstream, axis=(0, 1)),
    )


def shift_prev(values, persist_indicator):
    arrived = shifted(values[:, -1:, :], "tensor", 1)
    return jnp.concatenate([arrived, values[:, :-1]], axis=1) * persist_indicator[:, :, None]


def shift_back(upstream, persist_indicator):
    masked = upstream * persist_indicator[:, :, None]
    arrived = shifted(masked[:, :1, :], "tensor", -1)
    return jnp.concatenate([masked[:, 1:], arrived], axis=1)


def project(values, matrix):
    return jnp.einsum("rtd,de->rte", values, matrix, preferred_element_type=jnp.float32)


def project_back(upstream, matrix):
    return jnp.einsum("rte,de->rtd", upstream, matrix, preferred_element_type=jnp.float32)


def outer_sum(values, upstream):
    return jnp.einsum("rtd,rte->de", values, upstream, preferred_element_type=jnp.float32)


def mix_back(upstreams, shares, differ, persist_indicator):
    toward = jnp.zeros_like(differ)
    behind = jnp.zeros_like(differ)
    share_grads = []
    for upstream, share in zip(upstreams, shares):
        toward = toward + upstream * share
        behind = behind + upstream * (1.0 - share)
        share_grads.append(jnp.sum(upstream * differ, axis=(0, 1)))
    return (toward + shift_back(behind, persist_indicator), share_grads)


def chain_combine(earlier, later):
    return (
        earlier[0] * later[0],
        later[0] * earlier[1] + later[1],
        later[0] * earlier[2] + later[2],
    )


def scan_fragments(
    lookup_wide, payload_wide, fading_power, reward_coords, text_boundary_indicators
):
    decay_rate = jnp.exp(fading_power)
    row_count, span_len, width_len = lookup_wide.shape
    block_len = min(32, span_len)
    block_count = span_len // block_len
    places = jnp.arange(block_len, dtype=jnp.float32)
    rising = jnp.exp(places[:, None] * decay_rate)
    falling = jnp.exp(-(places[:, None] - 1.0) * decay_rate)
    trailing = jnp.exp(-(block_len - 1.0 - places)[:, None] * decay_rate)
    leading = jnp.exp(-places[:, None] * decay_rate)
    settle = jnp.exp(-block_len * decay_rate)
    before = places[:, None] > places[None, :]

    def split_blocks(values):
        return jnp.swapaxes(
            values.reshape((row_count, block_count, block_len) + values.shape[2:]), 0, 1
        )

    def advance(state_pair, scanned):
        accrued_dividend_sum, accrued_divisor_sum = state_pair
        lookup_narrow, payload_narrow, reset_b = scanned
        tree_levels = jnp.cumsum(reset_b, axis=1)
        linked = ((tree_levels[:, :, None] == tree_levels[:, None, :]) & before).astype(jnp.float32)
        key_term = jnp.exp(lookup_narrow)
        keyed_value = key_term * payload_narrow
        inside_numerator = falling * jnp.einsum(
            "rti,rid->rtd", linked, rising * keyed_value, precision=lax.Precision.HIGHEST
        )
        interior_divisor_sum = falling * jnp.einsum(
            "rti,rid->rtd", linked, rising * key_term, precision=lax.Precision.HIGHEST
        )
        leftover_multiplier = (tree_levels == 0).astype(jnp.float32)[:, :, None] * leading
        reward_multiplier = jnp.exp(reward_coords + lookup_narrow)
        above_total = (
            inside_numerator
            + reward_multiplier * payload_narrow
            + leftover_multiplier * accrued_dividend_sum[:, None, :]
        )
        below_total = (
            interior_divisor_sum
            + reward_multiplier
            + leftover_multiplier * accrued_divisor_sum[:, None, :]
        )
        ending = (tree_levels == tree_levels[:, -1:]).astype(jnp.float32)[:, :, None] * trailing
        intact = (tree_levels[:, -1] == 0).astype(jnp.float32)[:, None] * settle
        new_num = intact * accrued_dividend_sum + jnp.sum(ending * keyed_value, axis=1)
        new_den = intact * accrued_divisor_sum + jnp.sum(ending * key_term, axis=1)
        return ((new_num, new_den), (above_total, below_total))

    initial = jnp.zeros((row_count, width_len), jnp.float32)
    (total_num, total_den), (uppers, lowers) = lax.scan(
        advance,
        (initial, initial),
        (
            split_blocks(lookup_wide),
            split_blocks(payload_wide),
            split_blocks(text_boundary_indicators),
        ),
    )

    def join_blocks(values):
        return jnp.swapaxes(values, 0, 1).reshape(row_count, span_len, width_len)

    tree_levels = jnp.cumsum(text_boundary_indicators, axis=1)
    reaching = (tree_levels == 0).astype(jnp.float32)[:, :, None] * jnp.exp(
        -jnp.arange(span_len, dtype=jnp.float32)[:, None] * decay_rate
    )
    passing = (tree_levels[:, -1] == 0).astype(jnp.float32)[:, None] * jnp.exp(
        -span_len * decay_rate
    )
    return (join_blocks(uppers), join_blocks(lowers), reaching, total_num, total_den, passing)


def recurrence_finish(pieces_list, incoming_num, incoming_den):
    above_total = pieces_list[0] + pieces_list[2] * incoming_num[:, None, :]
    below_total = pieces_list[1] + pieces_list[2] * incoming_den[:, None, :]
    return (above_total / below_total, below_total)


def ffn_apply(inputs, key_weight, value_weight):
    hidden_pre = project(inputs, key_weight)
    hidden = jnp.square(jax.nn.relu(hidden_pre)).astype(jnp.bfloat16)
    return (hidden_pre, hidden, project(hidden, value_weight))


def ffn_grads(inputs, hidden_pre, hidden, upstream, key_weight, value_weight):
    g_hidden = jnp.einsum("rtd,fd->rtf", upstream, value_weight, preferred_element_type=jnp.float32)
    grad_value = jnp.einsum("rtf,rtd->fd", hidden, upstream, preferred_element_type=jnp.float32)
    g_pre = (2.0 * jax.nn.relu(hidden_pre) * g_hidden).astype(jnp.bfloat16)
    grad_key = jnp.einsum("rtd,rtf->df", inputs, g_pre, preferred_element_type=jnp.float32)
    g_inputs = jnp.einsum("rtf,df->rtd", g_pre, key_weight, preferred_element_type=jnp.float32)
    return (g_inputs, grad_key, grad_value)


def wide_shards(
    incoming_embeddings,
    text_boundary_indicators,
    upstream_sensitivity,
    primary_standardize_scaling,
    primary_standardize_offset,
    secondary_standardize_scaling,
    secondary_standardize_offset,
    feature_fading_logarithms,
    present_symbol_reward,
    timemix_lookup_blend,
    timemix_payload_blend,
    timemix_gate_blend,
    timemix_lookup_proj,
    timemix_payload_proj,
    timemix_gate_proj,
    timemix_emit_proj,
    feedmix_lookup_blend,
    feedmix_gate_blend,
    feedmix_gate_proj,
    feedmix_lookup_proj,
    feedmix_payload_proj,
):
    gathered_portions = (
        lax.all_gather(primary_standardize_scaling, ("dp", "tensor"), axis=0, tiled=True),
        lax.all_gather(primary_standardize_offset, ("dp", "tensor"), axis=0, tiled=True),
        lax.all_gather(secondary_standardize_scaling, ("dp", "tensor"), axis=0, tiled=True),
        lax.all_gather(secondary_standardize_offset, ("dp", "tensor"), axis=0, tiled=True),
        lax.all_gather(feature_fading_logarithms, ("dp", "tensor"), axis=0, tiled=True),
        lax.all_gather(present_symbol_reward, ("dp", "tensor"), axis=0, tiled=True),
        lax.all_gather(timemix_lookup_blend, ("dp", "tensor"), axis=0, tiled=True),
        lax.all_gather(timemix_payload_blend, ("dp", "tensor"), axis=0, tiled=True),
        lax.all_gather(timemix_gate_blend, ("dp", "tensor"), axis=0, tiled=True),
        lax.all_gather(timemix_lookup_proj, ("dp", "tensor"), axis=0, tiled=True),
        lax.all_gather(timemix_payload_proj, ("dp", "tensor"), axis=0, tiled=True),
        lax.all_gather(timemix_gate_proj, ("dp", "tensor"), axis=0, tiled=True),
        lax.all_gather(timemix_emit_proj, ("dp", "tensor"), axis=0, tiled=True),
        lax.all_gather(feedmix_lookup_blend, ("dp", "tensor"), axis=0, tiled=True),
        lax.all_gather(feedmix_gate_blend, ("dp", "tensor"), axis=0, tiled=True),
        lax.all_gather(feedmix_gate_proj, ("dp", "tensor"), axis=0, tiled=True),
    )
    initial_scaling_coords = gathered_portions[0].astype(jnp.float32)
    initial_offset_coords = gathered_portions[1].astype(jnp.float32)
    later_scaling_coords = gathered_portions[2].astype(jnp.float32)
    later_offset_coords = gathered_portions[3].astype(jnp.float32)
    fading_power = gathered_portions[4].astype(jnp.float32)
    reward_coords = gathered_portions[5].astype(jnp.float32)
    share_k1 = gathered_portions[6].astype(jnp.float32)
    share_v1 = gathered_portions[7].astype(jnp.float32)
    share_r1 = gathered_portions[8].astype(jnp.float32)
    lookup_coefficients_initial = gathered_portions[9]
    payload_coefficients_initial = gathered_portions[10]
    gate_coefficients_initial = gathered_portions[11]
    emit_coefficients_initial = gathered_portions[12]
    share_k2 = gathered_portions[13].astype(jnp.float32)
    share_r2 = gathered_portions[14].astype(jnp.float32)
    gate_coefficients_later = gathered_portions[15]
    lookup_coefficients_later, payload_coefficients_later = (
        lax.all_gather(feedmix_lookup_proj, "dp", axis=0, tiled=True),
        lax.all_gather(feedmix_payload_proj, "dp", axis=1, tiled=True),
    )
    persist_indicator = (1 - text_boundary_indicators).astype(jnp.float32)
    inputs = incoming_embeddings.astype(jnp.float32)
    normed_one, unit_one, inverse_one = wide_layer_norm(
        inputs, initial_scaling_coords, initial_offset_coords
    )
    prev_one = shift_prev(normed_one, persist_indicator)
    differ_one = normed_one - prev_one
    in_key = (prev_one + differ_one * share_k1).astype(jnp.bfloat16)
    in_value = (prev_one + differ_one * share_v1).astype(jnp.bfloat16)
    in_recept = (prev_one + differ_one * share_r1).astype(jnp.bfloat16)
    initial_lookup_lines = project(in_key, lookup_coefficients_initial)
    initial_payload_lines = project(in_value, payload_coefficients_initial)
    recept_one = project(in_recept, gate_coefficients_initial)
    pieces_list = scan_fragments(
        initial_lookup_lines,
        initial_payload_lines,
        fading_power,
        reward_coords,
        text_boundary_indicators,
    )
    passing = pieces_list[5]
    identity = (jnp.ones_like(passing), jnp.zeros_like(passing), jnp.zeros_like(passing))
    unused_item, incoming_num, incoming_den = carried_in(
        (passing, pieces_list[3], pieces_list[4]), "tensor", chain_combine, identity
    )
    blended_mean_state, below_total = recurrence_finish(pieces_list, incoming_num, incoming_den)
    sig_one = jax.nn.sigmoid(recept_one)
    mixed_att = (sig_one * blended_mean_state).astype(jnp.bfloat16)
    resid_one = inputs + project(mixed_att, emit_coefficients_initial)
    normed_two, unit_two, inverse_two = wide_layer_norm(
        resid_one, later_scaling_coords, later_offset_coords
    )
    prev_two = shift_prev(normed_two, persist_indicator)
    differ_two = normed_two - prev_two
    in_key_two = (prev_two + differ_two * share_k2).astype(jnp.bfloat16)
    in_recept_two = (prev_two + differ_two * share_r2).astype(jnp.bfloat16)
    recept_two = project(in_recept_two, gate_coefficients_later)
    sig_two = jax.nn.sigmoid(recept_two)
    row_inputs = lax.all_gather(in_key_two, "tensor", axis=1, tiled=True)
    hidden_pre, hidden, partial_value = ffn_apply(
        row_inputs, lookup_coefficients_later, payload_coefficients_later
    )
    value_two = lax.psum_scatter(
        partial_value.astype(jnp.bfloat16), "tensor", scatter_dimension=1, tiled=True
    ).astype(jnp.float32)
    layer_out = (resid_one + sig_two * value_two).astype(jnp.bfloat16)
    upstream = upstream_sensitivity.astype(jnp.float32)
    g_value_two = (upstream * sig_two).astype(jnp.bfloat16)
    g_recept_two = (upstream * value_two * sig_two * (1.0 - sig_two)).astype(jnp.bfloat16)
    grad_recept_two = outer_sum(in_recept_two, g_recept_two)
    g_mix_r2 = project_back(g_recept_two, gate_coefficients_later)
    row_grads = lax.all_gather(g_value_two, "tensor", axis=1, tiled=True)
    partial_grad, grad_key_two, grad_value_two = ffn_grads(
        row_inputs,
        hidden_pre,
        hidden,
        row_grads,
        lookup_coefficients_later,
        payload_coefficients_later,
    )
    g_mix_k2 = lax.psum_scatter(
        partial_grad.astype(jnp.bfloat16), "tensor", scatter_dimension=1, tiled=True
    ).astype(jnp.float32)
    sum_key_two, sum_value_two = (
        lax.psum_scatter(
            grad_key_two.astype(jnp.bfloat16), "dp", scatter_dimension=0, tiled=True
        ).astype(jnp.float32),
        lax.psum_scatter(
            grad_value_two.astype(jnp.bfloat16), "dp", scatter_dimension=1, tiled=True
        ).astype(jnp.float32),
    )
    g_normed_two, shares_two = mix_back(
        (g_mix_k2, g_mix_r2), (share_k2, share_r2), differ_two, persist_indicator
    )
    g_resid_part, grad_gain_two, grad_bias_two = wide_norm_back(
        g_normed_two, unit_two, inverse_two, later_scaling_coords
    )
    g_resid = upstream + g_resid_part
    g_branch = g_resid.astype(jnp.bfloat16)
    grad_out_one = outer_sum(mixed_att, g_branch)
    g_mixed = project_back(g_branch, emit_coefficients_initial)
    g_weighted = g_mixed * sig_one
    g_recept_one = (g_mixed * blended_mean_state * sig_one * (1.0 - sig_one)).astype(jnp.bfloat16)
    reaching = pieces_list[2]
    g_in_num = jnp.sum(g_weighted * reaching / below_total, axis=1)
    g_in_den = -jnp.sum(g_weighted * reaching * blended_mean_state / below_total, axis=1)
    unused_item, back_num, back_den = entering(
        (passing, g_in_num, g_in_den), "tensor", chain_combine, identity
    )
    g_passing = back_num * incoming_num + back_den * incoming_den

    def device_fragment(lookup_wide, payload_wide, fading_coords, reward_power):
        shard_pieces = scan_fragments(
            lookup_wide, payload_wide, fading_coords, reward_power, text_boundary_indicators
        )
        local_out, unused_item = recurrence_finish(shard_pieces, incoming_num, incoming_den)
        return (local_out, shard_pieces[3], shard_pieces[4], shard_pieces[5])

    unused_item, reverse_pass_rule = jax.vjp(
        device_fragment, initial_lookup_lines, initial_payload_lines, fading_power, reward_coords
    )
    derivative_lookup_wide, derivative_payload_wide, fading_derivative, reward_derivative = (
        reverse_pass_rule((g_weighted, back_num, back_den, g_passing))
    )
    g_key_one = derivative_lookup_wide.astype(jnp.bfloat16)
    g_value_one = derivative_payload_wide.astype(jnp.bfloat16)
    grad_key_one = outer_sum(in_key, g_key_one)
    grad_value_one = outer_sum(in_value, g_value_one)
    grad_recept_one = outer_sum(in_recept, g_recept_one)
    g_mix_k1 = project_back(g_key_one, lookup_coefficients_initial)
    g_mix_v1 = project_back(g_value_one, payload_coefficients_initial)
    g_mix_r1 = project_back(g_recept_one, gate_coefficients_initial)
    g_normed_one, shares_one = mix_back(
        (g_mix_k1, g_mix_v1, g_mix_r1),
        (share_k1, share_v1, share_r1),
        differ_one,
        persist_indicator,
    )
    g_input_part, grad_gain_one, grad_bias_one = wide_norm_back(
        g_normed_one, unit_one, inverse_one, initial_scaling_coords
    )
    grad_tokens = g_resid + g_input_part
    summed = (
        lax.psum_scatter(grad_gain_one, ("dp", "tensor"), scatter_dimension=0, tiled=True),
        lax.psum_scatter(grad_bias_one, ("dp", "tensor"), scatter_dimension=0, tiled=True),
        lax.psum_scatter(grad_gain_two, ("dp", "tensor"), scatter_dimension=0, tiled=True),
        lax.psum_scatter(grad_bias_two, ("dp", "tensor"), scatter_dimension=0, tiled=True),
        lax.psum_scatter(fading_derivative, ("dp", "tensor"), scatter_dimension=0, tiled=True),
        lax.psum_scatter(reward_derivative, ("dp", "tensor"), scatter_dimension=0, tiled=True),
        lax.psum_scatter(shares_one[0], ("dp", "tensor"), scatter_dimension=0, tiled=True),
        lax.psum_scatter(shares_one[1], ("dp", "tensor"), scatter_dimension=0, tiled=True),
        lax.psum_scatter(shares_one[2], ("dp", "tensor"), scatter_dimension=0, tiled=True),
        lax.psum_scatter(grad_key_one, ("dp", "tensor"), scatter_dimension=0, tiled=True),
        lax.psum_scatter(grad_value_one, ("dp", "tensor"), scatter_dimension=0, tiled=True),
        lax.psum_scatter(grad_recept_one, ("dp", "tensor"), scatter_dimension=0, tiled=True),
        lax.psum_scatter(grad_out_one, ("dp", "tensor"), scatter_dimension=0, tiled=True),
        lax.psum_scatter(shares_two[0], ("dp", "tensor"), scatter_dimension=0, tiled=True),
        lax.psum_scatter(shares_two[1], ("dp", "tensor"), scatter_dimension=0, tiled=True),
        lax.psum_scatter(grad_recept_two, ("dp", "tensor"), scatter_dimension=0, tiled=True),
    )
    return (
        layer_out,
        grad_tokens,
        summed[0],
        summed[1],
        summed[2],
        summed[3],
        summed[4],
        summed[5],
        summed[6],
        summed[7],
        summed[8],
        summed[9],
        summed[10],
        summed[11],
        summed[12],
        summed[13],
        summed[14],
        summed[15],
        sum_key_two,
        sum_value_two,
    )


def pack(tokens, starts, upstream, gain1, bias1, gain2, bias2, fading, reward, mk1, mv1, mr1, wk, wv, wr, wo, mk2, mr2, wg, fk, fv):
    i, c = lax.axis_index("dp"), lax.axis_index("tensor")
    own_rows = wk.shape[0]
    slots = 128 // own_rows
    everywhere = jnp.stack([gain1, bias1, gain2, bias2, fading, reward, mk1, mv1, mr1, mk2, mr2])
    own = jnp.stack([fading, reward, jnp.zeros_like(fading), jnp.zeros_like(fading), jnp.zeros_like(fading)])
    lane = jnp.arange(128)[None, :] // own_rows
    vec = jnp.concatenate([
        jnp.where(lane == (2 * i + c) % slots, jnp.tile(everywhere, (1, slots)), 0),
        jnp.where(lane == i % slots, jnp.tile(own, (1, slots)), 0),
    ]).astype(BF16)
    return wk, wv, wr, wg, wo, fk, fv.T, vec, tokens[0], upstream[0], starts


def land_kernel(*refs):
    count = (len(refs) - 2) // 3
    ins, outs, held = refs[:count], refs[count : 2 * count], refs[2 * count : 3 * count]
    came, left = refs[-2:]
    first = [pltpu.make_async_copy(ins[n], held[n], came.at[n]) for n in range(count)]
    second = [pltpu.make_async_copy(held[n], outs[n], left.at[n]) for n in range(count)]
    for copy in first:
        copy.start()
    for one, other in zip(first, second):
        one.wait()
        other.start()
    for copy in second:
        copy.wait()


def land(*arrays):
    any_, count = pl.BlockSpec(memory_space=pl.ANY), len(arrays)
    size = sum(a.size * a.dtype.itemsize for a in arrays)
    return pl.pallas_call(
        land_kernel,
        out_shape=tuple(jax.ShapeDtypeStruct(a.shape, a.dtype) for a in arrays),
        in_specs=[any_] * count,
        out_specs=(any_,) * count,
        scratch_shapes=[pltpu.VMEM(a.shape, a.dtype) for a in arrays] + [pltpu.SemaphoreType.DMA((count,))] * 2,
        compiler_params=pltpu.CompilerParams(vmem_limit_bytes=63 * MIB),
        cost_estimate=pl.CostEstimate(flops=0, transcendentals=0, bytes_accessed=2 * size),
        name="land",
    )(*arrays)


def shards(*args):
    c = lax.axis_index("tensor")
    i = lax.axis_index("dp")
    own_rows = args[12].shape[0]
    (
        g, layer_out, x, up, ins, kvr, sn, sd, mixed, resid, ins2, pre, act, g_value, g_recept2, vec, rows, keep,
    ) = forward_call(*pack(*args))

    out_k, out_v, out_r, out_g, out_o, out_fk, out_fv, vsum, vother, grad_tokens = backward_call(
        g, x, up, ins, kvr, sn, sd, mixed, resid, ins2, pre, act, g_value, g_recept2, vec, rows, keep
    )
    out_fv = out_fv.T
    layer_out, grad_tokens, out_k, out_v, out_r, out_g, out_o, out_fk = land(
        layer_out, grad_tokens, out_k, out_v, out_r, out_g, out_o, out_fk
    )
    slots = 128 // own_rows
    vtotal = lax.dynamic_slice_in_dim(vsum + vother, (2 * i + c) % slots * own_rows, own_rows, 1)
    own_scan = lax.dynamic_slice_in_dim(vsum, i % slots * own_rows, own_rows, 1)
    return (
        layer_out[None], grad_tokens[None], *(vtotal[n] for n in range(4)), own_scan[SUMS], own_scan[SUMS + 1],
        *(vtotal[n] for n in range(6, 9)), out_k, out_v, out_r, out_o, vtotal[9], vtotal[10], out_g, out_fk, out_fv,
    )


def solution(mesh):
    row, vector, matrix_ = P("dp", "tensor", None), P(("dp", "tensor")), P(("dp", "tensor"), None)
    key, value = P("dp", "tensor"), P("tensor", "dp")
    in_specs = (row, P("dp", "tensor"), row) + (vector,) * 9 + (matrix_,) * 4 + (vector,) * 2 + (matrix_, key, value)
    out_specs = (row, row) + (vector,) * 9 + (matrix_,) * 4 + (vector,) * 2 + (matrix_, key, value)
    body = shards if (mesh.shape["dp"], mesh.shape["tensor"]) == (16, 2) else wide_shards
    return jax.shard_map(body, mesh=mesh, in_specs=in_specs, out_specs=out_specs, check_vma=False)
```
